32 devices in a mesh: dp: 4 (over y, core), ctx: 8 (over z, x).
Axes of the slice: x: 2, y: 2, z: 4, core: 2. Of those that a mesh axis runs over, the one named last changes fastest.
Arguments:
- layer_input: bfloat16 [8, 1024, 1024], P('dp', 'ctx'), may hold values from -6 to 6
- doc_ids: int32 [8, 1024], P('dp'), may hold values from 0 to 4, as said below
- attn_gain: bfloat16 [1024], P(('dp', 'ctx')), may hold values from 0.099609375 to 1.8984375
- query_weight: bfloat16 [1024, 1024], P(('dp', 'ctx')), may hold values from -0.25 to 0.25
- key_weight: bfloat16 [1024, 1024], P(('dp', 'ctx')), may hold values from -0.1875 to 0.1875
- value_weight: bfloat16 [1024, 1024], P(('dp', 'ctx')), may hold values from -0.1875 to 0.1875
- out_weight: bfloat16 [1024, 1024], P(('dp', 'ctx')), may hold values from -1.5 to 1.5
- mlp_gain: bfloat16 [1024], P(('dp', 'ctx')), may hold values from 0.099609375 to 1.8984375
- gate_weight: bfloat16 [1024, 4096], P(('dp', 'ctx')), may hold values from -0.1875 to 0.1875
- up_weight: bfloat16 [1024, 4096], P(('dp', 'ctx')), may hold values from -0.1875 to 0.1875
- down_weight: bfloat16 [4096, 1024], P(('dp', 'ctx')), may hold values from -0.1875 to 0.1875
- out_grad: bfloat16 [8, 1024, 1024], P('dp', 'ctx'), may hold values from -6 to 6
Outputs:
- layer_output: bfloat16 [8, 1024, 1024], P('dp', 'ctx')
- input_grad: float32 [8, 1024, 1024], P('dp', 'ctx')
- attn_gain_grad: float32 [1024], P(('dp', 'ctx'))
- query_grad: float32 [1024, 1024], P(('dp', 'ctx'))
- key_grad: float32 [1024, 1024], P(('dp', 'ctx'))
- value_grad: float32 [1024, 1024], P(('dp', 'ctx'))
- out_proj_grad: float32 [1024, 1024], P(('dp', 'ctx'))
- mlp_gain_grad: float32 [1024], P(('dp', 'ctx'))
- gate_grad: float32 [1024, 4096], P(('dp', 'ctx'))
- up_grad: float32 [1024, 4096], P(('dp', 'ctx'))
- down_grad: float32 [4096, 1024], P(('dp', 'ctx'))
The draws below stay inside these ranges and needn't reach their ends.
Inputs may be any that keep to these rules, and one draw needn't show every extreme that they name: Within each sequence doc_ids start at 0 and never fall; the rows of one value form one document of 60 to 800 rows, except the document at one end of a sequence, which may be shorter; every sequence holds one document of exactly 800 rows, at its start or at its end; in the first sequence all other documents but the one at its other end have exactly 60 rows.
All inputs are finite; a program needn't handle non-finite values.
Results may differ from the reference program's by a relative error of at most 0.015.
Values may be sent and summed in bfloat16 or wider, within the bound.
A program may use at most 256 MiB of HBM per device.

```python
from functools import partial
import jax
import jax.numpy as jnp
from jax import lax

D = 1024
HEADS = 16
HEAD = 64
FF = 4096
SEQ = 1024
DOC_MIN = 60
DOC_MAX = 800
SEQS = 8


def draw_doc_ids(key, part):
    pieces = SEQ // DOC_MIN + 2
    lengths = jax.random.randint(jax.random.fold_in(key, 11), (SEQS, pieces), DOC_MIN, DOC_MAX + 1)
    lengths = lengths.at[0, :].set(DOC_MIN)
    lengths = lengths.at[:, 0].set(DOC_MAX)
    bounds = jnp.cumsum(lengths, axis=1)
    places = jnp.arange(SEQ)
    labels = jnp.sum((bounds[:, :, None] <= places[None, None, :]).astype(jnp.int32), axis=1)
    mirror = jax.random.randint(jax.random.fold_in(key, 12), (SEQS, 1), 0, 2)
    turned = labels[:, -1:] - labels[:, ::-1]
    return jnp.where(mirror == 1, turned, labels).astype(jnp.int32)


def levels(own_key, shape, cuts, smallest, top_value):
    def one(axis_at, parts):
        draws = jax.random.uniform(jax.random.fold_in(jax.random.fold_in(own_key, 6), axis_at), (parts,), jnp.float32, smallest / len(cuts), top_value / len(cuts))
        return jnp.repeat(jnp.exp(draws), shape[axis_at] // parts).reshape((-1,) + (1,) * (len(shape) - axis_at - 1))

    level = one(*cuts[0])
    for cut in cuts[1:]:
        level = level * one(*cut)
    return level


def centred(rng, extent, width, limit, split=(), held_as=jnp.bfloat16):
    values = jax.random.normal(rng, extent, jnp.float32) * width
    if len(split) > 0:
        values = levels(rng, extent, split, -0.22, 0.18) * values
    return jnp.clip(values, min=-limit, max=limit).astype(held_as)


def setup_inputs(seed: int = 0) -> dict:
    arg_keys = jax.random.split(jax.random.key(seed), 13)
    return {
        "layer_input": centred(arg_keys[0], (SEQS, SEQ, D), 1.0, 6.0, ((0, 4), (1, 8))),
        "doc_ids": draw_doc_ids(jax.random.fold_in(arg_keys[12], 71), 0),
        "attn_gain": jnp.clip(1.0 + 0.18 * jax.random.normal(arg_keys[2], (D,), jnp.float32), 0.099609375, 1.8984375).astype(jnp.bfloat16),
        "query_weight": centred(arg_keys[3], (D, D), (D // 2) ** -0.5, 0.25, ((0, 32),)),
        "key_weight": centred(arg_keys[4], (D, D), D ** -0.5, 0.1875, ((0, 32),)),
        "value_weight": centred(arg_keys[5], (D, D), D ** -0.5, 0.1875, ((0, 32),)),
        "out_weight": centred(arg_keys[6], (D, D), (D // 64) ** -0.5, 1.5, ((0, 32),)),
        "mlp_gain": jnp.clip(1.0 + 0.18 * jax.random.normal(arg_keys[7], (D,), jnp.float32), 0.099609375, 1.8984375).astype(jnp.bfloat16),
        "gate_weight": centred(arg_keys[8], (D, FF), D ** -0.5, 0.1875, ((0, 32),)),
        "up_weight": centred(arg_keys[9], (D, FF), D ** -0.5, 0.1875, ((0, 32),)),
        "down_weight": centred(arg_keys[10], (FF, D), (FF // 4) ** -0.5, 0.1875, ((0, 32),)),
        "out_grad": centred(arg_keys[11], (SEQS, SEQ, D), 1.0, 6.0, ((0, 4), (1, 8))),
    }


@jax.custom_vjp
def low(v):
    return lax.optimization_barrier(v.astype(jnp.bfloat16)).astype(jnp.float32)

@jax.custom_vjp
def low_back(v):
    return v

def low_keep(v):
    return (low(v), None)

def low_pass(kept, grad):
    return (grad,)

def back_keep(v):
    return (v, None)

def back_low(kept, grad):
    return (low(grad),)
low.defvjp(low_keep, low_pass)
low_back.defvjp(back_keep, back_low)
EPS = 1e-05
HIGH = lax.Precision.HIGHEST

def matmul(left, right):
    return jnp.dot(left, right, precision=HIGH, preferred_element_type=jnp.float32)

def rms_norm(rows, gain):
    return rows * lax.rsqrt(lax.optimization_barrier(jnp.mean(rows * rows, axis=-1, keepdims=True)) + EPS) * gain

def head_attend(allowed, operands):
    query, keys, values = operands
    scores = low_back(matmul(query, keys.T) * HEAD ** (-0.5))
    scores = jnp.where(allowed, scores, -1e+30)
    probs = jax.nn.softmax(scores, axis=-1)
    return matmul(low(probs), values)

def by_heads(array):
    return jnp.transpose(array.reshape(SEQ, HEADS, HEAD), (1, 0, 2))

def layer(params, rows, labels):
    attn_gain, query_weight, key_weight, value_weight, out_weight, mlp_gain, gate_weight, up_weight, down_weight = params
    normed = low(rms_norm(rows, attn_gain))
    query = low_back(low(matmul(normed, query_weight)))
    keys = low_back(low(matmul(normed, key_weight)))
    values = low_back(low(matmul(normed, value_weight)))
    places = jnp.arange(SEQ)
    allowed = (labels[:, None] == labels[None, :]) & (places[None, :] <= places[:, None])
    mixed = lax.map(jax.checkpoint(partial(head_attend, allowed)), (by_heads(query), by_heads(keys), by_heads(values)))
    attended = low_back(low(jnp.transpose(mixed, (1, 0, 2)).reshape(SEQ, D)))
    branch = low_back(matmul(attended, out_weight))
    middle = rows + branch
    normed_mlp = low(rms_norm(middle, mlp_gain))
    gate = low_back(matmul(normed_mlp, gate_weight))
    upward = low_back(matmul(normed_mlp, up_weight))
    hidden = low(jax.nn.silu(gate) * upward)
    return middle + low_back(matmul(hidden, down_weight))

def reference(layer_input, doc_ids, attn_gain, query_weight, key_weight, value_weight, out_weight, mlp_gain, gate_weight, up_weight, down_weight, out_grad):
    params = tuple((w.astype(jnp.float32) for w in (attn_gain, query_weight, key_weight, value_weight, out_weight, mlp_gain, gate_weight, up_weight, down_weight)))

    def one_sequence(totals, operands):
        rows, labels, cotangent = operands
        output, pullback = jax.vjp(lambda weights, inputs: layer(weights, inputs, labels), params, rows)
        grads, row_grad = pullback(cotangent)
        totals = jax.tree.map(lambda a, b: a + b, totals, grads)
        return (totals, (output.astype(jnp.bfloat16), row_grad))
    zeros = jax.tree.map(jnp.zeros_like, params)
    totals, results = lax.scan(one_sequence, zeros, (layer_input.astype(jnp.float32), doc_ids, out_grad.astype(jnp.float32)))
    outputs, row_grads = results
    return (outputs, row_grads, totals[0], totals[1], totals[2], totals[3], totals[4], totals[5], totals[6], totals[7], totals[8])
```

```python
import functools

import jax
import jax.numpy as jnp
from jax import lax
from jax.experimental import pallas as pl
from jax.experimental.pallas import tpu as pltpu
from jax.sharding import PartitionSpec as P

HEAD = 64


EPS = 1e-05
MESH = pl.DeviceIdType.MESH
F32 = jnp.float32
BF16 = jnp.bfloat16
LOG2E = 1.4426950408889634
ANY = pl.BlockSpec(memory_space=pl.ANY)
VMEM = pl.BlockSpec(memory_space=pltpu.VMEM)


class Wires:
    def __init__(self, send, recv):
        dp, ctx = lax.axis_index("dp"), lax.axis_index("ctx")
        self.x, self.y = ctx % 2, dp // 2
        self.z, self.k = ctx // 2, dp % 2
        self.send, self.recv = send, recv
        self.used = 0

    def slots(self, count):
        first = self.used
        self.used += count
        return first

    def at(self, x, y, z, k):
        return (2 * y + k, 2 * z + x)

    def copy(self, source, target, device, slot, recv_slot=None):
        return pltpu.make_async_remote_copy(
            src_ref=source,
            dst_ref=target,
            send_sem=self.send.at[slot],
            recv_sem=self.recv.at[slot if recv_slot is None else recv_slot],
            device_id=device,
            device_id_type=MESH,
        )

    def greet(self, peers):
        barrier = pltpu.get_barrier_semaphore()
        for peer in peers:
            pl.semaphore_signal(barrier, inc=1, device_id=peer, device_id_type=MESH)
        pl.semaphore_wait(barrier, len(peers))

    def group_peers(self):
        x, y, z, k = self.x, self.y, self.z, self.k
        return [self.at(1 - x, y, z, k), self.at(x, y, z, 1 - k), self.at(1 - x, y, z, 1 - k)]

    def line_peers(self):
        x, y, z, k = self.x, self.y, self.z, self.k
        return [self.at(x, y, (z + i) % 4, k) for i in (1, 2, 3)]

    def cross_peers(self):
        x, y, z, k = self.x, self.y, self.z, self.k
        return [self.at(x, y, (z + i) % 4, 1 - k) for i in (1, 2, 3)]

    def pair_peer(self):
        return self.at(self.x, 1 - self.y, self.z, self.k)


class Spread:
    def __init__(self, wires, block, own=None):
        self.w, self.block, self.own = wires, block, own
        self.lines, self.pairs = wires.slots(4), wires.slots(4)

    def line(self, i, z, own=None):
        w = self.w
        ref = self.block(w.y, z)
        target = w.at(w.x, w.y, (w.z + i) % 4, w.k)
        return w.copy(ref if own is None else own, ref, target, self.lines + i)

    def pair(self, i, y, own=None):
        w = self.w
        ref = self.block(y, (w.z + 4 - i) % 4)
        return w.copy(ref if own is None else own, ref, w.pair_peer(), self.pairs + i)

    def start(self):
        for i in (2, 1, 3):
            self.line(i, self.w.z, self.own).start()
        self.pair(0, self.w.y, self.own).start()

    def forward(self, i):
        self.line(i, (self.w.z + 4 - i) % 4).wait_recv()
        self.pair(i, self.w.y).start()

    def arrive(self, i):
        self.pair(i, 1 - self.w.y).wait_recv()

    def drain(self):
        for i in (1, 2, 3):
            self.line(i, self.w.z, self.own).wait_send()
        for i in range(4):
            self.pair(i, self.w.y).wait_send()


class Share:
    def __init__(self, wires, block, own=None):
        self.w, self.block, self.own = wires, block, own
        self.first = wires.slots(3)

    def piece(self, i):
        w = self.w
        core, across = w.at(w.x, w.y, w.z, 1 - w.k), w.at(1 - w.x, w.y, w.z, w.k)
        ref = self.block(w.x if i < 2 else 1 - w.x, w.k)
        source = ref if self.own is None or i == 2 else self.own
        return w.copy(source, ref, across if i == 0 else core, self.first + i)

    def landed(self, i):
        w = self.w
        ref = self.block(*[(1 - w.x, w.k), (w.x, 1 - w.k), (1 - w.x, 1 - w.k)][i])
        return w.copy(ref, ref, w.at(w.x, w.y, w.z, 1 - w.k), self.first + i)

    def start(self):
        self.piece(0).start()
        self.piece(1).start()

    def forward(self):
        self.landed(0).wait_recv()
        self.piece(2).start()

    def arrive(self):
        self.landed(1).wait_recv()
        self.landed(2).wait_recv()

    def drain(self):
        for i in range(3):
            self.piece(i).wait_send()


class Deal:
    def __init__(self, wires, outgoing, incoming):
        self.w, self.outgoing, self.incoming = wires, outgoing, incoming
        self.first = wires.slots(3)

    def mate(self, i):
        w = self.w
        return [(1 - w.x, w.k), (w.x, 1 - w.k), (1 - w.x, 1 - w.k)][i]

    def piece(self, i):
        w = self.w
        x, k = self.mate(i)
        return w.copy(
            self.outgoing(x, k), self.incoming(w.x, w.k), w.at(x, w.y, w.z, k), self.first + i
        )

    def landed(self, i):
        x, k = self.mate(i)
        ref = self.incoming(x, k)
        return self.w.copy(ref, ref, self.w.at(x, self.w.y, self.w.z, k), self.first + i)

    def start(self):
        for i in range(3):
            self.piece(i).start()

    def arrive(self):
        for i in range(3):
            self.landed(i).wait_recv()

    def drain(self):
        for i in range(3):
            self.piece(i).wait_send()


class Visit:
    def __init__(self, wires, home, full, local):
        self.w, self.home, self.full, self.local = wires, home, full, local
        self.first = wires.slots(2)
        w = wires
        self.own = [jnp.logical_and(w.z == 2 * w.k + j, w.z % 2 == w.k) for j in range(2)]

    def piece(self, j):
        w = self.w
        return w.copy(
            self.home.at[j],
            self.full(w.x, w.z),
            w.at(w.x, w.y, 2 * w.k + j, w.z % 2),
            self.first + j,
            self.first + w.z // 2,
        )

    def stay(self, j):
        return pltpu.make_async_copy(self.home.at[j], self.full(self.w.x, self.w.z), self.local)

    def landed(self, i):
        w = self.w
        ref = self.full(w.x, w.k + 2 * i)
        return w.copy(ref, ref, w.pair_peer(), self.first + i)

    def here(self, i):
        w = self.w
        return jnp.logical_and(w.k + 2 * i == w.z, w.z // 2 == w.k)

    def start(self):
        for j in range(2):
            pl.when(self.own[j])(lambda: self.stay(j).start())
            pl.when(jnp.logical_not(self.own[j]))(lambda: self.piece(j).start())

    def arrive(self):
        for j in range(2):
            pl.when(self.own[j])(lambda: self.stay(j).wait())
        for i in range(2):
            pl.when(jnp.logical_not(self.here(i)))(lambda: self.landed(i).wait_recv())

    def drain(self):
        for j in range(2):
            pl.when(jnp.logical_not(self.own[j]))(lambda: self.piece(j).wait_send())


class Return:
    def __init__(self, wires, done, home, local):
        self.w, self.done, self.home, self.local = wires, done, home, local
        self.first = wires.slots(2)

    def own(self, i):
        w = self.w
        return jnp.logical_and(2 * i + w.k == w.z, w.z // 2 == w.k)

    def piece(self, i):
        w = self.w
        return w.copy(
            self.done.at[i],
            self.home.at[w.z % 2],
            w.at(w.x, w.y, 2 * i + w.k, w.z // 2),
            self.first + i,
            self.first + w.z % 2,
        )

    def stay(self, i):
        return pltpu.make_async_copy(self.done.at[i], self.home.at[self.w.z % 2], self.local)

    def here(self, j):
        w = self.w
        return jnp.logical_and(2 * w.k + j == w.z, w.z % 2 == w.k)

    def landed(self, j):
        ref = self.home.at[j]
        return self.w.copy(ref, ref, self.w.pair_peer(), self.first + j)

    def start(self):
        for i in range(2):
            pl.when(self.own(i))(lambda: self.stay(i).start())
            pl.when(jnp.logical_not(self.own(i)))(lambda: self.piece(i).start())

    def arrive(self):
        for i in range(2):
            pl.when(self.own(i))(lambda: self.stay(i).wait())
        for j in range(2):
            pl.when(jnp.logical_not(self.here(j)))(lambda: self.landed(j).wait_recv())

    def drain(self):
        for i in range(2):
            pl.when(jnp.logical_not(self.own(i)))(lambda: self.piece(i).wait_send())


def sems(count):
    return [
        pltpu.SemaphoreType.DMA((count,)),
        pltpu.SemaphoreType.DMA((count,)),
        pltpu.SemaphoreType.DMA,
    ]


def kernel_call(body, name, outs, ins, out_specs, scratch, collective=None):
    return pl.pallas_call(
        body,
        name=name,
        out_shape=outs,
        in_specs=ins,
        out_specs=out_specs,
        scratch_shapes=scratch,
        compiler_params=pltpu.CompilerParams(
            collective_id=collective,
            has_side_effects=collective is not None,
            vmem_limit_bytes=58 << 20,
        ),
    )


def shaped(*shape, dtype=BF16):
    return jax.ShapeDtypeStruct(shape, dtype)


def pack_rows(columns, shards, packed):
    for rank in range(4):
        at = 0
        for shard in shards:
            for start, width in columns(rank):
                packed[rank, :, at : at + width] = shard[:, start : start + width]
                at += width


def head_columns(rank):
    return [(256 * rank, 256)]


def hidden_columns(rank):
    x, k = rank // 2, rank % 2
    return [(128 * (8 * (2 * y + k) + 2 * z + x), 128) for y in range(2) for z in range(4)]


def gather_body(
    rows, cots, ids, wq, wk, wv, wo, wg, wu, wd, gains,
    rows_all, cots_all, ids_all, heads_all, out_all, hidden_all, down_all, gains_all,
    heads_pack, hidden_pack, send, recv, local,
):
    w = Wires(send, recv)
    x, y, z, k = w.x, w.y, w.z, w.k
    w.greet(w.group_peers() + w.line_peers() + w.cross_peers() + [w.pair_peer()])

    def stay(source, target, index):
        copy = pltpu.make_async_copy(source, target, local.at[index])
        copy.start()
        return copy

    visit_rows = Visit(w, rows, lambda x, z: rows_all.at[z // 2, z % 2, x], local.at[0])
    visit_rows.start()
    pack_rows(head_columns, (wq, wk, wv), heads_pack)
    rank = 2 * x + k
    deal_heads = Deal(
        w, lambda x, k: heads_pack.at[2 * x + k], lambda sx, sk: heads_all.at[y, sk, z, sx]
    )
    deal_heads.start()
    stays = [
        stay(heads_pack.at[rank], heads_all.at[y, k, z, x], 1),
        stay(wo, out_all.at[y, k, z, x], 2),
        stay(gains, gains_all.at[y, k, z, x], 3),
        stay(wd, down_all.at[y, z], 4),
        stay(ids, ids_all.at[k], 5),
    ]
    slot = w.slots(1)
    swap = w.copy(ids, ids_all.at[k], w.at(x, y, z, 1 - k), slot)
    swap.start()
    spread_gains = Spread(w, lambda y, z: gains_all.at[y, k, z, x], gains)
    spread_gains.start()
    spread_out = Spread(w, lambda y, z: out_all.at[y, k, z, x], wo)
    spread_out.start()
    pack_rows(hidden_columns, (wg, wu), hidden_pack)
    deal_hidden = Deal(
        w, lambda x, k: hidden_pack.at[2 * x + k], lambda sx, sk: hidden_all.at[y, sk, z, sx]
    )
    deal_hidden.start()
    stays.append(stay(hidden_pack.at[rank], hidden_all.at[y, k, z, x], 6))
    visit_cots = Visit(w, cots, lambda x, z: cots_all.at[z // 2, z % 2, x], local.at[7])
    visit_cots.start()
    for copy in stays:
        copy.wait()
    deal_heads.arrive()
    spread_heads = Spread(w, lambda y, z: heads_all.at[y, :, z])
    spread_heads.start()
    visit_rows.arrive()
    share_rows = Share(w, lambda x, k: rows_all.at[:, k, x])
    share_rows.start()
    deal_hidden.arrive()
    spread_hidden = Spread(w, lambda y, z: hidden_all.at[y, :, z])
    spread_hidden.start()
    share_rows.forward()
    spread_down = Spread(w, lambda y, z: down_all.at[y, z], wd)
    spread_down.start()
    visit_cots.arrive()
    share_cots = Share(w, lambda x, k: cots_all.at[:, k, x])
    share_cots.start()
    spreads = [spread_gains, spread_heads, spread_out, spread_hidden, spread_down]
    for spread in spreads:
        for i in (1, 3, 2):
            spread.forward(i)
    share_cots.forward()
    for spread in (spread_gains, spread_out):
        for i in range(4):
            spread.arrive(i)
    share_gains = Share(w, lambda x, k: gains_all.at[:, k, :, x])
    share_gains.start()
    share_out = Share(w, lambda x, k: out_all.at[:, k, :, x])
    share_out.start()
    for spread in (spread_heads, spread_hidden, spread_down):
        for i in range(4):
            spread.arrive(i)
    share_gains.forward()
    share_out.forward()
    shares = [share_rows, share_cots, share_gains, share_out]
    for share in shares:
        share.arrive()
    swap.wait()
    for part in [visit_rows, visit_cots, deal_heads, deal_hidden] + spreads + shares:
        part.drain()


def gather(rows, cots, ids, wq, wk, wv, wo, wg, wu, wd, gains):
    r, d, f = rows.shape[1], rows.shape[2], wg.shape[1]
    piece = wq.shape[0]
    outs = (
        shaped(2, 2, 2, r, d),
        shaped(2, 2, 2, r, d),
        shaped(2, *ids.shape, dtype=jnp.int32),
        shaped(2, 2, 4, 2, piece, 3 * d // 4),
        shaped(2, 2, 4, 2, piece, d),
        shaped(2, 2, 4, 2, piece, f // 2),
        shaped(2, 4, wd.shape[0], d),
        shaped(2, 2, 4, 2, *gains.shape),
    )
    return kernel_call(
        gather_body,
        "gather",
        outs,
        [ANY, ANY, ANY, VMEM, VMEM, VMEM, ANY, VMEM, VMEM, ANY, ANY],
        (ANY,) * len(outs),
        [pltpu.VMEM((4, piece, 3 * d // 4), BF16), pltpu.VMEM((4, piece, f // 2), BF16)]
        + sems(96)[:2]
        + [pltpu.SemaphoreType.DMA((8,))],
        collective=0,
    )(rows, cots, ids, wq, wk, wv, wo, wg, wu, wd, gains)


def share_body(block, whole, send, recv, local):
    w = Wires(send, recv)
    w.greet(w.group_peers()[:2])
    share = Share(w, lambda x, k: whole.at[x, k], block)
    stay = pltpu.make_async_copy(block, whole.at[w.x, w.k], local)
    stay.start()
    share.start()
    share.forward()
    share.arrive()
    stay.wait()
    share.drain()


def share_group(block, collective):
    return kernel_call(
        share_body,
        "share",
        shaped(2, 2, *block.shape),
        [ANY],
        ANY,
        sems(4),
        collective=collective,
    )(block)


def sum_body(part, total, got_core, got_across, out_across, send, recv, local):
    w = Wires(send, recv)
    x, k = w.x, w.k
    w.greet(w.group_peers()[:2])
    slots = w.slots(2)
    first = w.copy(part.at[:, 1 - k], got_core, w.at(x, w.y, w.z, 1 - k), slots)
    second = w.copy(out_across, got_across, w.at(1 - x, w.y, w.z, k), slots + 1)
    first.start()
    first.wait()
    for i in range(2):
        out_across[i] = (
            part[i, k, 1 - x].astype(F32) + got_core[i, 1 - x].astype(F32)
        ).astype(BF16)
    second.start()
    for i in range(2):
        total[i] = part[i, k, x].astype(F32) + got_core[i, x].astype(F32)
    second.wait()
    for i in range(2):
        total[i] += got_across[i].astype(F32)


def sum_group(part, collective):
    _, _, _, r, d = part.shape
    return kernel_call(
        sum_body,
        "sum_group",
        shaped(2, r, d, dtype=F32),
        [VMEM],
        VMEM,
        [
            pltpu.VMEM((2, 2, r, d), BF16),
            pltpu.VMEM((2, r, d), BF16),
            pltpu.VMEM((2, r, d), BF16),
        ]
        + sems(2),
        collective=collective,
    )(part)


def home_body(done, home, send, recv, local):
    w = Wires(send, recv)
    x, y, z, k = w.x, w.y, w.z, w.k
    w.greet(w.line_peers() + w.cross_peers() + [w.at(x, y, z, 1 - k)])
    back = Return(w, done, home, local)
    back.start()
    back.arrive()
    back.drain()


def send_home(done, collective):
    return kernel_call(
        home_body,
        "send_home",
        shaped(*done.shape, dtype=done.dtype),
        [ANY],
        ANY,
        sems(2),
        collective=collective,
    )(done)


class Fold:
    def __init__(self, wires, part, got_pair, out_line, got_line, mine, ours):
        self.w, self.part = wires, part
        self.got_pair, self.out_line, self.got_line, self.mine = got_pair, out_line, got_line, mine
        self.ours = ours
        self.pairs, self.lines = wires.slots(1), wires.slots(4)

    def pair(self):
        w = self.w
        return w.copy(self.part(1 - w.y), self.got_pair, w.pair_peer(), self.pairs)

    def line(self, i):
        w = self.w
        z = (w.z + i) % 4
        return w.copy(
            self.out_line.at[z], self.got_line.at[i - 1], w.at(w.x, w.y, z, w.k), self.lines + i
        )

    def start(self):
        self.pair().start()

    def send(self):
        w = self.w
        self.pair().wait_recv()
        for i in (2, 1, 3):
            z = (w.z + i) % 4
            self.out_line[z] = (
                self.ours(z).astype(F32) + self.got_pair[z].astype(F32)
            ).astype(self.out_line.dtype)
            self.line(i).start()
        self.mine[...] = self.ours(w.z).astype(F32) + self.got_pair[w.z].astype(F32)

    def finish(self):
        for i in (2, 1, 3):
            self.line(i).wait_recv()
            self.mine[...] += self.got_line[i - 1].astype(F32)

    def drain(self):
        self.pair().wait_send()
        for i in (1, 2, 3):
            self.line(i).wait_send()


def reduce_body(
    heads, out, hidden, down, gains,
    q_out, k_out, v_out, o_out, g_out, u_out, d_out, gain_out,
    heads_pair, heads_line, heads_got, heads_mine, heads_deal, heads_all,
    hidden_pair, hidden_line, hidden_got, hidden_mine, hidden_deal, hidden_all,
    down_pair, down_line, down_got,
    out_pair, out_line, out_got, out_mine, out_deal, out_home,
    gains_pair, gains_line, gains_got, gains_mine, gains_all,
    send, recv, local,
):
    w = Wires(send, recv)
    x, y, z, k = w.x, w.y, w.z, w.k
    rank = 2 * x + k
    w.greet(w.group_peers() + w.line_peers() + [w.pair_peer()])
    folds = [
        Fold(w, lambda y: down.at[y], down_pair, down_line, down_got, d_out, lambda z: down[y, z]),
        Fold(
            w, lambda y: hidden.at[y], hidden_pair, hidden_line, hidden_got, hidden_mine,
            lambda z: hidden[y, z],
        ),
        Fold(
            w, lambda y: heads.at[y], heads_pair, heads_line, heads_got, heads_mine,
            lambda z: heads[y, z],
        ),
        Fold(
            w, lambda y: gains.at[y], gains_pair, gains_line, gains_got, gains_mine,
            lambda z: gains[y, z],
        ),
    ]
    for fold in folds:
        fold.start()
    base = w.slots(6)
    owner = y == x
    out_across = w.copy(out, out_pair, w.pair_peer(), base)
    pl.when(jnp.logical_not(owner))(lambda: out_across.start())

    def out_piece(i):
        zi = (z + i) % 4
        return w.copy(out_line.at[zi], out_got.at[i - 1], w.at(x, y, zi, k), base + i)

    for fold in folds[:2]:
        fold.send()

    @pl.when(owner)
    def _():
        out_across.wait_recv()
        for i in (2, 1, 3):
            zi = (z + i) % 4
            out_line[zi] = (out[zi].astype(F32) + out_pair[zi].astype(F32)).astype(BF16)
            out_piece(i).start()
        out_mine[...] = out[z].astype(F32) + out_pair[z].astype(F32)

    for fold in folds[2:]:
        fold.send()
    for fold in folds[:2]:
        fold.finish()
    hidden_deal[...] = hidden_mine[...].astype(BF16)
    deal_hidden = Deal(w, lambda x, k: hidden_deal.at[k, x], lambda x, k: hidden_all.at[2 * x + k])
    deal_hidden.start()
    for fold in folds[2:]:
        fold.finish()
    heads_deal[...] = heads_mine[...].astype(BF16)
    deal_heads = Deal(w, lambda x, k: heads_deal.at[k, x], lambda x, k: heads_all.at[2 * x + k])
    deal_heads.start()
    gains_all[rank] = gains_mine[...]
    deal_gains = Deal(w, lambda x, k: gains_mine, lambda x, k: gains_all.at[2 * x + k])
    deal_gains.start()
    out_last = w.copy(out_deal, out_home, w.at(1 - x, y, z, k), base + 4)

    @pl.when(owner)
    def _():
        for i in (2, 1, 3):
            out_piece(i).wait_recv()
            out_mine[...] += out_got[i - 1].astype(F32)
        out_deal[...] = out_mine[1 - x].astype(BF16)
        out_last.start()
        o_out[...] = out_mine[x]

    hidden_all[rank] = hidden_deal[k, x]
    heads_all[rank] = heads_deal[k, x]
    deal_hidden.arrive()
    for r in range(4):
        for half, target in enumerate((g_out, u_out)):
            for j, (start, width) in enumerate(hidden_columns(r)):
                at = 128 * j + half * 1024
                target[:, start : start + width] = hidden_all[r, :, at : at + width].astype(F32)
    deal_heads.arrive()
    for r in range(4):
        for j, target in enumerate((q_out, k_out, v_out)):
            at = 256 * j
            target[:, 256 * r : 256 * r + 256] = heads_all[r, :, at : at + 256].astype(F32)
    deal_gains.arrive()
    gain_out[...] = gains_all[0] + gains_all[1] + gains_all[2] + gains_all[3]

    @pl.when(jnp.logical_not(owner))
    def _():
        out_last.wait_recv()
        o_out[...] = out_home[...].astype(F32)

    for part in folds + [deal_hidden, deal_heads, deal_gains]:
        part.drain()

    @pl.when(owner)
    def _():
        for i in (1, 2, 3):
            out_piece(i).wait_send()
        out_last.wait_send()

    pl.when(jnp.logical_not(owner))(lambda: out_across.wait_send())


def reduce_all(heads, out, hidden, down, gains):
    p, h, u = heads.shape[4], heads.shape[5], hidden.shape[5]
    d = down.shape[3]
    r = down.shape[2]
    outs = (
        shaped(p, d, dtype=F32),
        shaped(p, d, dtype=F32),
        shaped(p, d, dtype=F32),
        shaped(p, d, dtype=F32),
        shaped(p, 2 * u, dtype=F32),
        shaped(p, 2 * u, dtype=F32),
        shaped(r, d, dtype=F32),
        shaped(8, 128, dtype=F32),
    )

    def room(*shape, dtype=BF16):
        return pltpu.VMEM(shape, dtype)

    scratch = []
    for width in (h, u):
        scratch += [
            room(4, 2, 2, p, width),
            room(4, 2, 2, p, width),
            room(3, 2, 2, p, width),
            room(2, 2, p, width, dtype=F32),
            room(2, 2, p, width),
            room(4, p, width),
        ]
    scratch += [room(4, r, d), room(4, r, d), room(3, r, d)]
    scratch += [
        room(4, 2, p, d),
        room(4, 2, p, d),
        room(3, 2, p, d),
        room(2, p, d, dtype=F32),
        room(p, d),
        room(p, d),
    ]
    scratch += [room(4, 8, 128, dtype=F32), room(4, 8, 128, dtype=F32)]
    scratch += [room(3, 8, 128, dtype=F32), room(8, 128, dtype=F32), room(4, 8, 128, dtype=F32)]
    return kernel_call(
        reduce_body,
        "reduce_all",
        outs,
        [VMEM] * 5,
        (VMEM,) * len(outs),
        scratch + sems(40),
        collective=7,
    )(heads, out, hidden, down, gains)


def allowed_keys(ids_col, ids_row, keys, start):
    same = ids_col[:keys, :1] == ids_row[:, start : start + 256]
    key = lax.broadcasted_iota(jnp.int32, (keys, 256), 0)
    query = lax.broadcasted_iota(jnp.int32, (keys, 256), 1) + start
    return jnp.logical_and(same, key <= query)


def dots(left, right, dims):
    return lax.dot_general(left, right, (dims, ((), ())), preferred_element_type=F32)


def only_head(array, head):
    lane = lax.broadcasted_iota(jnp.int32, array.shape, 1)
    return jnp.where(lane // HEAD == head, array, jnp.zeros_like(array))


def attend_body(q, k, v_turned, ids_col, ids_row, mixed, logsum):
    head = pl.program_id(0)
    for block in range(4):
        start, keys = 256 * block, 256 * block + 256
        query = only_head(q[start : start + 256, :], head)
        scores = dots(k[:keys, :], query, ((1,), (1,)))
        mask = allowed_keys(ids_col, ids_row, keys, start)
        scores = jnp.where(mask, scores * (HEAD**-0.5 * LOG2E), -1e30)
        top = jnp.max(scores, axis=0, keepdims=True)
        lifted = jnp.exp2(scores - top)
        total = jnp.sum(lifted, axis=0, keepdims=True)
        probs = (lifted * (1.0 / total)).astype(BF16)
        values = v_turned[pl.ds(pl.multiple_of(head * HEAD, HEAD), HEAD), :keys]
        mixed[:, start : start + 256] = dots(values, probs, ((1,), (0,))).astype(BF16)
        logsum[0, :, start : start + 256] = top + jnp.log2(total)


def attend(q, k, v_turned, ids_col, ids_row):
    rows, width = q.shape
    heads = width // HEAD
    fixed = pl.BlockSpec(memory_space=pltpu.VMEM)
    return pl.pallas_call(
        attend_body,
        name="attend",
        grid=(heads,),
        out_shape=(shaped(width, rows), shaped(heads, 1, rows, dtype=F32)),
        in_specs=[fixed] * 5,
        out_specs=(
            pl.BlockSpec((HEAD, rows), lambda h: (h, 0)),
            pl.BlockSpec((1, 1, rows), lambda h: (h, 0, 0)),
        ),
        compiler_params=pltpu.CompilerParams(vmem_limit_bytes=58 << 20),
    )(q, k, v_turned, ids_col, ids_row)


def attend_back_body(
    q, k, v, k_turned, grad, grad_turned, mixed_turned, logsum, ids_col, ids_row,
    grad_q, grad_k, grad_v,
):
    head = pl.program_id(0)

    @pl.when(head == 0)
    def _():
        grad_k[...] = jnp.zeros_like(grad_k)
        grad_v[...] = jnp.zeros_like(grad_v)

    own = pl.ds(pl.multiple_of(head * HEAD, HEAD), HEAD)
    for block in range(4):
        start, keys = 256 * block, 256 * block + 256
        span = slice(start, start + 256)
        query = only_head(q[span, :], head)
        upstream = only_head(grad[span, :], head)
        scores = dots(k[:keys, :], query, ((1,), (1,)))
        mask = allowed_keys(ids_col, ids_row, keys, start)
        scores = jnp.where(mask, scores * (HEAD**-0.5 * LOG2E), -1e30)
        probs = jnp.exp2(scores - logsum[0, :, span])
        grad_probs = dots(v[:keys, :], upstream, ((1,), (1,)))
        centre = jnp.sum(
            grad_turned[own, span].astype(F32) * mixed_turned[own, span].astype(F32),
            axis=0,
            keepdims=True,
        )
        grad_scores = (probs * (grad_probs - centre)).astype(BF16)
        grad_q[:, span] = (
            dots(k_turned[own, :keys], grad_scores, ((1,), (0,))) * HEAD**-0.5
        ).astype(BF16)
        grad_k[:keys, :] += dots(grad_scores, query, ((1,), (0,)))
        grad_v[:keys, :] += dots(probs.astype(BF16), upstream, ((1,), (0,)))


def attend_back(q, k, v, k_turned, grad, grad_turned, mixed_turned, logsum, ids_col, ids_row):
    rows, width = q.shape
    heads = width // HEAD
    fixed = pl.BlockSpec(memory_space=pltpu.VMEM)
    return pl.pallas_call(
        attend_back_body,
        name="attend_back",
        grid=(heads,),
        out_shape=(
            shaped(width, rows),
            shaped(rows, width, dtype=F32),
            shaped(rows, width, dtype=F32),
        ),
        in_specs=[fixed] * 7
        + [pl.BlockSpec((1, 1, rows), lambda h: (h, 0, 0))]
        + [fixed] * 2,
        out_specs=(
            pl.BlockSpec((HEAD, rows), lambda h: (h, 0)),
            pl.BlockSpec((rows, width), lambda h: (0, 0)),
            pl.BlockSpec((rows, width), lambda h: (0, 0)),
        ),
        compiler_params=pltpu.CompilerParams(vmem_limit_bytes=58 << 20),
    )(q, k, v, k_turned, grad, grad_turned, mixed_turned, logsum, ids_col, ids_row)


def product(left, right):
    return jnp.dot(left, right, preferred_element_type=F32)


def product_left(left, right):
    return dots(left, right, ((0,), (0,)))


def product_right(left, right):
    return dots(left, right, ((1,), (1,)))


def norm_back(rows, inverse, gain, upstream):
    normed = rows * inverse
    scaled = upstream * gain
    grad_rows = inverse * (scaled - normed * jnp.mean(scaled * normed, axis=-1, keepdims=True))
    return (grad_rows, jnp.sum(upstream * normed, axis=0))


def inverse_size(rows):
    return lax.rsqrt(jnp.mean(rows * rows, axis=-1, keepdims=True) + EPS)


def grouped(
    layer_input, doc_ids, attn_gain, query_weight, key_weight, value_weight, out_weight,
    mlp_gain, gate_weight, up_weight, down_weight, out_grad,
):
    dp, ctx = lax.axis_index("dp"), lax.axis_index("ctx")
    x, y, z, k = ctx % 2, dp // 2, ctx // 2, dp % 2
    rank = 2 * x + k
    _, block, width = layer_input.shape
    length = doc_ids.shape[1]
    piece = attn_gain.shape[0]
    gains = jnp.zeros((16, 128), BF16)
    gains = gains.at[0, :piece].set(attn_gain).at[1, :piece].set(mlp_gain)
    rows_all, cots_all, ids_all, heads_all, out_all, hidden_all, down_all, gains_all = gather(
        layer_input, out_grad, doc_ids, query_weight, key_weight, value_weight, out_weight,
        gate_weight, up_weight, down_weight, gains,
    )
    inputs16 = rows_all.reshape(length, width)
    cots = cots_all.reshape(length, width)
    ids = lax.dynamic_slice(ids_all, (z // 2, z % 2, 0), (1, 1, length)).reshape(1, length)
    ids_col = jnp.broadcast_to(ids.reshape(length, 1), (length, 128))
    w_heads = heads_all.reshape(width, -1)
    share = width // 4
    w_query, w_key, w_value = (w_heads[:, i * share : (i + 1) * share] for i in range(3))
    w_out = out_all.reshape(width, width)
    w_hidden = hidden_all.reshape(width, -1)
    units = w_hidden.shape[1] // 2
    w_gate, w_up = w_hidden[:, :units], w_hidden[:, units:]
    w_down = down_all.reshape(units, width)
    gain_one = gains_all[..., 0, :piece].reshape(width).astype(F32)
    gain_two = gains_all[..., 1, :piece].reshape(width).astype(F32)

    inputs = inputs16.astype(F32)
    inverse_one = inverse_size(inputs)
    normed = (inputs * inverse_one * gain_one).astype(BF16)
    query = product(normed, w_query).astype(BF16)
    keys = product(normed, w_key).astype(BF16)
    values = product(normed, w_value).astype(BF16)
    mixed_turned, logsum = attend(query, keys, values.T, ids_col, ids)
    mixed_all = share_group(mixed_turned.T, 1)
    mixed_all = jnp.transpose(mixed_all, (2, 0, 1, 3)).reshape(length, width)
    middle = inputs + product(mixed_all, w_out)
    inverse_two = inverse_size(middle)
    normed_two = (middle * inverse_two * gain_two).astype(BF16)
    gate = product(normed_two, w_gate)
    upward = product(normed_two, w_up)
    sigma = jax.nn.sigmoid(gate)
    hidden = (gate * sigma * upward).astype(BF16)
    out_part = product(hidden, w_down).astype(BF16)
    down_grad = product_left(hidden, cots).astype(BF16)
    grad_hidden = product_right(cots, w_down)
    grad_gate = (grad_hidden * upward * sigma * (1.0 + gate * (1.0 - sigma))).astype(BF16)
    grad_up = (grad_hidden * gate * sigma).astype(BF16)
    gate_grad = product_left(normed_two, grad_gate).astype(BF16)
    up_grad = product_left(normed_two, grad_up).astype(BF16)
    norm_part = (product_right(grad_gate, w_gate) + product_right(grad_up, w_up)).astype(BF16)

    six = (2, 2, 2, block, width)
    out_own = sum_group(out_part.reshape(six), 2)
    grad_normed_two = sum_group(norm_part.reshape(six), 3)

    def own_rows(array):
        parts = array.reshape(2, 2, 2, block, -1)
        return lax.dynamic_slice(
            parts, (0, k, x, 0, 0), (2, 1, 1, block, parts.shape[-1])
        ).reshape(2 * block, -1)

    middle_own = own_rows(middle)
    output_own = (middle_own + out_own.reshape(2 * block, width)).astype(BF16)
    grad_middle, mlp_gain_part = norm_back(
        middle_own, own_rows(inverse_two), gain_two, grad_normed_two.reshape(2 * block, width)
    )
    grad_middle = grad_middle + own_rows(cots).astype(F32)
    branch = share_group(grad_middle.astype(BF16).reshape(2, block, width), 4)
    branch = jnp.transpose(branch, (2, 1, 0, 3, 4)).reshape(length, width)
    layer_output = send_home(output_own.reshape(2, block, width), 5)
    w_out_own = lax.dynamic_slice(w_out, (rank * share, 0), (share, width))
    grad_mixed = product_right(branch, w_out_own).astype(BF16)
    out_proj_grad = dots(mixed_turned, branch, ((1,), (0,))).astype(BF16)
    grad_q, grad_k, grad_v = attend_back(
        query, keys, values, keys.T, grad_mixed, grad_mixed.T, mixed_turned, logsum, ids_col, ids
    )
    grad_heads = jnp.concatenate(
        [grad_q.T, (grad_k * HEAD**-0.5).astype(BF16), grad_v.astype(BF16)], axis=1
    )
    heads_grad = product_left(normed, grad_heads).astype(BF16)
    first_part = product_right(grad_heads, w_heads).astype(BF16)
    grad_normed = sum_group(first_part.reshape(six), 6)
    grad_inputs, attn_gain_part = norm_back(
        own_rows(inputs), own_rows(inverse_one), gain_one, grad_normed.reshape(2 * block, width)
    )
    input_own = (grad_middle + grad_inputs).astype(BF16)
    input_grad = send_home(input_own.reshape(2, block, width), 8).astype(F32)

    def by_owner(array):
        shaped_rows = array.reshape(2, 2, 4, 2, piece, -1)
        return jnp.transpose(shaped_rows, (0, 2, 1, 3, 4, 5))

    gain_parts = jnp.stack([attn_gain_part, mlp_gain_part])
    gain_parts = jnp.transpose(gain_parts.reshape(2, 2, 2, 4, 2, piece), (1, 3, 0, 2, 4, 5))
    gain_parts = jnp.pad(gain_parts.reshape(2, 4, 2, 4 * piece), ((0, 0), (0, 0), (0, 6), (0, 0)))
    q_grad, k_grad, v_grad, o_grad, g_grad, u_grad, d_grad, gain_grads = reduce_all(
        by_owner(heads_grad),
        out_proj_grad.reshape(4, 2, piece, width),
        by_owner(jnp.concatenate([gate_grad, up_grad], axis=1)),
        down_grad.reshape(2, 4, units // 8, width),
        gain_parts,
    )
    gain_own = lax.dynamic_slice(gain_grads, (0, piece * (2 * k + x)), (2, piece))
    return (
        layer_output, input_grad, gain_own[0], q_grad, k_grad, v_grad, o_grad, gain_own[1],
        g_grad, u_grad, d_grad,
    )


def plain_product(left, right):
    return jnp.dot(left, right, preferred_element_type=jnp.float32)


def plain_product_left(left, right):
    return lax.dot_general(
        left, right, (((0,), (0,)), ((), ())), preferred_element_type=jnp.float32
    )


def plain_product_right(left, right):
    return lax.dot_general(
        left, right, (((1,), (1,)), ((), ())), preferred_element_type=jnp.float32
    )


def normalize(rows, gain):
    inverse = lax.rsqrt(jnp.mean(rows * rows, axis=-1, keepdims=True) + EPS)
    return (rows * inverse * gain, inverse)


def plain_norm_back(rows, inverse, gain, upstream):
    normed = rows * inverse
    scaled = upstream * gain
    grad_rows = inverse * (scaled - normed * jnp.mean(scaled * normed, axis=-1, keepdims=True))
    return (grad_rows, jnp.sum(upstream * normed, axis=0))


def head_pair(array, start):
    piece = lax.dynamic_slice_in_dim(array, start, 2 * HEAD, 2)
    return piece.reshape(array.shape[0], array.shape[1], 2, HEAD)


def pair_scores(query, keys, allowed, start):
    scores = jnp.einsum(
        "sqhd,skhd->shqk",
        head_pair(query, start),
        head_pair(keys, start),
        preferred_element_type=jnp.float32,
    ) * HEAD ** (-0.5)
    return jnp.where(allowed[:, None], scores, -1e30)


def plain_attend(query, keys, values, allowed):
    groups, rows, width = query.shape

    def step(index, carry):
        mixed_all, logsum = carry
        start = index * 2 * HEAD
        scores = pair_scores(query, keys, allowed, start)
        top = jnp.max(scores, axis=-1, keepdims=True)
        lifted = jnp.exp(scores - top)
        total = jnp.sum(lifted, axis=-1, keepdims=True)
        probs = (lifted / total).astype(jnp.bfloat16)
        mixed = jnp.einsum(
            "shqk,skhd->sqhd", probs, head_pair(values, start), preferred_element_type=jnp.float32
        )
        mixed_all = lax.dynamic_update_slice_in_dim(
            mixed_all, mixed.reshape(groups, rows, 2 * HEAD).astype(jnp.bfloat16), start, 2
        )
        logsum = lax.dynamic_update_slice_in_dim(
            logsum, (top + jnp.log(total))[..., 0], index * 2, 1
        )
        return (mixed_all, logsum)

    start_state = (
        jnp.zeros((groups, rows, width), jnp.bfloat16),
        jnp.zeros((groups, width // HEAD, rows), jnp.float32),
    )
    return lax.fori_loop(0, width // (2 * HEAD), step, start_state)


def plain_attend_back(query, keys, values, allowed, logsum, grad_mixed):
    groups, rows, width = query.shape
    length = keys.shape[1]
    scale = HEAD ** (-0.5)

    def step(index, carry):
        grad_query, grad_keys, grad_values = carry
        start = index * 2 * HEAD
        scores = pair_scores(query, keys, allowed, start)
        kept = lax.dynamic_slice_in_dim(logsum, index * 2, 2, 1)
        probs = jnp.exp(scores - kept[..., None])
        upstream = head_pair(grad_mixed, start)
        grad_probs = jnp.einsum(
            "sqhd,skhd->shqk",
            upstream,
            head_pair(values, start),
            preferred_element_type=jnp.float32,
        )
        grad_scores = (
            probs * (grad_probs - jnp.sum(probs * grad_probs, axis=-1, keepdims=True))
        ).astype(jnp.bfloat16)
        part_query = (
            jnp.einsum(
                "shqk,skhd->sqhd",
                grad_scores,
                head_pair(keys, start),
                preferred_element_type=jnp.float32,
            )
            * scale
        )
        part_keys = (
            jnp.einsum(
                "shqk,sqhd->skhd",
                grad_scores,
                head_pair(query, start),
                preferred_element_type=jnp.float32,
            )
            * scale
        )
        part_values = jnp.einsum(
            "shqk,sqhd->skhd",
            probs.astype(jnp.bfloat16),
            upstream,
            preferred_element_type=jnp.float32,
        )
        grad_query = lax.dynamic_update_slice_in_dim(
            grad_query, part_query.reshape(groups, rows, 2 * HEAD), start, 2
        )
        grad_keys = lax.dynamic_update_slice_in_dim(
            grad_keys, part_keys.reshape(groups, length, 2 * HEAD), start, 2
        )
        grad_values = lax.dynamic_update_slice_in_dim(
            grad_values, part_values.reshape(groups, length, 2 * HEAD), start, 2
        )
        return (grad_query, grad_keys, grad_values)

    start_state = (
        jnp.zeros((groups, rows, width), jnp.float32),
        jnp.zeros((groups, length, width), jnp.float32),
        jnp.zeros((groups, length, width), jnp.float32),
    )
    return lax.fori_loop(0, width // (2 * HEAD), step, start_state)


def on_device(
    layer_input,
    doc_ids,
    attn_gain,
    query_weight,
    key_weight,
    value_weight,
    out_weight,
    mlp_gain,
    gate_weight,
    up_weight,
    down_weight,
    out_grad,
):
    groups, rows, width = layer_input.shape
    length = doc_ids.shape[1]
    gathered = (
        lax.all_gather(attn_gain, ("dp", "ctx"), axis=0, tiled=True),
        lax.all_gather(query_weight, ("dp", "ctx"), axis=0, tiled=True),
        lax.all_gather(key_weight, ("dp", "ctx"), axis=0, tiled=True),
        lax.all_gather(value_weight, ("dp", "ctx"), axis=0, tiled=True),
        lax.all_gather(out_weight, ("dp", "ctx"), axis=0, tiled=True),
        lax.all_gather(mlp_gain, ("dp", "ctx"), axis=0, tiled=True),
        lax.all_gather(gate_weight, ("dp", "ctx"), axis=0, tiled=True),
        lax.all_gather(up_weight, ("dp", "ctx"), axis=0, tiled=True),
        lax.all_gather(down_weight, ("dp", "ctx"), axis=0, tiled=True),
    )
    gain_one, w_query, w_key, w_value, w_out, gain_two, w_gate, w_up, w_down = gathered
    first = lax.axis_index("ctx") * rows
    places = jnp.arange(length)
    own_ids = lax.dynamic_slice_in_dim(doc_ids, first, rows, 1)
    own_places = first + jnp.arange(rows)
    allowed = (own_ids[:, :, None] == doc_ids[:, None, :]) & (
        places[None, None, :] <= own_places[None, :, None]
    )
    inputs = layer_input.reshape(groups * rows, width).astype(jnp.float32)
    gain_attn = gain_one.astype(jnp.float32)
    normed_full, inverse_one = normalize(inputs, gain_attn)
    normed = normed_full.astype(jnp.bfloat16)
    query = plain_product(normed, w_query).astype(jnp.bfloat16).reshape(groups, rows, width)
    keys_own = plain_product(normed, w_key).astype(jnp.bfloat16).reshape(groups, rows, width)
    values_own = plain_product(normed, w_value).astype(jnp.bfloat16).reshape(groups, rows, width)
    keys, values = (
        lax.all_gather(keys_own, "ctx", axis=1, tiled=True),
        lax.all_gather(values_own, "ctx", axis=1, tiled=True),
    )
    attended, logsum = plain_attend(query, keys, values, allowed)
    attended_rows = attended.reshape(groups * rows, width)
    middle = inputs + plain_product(attended_rows, w_out)
    gain_mlp = gain_two.astype(jnp.float32)
    normed_two_full, inverse_two = normalize(middle, gain_mlp)
    normed_two = normed_two_full.astype(jnp.bfloat16)
    gate = plain_product(normed_two, w_gate)
    upward = plain_product(normed_two, w_up)
    sigma = jax.nn.sigmoid(gate)
    hidden = (gate * sigma * upward).astype(jnp.bfloat16)
    layer_output = (middle + plain_product(hidden, w_down)).astype(jnp.bfloat16)
    gathered_back = (
        lax.all_gather(attn_gain, ("dp", "ctx"), axis=0, tiled=True),
        lax.all_gather(query_weight, ("dp", "ctx"), axis=0, tiled=True),
        lax.all_gather(key_weight, ("dp", "ctx"), axis=0, tiled=True),
        lax.all_gather(value_weight, ("dp", "ctx"), axis=0, tiled=True),
        lax.all_gather(out_weight, ("dp", "ctx"), axis=0, tiled=True),
        lax.all_gather(mlp_gain, ("dp", "ctx"), axis=0, tiled=True),
        lax.all_gather(gate_weight, ("dp", "ctx"), axis=0, tiled=True),
        lax.all_gather(up_weight, ("dp", "ctx"), axis=0, tiled=True),
        lax.all_gather(down_weight, ("dp", "ctx"), axis=0, tiled=True),
    )
    gain_one, w_query, w_key, w_value, w_out, gain_two, w_gate, w_up, w_down = gathered_back
    upstream = out_grad.reshape(groups * rows, width)
    down_grad = plain_product_left(hidden, upstream)
    grad_hidden = plain_product_right(upstream, w_down)
    grad_gate = (grad_hidden * upward * sigma * (1.0 + gate * (1.0 - sigma))).astype(jnp.bfloat16)
    grad_up = (grad_hidden * gate * sigma).astype(jnp.bfloat16)
    gate_grad = plain_product_left(normed_two, grad_gate)
    up_grad = plain_product_left(normed_two, grad_up)
    grad_normed_two = plain_product_right(grad_gate, w_gate) + plain_product_right(grad_up, w_up)
    grad_middle, mlp_gain_grad = plain_norm_back(
        middle, inverse_two, gain_two.astype(jnp.float32), grad_normed_two
    )
    grad_middle = grad_middle + upstream.astype(jnp.float32)
    grad_branch = grad_middle.astype(jnp.bfloat16)
    out_proj_grad = plain_product_left(attended_rows, grad_branch)
    grad_attended = (
        plain_product_right(grad_branch, w_out).astype(jnp.bfloat16).reshape(groups, rows, width)
    )
    grad_query, grad_keys_all, grad_values_all = plain_attend_back(
        query, keys, values, allowed, logsum, grad_attended
    )
    grad_keys, grad_values = (
        lax.psum_scatter(
            grad_keys_all.astype(jnp.bfloat16), "ctx", scatter_dimension=1, tiled=True
        ).astype(jnp.float32),
        lax.psum_scatter(
            grad_values_all.astype(jnp.bfloat16), "ctx", scatter_dimension=1, tiled=True
        ).astype(jnp.float32),
    )
    grad_query = grad_query.astype(jnp.bfloat16).reshape(groups * rows, width)
    grad_keys = grad_keys.astype(jnp.bfloat16).reshape(groups * rows, width)
    grad_values = grad_values.astype(jnp.bfloat16).reshape(groups * rows, width)
    query_grad = plain_product_left(normed, grad_query)
    key_grad = plain_product_left(normed, grad_keys)
    value_grad = plain_product_left(normed, grad_values)
    grad_normed = (
        plain_product_right(grad_query, w_query)
        + plain_product_right(grad_keys, w_key)
        + plain_product_right(grad_values, w_value)
    )
    grad_inputs, attn_gain_grad = plain_norm_back(
        inputs, inverse_one, gain_one.astype(jnp.float32), grad_normed
    )
    input_grad = (grad_middle + grad_inputs).reshape(groups, rows, width)
    shares = (
        lax.psum_scatter(attn_gain_grad, ("dp", "ctx"), scatter_dimension=0, tiled=True),
        lax.psum_scatter(query_grad, ("dp", "ctx"), scatter_dimension=0, tiled=True),
        lax.psum_scatter(key_grad, ("dp", "ctx"), scatter_dimension=0, tiled=True),
        lax.psum_scatter(value_grad, ("dp", "ctx"), scatter_dimension=0, tiled=True),
        lax.psum_scatter(out_proj_grad, ("dp", "ctx"), scatter_dimension=0, tiled=True),
        lax.psum_scatter(mlp_gain_grad, ("dp", "ctx"), scatter_dimension=0, tiled=True),
        lax.psum_scatter(gate_grad, ("dp", "ctx"), scatter_dimension=0, tiled=True),
        lax.psum_scatter(up_grad, ("dp", "ctx"), scatter_dimension=0, tiled=True),
        lax.psum_scatter(down_grad, ("dp", "ctx"), scatter_dimension=0, tiled=True),
    )
    return (
        layer_output.reshape(groups, rows, width),
        input_grad,
        shares[0],
        shares[1],
        shares[2],
        shares[3],
        shares[4],
        shares[5],
        shares[6],
        shares[7],
        shares[8],
    )


def solution(mesh):
    placed = (
        P("dp", "ctx", None),
        P("dp", None),
        P(("dp", "ctx")),
        P(("dp", "ctx"), None),
        P(("dp", "ctx"), None),
        P(("dp", "ctx"), None),
        P(("dp", "ctx"), None),
        P(("dp", "ctx")),
        P(("dp", "ctx"), None),
        P(("dp", "ctx"), None),
        P(("dp", "ctx"), None),
        P("dp", "ctx", None),
    )
    fits = mesh.shape["dp"] == 4 and mesh.shape["ctx"] == 8
    body = grouped if fits else on_device
    return jax.shard_map(
        body,
        mesh=mesh,
        in_specs=placed,
        out_specs=(
            P("dp", "ctx", None),
            P("dp", "ctx", None),
            P(("dp", "ctx")),
            P(("dp", "ctx"), None),
            P(("dp", "ctx"), None),
            P(("dp", "ctx"), None),
            P(("dp", "ctx"), None),
            P(("dp", "ctx")),
            P(("dp", "ctx"), None),
            P(("dp", "ctx"), None),
            P(("dp", "ctx"), None),
        ),
        check_vma=False,
    )
```

```python
import functools

import jax
import jax.numpy as jnp
from jax import lax
from jax.experimental import pallas as pl
from jax.experimental.pallas import tpu as pltpu
from jax.sharding import PartitionSpec as P

HEAD = 64


EPS = 1e-05
MESH = pl.DeviceIdType.MESH
F32 = jnp.float32
BF16 = jnp.bfloat16
LOG2E = 1.4426950408889634
ANY = pl.BlockSpec(memory_space=pl.ANY)
VMEM = pl.BlockSpec(memory_space=pltpu.VMEM)


class Wires:
    def __init__(self, send, recv):
        dp, ctx = lax.axis_index("dp"), lax.axis_index("ctx")
        self.x, self.y = ctx % 2, dp // 2
        self.z, self.k = ctx // 2, dp % 2
        self.send, self.recv = send, recv
        self.used = 0

    def slots(self, count):
        first = self.used
        self.used += count
        return first

    def at(self, x, y, z, k):
        return (2 * y + k, 2 * z + x)

    def copy(self, source, target, device, slot, recv_slot=None):
        return pltpu.make_async_remote_copy(
            src_ref=source,
            dst_ref=target,
            send_sem=self.send.at[slot],
            recv_sem=self.recv.at[slot if recv_slot is None else recv_slot],
            device_id=device,
            device_id_type=MESH,
        )

    def greet(self, peers):
        barrier = pltpu.get_barrier_semaphore()
        for peer in peers:
            pl.semaphore_signal(barrier, inc=1, device_id=peer, device_id_type=MESH)
        pl.semaphore_wait(barrier, len(peers))

    def group_peers(self):
        x, y, z, k = self.x, self.y, self.z, self.k
        return [self.at(1 - x, y, z, k), self.at(x, y, z, 1 - k), self.at(1 - x, y, z, 1 - k)]

    def line_peers(self):
        x, y, z, k = self.x, self.y, self.z, self.k
        return [self.at(x, y, (z + i) % 4, k) for i in (1, 2, 3)]

    def cross_peers(self):
        x, y, z, k = self.x, self.y, self.z, self.k
        return [self.at(x, y, (z + i) % 4, 1 - k) for i in (1, 2, 3)]

    def pair_peer(self):
        return self.at(self.x, 1 - self.y, self.z, self.k)


class Spread:
    def __init__(self, wires, block, own=None):
        self.w, self.block, self.own = wires, block, own
        self.lines, self.pairs = wires.slots(4), wires.slots(4)

    def line(self, i, z, own=None):
        w = self.w
        ref = self.block(w.y, z)
        target = w.at(w.x, w.y, (w.z + i) % 4, w.k)
        return w.copy(ref if own is None else own, ref, target, self.lines + i)

    def pair(self, i, y, own=None):
        w = self.w
        ref = self.block(y, (w.z + 4 - i) % 4)
        return w.copy(ref if own is None else own, ref, w.pair_peer(), self.pairs + i)

    def start(self):
        for i in (2, 1, 3):
            self.line(i, self.w.z, self.own).start()
        self.pair(0, self.w.y, self.own).start()

    def forward(self, i):
        self.line(i, (self.w.z + 4 - i) % 4).wait_recv()
        self.pair(i, self.w.y).start()

    def arrive(self, i):
        self.pair(i, 1 - self.w.y).wait_recv()

    def drain(self):
        for i in (1, 2, 3):
            self.line(i, self.w.z, self.own).wait_send()
        for i in range(4):
            self.pair(i, self.w.y).wait_send()


class Share:
    def __init__(self, wires, block, own=None):
        self.w, self.block, self.own = wires, block, own
        self.first = wires.slots(3)

    def piece(self, i):
        w = self.w
        core, across = w.at(w.x, w.y, w.z, 1 - w.k), w.at(1 - w.x, w.y, w.z, w.k)
        ref = self.block(w.x if i < 2 else 1 - w.x, w.k)
        source = ref if self.own is None or i == 2 else self.own
        return w.copy(source, ref, across if i == 0 else core, self.first + i)

    def landed(self, i):
        w = self.w
        ref = self.block(*[(1 - w.x, w.k), (w.x, 1 - w.k), (1 - w.x, 1 - w.k)][i])
        return w.copy(ref, ref, w.at(w.x, w.y, w.z, 1 - w.k), self.first + i)

    def start(self):
        self.piece(0).start()
        self.piece(1).start()

    def forward(self):
        self.landed(0).wait_recv()
        self.piece(2).start()

    def arrive(self):
        self.landed(1).wait_recv()
        self.landed(2).wait_recv()

    def drain(self):
        for i in range(3):
            self.piece(i).wait_send()


class Deal:
    def __init__(self, wires, outgoing, incoming):
        self.w, self.outgoing, self.incoming = wires, outgoing, incoming
        self.first = wires.slots(3)

    def mate(self, i):
        w = self.w
        return [(1 - w.x, w.k), (w.x, 1 - w.k), (1 - w.x, 1 - w.k)][i]

    def piece(self, i):
        w = self.w
        x, k = self.mate(i)
        return w.copy(
            self.outgoing(x, k), self.incoming(w.x, w.k), w.at(x, w.y, w.z, k), self.first + i
        )

    def landed(self, i):
        x, k = self.mate(i)
        ref = self.incoming(x, k)
        return self.w.copy(ref, ref, self.w.at(x, self.w.y, self.w.z, k), self.first + i)

    def start(self):
        for i in range(3):
            self.piece(i).start()

    def arrive(self):
        for i in range(3):
            self.landed(i).wait_recv()

    def drain(self):
        for i in range(3):
            self.piece(i).wait_send()


class Visit:
    def __init__(self, wires, home, full, local):
        self.w, self.home, self.full, self.local = wires, home, full, local
        self.first = wires.slots(2)
        w = wires
        self.own = [jnp.logical_and(w.z == 2 * w.k + j, w.z % 2 == w.k) for j in range(2)]

    def piece(self, j):
        w = self.w
        return w.copy(
            self.home.at[j],
            self.full(w.x, w.z),
            w.at(w.x, w.y, 2 * w.k + j, w.z % 2),
            self.first + j,
            self.first + w.z // 2,
        )

    def stay(self, j):
        return pltpu.make_async_copy(self.home.at[j], self.full(self.w.x, self.w.z), self.local)

    def landed(self, i):
        w = self.w
        ref = self.full(w.x, w.k + 2 * i)
        return w.copy(ref, ref, w.pair_peer(), self.first + i)

    def here(self, i):
        w = self.w
        return jnp.logical_and(w.k + 2 * i == w.z, w.z // 2 == w.k)

    def start(self):
        for j in range(2):
            pl.when(self.own[j])(lambda: self.stay(j).start())
            pl.when(jnp.logical_not(self.own[j]))(lambda: self.piece(j).start())

    def arrive(self):
        for j in range(2):
            pl.when(self.own[j])(lambda: self.stay(j).wait())
        for i in range(2):
            pl.when(jnp.logical_not(self.here(i)))(lambda: self.landed(i).wait_recv())

    def drain(self):
        for j in range(2):
            pl.when(jnp.logical_not(self.own[j]))(lambda: self.piece(j).wait_send())


class Return:
    def __init__(self, wires, done, home, local):
        self.w, self.done, self.home, self.local = wires, done, home, local
        self.first = wires.slots(2)

    def own(self, i):
        w = self.w
        return jnp.logical_and(2 * i + w.k == w.z, w.z // 2 == w.k)

    def piece(self, i):
        w = self.w
        return w.copy(
            self.done(i),
            self.home.at[w.z % 2],
            w.at(w.x, w.y, 2 * i + w.k, w.z // 2),
            self.first + i,
            self.first + w.z % 2,
        )

    def stay(self, i):
        return pltpu.make_async_copy(self.done(i), self.home.at[self.w.z % 2], self.local)

    def here(self, j):
        w = self.w
        return jnp.logical_and(2 * w.k + j == w.z, w.z % 2 == w.k)

    def landed(self, j):
        ref = self.home.at[j]
        return self.w.copy(ref, ref, self.w.pair_peer(), self.first + j)

    def start(self):
        for i in range(2):
            pl.when(self.own(i))(lambda: self.stay(i).start())
            pl.when(jnp.logical_not(self.own(i)))(lambda: self.piece(i).start())

    def arrive(self):
        for i in range(2):
            pl.when(self.own(i))(lambda: self.stay(i).wait())
        for j in range(2):
            pl.when(jnp.logical_not(self.here(j)))(lambda: self.landed(j).wait_recv())

    def drain(self):
        for i in range(2):
            pl.when(jnp.logical_not(self.own(i)))(lambda: self.piece(i).wait_send())


def shaped(*shape, dtype=BF16):
    return jax.ShapeDtypeStruct(shape, dtype)


def pack_rows(columns, shards, packed):
    for rank in range(4):
        at = 0
        for shard in shards:
            for start, width in columns(rank):
                packed[rank, :, at : at + width] = shard[:, start : start + width]
                at += width


def head_columns(rank):
    return [(256 * rank, 256)]


def hidden_columns(rank):
    x, k = rank // 2, rank % 2
    return [(128 * (8 * (2 * y + k) + 2 * z + x), 128) for y in range(2) for z in range(4)]


class Total:
    def __init__(self, wires, part, got_core, got_across):
        self.w, self.part, self.got_core, self.got_across = wires, part, got_core, got_across
        self.first = wires.slots(4)
        self.half = part.shape[2] // 2

    def core(self, i):
        w = self.w
        return w.copy(
            self.part.at[0, i], self.got_core.at[i], w.at(w.x, w.y, w.z, 1 - w.k), self.first + i
        )

    def rows(self, x):
        return pl.ds(pl.multiple_of(self.half * x, self.half), self.half)

    def across(self, i):
        w = self.w
        return w.copy(
            self.part.at[1, i, self.rows(1 - w.x)],
            self.got_across.at[i],
            w.at(1 - w.x, w.y, w.z, w.k),
            self.first + 2 + i,
        )

    def give(self, i, value):
        self.part[0, i] = value.astype(BF16)
        self.core(i).start()

    def keep(self, i, value):
        self.core(i).wait_recv()
        self.part[1, i] = (value + self.got_core[i].astype(F32)).astype(BF16)
        self.across(i).start()

    def take(self, i):
        self.across(i).wait_recv()
        own = self.part[1, i, self.rows(self.w.x)]
        return own.astype(F32) + self.got_across[i].astype(F32)

    def drain(self):
        for i in range(2):
            self.core(i).wait_send()
            self.across(i).wait_send()


class Fold:
    def __init__(self, wires, whole, block, got_pair, pair_block, got_line):
        self.w, self.whole, self.block = wires, whole, block
        self.got_pair, self.pair_block, self.got_line = got_pair, pair_block, got_line
        self.pairs, self.lines = wires.slots(1), wires.slots(4)

    def pair(self):
        w = self.w
        return w.copy(self.whole(1 - w.y), self.got_pair, w.pair_peer(), self.pairs)

    def line(self, i):
        w = self.w
        z = (w.z + i) % 4
        return w.copy(
            self.block(w.y, z), self.got_line.at[i - 1], w.at(w.x, w.y, z, w.k), self.lines + i
        )

    def both(self, z):
        return self.block(self.w.y, z)[...].astype(F32) + self.pair_block(z)[...].astype(F32)

    def start(self):
        self.pair().start()

    def send(self):
        w = self.w
        self.pair().wait_recv()
        for i in (2, 1, 3):
            z = (w.z + i) % 4
            self.block(w.y, z)[...] = self.both(z).astype(self.got_line.dtype)
            self.line(i).start()

    def finish(self):
        total = self.both(self.w.z)
        for i in (1, 3, 2):
            self.line(i).wait_recv()
            total += self.got_line[i - 1].astype(F32)
        return total

    def drain(self):
        self.pair().wait_send()
        for i in (1, 2, 3):
            self.line(i).wait_send()


def dots(left, right, dims):
    return lax.dot_general(left, right, (dims, ((), ())), preferred_element_type=F32)


NN, NT, TN = ((1,), (0,)), ((1,), (1,)), ((0,), (0,))


def only_head(array, head):
    lane = lax.broadcasted_iota(jnp.int32, array.shape, 1)
    return jnp.where(lane // HEAD == head, array, jnp.zeros_like(array))


def inverse_size(rows):
    return lax.rsqrt(jnp.mean(rows * rows, axis=-1, keepdims=True) + EPS)


def norm_back(rows, gain, upstream):
    inverse = inverse_size(rows)
    normed = rows * inverse
    scaled = upstream * gain
    grad_rows = inverse * (scaled - normed * jnp.mean(scaled * normed, axis=-1, keepdims=True))
    return grad_rows, jnp.sum(upstream * normed, axis=0, keepdims=True)


SCRATCH = [
    ("rows_all", (2, 2, 2, 128, 1024), BF16),
    ("cots_all", (2, 2, 2, 128, 1024), BF16),
    ("ids_all", (2, 2, 1, 1024), jnp.int32),
    ("heads_all", (2, 2, 4, 2, 32, 768), BF16),
    ("out_all", (2, 2, 4, 2, 32, 1024), BF16),
    ("hidden_all", (2, 2, 4, 2, 32, 2048), BF16),
    ("down_all", (2, 4, 128, 1024), BF16),
    ("gains_all", (2, 2, 4, 2, 16, 128), BF16),
    ("heads_pack", (4, 32, 768), BF16),
    ("hidden_pack", (4, 32, 2048), BF16),
    ("normed", (1024, 1024), BF16),
    ("query", (1024, 256), BF16),
    ("keys", (1024, 256), BF16),
    ("values", (1024, 256), BF16),
    ("keys_turned", (256, 1024), BF16),
    ("values_turned", (256, 1024), BF16),
    ("mixed_turned", (256, 1024), BF16),
    ("mixed_all", (2, 2, 256, 1024), BF16),
    ("logsum", (4, 1, 1024), F32),
    ("gain_rows", (2, 1, 1024), F32),
    ("ids_row", (1, 1024), F32),
    ("ids_col", (1024, 128), F32),
    ("middle_keep", (2, 256, 1024), F32),
    ("normed_two", (1024, 1024), BF16),
    ("hidden", (1024, 1024), BF16),
    ("grad_gate", (1024, 1024), BF16),
    ("grad_up", (1024, 1024), BF16),
    ("part_norm", (2, 2, 256, 1024), BF16),
    ("core_out", (2, 256, 1024), BF16),
    ("core_norm", (2, 256, 1024), BF16),
    ("across_out", (2, 128, 1024), BF16),
    ("across_norm", (2, 128, 1024), BF16),
    ("branch", (2, 2, 2, 128, 1024), BF16),
    ("grad_keys", (1024, 256), F32),
    ("grad_values", (1024, 256), F32),
    ("heads_part", (2, 2, 4, 2, 32, 768), BF16),
    ("out_part", (4, 2, 32, 1024), BF16),
    ("gains_part", (2, 4, 8, 128), F32),
    ("heads_pair", (2, 4, 2, 32, 768), BF16),
    ("hidden_pair", (2, 4, 2, 32, 2048), BF16),
    ("down_pair", (4, 128, 1024), BF16),
    ("out_pair", (4, 2, 32, 1024), BF16),
    ("gains_pair", (4, 8, 128), F32),
    ("heads_line", (3, 2, 2, 32, 768), BF16),
    ("hidden_line", (3, 2, 2, 32, 2048), BF16),
    ("down_line", (3, 128, 1024), BF16),
    ("out_line", (3, 2, 32, 1024), BF16),
    ("gains_line", (3, 8, 128), F32),
    ("heads_dealt", (4, 32, 768), BF16),
    ("hidden_dealt", (4, 32, 2048), BF16),
    ("gains_deal", (8, 128), F32),
    ("gains_dealt", (4, 8, 128), F32),
    ("out_deal", (32, 1024), BF16),
    ("out_home", (32, 1024), BF16),
    ("done_out", (2, 128, 1024), BF16),
    ("input_home", (2, 128, 1024), BF16),
]


def layer_body(
    rows, cots, ids, wq, wk, wv, wo, wg, wu, wd, gains,
    output, input_grad, q_out, k_out, v_out, o_out, g_out, u_out, d_out, gain_out,
    *scratch,
):
    send, recv, local = scratch[-3:]
    m = type("Memory", (), dict(zip([name for name, _, _ in SCRATCH], scratch)))
    w = Wires(send, recv)
    x, y, z, k = w.x, w.y, w.z, w.k
    rank = 2 * x + k
    w.greet(w.group_peers() + w.line_peers() + w.cross_peers() + [w.pair_peer()])

    used = [0]

    def spare():
        used[0] += 1
        return local.at[used[0] - 1]

    def stay(source, target):
        copy = pltpu.make_async_copy(source, target, spare())
        copy.start()
        return copy

    def sequence_block(ref):
        return lambda x, z: ref.at[z // 2, z % 2, x]

    visit_rows = Visit(w, rows, sequence_block(m.rows_all), spare())
    visit_rows.start()
    pack_rows(head_columns, (wq, wk, wv), m.heads_pack)
    deal_heads = Deal(
        w, lambda x, k: m.heads_pack.at[2 * x + k], lambda sx, sk: m.heads_all.at[y, sk, z, sx]
    )
    deal_heads.start()
    stays = [
        stay(m.heads_pack.at[rank], m.heads_all.at[y, k, z, x]),
        stay(wo, m.out_all.at[y, k, z, x]),
        stay(gains, m.gains_all.at[y, k, z, x]),
        stay(wd, m.down_all.at[y, z]),
        stay(ids, m.ids_all.at[k]),
    ]
    swap = w.copy(ids, m.ids_all.at[k], w.at(x, y, z, 1 - k), w.slots(1))
    swap.start()
    spread_gains = Spread(w, lambda y, z: m.gains_all.at[y, k, z, x], gains)
    spread_gains.start()
    pack_rows(hidden_columns, (wg, wu), m.hidden_pack)
    stays.append(stay(m.hidden_pack.at[rank], m.hidden_all.at[y, k, z, x]))
    deal_hidden = Deal(
        w, lambda x, k: m.hidden_pack.at[2 * x + k], lambda sx, sk: m.hidden_all.at[y, sk, z, sx]
    )
    for copy in stays:
        copy.wait()
    deal_heads.arrive()
    spread_heads = Spread(w, lambda y, z: m.heads_all.at[y, :, z])
    spread_heads.start()
    visit_rows.arrive()
    share_rows = Share(w, lambda x, k: m.rows_all.at[:, k, x])
    share_rows.start()
    deal_hidden.start()
    for i in (1, 3, 2):
        spread_gains.forward(i)
    spread_out = Spread(w, lambda y, z: m.out_all.at[y, k, z, x], wo)
    spread_out.start()
    share_rows.forward()
    deal_hidden.arrive()
    spread_hidden = Spread(w, lambda y, z: m.hidden_all.at[y, :, z])
    spread_hidden.start()
    for i in (1, 3, 2):
        spread_heads.forward(i)
    for i in range(4):
        spread_gains.arrive(i)
    share_gains = Share(w, lambda x, k: m.gains_all.at[:, k, :, x])
    share_gains.start()
    swap.wait()
    m.ids_row[...] = m.ids_all[z // 2, z % 2].astype(F32)
    for j in range(8):
        piece = slice(128 * j, 128 * j + 128)
        m.ids_col[piece, :] = jnp.broadcast_to(m.ids_row[:, piece], (128, 128)).T
    share_gains.forward()
    share_rows.arrive()
    share_gains.arrive()
    for j in range(8):
        four = [
            m.gains_all[j // 4, (j // 2) % 2, 2 * (j % 2) + i // 2, i % 2].astype(F32)
            for i in range(4)
        ]
        total = four[0] + four[1] + four[2] + four[3]
        for i in range(2):
            m.gain_rows[i, :, 128 * j : 128 * j + 128] = total[i : i + 1, :]

    def first_norm(b, _):
        block = m.rows_all[b // 2, b % 2].reshape(256, 1024).astype(F32)
        span = pl.ds(pl.multiple_of(256 * b, 256), 256)
        m.normed[span, :] = (block * inverse_size(block) * m.gain_rows[0]).astype(BF16)
        return 0

    lax.fori_loop(0, 4, first_norm, 0)
    visit_cots = Visit(w, cots, sequence_block(m.cots_all), spare())
    visit_cots.start()
    for i in (1, 3, 2):
        spread_out.forward(i)
    for i in range(4):
        spread_heads.arrive(i)
    heads = m.heads_all[...].reshape(1024, 768)
    for b in range(4):
        span = slice(256 * b, 256 * b + 256)
        made = dots(m.normed[span, :], heads, NN).astype(BF16)
        m.query[span, :], m.keys[span, :] = made[:, :256], made[:, 256:512]
        m.values[span, :] = made[:, 512:]
        m.keys_turned[:, span] = made[:, 256:512].T
        m.values_turned[:, span] = made[:, 512:].T
    for i in range(4):
        spread_out.arrive(i)
    share_out = Share(w, lambda x, k: m.out_all.at[:, k, :, x])
    share_out.start()
    spread_down = Spread(w, lambda y, z: m.down_all.at[y, z], wd)
    spread_down.start()
    visit_cots.arrive()
    share_cots = Share(w, lambda x, k: m.cots_all.at[:, k, x])
    share_cots.start()

    def bias_of(b):
        start, count = 256 * b, 256 * b + 256
        column = m.ids_col[:count, :]
        same = jnp.concatenate([column, column], axis=1) == m.ids_row[:, start : start + 256]
        key = lax.broadcasted_iota(jnp.int32, (count, 256), 0)
        place = lax.broadcasted_iota(jnp.int32, (count, 256), 1) + start
        return jnp.where(jnp.logical_and(same, key <= place), 0.0, -1e30).astype(F32)

    def head_rows(h):
        return pl.ds(pl.multiple_of(h * HEAD, HEAD), HEAD)

    def rank_columns(x, k):
        return pl.ds(pl.multiple_of(256 * (2 * x + k), 256), 256)

    def mix(b):
        span, count = slice(256 * b, 256 * b + 256), 256 * b + 256
        bias = bias_of(b)

        def one(h, _):
            scores = dots(m.keys[:count, :], only_head(m.query[span, :], h), NT)
            scores = scores * (HEAD**-0.5 * LOG2E) + bias
            top = jnp.max(scores, axis=0, keepdims=True)
            lifted = jnp.exp2(scores - top)
            total = jnp.sum(lifted, axis=0, keepdims=True)
            probs = (lifted * (1.0 / total)).astype(BF16)
            mixed = dots(m.values_turned[head_rows(h), :count], probs, NN)
            m.mixed_turned[head_rows(h), span] = mixed.astype(BF16)
            m.logsum[h, :, span] = top + jnp.log2(total)
            return 0

        lax.fori_loop(0, 4, one, 0)
        m.mixed_all[b // 2, b % 2, :, rank_columns(x, k)] = m.mixed_turned[:, span].T

    def share_mixed(b):
        return Share(w, lambda x, k: m.mixed_all.at[b // 2, b % 2, :, rank_columns(x, k)])

    shares = [share_mixed(b) for b in range(4)]
    mix(0)
    shares[0].start()
    spread_hidden.forward(1)
    mix(1)
    shares[1].start()
    shares[0].forward()
    share_out.forward()
    share_cots.forward()
    spread_hidden.forward(3)
    mix(2)
    shares[2].start()
    shares[1].forward()
    spread_hidden.forward(2)
    mix(3)
    shares[3].start()
    shares[2].forward()
    share_out.arrive()

    for b in range(4):
        span = slice(256 * b, 256 * b + 256)
        if b == 2:
            shares[3].forward()
        shares[b].arrive()
        middle = m.rows_all[b // 2, b % 2].reshape(256, 1024).astype(F32)
        whole = m.out_all[...].reshape(1024, 1024)
        middle = middle + dots(m.mixed_all[b // 2, b % 2], whole, NN)
        m.normed_two[span, :] = (middle * inverse_size(middle) * m.gain_rows[1]).astype(BF16)

        @pl.when(k == b % 2)
        def _():
            m.middle_keep[b // 2] = middle

    for i in (1, 3, 2):
        spread_down.forward(i)
    for i in range(4):
        spread_hidden.arrive(i)
    for i in range(4):
        spread_down.arrive(i)
    share_cots.arrive()
    for share in shares:
        share.drain()
    total_out = Total(w, m.mixed_all, m.core_out, m.across_out)
    total_norm = Total(w, m.part_norm, m.core_norm, m.across_norm)

    def feed(i, part):
        span = pl.ds(pl.multiple_of(256 * (2 * i + part), 256), 256)
        upstream = m.cots_all[i, part].reshape(256, 1024)
        normed_two = m.normed_two[span, :]
        for n in range(4):
            columns = slice(256 * n, 256 * n + 256)
            gate_tile = m.hidden_all[..., 256 * n : 256 * n + 256].reshape(1024, 256)
            up_tile = m.hidden_all[..., 1024 + 256 * n : 1280 + 256 * n].reshape(1024, 256)
            down_tile = m.down_all[n // 2, 2 * (n % 2) : 2 * (n % 2) + 2].reshape(256, 1024)
            gate = dots(normed_two, gate_tile, NN)
            upward = dots(normed_two, up_tile, NN)
            grad_hidden = dots(upstream, down_tile, NT)
            sigma = 1.0 / (1.0 + jnp.exp(-gate))
            silu = gate * sigma
            m.hidden[span, columns] = (silu * upward).astype(BF16)
            m.grad_up[span, columns] = (grad_hidden * silu).astype(BF16)
            m.grad_gate[span, columns] = (
                grad_hidden * upward * (sigma + silu * (1.0 - sigma))
            ).astype(BF16)
        norm_part = dots(
            m.grad_gate[span, :], m.hidden_all[..., :1024].reshape(1024, 1024), NT
        ) + dots(m.grad_up[span, :], m.hidden_all[..., 1024:].reshape(1024, 1024), NT)
        return span, norm_part

    def out_of(span):
        return dots(m.hidden[span, :], m.down_all[...].reshape(1024, 1024), NN)

    def give(i, _):
        span, norm_part = feed(i, 1 - k)
        total_norm.give(i, norm_part)
        total_out.give(i, out_of(span))
        return 0

    def keep(i, _):
        span, norm_part = feed(i, k)
        total_norm.keep(i, norm_part)
        total_out.keep(i, out_of(span))
        return 0

    lax.fori_loop(0, 2, give, 0)
    lax.fori_loop(0, 2, keep, 0)
    spread_down.drain()
    spread_hidden.drain()

    def lanes(plane, half):
        return pl.ds(pl.multiple_of(512 * plane + 256 * half, 256), 256)

    def down_part(plane):
        def one(half, _):
            made = dots(m.hidden[:, lanes(plane, half)], m.cots_all[...].reshape(1024, 1024), TN)
            m.down_all[plane, pl.ds(2 * half, 2)] = made.astype(BF16).reshape(2, 128, 1024)
            return 0

        lax.fori_loop(0, 2, one, 0)

    def hidden_part(plane):
        def one(half, _):
            left = m.normed_two[:, lanes(plane, half)]
            for j, right in enumerate((m.grad_gate, m.grad_up)):
                made = dots(left, right[...], TN).astype(BF16).reshape(4, 2, 32, 1024)
                m.hidden_all[plane, half, :, :, :, 1024 * j : 1024 * j + 1024] = made
            return 0

        lax.fori_loop(0, 2, one, 0)

    fold_down = Fold(
        w, lambda y: m.down_all.at[y], lambda y, z: m.down_all.at[y, z],
        m.down_pair, lambda z: m.down_pair.at[z], m.down_line,
    )
    fold_hidden = Fold(
        w, lambda y: m.hidden_all.at[y], lambda y, z: m.hidden_all.at[y, :, z],
        m.hidden_pair, lambda z: m.hidden_pair.at[:, z], m.hidden_line,
    )
    fold_heads = Fold(
        w, lambda y: m.heads_part.at[y], lambda y, z: m.heads_part.at[y, :, z],
        m.heads_pair, lambda z: m.heads_pair.at[:, z], m.heads_line,
    )
    fold_gains = Fold(
        w, lambda y: m.gains_part.at[y], lambda y, z: m.gains_part.at[y, z],
        m.gains_pair, lambda z: m.gains_pair.at[z], m.gains_line,
    )
    down_part(1 - y)
    fold_down.start()
    hidden_part(1 - y)
    fold_hidden.start()

    share_branch = Share(w, lambda x, k: m.branch.at[:, k, x])
    own_half = total_norm.rows(x)
    gain_sum = jnp.zeros((1, 1024), F32)
    for i in range(2):
        grad, term = norm_back(
            m.middle_keep[i, own_half], m.gain_rows[1], total_norm.take(i)
        )
        gain_sum = gain_sum + term
        m.done_out[i] = (m.middle_keep[i, own_half] + total_out.take(i)).astype(BF16)
        grad = grad + m.cots_all[i, k, x].astype(F32)
        m.middle_keep[i, own_half] = grad
        m.branch[i, k, x] = grad.astype(BF16)
    share_branch.start()
    return_out = Return(w, lambda i: m.done_out.at[i], output, spare())
    return_out.start()

    def gain_rows_part(row, total):
        for plane in range(2):
            for zz in range(4):
                for half in range(2):
                    at = 512 * plane + 256 * half + 128 * (zz // 2)
                    m.gains_part[plane, zz, 2 * row + half : 2 * row + half + 1, :] = total[
                        :, at : at + 128
                    ]

    m.gains_part[...] = jnp.zeros_like(m.gains_part)
    gain_rows_part(1, gain_sum)
    down_part(y)
    share_branch.forward()
    hidden_part(y)
    share_branch.arrive()

    grad_mixed, grad_mixed_turned = m.grad_up.at[:, :256], m.hidden.at[:256]
    grad_heads = m.grad_gate.at[:, :768]
    out_own = m.out_all[x, k].reshape(256, 1024)
    for b in range(4):
        span = slice(256 * b, 256 * b + 256)
        made = dots(m.branch[b // 2, b % 2].reshape(256, 1024), out_own, NT).astype(BF16)
        grad_mixed[span, :] = made
        grad_mixed_turned[:, span] = made.T
    m.out_part[...] = (
        dots(m.mixed_turned[...], m.branch[...].reshape(1024, 1024), NN)
        .astype(BF16)
        .reshape(4, 2, 32, 1024)
    )
    base = w.slots(6)
    owner = y == x
    out_across = w.copy(m.out_part, m.out_pair, w.pair_peer(), base)
    pl.when(jnp.logical_not(owner))(lambda: out_across.start())
    m.grad_keys[...] = jnp.zeros_like(m.grad_keys)
    m.grad_values[...] = jnp.zeros_like(m.grad_values)

    def unmix(b):
        span, count = slice(256 * b, 256 * b + 256), 256 * b + 256
        bias = bias_of(b)

        def one(h, _):
            query, upstream = only_head(m.query[span, :], h), only_head(grad_mixed[span, :], h)
            scores = dots(m.keys[:count, :], query, NT)
            scores = scores * (HEAD**-0.5 * LOG2E) + bias
            probs = jnp.exp2(scores - m.logsum[h, :, span])
            grad_probs = dots(m.values[:count, :], upstream, NT)
            centre = jnp.sum(
                grad_mixed_turned[head_rows(h), span].astype(F32)
                * m.mixed_turned[head_rows(h), span].astype(F32),
                axis=0,
                keepdims=True,
            )
            grad_scores = (probs * (grad_probs - centre)).astype(BF16)
            turned = dots(m.keys_turned[head_rows(h), :count], grad_scores, NN)
            grad_mixed_turned[head_rows(h), span] = (turned * HEAD**-0.5).astype(BF16)
            m.grad_keys[:count, :] += dots(grad_scores, query, NN)
            m.grad_values[:count, :] += dots(probs.astype(BF16), upstream, NN)
            return 0

        lax.fori_loop(0, 4, one, 0)
        grad_heads[span, :256] = grad_mixed_turned[:, span].T

    for b in range(4):
        unmix(b)
    grad_heads[:, 256:512] = (m.grad_keys[...] * HEAD**-0.5).astype(BF16)
    grad_heads[:, 512:] = m.grad_values[...].astype(BF16)

    def heads_part(plane):
        for half in range(2):
            made = dots(m.normed[:, lanes(plane, half)], grad_heads[...], TN)
            m.heads_part[plane, half] = made.astype(BF16).reshape(4, 2, 32, 768)

    heads_part(1 - y)
    fold_heads.start()
    total_norm.drain()
    total_first = Total(w, m.part_norm, m.core_norm, m.across_norm)

    def first_part(i, part):
        span = pl.ds(pl.multiple_of(256 * (2 * i + part), 256), 256)
        return dots(grad_heads[span, :], m.heads_all[...].reshape(1024, 768), NT)

    for i in range(2):
        total_first.give(i, first_part(i, 1 - k))
    for i in range(2):
        total_first.keep(i, first_part(i, k))
    heads_part(y)
    fold_down.send()
    gain_sum = jnp.zeros((1, 1024), F32)

    def done_in(i):
        return m.normed_two.at[pl.ds(128 * i, 128)]

    for i in range(2):
        grad, term = norm_back(
            m.rows_all[i, k, x].astype(F32), m.gain_rows[0], total_first.take(i)
        )
        gain_sum = gain_sum + term
        done_in(i)[...] = (m.middle_keep[i, own_half] + grad).astype(BF16)
    return_in = Return(w, done_in, m.input_home, spare())
    return_in.start()
    gain_rows_part(0, gain_sum)
    fold_gains.start()

    def out_piece(i):
        zi = (z + i) % 4
        return w.copy(m.out_part.at[zi], m.out_line.at[i - 1], w.at(x, y, zi, k), base + i)

    @pl.when(owner)
    def _():
        out_across.wait_recv()
        for i in (2, 1, 3):
            zi = (z + i) % 4
            m.out_part[zi] = (m.out_part[zi].astype(F32) + m.out_pair[zi].astype(F32)).astype(BF16)
            out_piece(i).start()

    fold_hidden.send()
    d_out[...] = fold_down.finish()
    fold_gains.send()
    fold_heads.send()
    return_in.arrive()
    input_grad[...] = m.input_home[...].astype(F32)
    out_last = w.copy(m.out_deal, m.out_home, w.at(1 - x, y, z, k), base + 4)

    @pl.when(owner)
    def _():
        out_total = m.out_part[z].astype(F32) + m.out_pair[z].astype(F32)
        for i in (1, 3, 2):
            out_piece(i).wait_recv()
            out_total += m.out_line[i - 1].astype(F32)
        first, second = out_total[0], out_total[1]
        m.out_deal[...] = jnp.where(x == 0, second, first).astype(BF16)
        out_last.start()
        o_out[...] = jnp.where(x == 0, first, second)

    deal_hidden.drain()
    deal_heads.drain()
    m.hidden_pack[...] = fold_hidden.finish().astype(BF16).reshape(4, 32, 2048)
    deal_hidden_grad = Deal(
        w, lambda x, k: m.hidden_pack.at[2 * k + x], lambda x, k: m.hidden_dealt.at[2 * x + k]
    )
    deal_hidden_grad.start()
    m.gains_deal[...] = fold_gains.finish()
    m.gains_dealt[rank] = m.gains_deal[...]
    deal_gains = Deal(w, lambda x, k: m.gains_deal, lambda x, k: m.gains_dealt.at[2 * x + k])
    deal_gains.start()
    m.heads_pack[...] = fold_heads.finish().astype(BF16).reshape(4, 32, 768)
    deal_heads_grad = Deal(
        w, lambda x, k: m.heads_pack.at[2 * k + x], lambda x, k: m.heads_dealt.at[2 * x + k]
    )
    deal_heads_grad.start()
    m.hidden_dealt[rank] = m.hidden_pack[2 * k + x]
    m.heads_dealt[rank] = m.heads_pack[2 * k + x]
    deal_hidden_grad.arrive()
    for r in range(4):
        for half, target in enumerate((g_out, u_out)):
            for j, (start, width) in enumerate(hidden_columns(r)):
                at = 128 * j + half * 1024
                target[:, start : start + width] = m.hidden_dealt[r, :, at : at + width].astype(F32)
    deal_gains.arrive()
    gain_out[...] = m.gains_dealt[0] + m.gains_dealt[1] + m.gains_dealt[2] + m.gains_dealt[3]
    deal_heads_grad.arrive()
    for r in range(4):
        for j, target in enumerate((q_out, k_out, v_out)):
            at = 256 * j
            target[:, 256 * r : 256 * r + 256] = m.heads_dealt[r, :, at : at + 256].astype(F32)

    @pl.when(jnp.logical_not(owner))
    def _():
        out_last.wait_recv()
        o_out[...] = m.out_home[...].astype(F32)

    return_out.arrive()
    for part in [
        visit_rows, visit_cots, spread_gains, spread_heads, spread_out,
        share_rows, share_cots, share_gains, share_out, share_branch, total_out, total_first,
        fold_down, fold_hidden, fold_heads, fold_gains, return_out, return_in,
        deal_hidden_grad, deal_heads_grad, deal_gains,
    ]:
        part.drain()

    @pl.when(owner)
    def _():
        for i in (1, 2, 3):
            out_piece(i).wait_send()
        out_last.wait_send()

    pl.when(jnp.logical_not(owner))(lambda: out_across.wait_send())


def grouped(
    layer_input, doc_ids, attn_gain, query_weight, key_weight, value_weight, out_weight,
    mlp_gain, gate_weight, up_weight, down_weight, out_grad,
):
    dp, ctx = lax.axis_index("dp"), lax.axis_index("ctx")
    x, y, z, k = ctx % 2, dp // 2, ctx // 2, dp % 2
    piece = attn_gain.shape[0]
    lane = piece * (2 * (z % 2) + x)
    gains = jnp.zeros((16, 128), BF16)
    gains = lax.dynamic_update_slice(gains, jnp.stack([attn_gain, mlp_gain]), (0, lane))
    d, f = layer_input.shape[2], gate_weight.shape[1]
    outs = (
        shaped(*layer_input.shape),
        shaped(*layer_input.shape, dtype=F32),
        shaped(piece, d, dtype=F32),
        shaped(piece, d, dtype=F32),
        shaped(piece, d, dtype=F32),
        shaped(piece, d, dtype=F32),
        shaped(piece, f, dtype=F32),
        shaped(piece, f, dtype=F32),
        shaped(*down_weight.shape, dtype=F32),
        shaped(8, 128, dtype=F32),
    )
    rooms = [pltpu.VMEM(shape, dtype) for _, shape, dtype in SCRATCH]
    made = pl.pallas_call(
        layer_body,
        name="layer",
        out_shape=outs,
        in_specs=[ANY, ANY, ANY, VMEM, VMEM, VMEM, ANY, VMEM, VMEM, ANY, ANY],
        out_specs=(ANY,) + (VMEM,) * 9,
        scratch_shapes=rooms
        + [
            pltpu.SemaphoreType.DMA((160,)),
            pltpu.SemaphoreType.DMA((160,)),
            pltpu.SemaphoreType.DMA((16,)),
        ],
        compiler_params=pltpu.CompilerParams(
            collective_id=0, has_side_effects=True, vmem_limit_bytes=61 << 20
        ),
    )(
        layer_input, out_grad, doc_ids.reshape(2, 1, -1), query_weight, key_weight, value_weight,
        out_weight, gate_weight, up_weight, down_weight, gains,
    )
    output, input_grad, q, k_, v, o, g, u, down, gain = made

    def gain_of(row):
        return lax.dynamic_slice(gain, (row + k, lane), (1, piece)).reshape(piece)

    return (output, input_grad, gain_of(0), q, k_, v, o, gain_of(2), g, u, down)


def plain_product(left, right):
    return jnp.dot(left, right, preferred_element_type=jnp.float32)


def plain_product_left(left, right):
    return lax.dot_general(
        left, right, (((0,), (0,)), ((), ())), preferred_element_type=jnp.float32
    )


def plain_product_right(left, right):
    return lax.dot_general(
        left, right, (((1,), (1,)), ((), ())), preferred_element_type=jnp.float32
    )


def normalize(rows, gain):
    inverse = lax.rsqrt(jnp.mean(rows * rows, axis=-1, keepdims=True) + EPS)
    return (rows * inverse * gain, inverse)


def plain_norm_back(rows, inverse, gain, upstream):
    normed = rows * inverse
    scaled = upstream * gain
    grad_rows = inverse * (scaled - normed * jnp.mean(scaled * normed, axis=-1, keepdims=True))
    return (grad_rows, jnp.sum(upstream * normed, axis=0))


def head_pair(array, start):
    piece = lax.dynamic_slice_in_dim(array, start, 2 * HEAD, 2)
    return piece.reshape(array.shape[0], array.shape[1], 2, HEAD)


def pair_scores(query, keys, allowed, start):
    scores = jnp.einsum(
        "sqhd,skhd->shqk",
        head_pair(query, start),
        head_pair(keys, start),
        preferred_element_type=jnp.float32,
    ) * HEAD ** (-0.5)
    return jnp.where(allowed[:, None], scores, -1e30)


def plain_attend(query, keys, values, allowed):
    groups, rows, width = query.shape

    def step(index, carry):
        mixed_all, logsum = carry
        start = index * 2 * HEAD
        scores = pair_scores(query, keys, allowed, start)
        top = jnp.max(scores, axis=-1, keepdims=True)
        lifted = jnp.exp(scores - top)
        total = jnp.sum(lifted, axis=-1, keepdims=True)
        probs = (lifted / total).astype(jnp.bfloat16)
        mixed = jnp.einsum(
            "shqk,skhd->sqhd", probs, head_pair(values, start), preferred_element_type=jnp.float32
        )
        mixed_all = lax.dynamic_update_slice_in_dim(
            mixed_all, mixed.reshape(groups, rows, 2 * HEAD).astype(jnp.bfloat16), start, 2
        )
        logsum = lax.dynamic_update_slice_in_dim(
            logsum, (top + jnp.log(total))[..., 0], index * 2, 1
        )
        return (mixed_all, logsum)

    start_state = (
        jnp.zeros((groups, rows, width), jnp.bfloat16),
        jnp.zeros((groups, width // HEAD, rows), jnp.float32),
    )
    return lax.fori_loop(0, width // (2 * HEAD), step, start_state)


def plain_attend_back(query, keys, values, allowed, logsum, grad_mixed):
    groups, rows, width = query.shape
    length = keys.shape[1]
    scale = HEAD ** (-0.5)

    def step(index, carry):
        grad_query, grad_keys, grad_values = carry
        start = index * 2 * HEAD
        scores = pair_scores(query, keys, allowed, start)
        kept = lax.dynamic_slice_in_dim(logsum, index * 2, 2, 1)
        probs = jnp.exp(scores - kept[..., None])
        upstream = head_pair(grad_mixed, start)
        grad_probs = jnp.einsum(
            "sqhd,skhd->shqk",
            upstream,
            head_pair(values, start),
            preferred_element_type=jnp.float32,
        )
        grad_scores = (
            probs * (grad_probs - jnp.sum(probs * grad_probs, axis=-1, keepdims=True))
        ).astype(jnp.bfloat16)
        part_query = (
            jnp.einsum(
                "shqk,skhd->sqhd",
                grad_scores,
                head_pair(keys, start),
                preferred_element_type=jnp.float32,
            )
            * scale
        )
        part_keys = (
            jnp.einsum(
                "shqk,sqhd->skhd",
                grad_scores,
                head_pair(query, start),
                preferred_element_type=jnp.float32,
            )
            * scale
        )
        part_values = jnp.einsum(
            "shqk,sqhd->skhd",
            probs.astype(jnp.bfloat16),
            upstream,
            preferred_element_type=jnp.float32,
        )
        grad_query = lax.dynamic_update_slice_in_dim(
            grad_query, part_query.reshape(groups, rows, 2 * HEAD), start, 2
        )
        grad_keys = lax.dynamic_update_slice_in_dim(
            grad_keys, part_keys.reshape(groups, length, 2 * HEAD), start, 2
        )
        grad_values = lax.dynamic_update_slice_in_dim(
            grad_values, part_values.reshape(groups, length, 2 * HEAD), start, 2
        )
        return (grad_query, grad_keys, grad_values)

    start_state = (
        jnp.zeros((groups, rows, width), jnp.float32),
        jnp.zeros((groups, length, width), jnp.float32),
        jnp.zeros((groups, length, width), jnp.float32),
    )
    return lax.fori_loop(0, width // (2 * HEAD), step, start_state)


def on_device(
    layer_input,
    doc_ids,
    attn_gain,
    query_weight,
    key_weight,
    value_weight,
    out_weight,
    mlp_gain,
    gate_weight,
    up_weight,
    down_weight,
    out_grad,
):
    groups, rows, width = layer_input.shape
    length = doc_ids.shape[1]
    gathered = (
        lax.all_gather(attn_gain, ("dp", "ctx"), axis=0, tiled=True),
        lax.all_gather(query_weight, ("dp", "ctx"), axis=0, tiled=True),
        lax.all_gather(key_weight, ("dp", "ctx"), axis=0, tiled=True),
        lax.all_gather(value_weight, ("dp", "ctx"), axis=0, tiled=True),
        lax.all_gather(out_weight, ("dp", "ctx"), axis=0, tiled=True),
        lax.all_gather(mlp_gain, ("dp", "ctx"), axis=0, tiled=True),
        lax.all_gather(gate_weight, ("dp", "ctx"), axis=0, tiled=True),
        lax.all_gather(up_weight, ("dp", "ctx"), axis=0, tiled=True),
        lax.all_gather(down_weight, ("dp", "ctx"), axis=0, tiled=True),
    )
    gain_one, w_query, w_key, w_value, w_out, gain_two, w_gate, w_up, w_down = gathered
    first = lax.axis_index("ctx") * rows
    places = jnp.arange(length)
    own_ids = lax.dynamic_slice_in_dim(doc_ids, first, rows, 1)
    own_places = first + jnp.arange(rows)
    allowed = (own_ids[:, :, None] == doc_ids[:, None, :]) & (
        places[None, None, :] <= own_places[None, :, None]
    )
    inputs = layer_input.reshape(groups * rows, width).astype(jnp.float32)
    gain_attn = gain_one.astype(jnp.float32)
    normed_full, inverse_one = normalize(inputs, gain_attn)
    normed = normed_full.astype(jnp.bfloat16)
    query = plain_product(normed, w_query).astype(jnp.bfloat16).reshape(groups, rows, width)
    keys_own = plain_product(normed, w_key).astype(jnp.bfloat16).reshape(groups, rows, width)
    values_own = plain_product(normed, w_value).astype(jnp.bfloat16).reshape(groups, rows, width)
    keys, values = (
        lax.all_gather(keys_own, "ctx", axis=1, tiled=True),
        lax.all_gather(values_own, "ctx", axis=1, tiled=True),
    )
    attended, logsum = plain_attend(query, keys, values, allowed)
    attended_rows = attended.reshape(groups * rows, width)
    middle = inputs + plain_product(attended_rows, w_out)
    gain_mlp = gain_two.astype(jnp.float32)
    normed_two_full, inverse_two = normalize(middle, gain_mlp)
    normed_two = normed_two_full.astype(jnp.bfloat16)
    gate = plain_product(normed_two, w_gate)
    upward = plain_product(normed_two, w_up)
    sigma = jax.nn.sigmoid(gate)
    hidden = (gate * sigma * upward).astype(jnp.bfloat16)
    layer_output = (middle + plain_product(hidden, w_down)).astype(jnp.bfloat16)
    gathered_back = (
        lax.all_gather(attn_gain, ("dp", "ctx"), axis=0, tiled=True),
        lax.all_gather(query_weight, ("dp", "ctx"), axis=0, tiled=True),
        lax.all_gather(key_weight, ("dp", "ctx"), axis=0, tiled=True),
        lax.all_gather(value_weight, ("dp", "ctx"), axis=0, tiled=True),
        lax.all_gather(out_weight, ("dp", "ctx"), axis=0, tiled=True),
        lax.all_gather(mlp_gain, ("dp", "ctx"), axis=0, tiled=True),
        lax.all_gather(gate_weight, ("dp", "ctx"), axis=0, tiled=True),
        lax.all_gather(up_weight, ("dp", "ctx"), axis=0, tiled=True),
        lax.all_gather(down_weight, ("dp", "ctx"), axis=0, tiled=True),
    )
    gain_one, w_query, w_key, w_value, w_out, gain_two, w_gate, w_up, w_down = gathered_back
    upstream = out_grad.reshape(groups * rows, width)
    down_grad = plain_product_left(hidden, upstream)
    grad_hidden = plain_product_right(upstream, w_down)
    grad_gate = (grad_hidden * upward * sigma * (1.0 + gate * (1.0 - sigma))).astype(jnp.bfloat16)
    grad_up = (grad_hidden * gate * sigma).astype(jnp.bfloat16)
    gate_grad = plain_product_left(normed_two, grad_gate)
    up_grad = plain_product_left(normed_two, grad_up)
    grad_normed_two = plain_product_right(grad_gate, w_gate) + plain_product_right(grad_up, w_up)
    grad_middle, mlp_gain_grad = plain_norm_back(
        middle, inverse_two, gain_two.astype(jnp.float32), grad_normed_two
    )
    grad_middle = grad_middle + upstream.astype(jnp.float32)
    grad_branch = grad_middle.astype(jnp.bfloat16)
    out_proj_grad = plain_product_left(attended_rows, grad_branch)
    grad_attended = (
        plain_product_right(grad_branch, w_out).astype(jnp.bfloat16).reshape(groups, rows, width)
    )
    grad_query, grad_keys_all, grad_values_all = plain_attend_back(
        query, keys, values, allowed, logsum, grad_attended
    )
    grad_keys, grad_values = (
        lax.psum_scatter(
            grad_keys_all.astype(jnp.bfloat16), "ctx", scatter_dimension=1, tiled=True
        ).astype(jnp.float32),
        lax.psum_scatter(
            grad_values_all.astype(jnp.bfloat16), "ctx", scatter_dimension=1, tiled=True
        ).astype(jnp.float32),
    )
    grad_query = grad_query.astype(jnp.bfloat16).reshape(groups * rows, width)
    grad_keys = grad_keys.astype(jnp.bfloat16).reshape(groups * rows, width)
    grad_values = grad_values.astype(jnp.bfloat16).reshape(groups * rows, width)
    query_grad = plain_product_left(normed, grad_query)
    key_grad = plain_product_left(normed, grad_keys)
    value_grad = plain_product_left(normed, grad_values)
    grad_normed = (
        plain_product_right(grad_query, w_query)
        + plain_product_right(grad_keys, w_key)
        + plain_product_right(grad_values, w_value)
    )
    grad_inputs, attn_gain_grad = plain_norm_back(
        inputs, inverse_one, gain_one.astype(jnp.float32), grad_normed
    )
    input_grad = (grad_middle + grad_inputs).reshape(groups, rows, width)
    shares = (
        lax.psum_scatter(attn_gain_grad, ("dp", "ctx"), scatter_dimension=0, tiled=True),
        lax.psum_scatter(query_grad, ("dp", "ctx"), scatter_dimension=0, tiled=True),
        lax.psum_scatter(key_grad, ("dp", "ctx"), scatter_dimension=0, tiled=True),
        lax.psum_scatter(value_grad, ("dp", "ctx"), scatter_dimension=0, tiled=True),
        lax.psum_scatter(out_proj_grad, ("dp", "ctx"), scatter_dimension=0, tiled=True),
        lax.psum_scatter(mlp_gain_grad, ("dp", "ctx"), scatter_dimension=0, tiled=True),
        lax.psum_scatter(gate_grad, ("dp", "ctx"), scatter_dimension=0, tiled=True),
        lax.psum_scatter(up_grad, ("dp", "ctx"), scatter_dimension=0, tiled=True),
        lax.psum_scatter(down_grad, ("dp", "ctx"), scatter_dimension=0, tiled=True),
    )
    return (
        layer_output.reshape(groups, rows, width),
        input_grad,
        shares[0],
        shares[1],
        shares[2],
        shares[3],
        shares[4],
        shares[5],
        shares[6],
        shares[7],
        shares[8],
    )


def solution(mesh):
    placed = (
        P("dp", "ctx", None),
        P("dp", None),
        P(("dp", "ctx")),
        P(("dp", "ctx"), None),
        P(("dp", "ctx"), None),
        P(("dp", "ctx"), None),
        P(("dp", "ctx"), None),
        P(("dp", "ctx")),
        P(("dp", "ctx"), None),
        P(("dp", "ctx"), None),
        P(("dp", "ctx"), None),
        P("dp", "ctx", None),
    )
    fits = mesh.shape["dp"] == 4 and mesh.shape["ctx"] == 8
    body = grouped if fits else on_device
    return jax.shard_map(
        body,
        mesh=mesh,
        in_specs=placed,
        out_specs=(
            P("dp", "ctx", None),
            P("dp", "ctx", None),
            P(("dp", "ctx")),
            P(("dp", "ctx"), None),
            P(("dp", "ctx"), None),
            P(("dp", "ctx"), None),
            P(("dp", "ctx"), None),
            P(("dp", "ctx")),
            P(("dp", "ctx"), None),
            P(("dp", "ctx"), None),
            P(("dp", "ctx"), None),
        ),
        check_vma=False,
    )
```

```python
import functools

import jax
import jax.numpy as jnp
from jax import lax
from jax.experimental import pallas as pl
from jax.experimental.pallas import tpu as pltpu
from jax.sharding import PartitionSpec as P

HEAD = 64


EPS = 1e-05
MESH = pl.DeviceIdType.MESH
F32 = jnp.float32
BF16 = jnp.bfloat16
LOG2E = 1.4426950408889634
ANY = pl.BlockSpec(memory_space=pl.ANY)
VMEM = pl.BlockSpec(memory_space=pltpu.VMEM)


class Wires:
    def __init__(self, send, recv):
        dp, ctx = lax.axis_index("dp"), lax.axis_index("ctx")
        self.x, self.y = ctx % 2, dp // 2
        self.zh, self.zb = ctx // 4, (ctx // 2) % 2
        self.zl, self.k = (self.zb + self.zh) % 2, dp % 2
        self.send, self.recv = send, recv
        self.used = 0

    def slots(self, count):
        first = self.used
        self.used += count
        return first

    def at(self, x=None, y=None, zh=None, zl=None, k=None):
        x = self.x if x is None else x
        y = self.y if y is None else y
        zh = self.zh if zh is None else zh
        zl = self.zl if zl is None else zl
        k = self.k if k is None else k
        return (2 * y + k, 4 * zh + 2 * ((zl + zh) % 2) + x)

    def across(self):
        return self.at(zl=1 - self.zl)

    def core(self):
        return self.at(k=1 - self.k)

    def copy(self, source, target, device, slot, recv_slot=None):
        return pltpu.make_async_remote_copy(
            src_ref=source,
            dst_ref=target,
            send_sem=self.send.at[slot],
            recv_sem=self.recv.at[slot if recv_slot is None else recv_slot],
            device_id=device,
            device_id_type=MESH,
        )

    def greet(self):
        barrier = pltpu.get_barrier_semaphore()
        peers = [self.at(y=1 - self.y)]
        for n in range(1, 16):
            bits = [(n >> i) % 2 for i in range(4)]
            x, zh, zl, k = [
                1 - own if bit else own
                for own, bit in zip((self.x, self.zh, self.zl, self.k), bits)
            ]
            peers.append(self.at(x=x, zh=zh, zl=zl, k=k))
        for peer in peers:
            pl.semaphore_signal(barrier, inc=1, device_id=peer, device_id_type=MESH)
        pl.semaphore_wait(barrier, len(peers))


class Pairs:
    def __init__(self, wires, order):
        self.w, self.order = wires, order

    def place(self, z, a, b):
        w = self.w
        x, y = (a, b) if self.order == "xy" else (b, a)
        flip = lambda own, turn: 1 - own if turn else own
        return flip(w.x, x), flip(w.y, y), flip(w.zh, z)

    def partner(self, z, a, b):
        x, y, zh = self.place(z, a, b)
        return self.w.at(x=x, y=y, zh=zh)


class Spread(Pairs):
    SENDS = ((0, 0, 0), (0, 0, 0), (1, 0, 0), (0, 0, 0), (1, 0, 0), (0, 1, 0), (1, 1, 0))
    STEPS = ((1, 0, 0), (0, 1, 0), (0, 1, 0), (0, 0, 1), (0, 0, 1), (0, 0, 1), (0, 0, 1))

    def __init__(self, wires, order, block, own=None):
        super().__init__(wires, order)
        self.block, self.own = block, own
        self.first = wires.slots(7)

    def piece(self, n):
        ref = self.block(*self.place(*self.SENDS[n]))
        source = self.own if self.own is not None and not any(self.SENDS[n]) else ref
        return self.w.copy(source, ref, self.partner(*self.STEPS[n]), self.first + n)

    def landed(self, n):
        came = [i ^ j for i, j in zip(self.SENDS[n], self.STEPS[n])]
        ref = self.block(*self.place(*came))
        return self.w.copy(ref, ref, self.partner(*self.STEPS[n]), self.first + n)

    def start(self):
        for n in (0, 1, 3):
            self.piece(n).start()

    def got_first(self):
        self.landed(1).wait_recv()
        self.piece(5).start()

    def got_z(self):
        self.landed(0).wait_recv()
        self.piece(2).start()
        self.piece(4).start()

    def got_last(self):
        self.landed(2).wait_recv()
        self.piece(6).start()

    def arrive(self):
        for n in (3, 4, 5, 6):
            self.landed(n).wait_recv()

    def drain(self):
        for n in range(7):
            self.piece(n).wait_send()


class Share:
    def __init__(self, wires, block):
        self.w, self.block = wires, block
        self.first = wires.slots(3)

    def piece(self, i):
        w = self.w
        ref = self.block(w.zl if i < 2 else 1 - w.zl, w.k)
        return w.copy(ref, ref, w.across() if i == 0 else w.core(), self.first + i)

    def landed(self, i):
        w = self.w
        ref = self.block(*[(1 - w.zl, w.k), (w.zl, 1 - w.k), (1 - w.zl, 1 - w.k)][i])
        return w.copy(ref, ref, w.core(), self.first + i)

    def start(self):
        self.piece(0).start()
        self.piece(1).start()

    def forward(self):
        self.landed(0).wait_recv()
        self.piece(2).start()

    def arrive(self):
        self.landed(1).wait_recv()
        self.landed(2).wait_recv()

    def drain(self):
        for i in range(3):
            self.piece(i).wait_send()


class Deal:
    def __init__(self, wires, outgoing, incoming):
        self.w, self.outgoing, self.incoming = wires, outgoing, incoming
        self.first = wires.slots(3)

    def mate(self, i):
        w = self.w
        return [(1 - w.zl, w.k), (w.zl, 1 - w.k), (1 - w.zl, 1 - w.k)][i]

    def piece(self, i):
        w = self.w
        zl, k = self.mate(i)
        return w.copy(
            self.outgoing(zl, k), self.incoming(w.zl, w.k), w.at(zl=zl, k=k), self.first + i
        )

    def landed(self, i):
        zl, k = self.mate(i)
        ref = self.incoming(zl, k)
        return self.w.copy(ref, ref, self.w.at(zl=zl, k=k), self.first + i)

    def start(self):
        for i in range(3):
            self.piece(i).start()

    def arrive(self):
        for i in range(3):
            self.landed(i).wait_recv()

    def drain(self):
        for i in range(3):
            self.piece(i).wait_send()


def every(*tests):
    all_of = tests[0]
    for test in tests[1:]:
        all_of = jnp.logical_and(all_of, test)
    return all_of


class Visit:
    def __init__(self, wires, home, full, local):
        self.w, self.home, self.full, self.local = wires, home, full, local
        self.first = wires.slots(2)
        w = wires
        self.own = [every(w.x == j, w.zh == w.k, w.zl == w.x, w.zb == w.k) for j in range(2)]
        self.here = [every(w.zh == i, w.zl == w.x, w.zb == w.k, w.zh == w.k) for i in range(2)]

    def piece(self, j):
        w = self.w
        return w.copy(
            self.home.at[j],
            self.full(w.zh, w.zb, w.x),
            w.at(x=j, zh=w.k, zl=w.x, k=w.zb),
            self.first + j,
            self.first + w.zh,
        )

    def stay(self, j):
        w = self.w
        return pltpu.make_async_copy(self.home.at[j], self.full(w.zh, w.zb, w.x), self.local)

    def landed(self, i):
        w = self.w
        ref = self.full(i, w.k, w.zl)
        return w.copy(ref, ref, w.core(), self.first + i)

    def start(self):
        for j in range(2):
            pl.when(self.own[j])(lambda: self.stay(j).start())
            pl.when(jnp.logical_not(self.own[j]))(lambda: self.piece(j).start())

    def arrive(self):
        for j in range(2):
            pl.when(self.own[j])(lambda: self.stay(j).wait())
        for i in range(2):
            pl.when(jnp.logical_not(self.here[i]))(lambda: self.landed(i).wait_recv())

    def drain(self):
        for j in range(2):
            pl.when(jnp.logical_not(self.own[j]))(lambda: self.piece(j).wait_send())


class Return:
    def __init__(self, wires, done, home, local):
        self.w, self.done, self.home, self.local = wires, done, home, local
        self.first = wires.slots(2)
        w = wires
        self.own = [every(w.x == w.zl, w.zh == i, w.zb == w.k, w.k == w.zh) for i in range(2)]
        self.here = [every(w.x == j, w.zh == w.k, w.zl == w.x, w.zb == w.k) for j in range(2)]

    def piece(self, i):
        w = self.w
        return w.copy(
            self.done(i),
            self.home.at[w.x],
            w.at(x=w.zl, zh=i, zl=(w.k + i) % 2, k=w.zh),
            self.first + i,
            self.first + w.x,
        )

    def stay(self, i):
        return pltpu.make_async_copy(self.done(i), self.home.at[self.w.x], self.local)

    def landed(self, j):
        ref = self.home.at[j]
        return self.w.copy(ref, ref, self.w.core(), self.first + j)

    def start(self):
        for i in range(2):
            pl.when(self.own[i])(lambda: self.stay(i).start())
            pl.when(jnp.logical_not(self.own[i]))(lambda: self.piece(i).start())

    def arrive(self):
        for i in range(2):
            pl.when(self.own[i])(lambda: self.stay(i).wait())
        for j in range(2):
            pl.when(jnp.logical_not(self.here[j]))(lambda: self.landed(j).wait_recv())

    def drain(self):
        for i in range(2):
            pl.when(jnp.logical_not(self.own[i]))(lambda: self.piece(i).wait_send())


def shaped(*shape, dtype=BF16):
    return jax.ShapeDtypeStruct(shape, dtype)


def pack_rows(columns, shards, packed):
    for rank in range(4):
        at = 0
        for shard in shards:
            for start, width in columns(rank):
                packed[rank, :, at : at + width] = shard[:, start : start + width]
                at += width


def head_columns(rank):
    return [(256 * rank, 256)]


def hidden_columns(rank):
    zl, k = rank // 2, rank % 2
    return [
        (128 * (16 * y + 8 * k + 4 * zh + 2 * (zl ^ zh) + x), 128)
        for y in range(2)
        for zh in range(2)
        for x in range(2)
    ]


class Total:
    def __init__(self, wires, part, got_core, got_across):
        self.w, self.part, self.got_core, self.got_across = wires, part, got_core, got_across
        self.first = wires.slots(4)
        self.half = part.shape[2] // 2

    def core(self, i):
        w = self.w
        return w.copy(
            self.part.at[0, i], self.got_core.at[i], w.core(), self.first + i
        )

    def rows(self, x):
        return pl.ds(pl.multiple_of(self.half * x, self.half), self.half)

    def across(self, i):
        w = self.w
        return w.copy(
            self.part.at[1, i, self.rows(1 - w.zl)],
            self.got_across.at[i],
            w.across(),
            self.first + 2 + i,
        )

    def give(self, i, value):
        self.part[0, i] = value.astype(BF16)
        self.core(i).start()

    def keep(self, i, value):
        self.core(i).wait_recv()
        self.part[1, i] = (value + self.got_core[i].astype(F32)).astype(BF16)
        self.across(i).start()

    def take(self, i):
        self.across(i).wait_recv()
        own = self.part[1, i, self.rows(self.w.zl)]
        return own.astype(F32) + self.got_across[i].astype(F32)

    def drain(self):
        for i in range(2):
            self.core(i).wait_send()
            self.across(i).wait_send()


class Fold(Pairs):
    def __init__(self, wires, order, whole, block, got_b, got_b_block, got_a, got_z):
        super().__init__(wires, order)
        self.whole, self.block = whole, block
        self.got_b, self.got_b_block, self.got_a, self.got_z = got_b, got_b_block, got_a, got_z
        self.first = wires.slots(4)

    def stage_b(self):
        w = self.w
        b = w.y if self.order == "xy" else w.x
        return w.copy(self.whole(1 - b), self.got_b, self.partner(0, 0, 1), self.first)

    def stage_a(self, z):
        x, y, zh = self.place(z, 1, 0)
        return self.w.copy(
            self.block(x, y, zh), self.got_a.at[zh], self.partner(0, 1, 0), self.first + 1 + z,
            self.first + 1 + z,
        )

    def landed_a(self, z):
        x, y, zh = self.place(z, 0, 0)
        ref = self.got_a.at[zh]
        return self.w.copy(ref, ref, self.partner(0, 1, 0), self.first + 1 + z)

    def stage_z(self):
        ref = self.block(*self.place(1, 0, 0))
        return self.w.copy(ref, self.got_z, self.partner(1, 0, 0), self.first + 3)

    def two(self, z, a):
        x, y, zh = self.place(z, a, 0)
        own = self.block(x, y, zh)[...].astype(F32)
        return own + self.got_b_block(x if self.order == "xy" else y, zh)[...].astype(F32)

    def three(self, z):
        return self.two(z, 0) + self.got_a[self.place(z, 0, 0)[2]].astype(F32)

    def start(self):
        self.stage_b().start()

    def second(self):
        self.stage_b().wait_recv()
        for z in (1, 0):
            ref = self.block(*self.place(z, 1, 0))
            ref[...] = self.two(z, 1).astype(self.got_z.dtype)
            self.stage_a(z).start()

    def third(self):
        self.landed_a(1).wait_recv()
        ref = self.block(*self.place(1, 0, 0))
        ref[...] = self.three(1).astype(self.got_z.dtype)
        self.stage_z().start()

    def finish(self):
        self.landed_a(0).wait_recv()
        total = self.three(0)
        self.stage_z().wait_recv()
        return total + self.got_z[...].astype(F32)

    def drain(self):
        self.stage_b().wait_send()
        for z in range(2):
            self.stage_a(z).wait_send()
        self.stage_z().wait_send()


def dots(left, right, dims):
    return lax.dot_general(left, right, (dims, ((), ())), preferred_element_type=F32)


NN, NT, TN = ((1,), (0,)), ((1,), (1,)), ((0,), (0,))


def only_head(array, head):
    lane = lax.broadcasted_iota(jnp.int32, array.shape, 1)
    return jnp.where(lane // HEAD == head, array, jnp.zeros_like(array))


def inverse_size(rows):
    return lax.rsqrt(jnp.mean(rows * rows, axis=-1, keepdims=True) + EPS)


def norm_back(rows, gain, upstream):
    inverse = inverse_size(rows)
    normed = rows * inverse
    scaled = upstream * gain
    grad_rows = inverse * (scaled - normed * jnp.mean(scaled * normed, axis=-1, keepdims=True))
    return grad_rows, jnp.sum(upstream * normed, axis=0, keepdims=True)


SCRATCH = [
    ("rows_all", (2, 2, 2, 128, 1024), BF16),
    ("cots_all", (2, 2, 2, 128, 1024), BF16),
    ("ids_all", (2, 2, 1, 1024), jnp.int32),
    ("heads_all", (2, 2, 2, 2, 2, 32, 768), BF16),
    ("out_all", (2, 2, 2, 2, 2, 32, 1024), BF16),
    ("gate_all", (2, 2, 2, 2, 2, 32, 1024), BF16),
    ("up_all", (2, 2, 2, 2, 2, 32, 1024), BF16),
    ("down_all", (2, 2, 2, 128, 1024), BF16),
    ("gains_all", (2, 2, 2, 2, 2, 16, 128), BF16),
    ("heads_pack", (4, 32, 768), BF16),
    ("gate_pack", (4, 32, 1024), BF16),
    ("up_pack", (4, 32, 1024), BF16),
    ("normed", (1024, 1024), BF16),
    ("query", (1024, 256), BF16),
    ("keys", (1024, 256), BF16),
    ("values", (1024, 256), BF16),
    ("keys_turned", (256, 1024), BF16),
    ("values_turned", (256, 1024), BF16),
    ("mixed_turned", (256, 1024), BF16),
    ("mixed_all", (2, 2, 256, 1024), BF16),
    ("logsum", (4, 1, 1024), F32),
    ("gain_rows", (2, 1, 1024), F32),
    ("ids_row", (1, 1024), F32),
    ("ids_col", (1024, 128), F32),
    ("middle_keep", (2, 256, 1024), F32),
    ("normed_two", (1024, 1024), BF16),
    ("hidden", (1024, 1024), BF16),
    ("grad_gate", (1024, 1024), BF16),
    ("grad_up", (1024, 1024), BF16),
    ("part_norm", (2, 2, 256, 1024), BF16),
    ("core_out", (2, 256, 1024), BF16),
    ("core_norm", (2, 256, 1024), BF16),
    ("across_out", (2, 128, 1024), BF16),
    ("across_norm", (2, 128, 1024), BF16),
    ("branch", (2, 2, 2, 128, 1024), BF16),
    ("grad_keys", (1024, 256), F32),
    ("grad_values", (1024, 256), F32),
    ("heads_part", (2, 2, 2, 2, 2, 32, 768), BF16),
    ("out_part", (2, 2, 2, 32, 1024), BF16),
    ("gains_part", (2, 2, 2, 8, 128), F32),
    ("heads_b", (2, 2, 2, 2, 32, 768), BF16),
    ("heads_a", (2, 2, 2, 32, 768), BF16),
    ("heads_z", (2, 2, 32, 768), BF16),
    ("gate_b", (2, 2, 2, 2, 32, 1024), BF16),
    ("gate_a", (2, 2, 2, 32, 1024), BF16),
    ("gate_z", (2, 2, 32, 1024), BF16),
    ("up_b", (2, 2, 2, 2, 32, 1024), BF16),
    ("up_a", (2, 2, 2, 32, 1024), BF16),
    ("up_z", (2, 2, 32, 1024), BF16),
    ("down_b", (2, 2, 128, 1024), BF16),
    ("down_a", (2, 128, 1024), BF16),
    ("down_z", (128, 1024), BF16),
    ("out_b", (2, 2, 2, 32, 1024), BF16),
    ("out_a", (2, 2, 32, 1024), BF16),
    ("out_z", (2, 32, 1024), BF16),
    ("gains_b", (2, 2, 8, 128), F32),
    ("gains_a", (2, 8, 128), F32),
    ("gains_z", (8, 128), F32),
    ("heads_dealt", (4, 32, 768), BF16),
    ("gate_dealt", (4, 32, 1024), BF16),
    ("up_dealt", (4, 32, 1024), BF16),
    ("gains_deal", (8, 128), F32),
    ("gains_dealt", (4, 8, 128), F32),
    ("out_deal", (32, 1024), BF16),
    ("out_home", (32, 1024), BF16),
    ("done_out", (2, 128, 1024), BF16),
    ("input_home", (2, 128, 1024), BF16),
]


def layer_body(
    rows, cots, ids, wq, wk, wv, wo, wg, wu, wd, gains,
    output, input_grad, q_out, k_out, v_out, o_out, g_out, u_out, d_out, gain_out,
    *scratch,
):
    send, recv, local = scratch[-3:]
    m = type("Memory", (), dict(zip([name for name, _, _ in SCRATCH], scratch)))
    w = Wires(send, recv)
    x, y, zh, zb, zl, k = w.x, w.y, w.zh, w.zb, w.zl, w.k
    rank = 2 * zl + k
    w.greet()

    used = [0]

    def spare():
        used[0] += 1
        return local.at[used[0] - 1]

    def stay(source, target):
        copy = pltpu.make_async_copy(source, target, spare())
        copy.start()
        return copy

    def sequence_block(ref):
        return lambda zh, zb, x: ref.at[zh, zb, x]

    def deal_rows(packed, whole):
        return Deal(
            w,
            lambda zl, k: packed.at[2 * zl + k],
            lambda szl, sk: whole.at[y, sk, zh, (szl + zh) % 2, x],
        )

    def group_rows(ref):
        return lambda x, y, zh: ref.at[y, :, zh, :, x]

    def own_rows(ref):
        return lambda x, y, zh: ref.at[y, k, zh, (zl + zh) % 2, x]

    visit_rows = Visit(w, rows, sequence_block(m.rows_all), spare())
    visit_rows.start()
    pack_rows(head_columns, (wq, wk, wv), m.heads_pack)
    deal_heads = deal_rows(m.heads_pack, m.heads_all)
    deal_heads.start()
    stays = [
        stay(m.heads_pack.at[rank], m.heads_all.at[y, k, zh, zb, x]),
        stay(wo, m.out_all.at[y, k, zh, zb, x]),
        stay(gains, m.gains_all.at[y, k, zh, zb, x]),
        stay(wd, m.down_all.at[y, zh, x]),
        stay(ids, m.ids_all.at[k]),
    ]
    swap = w.copy(ids, m.ids_all.at[k], w.core(), w.slots(1))
    swap.start()
    spread_gains = Spread(w, "xy", own_rows(m.gains_all), gains)
    spread_gains.start()
    pack_rows(hidden_columns, (wg,), m.gate_pack)
    pack_rows(hidden_columns, (wu,), m.up_pack)
    stays.append(stay(m.gate_pack.at[rank], m.gate_all.at[y, k, zh, zb, x]))
    stays.append(stay(m.up_pack.at[rank], m.up_all.at[y, k, zh, zb, x]))
    deal_gate = deal_rows(m.gate_pack, m.gate_all)
    deal_up = deal_rows(m.up_pack, m.up_all)
    for copy in stays:
        copy.wait()
    deal_heads.arrive()
    spread_heads = Spread(w, "yx", group_rows(m.heads_all))
    spread_heads.start()
    spread_out = Spread(w, "yx", own_rows(m.out_all), wo)
    spread_out.start()
    visit_rows.arrive()
    share_rows = Share(w, lambda zl, k: m.rows_all.at[:, k, zl])
    share_rows.start()
    deal_gate.start()
    deal_up.start()
    spread_gains.got_first()
    spread_gains.got_z()
    spread_gains.got_last()
    spread_heads.got_first()
    spread_heads.got_z()
    share_rows.forward()
    deal_gate.arrive()
    spread_gate = Spread(w, "xy", group_rows(m.gate_all))
    spread_gate.start()
    deal_up.arrive()
    spread_up = Spread(w, "yx", group_rows(m.up_all))
    spread_up.start()
    spread_down = Spread(w, "xy", lambda x, y, zh: m.down_all.at[y, zh, x], wd)
    spread_down.start()
    spread_heads.got_last()
    spread_gains.arrive()
    share_gains = [
        Share(w, lambda zl, k: m.gains_all.at[:, k, 0, zl]),
        Share(w, lambda zl, k: m.gains_all.at[:, k, 1, 1 - zl]),
    ]
    for share in share_gains:
        share.start()
    swap.wait()
    m.ids_row[...] = m.ids_all[zh, x].astype(F32)
    for j in range(8):
        piece = slice(128 * j, 128 * j + 128)
        m.ids_col[piece, :] = jnp.broadcast_to(m.ids_row[:, piece], (128, 128)).T
    for share in share_gains:
        share.forward()
    share_rows.arrive()
    for share in share_gains:
        share.arrive()
    for j in range(8):
        four = [
            m.gains_all[j // 4, (j // 2) % 2, j % 2, i // 2, i % 2].astype(F32) for i in range(4)
        ]
        total = four[0] + four[1] + four[2] + four[3]
        for i in range(2):
            m.gain_rows[i, :, 128 * j : 128 * j + 128] = total[i : i + 1, :]

    def first_norm(b, _):
        block = m.rows_all[b // 2, b % 2].reshape(256, 1024).astype(F32)
        span = pl.ds(pl.multiple_of(256 * b, 256), 256)
        m.normed[span, :] = (block * inverse_size(block) * m.gain_rows[0]).astype(BF16)
        return 0

    lax.fori_loop(0, 4, first_norm, 0)
    spread_out.got_first()
    spread_out.got_z()
    visit_cots = Visit(w, cots, sequence_block(m.cots_all), spare())
    visit_cots.start()
    spread_gate.got_first()
    spread_up.got_first()
    spread_down.got_first()
    spread_heads.arrive()
    heads = m.heads_all[...].reshape(1024, 768)
    for b in range(4):
        span = slice(256 * b, 256 * b + 256)
        made = dots(m.normed[span, :], heads, NN).astype(BF16)
        m.query[span, :], m.keys[span, :] = made[:, :256], made[:, 256:512]
        m.values[span, :] = made[:, 512:]
        m.keys_turned[:, span] = made[:, 256:512].T
        m.values_turned[:, span] = made[:, 512:].T
    spread_out.got_last()

    def bias_of(b):
        start, count = 256 * b, 256 * b + 256
        column = m.ids_col[:count, :]
        same = jnp.concatenate([column, column], axis=1) == m.ids_row[:, start : start + 256]
        key = lax.broadcasted_iota(jnp.int32, (count, 256), 0)
        place = lax.broadcasted_iota(jnp.int32, (count, 256), 1) + start
        return jnp.where(jnp.logical_and(same, key <= place), 0.0, -1e30).astype(F32)

    def head_rows(h):
        return pl.ds(pl.multiple_of(h * HEAD, HEAD), HEAD)

    def rank_columns(zl, k):
        return pl.ds(pl.multiple_of(256 * (2 * zl + k), 256), 256)

    def mix(b):
        span, count = slice(256 * b, 256 * b + 256), 256 * b + 256
        bias = bias_of(b)

        def one(h, _):
            scores = dots(m.keys[:count, :], only_head(m.query[span, :], h), NT)
            scores = scores * (HEAD**-0.5 * LOG2E) + bias
            top = jnp.max(scores, axis=0, keepdims=True)
            lifted = jnp.exp2(scores - top)
            total = jnp.sum(lifted, axis=0, keepdims=True)
            probs = (lifted * (1.0 / total)).astype(BF16)
            mixed = dots(m.values_turned[head_rows(h), :count], probs, NN)
            m.mixed_turned[head_rows(h), span] = mixed.astype(BF16)
            m.logsum[h, :, span] = top + jnp.log2(total)
            return 0

        lax.fori_loop(0, 4, one, 0)
        m.mixed_all[b // 2, b % 2, :, rank_columns(zl, k)] = m.mixed_turned[:, span].T

    def share_mixed(b):
        return Share(w, lambda zl, k: m.mixed_all.at[b // 2, b % 2, :, rank_columns(zl, k)])

    shares = [share_mixed(b) for b in range(4)]
    mix(0)
    shares[0].start()
    visit_cots.arrive()
    share_cots = Share(w, lambda zl, k: m.cots_all.at[:, k, zl])
    share_cots.start()
    spread_gate.got_z()
    mix(1)
    shares[1].start()
    shares[0].forward()
    spread_out.arrive()
    share_out = [
        Share(w, lambda zl, k: m.out_all.at[:, k, 0, zl]),
        Share(w, lambda zl, k: m.out_all.at[:, k, 1, 1 - zl]),
    ]
    for share in share_out:
        share.start()
    spread_up.got_z()
    mix(2)
    shares[2].start()
    shares[1].forward()
    spread_down.got_z()
    for share in share_out:
        share.forward()
    share_cots.forward()
    mix(3)
    shares[3].start()
    shares[2].forward()
    spread_gate.got_last()
    for share in share_out:
        share.arrive()

    for b in range(4):
        span = slice(256 * b, 256 * b + 256)
        if b == 2:
            shares[3].forward()
        if b == 1:
            spread_up.got_last()
        if b == 3:
            spread_down.got_last()
        shares[b].arrive()
        middle = m.rows_all[b // 2, b % 2].reshape(256, 1024).astype(F32)
        whole = m.out_all[...].reshape(1024, 1024)
        middle = middle + dots(m.mixed_all[b // 2, b % 2], whole, NN)
        m.normed_two[span, :] = (middle * inverse_size(middle) * m.gain_rows[1]).astype(BF16)

        @pl.when(k == b % 2)
        def _():
            m.middle_keep[b // 2] = middle

    for spread in (spread_gate, spread_up, spread_down):
        spread.arrive()
    share_cots.arrive()
    for share in shares:
        share.drain()
    total_out = Total(w, m.mixed_all, m.core_out, m.across_out)
    total_norm = Total(w, m.part_norm, m.core_norm, m.across_norm)

    def feed(i, part):
        span = pl.ds(pl.multiple_of(256 * (2 * i + part), 256), 256)
        upstream = m.cots_all[i, part].reshape(256, 1024)
        normed_two = m.normed_two[span, :]
        for n in range(4):
            columns = slice(256 * n, 256 * n + 256)
            gate_tile = m.gate_all[..., columns].reshape(1024, 256)
            up_tile = m.up_all[..., columns].reshape(1024, 256)
            down_tile = m.down_all[n // 2, n % 2].reshape(256, 1024)
            gate = dots(normed_two, gate_tile, NN)
            upward = dots(normed_two, up_tile, NN)
            grad_hidden = dots(upstream, down_tile, NT)
            sigma = 1.0 / (1.0 + jnp.exp(-gate))
            silu = gate * sigma
            m.hidden[span, columns] = (silu * upward).astype(BF16)
            m.grad_up[span, columns] = (grad_hidden * silu).astype(BF16)
            m.grad_gate[span, columns] = (
                grad_hidden * upward * (sigma + silu * (1.0 - sigma))
            ).astype(BF16)
        norm_part = dots(m.grad_gate[span, :], m.gate_all[...].reshape(1024, 1024), NT)
        norm_part = norm_part + dots(m.grad_up[span, :], m.up_all[...].reshape(1024, 1024), NT)
        return span, norm_part

    def out_of(span):
        return dots(m.hidden[span, :], m.down_all[...].reshape(1024, 1024), NN)

    def give(i, _):
        span, norm_part = feed(i, 1 - k)
        total_norm.give(i, norm_part)
        total_out.give(i, out_of(span))
        return 0

    def keep(i, _):
        span, norm_part = feed(i, k)
        total_norm.keep(i, norm_part)
        total_out.keep(i, out_of(span))
        return 0

    lax.fori_loop(0, 2, give, 0)
    lax.fori_loop(0, 2, keep, 0)
    for spread in (spread_gate, spread_up, spread_down):
        spread.drain()

    def lanes(plane, half):
        return pl.ds(pl.multiple_of(512 * plane + 256 * half, 256), 256)

    def down_part(plane):
        def one(half, _):
            made = dots(m.hidden[:, lanes(plane, half)], m.cots_all[...].reshape(1024, 1024), TN)
            m.down_all[plane, half] = made.astype(BF16).reshape(2, 128, 1024)
            return 0

        lax.fori_loop(0, 2, one, 0)

    def wide_part(whole, right, plane):
        def one(half, _):
            made = dots(m.normed_two[:, lanes(plane, half)], right[...], TN).astype(BF16)
            whole[plane, half] = made.reshape(2, 2, 2, 32, 1024)
            return 0

        lax.fori_loop(0, 2, one, 0)

    def fold_plane(whole, got_b, got_a, got_z):
        return Fold(
            w, "xy", lambda y: whole.at[y], lambda x, y, zh: whole.at[y, :, zh, :, x],
            got_b, lambda x, zh: got_b.at[:, zh, :, x], got_a, got_z,
        )

    def fold_side(whole, got_b, got_a, got_z):
        return Fold(
            w, "yx", lambda x: whole.at[:, :, :, :, x], lambda x, y, zh: whole.at[y, :, zh, :, x],
            got_b, lambda y, zh: got_b.at[y, :, zh], got_a, got_z,
        )

    def fold_block(whole, got_b, got_a, got_z):
        return Fold(
            w, "xy", lambda y: whole.at[y], lambda x, y, zh: whole.at[y, zh, x],
            got_b, lambda x, zh: got_b.at[zh, x], got_a, got_z,
        )

    fold_down = fold_block(m.down_all, m.down_b, m.down_a, m.down_z)
    fold_gate = fold_plane(m.gate_all, m.gate_b, m.gate_a, m.gate_z)
    fold_up = fold_side(m.up_all, m.up_b, m.up_a, m.up_z)
    fold_heads = fold_side(m.heads_part, m.heads_b, m.heads_a, m.heads_z)
    fold_gains = fold_block(m.gains_part, m.gains_b, m.gains_a, m.gains_z)
    down_part(1 - y)
    fold_down.start()
    wide_part(m.up_all, m.grad_up, 0)
    wide_part(m.up_all, m.grad_up, 1)
    fold_up.start()
    wide_part(m.gate_all, m.grad_gate, 1 - y)
    fold_gate.start()

    share_branch = Share(w, lambda zl, k: m.branch.at[:, k, zl])
    own_half = total_norm.rows(zl)
    gain_sum = jnp.zeros((1, 1024), F32)
    for i in range(2):
        grad, term = norm_back(
            m.middle_keep[i, own_half], m.gain_rows[1], total_norm.take(i)
        )
        gain_sum = gain_sum + term
        m.done_out[i] = (m.middle_keep[i, own_half] + total_out.take(i)).astype(BF16)
        grad = grad + m.cots_all[i, k, zl].astype(F32)
        m.middle_keep[i, own_half] = grad
        m.branch[i, k, zl] = grad.astype(BF16)
    share_branch.start()
    return_out = Return(w, lambda i: m.done_out.at[i], output, spare())
    return_out.start()

    def gain_rows_part(row, total):
        for plane in range(2):
            for place in range(4):
                for half in range(2):
                    at = 512 * plane + 256 * half + 128 * (place // 2)
                    row_at = slice(2 * row + half, 2 * row + half + 1)
                    m.gains_part[plane, place // 2, place % 2, row_at, :] = total[:, at : at + 128]

    m.gains_part[...] = jnp.zeros_like(m.gains_part)
    gain_rows_part(1, gain_sum)
    down_part(y)
    share_branch.forward()
    wide_part(m.gate_all, m.grad_gate, y)
    share_branch.arrive()

    grad_mixed, grad_mixed_turned = m.grad_up.at[:, :256], m.hidden.at[:256]
    grad_heads = m.grad_gate.at[:, :768]
    out_own = m.out_all[zl, k].reshape(256, 1024)
    for b in range(4):
        span = slice(256 * b, 256 * b + 256)
        made = dots(m.branch[b // 2, b % 2].reshape(256, 1024), out_own, NT).astype(BF16)
        grad_mixed[span, :] = made
        grad_mixed_turned[:, span] = made.T
    m.out_part[...] = (
        dots(m.mixed_turned[...], m.branch[...].reshape(1024, 1024), NN)
        .astype(BF16)
        .reshape(2, 2, 2, 32, 1024)
    )
    base = w.slots(6)
    owner = y == zl
    out_across = w.copy(m.out_part, m.out_b, w.at(y=1 - y), base)
    pl.when(jnp.logical_not(owner))(lambda: out_across.start())
    m.grad_keys[...] = jnp.zeros_like(m.grad_keys)
    m.grad_values[...] = jnp.zeros_like(m.grad_values)

    def unmix(b):
        span, count = slice(256 * b, 256 * b + 256), 256 * b + 256
        bias = bias_of(b)

        def one(h, _):
            query, upstream = only_head(m.query[span, :], h), only_head(grad_mixed[span, :], h)
            scores = dots(m.keys[:count, :], query, NT)
            scores = scores * (HEAD**-0.5 * LOG2E) + bias
            probs = jnp.exp2(scores - m.logsum[h, :, span])
            grad_probs = dots(m.values[:count, :], upstream, NT)
            centre = jnp.sum(
                grad_mixed_turned[head_rows(h), span].astype(F32)
                * m.mixed_turned[head_rows(h), span].astype(F32),
                axis=0,
                keepdims=True,
            )
            grad_scores = (probs * (grad_probs - centre)).astype(BF16)
            turned = dots(m.keys_turned[head_rows(h), :count], grad_scores, NN)
            grad_mixed_turned[head_rows(h), span] = (turned * HEAD**-0.5).astype(BF16)
            m.grad_keys[:count, :] += dots(grad_scores, query, NN)
            m.grad_values[:count, :] += dots(probs.astype(BF16), upstream, NN)
            return 0

        lax.fori_loop(0, 4, one, 0)
        grad_heads[span, :256] = grad_mixed_turned[:, span].T

    unmix(0)
    unmix(1)
    fold_up.second()
    unmix(2)
    fold_down.second()
    unmix(3)
    grad_heads[:, 256:512] = (m.grad_keys[...] * HEAD**-0.5).astype(BF16)
    grad_heads[:, 512:] = m.grad_values[...].astype(BF16)

    for plane in range(2):
        for half in range(2):
            made = dots(m.normed[:, lanes(plane, half)], grad_heads[...], TN)
            m.heads_part[plane, half] = made.astype(BF16).reshape(2, 2, 2, 32, 768)
    fold_heads.start()
    total_norm.drain()
    total_first = Total(w, m.part_norm, m.core_norm, m.across_norm)

    def first_part(i, part):
        span = pl.ds(pl.multiple_of(256 * (2 * i + part), 256), 256)
        return dots(grad_heads[span, :], m.heads_all[...].reshape(1024, 768), NT)

    for i in range(2):
        total_first.give(i, first_part(i, 1 - k))
    for i in range(2):
        total_first.keep(i, first_part(i, k))
    fold_up.third()
    fold_down.third()
    gain_sum = jnp.zeros((1, 1024), F32)

    def done_in(i):
        return m.normed_two.at[pl.ds(128 * i, 128)]

    for i in range(2):
        grad, term = norm_back(
            m.rows_all[i, k, zl].astype(F32), m.gain_rows[0], total_first.take(i)
        )
        gain_sum = gain_sum + term
        done_in(i)[...] = (m.middle_keep[i, own_half] + grad).astype(BF16)
    return_in = Return(w, done_in, m.input_home, spare())
    return_in.start()
    gain_rows_part(0, gain_sum)
    fold_gains.start()

    fold_gate.second()

    def out_side(z):
        side = 1 - zh if z else zh
        return w.copy(
            m.out_part.at[side, :, 1 - x], m.out_a.at[side], w.at(x=1 - x), base + 1 + z
        )

    def out_side_landed(z):
        ref = m.out_a.at[1 - zh if z else zh]
        return w.copy(ref, ref, w.at(x=1 - x), base + 1 + z)

    def out_two(side, x):
        return m.out_part[side, :, x].astype(F32) + m.out_b[side, :, x].astype(F32)

    out_half = w.copy(m.out_part.at[1 - zh, :, x], m.out_z, w.at(zh=1 - zh), base + 3)
    out_last = w.copy(m.out_deal, m.out_home, w.across(), base + 4)

    @pl.when(owner)
    def _():
        out_across.wait_recv()
        for side in (1, 0):
            at = 1 - zh if side else zh
            m.out_part[at, :, 1 - x] = out_two(at, 1 - x).astype(BF16)
            out_side(side).start()

    fold_heads.second()
    fold_gains.second()
    fold_gate.third()

    @pl.when(owner)
    def _():
        out_side_landed(1).wait_recv()
        m.out_part[1 - zh, :, x] = (
            out_two(1 - zh, x) + m.out_a[1 - zh].astype(F32)
        ).astype(BF16)
        out_half.start()

    d_out[...] = fold_down.finish()

    def deal_grads(packed, dealt):
        return Deal(
            w, lambda zl, k: packed.at[2 * k + (zl + zh) % 2], lambda zl, k: dealt.at[2 * zl + k]
        )

    deal_up.drain()
    deal_gate.drain()
    deal_heads.drain()
    m.up_pack[...] = fold_up.finish().astype(BF16).reshape(4, 32, 1024)
    deal_up_grad = deal_grads(m.up_pack, m.up_dealt)
    deal_up_grad.start()
    fold_heads.third()
    fold_gains.third()
    m.gate_pack[...] = fold_gate.finish().astype(BF16).reshape(4, 32, 1024)
    deal_gate_grad = deal_grads(m.gate_pack, m.gate_dealt)
    deal_gate_grad.start()

    @pl.when(owner)
    def _():
        out_side_landed(0).wait_recv()
        out_half.wait_recv()
        out_total = out_two(zh, x) + m.out_a[zh].astype(F32) + m.out_z[...].astype(F32)
        first, second = out_total[0], out_total[1]
        m.out_deal[...] = jnp.where(zb == 0, second, first).astype(BF16)
        out_last.start()
        o_out[...] = jnp.where(zb == 0, first, second)

    return_in.arrive()
    input_grad[...] = m.input_home[...].astype(F32)
    m.gains_deal[...] = fold_gains.finish()
    m.gains_dealt[rank] = m.gains_deal[...]
    deal_gains = Deal(w, lambda zl, k: m.gains_deal, lambda zl, k: m.gains_dealt.at[2 * zl + k])
    deal_gains.start()
    m.heads_pack[...] = fold_heads.finish().astype(BF16).reshape(4, 32, 768)
    deal_heads_grad = deal_grads(m.heads_pack, m.heads_dealt)
    deal_heads_grad.start()
    m.up_dealt[rank] = m.up_pack[2 * k + zb]
    m.gate_dealt[rank] = m.gate_pack[2 * k + zb]
    m.heads_dealt[rank] = m.heads_pack[2 * k + zb]
    for deal, dealt, target in (
        (deal_up_grad, m.up_dealt, u_out),
        (deal_gate_grad, m.gate_dealt, g_out),
    ):
        deal.arrive()
        for r in range(4):
            for j, (start, width) in enumerate(hidden_columns(r)):
                target[:, start : start + width] = dealt[
                    r, :, 128 * j : 128 * j + width
                ].astype(F32)
    deal_gains.arrive()
    gain_out[...] = m.gains_dealt[0] + m.gains_dealt[1] + m.gains_dealt[2] + m.gains_dealt[3]
    deal_heads_grad.arrive()
    for r in range(4):
        for j, target in enumerate((q_out, k_out, v_out)):
            at = 256 * j
            target[:, 256 * r : 256 * r + 256] = m.heads_dealt[r, :, at : at + 256].astype(F32)

    @pl.when(jnp.logical_not(owner))
    def _():
        out_last.wait_recv()
        o_out[...] = m.out_home[...].astype(F32)

    return_out.arrive()
    for part in [
        visit_rows, visit_cots, spread_gains, spread_heads, spread_out, share_rows, share_cots,
        share_branch, total_out, total_first, fold_down, fold_gate, fold_up, fold_heads,
        fold_gains, return_out, return_in, deal_up_grad, deal_gate_grad, deal_heads_grad,
        deal_gains,
    ] + share_gains + share_out:
        part.drain()

    @pl.when(owner)
    def _():
        for side in range(2):
            out_side(side).wait_send()
        out_half.wait_send()
        out_last.wait_send()

    pl.when(jnp.logical_not(owner))(lambda: out_across.wait_send())


def grouped(
    layer_input, doc_ids, attn_gain, query_weight, key_weight, value_weight, out_weight,
    mlp_gain, gate_weight, up_weight, down_weight, out_grad,
):
    dp, ctx = lax.axis_index("dp"), lax.axis_index("ctx")
    k = dp % 2
    piece = attn_gain.shape[0]
    lane = piece * (ctx % 4)
    gains = jnp.zeros((16, 128), BF16)
    gains = lax.dynamic_update_slice(gains, jnp.stack([attn_gain, mlp_gain]), (0, lane))
    d, f = layer_input.shape[2], gate_weight.shape[1]
    outs = (
        shaped(*layer_input.shape),
        shaped(*layer_input.shape, dtype=F32),
        shaped(piece, d, dtype=F32),
        shaped(piece, d, dtype=F32),
        shaped(piece, d, dtype=F32),
        shaped(piece, d, dtype=F32),
        shaped(piece, f, dtype=F32),
        shaped(piece, f, dtype=F32),
        shaped(*down_weight.shape, dtype=F32),
        shaped(8, 128, dtype=F32),
    )
    rooms = [pltpu.VMEM(shape, dtype) for _, shape, dtype in SCRATCH]
    made = pl.pallas_call(
        layer_body,
        name="layer",
        out_shape=outs,
        in_specs=[ANY, ANY, ANY, VMEM, VMEM, VMEM, ANY, VMEM, VMEM, ANY, ANY],
        out_specs=(ANY,) + (VMEM,) * 9,
        scratch_shapes=rooms
        + [
            pltpu.SemaphoreType.DMA((192,)),
            pltpu.SemaphoreType.DMA((192,)),
            pltpu.SemaphoreType.DMA((16,)),
        ],
        compiler_params=pltpu.CompilerParams(
            collective_id=0, has_side_effects=True, vmem_limit_bytes=61 << 20
        ),
    )(
        layer_input, out_grad, doc_ids.reshape(2, 1, -1), query_weight, key_weight, value_weight,
        out_weight, gate_weight, up_weight, down_weight, gains,
    )
    output, input_grad, q, k_, v, o, g, u, down, gain = made

    def gain_of(row):
        return lax.dynamic_slice(gain, (row + k, lane), (1, piece)).reshape(piece)

    return (output, input_grad, gain_of(0), q, k_, v, o, gain_of(2), g, u, down)


def plain_product(left, right):
    return jnp.dot(left, right, preferred_element_type=jnp.float32)


def plain_product_left(left, right):
    return lax.dot_general(
        left, right, (((0,), (0,)), ((), ())), preferred_element_type=jnp.float32
    )


def plain_product_right(left, right):
    return lax.dot_general(
        left, right, (((1,), (1,)), ((), ())), preferred_element_type=jnp.float32
    )


def normalize(rows, gain):
    inverse = lax.rsqrt(jnp.mean(rows * rows, axis=-1, keepdims=True) + EPS)
    return (rows * inverse * gain, inverse)


def plain_norm_back(rows, inverse, gain, upstream):
    normed = rows * inverse
    scaled = upstream * gain
    grad_rows = inverse * (scaled - normed * jnp.mean(scaled * normed, axis=-1, keepdims=True))
    return (grad_rows, jnp.sum(upstream * normed, axis=0))


def head_pair(array, start):
    piece = lax.dynamic_slice_in_dim(array, start, 2 * HEAD, 2)
    return piece.reshape(array.shape[0], array.shape[1], 2, HEAD)


def pair_scores(query, keys, allowed, start):
    scores = jnp.einsum(
        "sqhd,skhd->shqk",
        head_pair(query, start),
        head_pair(keys, start),
        preferred_element_type=jnp.float32,
    ) * HEAD ** (-0.5)
    return jnp.where(allowed[:, None], scores, -1e30)


def plain_attend(query, keys, values, allowed):
    groups, rows, width = query.shape

    def step(index, carry):
        mixed_all, logsum = carry
        start = index * 2 * HEAD
        scores = pair_scores(query, keys, allowed, start)
        top = jnp.max(scores, axis=-1, keepdims=True)
        lifted = jnp.exp(scores - top)
        total = jnp.sum(lifted, axis=-1, keepdims=True)
        probs = (lifted / total).astype(jnp.bfloat16)
        mixed = jnp.einsum(
            "shqk,skhd->sqhd", probs, head_pair(values, start), preferred_element_type=jnp.float32
        )
        mixed_all = lax.dynamic_update_slice_in_dim(
            mixed_all, mixed.reshape(groups, rows, 2 * HEAD).astype(jnp.bfloat16), start, 2
        )
        logsum = lax.dynamic_update_slice_in_dim(
            logsum, (top + jnp.log(total))[..., 0], index * 2, 1
        )
        return (mixed_all, logsum)

    start_state = (
        jnp.zeros((groups, rows, width), jnp.bfloat16),
        jnp.zeros((groups, width // HEAD, rows), jnp.float32),
    )
    return lax.fori_loop(0, width // (2 * HEAD), step, start_state)


def plain_attend_back(query, keys, values, allowed, logsum, grad_mixed):
    groups, rows, width = query.shape
    length = keys.shape[1]
    scale = HEAD ** (-0.5)

    def step(index, carry):
        grad_query, grad_keys, grad_values = carry
        start = index * 2 * HEAD
        scores = pair_scores(query, keys, allowed, start)
        kept = lax.dynamic_slice_in_dim(logsum, index * 2, 2, 1)
        probs = jnp.exp(scores - kept[..., None])
        upstream = head_pair(grad_mixed, start)
        grad_probs = jnp.einsum(
            "sqhd,skhd->shqk",
            upstream,
            head_pair(values, start),
            preferred_element_type=jnp.float32,
        )
        grad_scores = (
            probs * (grad_probs - jnp.sum(probs * grad_probs, axis=-1, keepdims=True))
        ).astype(jnp.bfloat16)
        part_query = (
            jnp.einsum(
                "shqk,skhd->sqhd",
                grad_scores,
                head_pair(keys, start),
                preferred_element_type=jnp.float32,
            )
            * scale
        )
        part_keys = (
            jnp.einsum(
                "shqk,sqhd->skhd",
                grad_scores,
                head_pair(query, start),
                preferred_element_type=jnp.float32,
            )
            * scale
        )
        part_values = jnp.einsum(
            "shqk,sqhd->skhd",
            probs.astype(jnp.bfloat16),
            upstream,
            preferred_element_type=jnp.float32,
        )
        grad_query = lax.dynamic_update_slice_in_dim(
            grad_query, part_query.reshape(groups, rows, 2 * HEAD), start, 2
        )
        grad_keys = lax.dynamic_update_slice_in_dim(
            grad_keys, part_keys.reshape(groups, length, 2 * HEAD), start, 2
        )
        grad_values = lax.dynamic_update_slice_in_dim(
            grad_values, part_values.reshape(groups, length, 2 * HEAD), start, 2
        )
        return (grad_query, grad_keys, grad_values)

    start_state = (
        jnp.zeros((groups, rows, width), jnp.float32),
        jnp.zeros((groups, length, width), jnp.float32),
        jnp.zeros((groups, length, width), jnp.float32),
    )
    return lax.fori_loop(0, width // (2 * HEAD), step, start_state)


def on_device(
    layer_input,
    doc_ids,
    attn_gain,
    query_weight,
    key_weight,
    value_weight,
    out_weight,
    mlp_gain,
    gate_weight,
    up_weight,
    down_weight,
    out_grad,
):
    groups, rows, width = layer_input.shape
    length = doc_ids.shape[1]
    gathered = (
        lax.all_gather(attn_gain, ("dp", "ctx"), axis=0, tiled=True),
        lax.all_gather(query_weight, ("dp", "ctx"), axis=0, tiled=True),
        lax.all_gather(key_weight, ("dp", "ctx"), axis=0, tiled=True),
        lax.all_gather(value_weight, ("dp", "ctx"), axis=0, tiled=True),
        lax.all_gather(out_weight, ("dp", "ctx"), axis=0, tiled=True),
        lax.all_gather(mlp_gain, ("dp", "ctx"), axis=0, tiled=True),
        lax.all_gather(gate_weight, ("dp", "ctx"), axis=0, tiled=True),
        lax.all_gather(up_weight, ("dp", "ctx"), axis=0, tiled=True),
        lax.all_gather(down_weight, ("dp", "ctx"), axis=0, tiled=True),
    )
    gain_one, w_query, w_key, w_value, w_out, gain_two, w_gate, w_up, w_down = gathered
    first = lax.axis_index("ctx") * rows
    places = jnp.arange(length)
    own_ids = lax.dynamic_slice_in_dim(doc_ids, first, rows, 1)
    own_places = first + jnp.arange(rows)
    allowed = (own_ids[:, :, None] == doc_ids[:, None, :]) & (
        places[None, None, :] <= own_places[None, :, None]
    )
    inputs = layer_input.reshape(groups * rows, width).astype(jnp.float32)
    gain_attn = gain_one.astype(jnp.float32)
    normed_full, inverse_one = normalize(inputs, gain_attn)
    normed = normed_full.astype(jnp.bfloat16)
    query = plain_product(normed, w_query).astype(jnp.bfloat16).reshape(groups, rows, width)
    keys_own = plain_product(normed, w_key).astype(jnp.bfloat16).reshape(groups, rows, width)
    values_own = plain_product(normed, w_value).astype(jnp.bfloat16).reshape(groups, rows, width)
    keys, values = (
        lax.all_gather(keys_own, "ctx", axis=1, tiled=True),
        lax.all_gather(values_own, "ctx", axis=1, tiled=True),
    )
    attended, logsum = plain_attend(query, keys, values, allowed)
    attended_rows = attended.reshape(groups * rows, width)
    middle = inputs + plain_product(attended_rows, w_out)
    gain_mlp = gain_two.astype(jnp.float32)
    normed_two_full, inverse_two = normalize(middle, gain_mlp)
    normed_two = normed_two_full.astype(jnp.bfloat16)
    gate = plain_product(normed_two, w_gate)
    upward = plain_product(normed_two, w_up)
    sigma = jax.nn.sigmoid(gate)
    hidden = (gate * sigma * upward).astype(jnp.bfloat16)
    layer_output = (middle + plain_product(hidden, w_down)).astype(jnp.bfloat16)
    gathered_back = (
        lax.all_gather(attn_gain, ("dp", "ctx"), axis=0, tiled=True),
        lax.all_gather(query_weight, ("dp", "ctx"), axis=0, tiled=True),
        lax.all_gather(key_weight, ("dp", "ctx"), axis=0, tiled=True),
        lax.all_gather(value_weight, ("dp", "ctx"), axis=0, tiled=True),
        lax.all_gather(out_weight, ("dp", "ctx"), axis=0, tiled=True),
        lax.all_gather(mlp_gain, ("dp", "ctx"), axis=0, tiled=True),
        lax.all_gather(gate_weight, ("dp", "ctx"), axis=0, tiled=True),
        lax.all_gather(up_weight, ("dp", "ctx"), axis=0, tiled=True),
        lax.all_gather(down_weight, ("dp", "ctx"), axis=0, tiled=True),
    )
    gain_one, w_query, w_key, w_value, w_out, gain_two, w_gate, w_up, w_down = gathered_back
    upstream = out_grad.reshape(groups * rows, width)
    down_grad = plain_product_left(hidden, upstream)
    grad_hidden = plain_product_right(upstream, w_down)
    grad_gate = (grad_hidden * upward * sigma * (1.0 + gate * (1.0 - sigma))).astype(jnp.bfloat16)
    grad_up = (grad_hidden * gate * sigma).astype(jnp.bfloat16)
    gate_grad = plain_product_left(normed_two, grad_gate)
    up_grad = plain_product_left(normed_two, grad_up)
    grad_normed_two = plain_product_right(grad_gate, w_gate) + plain_product_right(grad_up, w_up)
    grad_middle, mlp_gain_grad = plain_norm_back(
        middle, inverse_two, gain_two.astype(jnp.float32), grad_normed_two
    )
    grad_middle = grad_middle + upstream.astype(jnp.float32)
    grad_branch = grad_middle.astype(jnp.bfloat16)
    out_proj_grad = plain_product_left(attended_rows, grad_branch)
    grad_attended = (
        plain_product_right(grad_branch, w_out).astype(jnp.bfloat16).reshape(groups, rows, width)
    )
    grad_query, grad_keys_all, grad_values_all = plain_attend_back(
        query, keys, values, allowed, logsum, grad_attended
    )
    grad_keys, grad_values = (
        lax.psum_scatter(
            grad_keys_all.astype(jnp.bfloat16), "ctx", scatter_dimension=1, tiled=True
        ).astype(jnp.float32),
        lax.psum_scatter(
            grad_values_all.astype(jnp.bfloat16), "ctx", scatter_dimension=1, tiled=True
        ).astype(jnp.float32),
    )
    grad_query = grad_query.astype(jnp.bfloat16).reshape(groups * rows, width)
    grad_keys = grad_keys.astype(jnp.bfloat16).reshape(groups * rows, width)
    grad_values = grad_values.astype(jnp.bfloat16).reshape(groups * rows, width)
    query_grad = plain_product_left(normed, grad_query)
    key_grad = plain_product_left(normed, grad_keys)
    value_grad = plain_product_left(normed, grad_values)
    grad_normed = (
        plain_product_right(grad_query, w_query)
        + plain_product_right(grad_keys, w_key)
        + plain_product_right(grad_values, w_value)
    )
    grad_inputs, attn_gain_grad = plain_norm_back(
        inputs, inverse_one, gain_one.astype(jnp.float32), grad_normed
    )
    input_grad = (grad_middle + grad_inputs).reshape(groups, rows, width)
    shares = (
        lax.psum_scatter(attn_gain_grad, ("dp", "ctx"), scatter_dimension=0, tiled=True),
        lax.psum_scatter(query_grad, ("dp", "ctx"), scatter_dimension=0, tiled=True),
        lax.psum_scatter(key_grad, ("dp", "ctx"), scatter_dimension=0, tiled=True),
        lax.psum_scatter(value_grad, ("dp", "ctx"), scatter_dimension=0, tiled=True),
        lax.psum_scatter(out_proj_grad, ("dp", "ctx"), scatter_dimension=0, tiled=True),
        lax.psum_scatter(mlp_gain_grad, ("dp", "ctx"), scatter_dimension=0, tiled=True),
        lax.psum_scatter(gate_grad, ("dp", "ctx"), scatter_dimension=0, tiled=True),
        lax.psum_scatter(up_grad, ("dp", "ctx"), scatter_dimension=0, tiled=True),
        lax.psum_scatter(down_grad, ("dp", "ctx"), scatter_dimension=0, tiled=True),
    )
    return (
        layer_output.reshape(groups, rows, width),
        input_grad,
        shares[0],
        shares[1],
        shares[2],
        shares[3],
        shares[4],
        shares[5],
        shares[6],
        shares[7],
        shares[8],
    )


def solution(mesh):
    placed = (
        P("dp", "ctx", None),
        P("dp", None),
        P(("dp", "ctx")),
        P(("dp", "ctx"), None),
        P(("dp", "ctx"), None),
        P(("dp", "ctx"), None),
        P(("dp", "ctx"), None),
        P(("dp", "ctx")),
        P(("dp", "ctx"), None),
        P(("dp", "ctx"), None),
        P(("dp", "ctx"), None),
        P("dp", "ctx", None),
    )
    fits = mesh.shape["dp"] == 4 and mesh.shape["ctx"] == 8
    body = grouped if fits else on_device
    return jax.shard_map(
        body,
        mesh=mesh,
        in_specs=placed,
        out_specs=(
            P("dp", "ctx", None),
            P("dp", "ctx", None),
            P(("dp", "ctx")),
            P(("dp", "ctx"), None),
            P(("dp", "ctx"), None),
            P(("dp", "ctx"), None),
            P(("dp", "ctx"), None),
            P(("dp", "ctx")),
            P(("dp", "ctx"), None),
            P(("dp", "ctx"), None),
            P(("dp", "ctx"), None),
        ),
        check_vma=False,
    )
```

```python
import functools

import jax
import jax.numpy as jnp
from jax import lax
from jax.experimental import pallas as pl
from jax.experimental.pallas import tpu as pltpu
from jax.sharding import PartitionSpec as P

HEAD = 64


EPS = 1e-05
MESH = pl.DeviceIdType.MESH
F32 = jnp.float32
BF16 = jnp.bfloat16
LOG2E = 1.4426950408889634
ANY = pl.BlockSpec(memory_space=pl.ANY)
VMEM = pl.BlockSpec(memory_space=pltpu.VMEM)


class Wires:
    def __init__(self, send, recv):
        dp, ctx = lax.axis_index("dp"), lax.axis_index("ctx")
        self.x, self.y = ctx % 2, dp // 2
        self.zh, self.zb = ctx // 4, (ctx // 2) % 2
        self.v, self.k = (self.zb + self.zh) % 2, dp % 2
        self.send, self.recv = send, recv
        self.used = 0

    def slots(self, count):
        first = self.used
        self.used += count
        return first

    def at(self, v=None, y=None, zh=None, x=None, k=None):
        v = self.v if v is None else v
        y = self.y if y is None else y
        zh = self.zh if zh is None else zh
        x = self.x if x is None else x
        k = self.k if k is None else k
        return (2 * y + k, 4 * zh + 2 * ((v + zh) % 2) + x)

    def across(self):
        return self.at(x=1 - self.x)

    def core(self):
        return self.at(k=1 - self.k)

    def copy(self, source, target, device, slot, recv_slot=None):
        return pltpu.make_async_remote_copy(
            src_ref=source,
            dst_ref=target,
            send_sem=self.send.at[slot],
            recv_sem=self.recv.at[slot if recv_slot is None else recv_slot],
            device_id=device,
            device_id_type=MESH,
        )

    def greet(self):
        v, zh, zb, k = self.v, self.zh, self.zb, self.k
        barrier = pltpu.get_barrier_semaphore()

        def call(peer):
            pl.semaphore_signal(barrier, inc=1, device_id=peer, device_id_type=MESH)

        for peer in (
            self.across(), self.core(), self.at(x=1 - self.x, k=1 - k),
            self.at(v=1 - v), self.at(y=1 - self.y), self.at(zh=1 - zh),
        ):
            call(peer)
        count = 6
        for n in range(2):
            away = jnp.logical_not(every(v == n, zh == k, zb == k))
            pl.when(away)(lambda: call(self.at(v=n, zh=k, k=zb)))
            count = count + jnp.where(away, 1, 0)
            away = jnp.logical_not(every(zh == n, zb == k, zh == k))
            pl.when(away)(lambda: call(self.at(zh=n, v=(k + n) % 2, k=zh)))
            count = count + jnp.where(away, 1, 0)
        pl.semaphore_wait(barrier, count)


def every(*tests):
    all_of = tests[0]
    for test in tests[1:]:
        all_of = jnp.logical_and(all_of, test)
    return all_of


class Pairs:
    def __init__(self, wires, order):
        self.w, self.order = wires, order

    def place(self, z, a, b):
        w = self.w
        v, y = (a, b) if self.order == "vy" else (b, a)
        flip = lambda own, turn: 1 - own if turn else own
        return flip(w.v, v), flip(w.y, y), flip(w.zh, z)

    def partner(self, z, a, b):
        v, y, zh = self.place(z, a, b)
        return self.w.at(v=v, y=y, zh=zh)


class Spread(Pairs):
    SENDS = ((0, 0, 0), (0, 0, 0), (1, 0, 0), (0, 0, 0), (1, 0, 0), (0, 1, 0), (1, 1, 0))
    STEPS = ((1, 0, 0), (0, 1, 0), (0, 1, 0), (0, 0, 1), (0, 0, 1), (0, 0, 1), (0, 0, 1))

    def __init__(self, wires, order, block, own=None):
        super().__init__(wires, order)
        self.block, self.own = block, own
        self.first = wires.slots(7)

    def piece(self, n):
        ref = self.block(*self.place(*self.SENDS[n]))
        source = self.own if self.own is not None and not any(self.SENDS[n]) else ref
        return self.w.copy(source, ref, self.partner(*self.STEPS[n]), self.first + n)

    def landed(self, n):
        came = [i ^ j for i, j in zip(self.SENDS[n], self.STEPS[n])]
        ref = self.block(*self.place(*came))
        return self.w.copy(ref, ref, self.partner(*self.STEPS[n]), self.first + n)

    def start(self):
        self.start_z()
        self.start_rest()

    def start_z(self):
        self.piece(0).start()

    def start_rest(self):
        self.piece(1).start()
        self.piece(3).start()

    def got_first(self):
        self.landed(1).wait_recv()
        self.piece(5).start()

    def got_z(self):
        self.landed(0).wait_recv()
        self.piece(2).start()
        self.piece(4).start()

    def got_last(self):
        self.landed(2).wait_recv()
        self.piece(6).start()

    def arrive(self):
        for n in (3, 4, 5, 6):
            self.landed(n).wait_recv()

    def drain(self):
        for n in range(7):
            self.piece(n).wait_send()


class Share:
    def __init__(self, wires, block):
        self.w, self.block = wires, block
        self.first = wires.slots(3)

    def piece(self, i):
        w = self.w
        ref = self.block(w.x if i < 2 else 1 - w.x, w.k)
        return w.copy(ref, ref, w.across() if i == 0 else w.core(), self.first + i)

    def landed(self, i):
        w = self.w
        ref = self.block(*[(1 - w.x, w.k), (w.x, 1 - w.k), (1 - w.x, 1 - w.k)][i])
        return w.copy(ref, ref, w.core(), self.first + i)

    def start(self):
        self.piece(0).start()
        self.piece(1).start()

    def forward(self):
        self.landed(0).wait_recv()
        self.piece(2).start()

    def arrive(self):
        self.landed(1).wait_recv()
        self.landed(2).wait_recv()

    def drain(self):
        for i in range(3):
            self.piece(i).wait_send()


class Deal:
    def __init__(self, wires, outgoing, incoming):
        self.w, self.outgoing, self.incoming = wires, outgoing, incoming
        self.first = wires.slots(3)

    def mate(self, i):
        w = self.w
        return [(1 - w.x, w.k), (w.x, 1 - w.k), (1 - w.x, 1 - w.k)][i]

    def piece(self, i):
        w = self.w
        x, k = self.mate(i)
        return w.copy(
            self.outgoing(x, k), self.incoming(w.x, w.k), w.at(x=x, k=k), self.first + i
        )

    def landed(self, i):
        x, k = self.mate(i)
        ref = self.incoming(x, k)
        return self.w.copy(ref, ref, self.w.at(x=x, k=k), self.first + i)

    def start(self):
        for i in range(3):
            self.piece(i).start()

    def arrive(self):
        for i in range(3):
            self.landed(i).wait_recv()

    def drain(self):
        for i in range(3):
            self.piece(i).wait_send()


class Visit:
    def __init__(self, wires, home, full, local):
        self.w, self.home, self.full, self.local = wires, home, full, local
        self.first = wires.slots(2)
        w = wires
        self.own = [every(w.v == j, w.zh == w.k, w.zb == w.k) for j in range(2)]
        self.here = [every(w.zh == i, w.zb == w.k, w.zh == w.k) for i in range(2)]

    def piece(self, j):
        w = self.w
        return w.copy(
            self.home.at[j],
            self.full(w.zh, w.zb, w.x),
            w.at(v=j, zh=w.k, k=w.zb),
            self.first + j,
            self.first + w.zh,
        )

    def stay(self, j):
        w = self.w
        return pltpu.make_async_copy(self.home.at[j], self.full(w.zh, w.zb, w.x), self.local)

    def landed(self, i):
        w = self.w
        ref = self.full(i, w.k, w.x)
        return w.copy(ref, ref, w.core(), self.first + i)

    def start(self):
        for j in range(2):
            pl.when(self.own[j])(lambda: self.stay(j).start())
            pl.when(jnp.logical_not(self.own[j]))(lambda: self.piece(j).start())

    def arrive(self):
        for j in range(2):
            pl.when(self.own[j])(lambda: self.stay(j).wait())
        for i in range(2):
            pl.when(jnp.logical_not(self.here[i]))(lambda: self.landed(i).wait_recv())

    def drain(self):
        for j in range(2):
            pl.when(jnp.logical_not(self.own[j]))(lambda: self.piece(j).wait_send())


class Return:
    def __init__(self, wires, done, home, local):
        self.w, self.done, self.home, self.local = wires, done, home, local
        self.first = wires.slots(2)
        w = wires
        self.own = [every(w.zh == i, w.zb == w.k, w.k == w.zh) for i in range(2)]
        self.here = [every(w.v == j, w.zh == w.k, w.zb == w.k) for j in range(2)]

    def piece(self, i):
        w = self.w
        return w.copy(
            self.done(i),
            self.home.at[w.v],
            w.at(zh=i, v=(w.k + i) % 2, k=w.zh),
            self.first + i,
            self.first + w.v,
        )

    def stay(self, i):
        return pltpu.make_async_copy(self.done(i), self.home.at[self.w.v], self.local)

    def landed(self, j):
        ref = self.home.at[j]
        return self.w.copy(ref, ref, self.w.core(), self.first + j)

    def start(self):
        for i in range(2):
            pl.when(self.own[i])(lambda: self.stay(i).start())
            pl.when(jnp.logical_not(self.own[i]))(lambda: self.piece(i).start())

    def arrive(self):
        for i in range(2):
            pl.when(self.own[i])(lambda: self.stay(i).wait())
        for j in range(2):
            pl.when(jnp.logical_not(self.here[j]))(lambda: self.landed(j).wait_recv())

    def drain(self):
        for i in range(2):
            pl.when(jnp.logical_not(self.own[i]))(lambda: self.piece(i).wait_send())


def shaped(*shape, dtype=BF16):
    return jax.ShapeDtypeStruct(shape, dtype)


def pack_rows(columns, shards, packed):
    for rank in range(4):
        at = 0
        for shard in shards:
            for start, width in columns(rank):
                packed[rank, :, at : at + width] = shard[:, start : start + width]
                at += width


def head_columns(rank):
    return [(256 * rank, 256)]


def hidden_columns(rank):
    x, k = rank // 2, rank % 2
    return [
        (128 * (16 * y + 8 * k + 4 * zh + 2 * (v ^ zh) + x), 128)
        for y in range(2)
        for zh in range(2)
        for v in range(2)
    ]


class Total:
    def __init__(self, wires, part, got_core, got_across):
        self.w, self.part, self.got_core, self.got_across = wires, part, got_core, got_across
        self.first = wires.slots(4)
        self.half = part.shape[2] // 2

    def core(self, i):
        w = self.w
        return w.copy(
            self.part.at[0, i], self.got_core.at[i], w.core(), self.first + i
        )

    def rows(self, v):
        return pl.ds(pl.multiple_of(self.half * v, self.half), self.half)

    def across(self, i):
        w = self.w
        return w.copy(
            self.part.at[1, i, self.rows(1 - w.x)],
            self.got_across.at[i],
            w.across(),
            self.first + 2 + i,
        )

    def give(self, i, value):
        self.part[0, i] = value.astype(BF16)
        self.core(i).start()

    def keep(self, i, value):
        self.core(i).wait_recv()
        self.part[1, i] = (value + self.got_core[i].astype(F32)).astype(BF16)
        self.across(i).start()

    def take(self, i):
        self.across(i).wait_recv()
        own = self.part[1, i, self.rows(self.w.x)]
        return own.astype(F32) + self.got_across[i].astype(F32)

    def drain(self):
        for i in range(2):
            self.core(i).wait_send()
            self.across(i).wait_send()


class Parts:
    def __init__(self, copies):
        self.copies = copies

    def start(self):
        for copy in self.copies:
            copy.start()

    def wait_send(self):
        for copy in self.copies:
            copy.wait_send()

    def wait_recv(self):
        for copy in self.copies:
            copy.wait_recv()


class Fold(Pairs):
    def __init__(self, wires, order, whole, block, got_b, got_b_block, got_a, got_z):
        super().__init__(wires, order)
        self.whole, self.block = whole, block
        self.got_b, self.got_b_block, self.got_a, self.got_z = got_b, got_b_block, got_a, got_z
        self.first = wires.slots(5)

    def stage_b(self):
        w = self.w
        b = w.y if self.order == "vy" else w.v
        return Parts(
            [
                w.copy(source, target, self.partner(0, 0, 1), self.first + 4 * i)
                for i, (source, target) in enumerate(zip(self.whole(1 - b), self.got_b))
            ]
        )

    def stage_a(self, z):
        v, y, zh = self.place(z, 1, 0)
        return self.w.copy(
            self.block(v, y, zh), self.got_a.at[zh], self.partner(0, 1, 0), self.first + 1 + z,
            self.first + 1 + z,
        )

    def landed_a(self, z):
        v, y, zh = self.place(z, 0, 0)
        ref = self.got_a.at[zh]
        return self.w.copy(ref, ref, self.partner(0, 1, 0), self.first + 1 + z)

    def stage_z(self):
        ref = self.block(*self.place(1, 0, 0))
        return self.w.copy(ref, self.got_z, self.partner(1, 0, 0), self.first + 3)

    def two(self, z, a):
        v, y, zh = self.place(z, a, 0)
        own = self.block(v, y, zh)[...].astype(F32)
        return own + self.got_b_block(v if self.order == "vy" else y, zh)[...].astype(F32)

    def three(self, z):
        return self.two(z, 0) + self.got_a[self.place(z, 0, 0)[2]].astype(F32)

    def start(self):
        self.stage_b().start()

    def second(self):
        self.stage_b().wait_recv()
        for z in (1, 0):
            ref = self.block(*self.place(z, 1, 0))
            ref[...] = self.two(z, 1).astype(self.got_z.dtype)
            self.stage_a(z).start()

    def third(self):
        self.landed_a(1).wait_recv()
        ref = self.block(*self.place(1, 0, 0))
        ref[...] = self.three(1).astype(self.got_z.dtype)
        self.stage_z().start()

    def finish(self):
        self.landed_a(0).wait_recv()
        total = self.three(0)
        self.stage_z().wait_recv()
        return total + self.got_z[...].astype(F32)

    def drain(self):
        self.stage_b().wait_send()
        for z in range(2):
            self.stage_a(z).wait_send()
        self.stage_z().wait_send()


def dots(left, right, dims):
    return lax.dot_general(left, right, (dims, ((), ())), preferred_element_type=F32)


NN, NT, TN = ((1,), (0,)), ((1,), (1,)), ((0,), (0,))


def only_head(array, head):
    lane = lax.broadcasted_iota(jnp.int32, array.shape, 1)
    return jnp.where(lane // HEAD == head, array, jnp.zeros_like(array))


def inverse_size(rows):
    return lax.rsqrt(jnp.mean(rows * rows, axis=-1, keepdims=True) + EPS)


def norm_back(rows, gain, upstream):
    inverse = inverse_size(rows)
    normed = rows * inverse
    scaled = upstream * gain
    grad_rows = inverse * (scaled - normed * jnp.mean(scaled * normed, axis=-1, keepdims=True))
    return grad_rows, jnp.sum(upstream * normed, axis=0, keepdims=True)


SCRATCH = [
    ("rows_all", (2, 2, 2, 128, 1024), BF16),
    ("cots_all", (2, 2, 2, 128, 1024), BF16),
    ("ids_all", (2, 2, 1, 1024), jnp.int32),
    ("heads_all", (2, 2, 2, 2, 2, 32, 768), BF16),
    ("out_all", (2, 2, 2, 2, 2, 32, 1024), BF16),
    ("gate_all", (2, 2, 2, 2, 2, 32, 1024), BF16),
    ("up_all", (2, 2, 2, 2, 2, 32, 1024), BF16),
    ("down_all", (2, 2, 2, 128, 1024), BF16),
    ("gains_all", (2, 2, 2, 2, 2, 16, 128), BF16),
    ("heads_pack", (4, 32, 768), BF16),
    ("gate_pack", (4, 32, 1024), BF16),
    ("up_pack", (4, 32, 1024), BF16),
    ("normed", (1024, 1024), BF16),
    ("query", (1024, 256), BF16),
    ("keys", (1024, 256), BF16),
    ("values", (1024, 256), BF16),
    ("keys_turned", (256, 1024), BF16),
    ("values_turned", (256, 1024), BF16),
    ("mixed_turned", (256, 1024), BF16),
    ("mixed_all", (2, 2, 256, 1024), BF16),
    ("logsum", (4, 1, 1024), F32),
    ("gain_rows", (2, 1, 1024), F32),
    ("ids_row", (1, 1024), F32),
    ("ids_col", (1024, 128), F32),
    ("middle_keep", (2, 256, 1024), F32),
    ("normed_two", (1024, 1024), BF16),
    ("hidden", (1024, 1024), BF16),
    ("grad_gate", (1024, 1024), BF16),
    ("grad_up", (1024, 1024), BF16),
    ("part_norm", (2, 2, 256, 1024), BF16),
    ("core_out", (2, 256, 1024), BF16),
    ("core_norm", (2, 256, 1024), BF16),
    ("across_out", (2, 128, 1024), BF16),
    ("across_norm", (2, 128, 1024), BF16),
    ("branch", (2, 2, 2, 128, 1024), BF16),
    ("grad_keys", (1024, 256), F32),
    ("grad_values", (1024, 256), F32),
    ("heads_part", (2, 2, 2, 2, 2, 32, 768), BF16),
    ("out_part", (2, 2, 2, 32, 1024), BF16),
    ("gains_part", (2, 2, 2, 8, 128), F32),
    ("heads_b", (2, 2, 2, 2, 32, 768), BF16),
    ("heads_a", (2, 2, 2, 32, 768), BF16),
    ("heads_z", (2, 2, 32, 768), BF16),
    ("gate_b", (2, 2, 2, 2, 32, 1024), BF16),
    ("gate_a", (2, 2, 2, 32, 1024), BF16),
    ("gate_z", (2, 2, 32, 1024), BF16),
    ("up_b", (2, 2, 2, 2, 32, 1024), BF16),
    ("up_a", (2, 2, 2, 32, 1024), BF16),
    ("up_z", (2, 2, 32, 1024), BF16),
    ("down_b", (2, 2, 128, 1024), BF16),
    ("down_a", (2, 128, 1024), BF16),
    ("down_z", (128, 1024), BF16),
    ("out_b", (2, 2, 2, 32, 1024), BF16),
    ("out_a", (2, 2, 32, 1024), BF16),
    ("out_z", (2, 32, 1024), BF16),
    ("gains_b", (2, 2, 8, 128), F32),
    ("gains_a", (2, 8, 128), F32),
    ("gains_z", (8, 128), F32),
    ("gains_deal", (8, 128), F32),
    ("gains_dealt", (4, 8, 128), F32),
    ("out_deal", (32, 1024), BF16),
    ("out_home", (32, 1024), BF16),
    ("done_out", (2, 128, 1024), BF16),
]


def layer_body(
    rows, cots, ids, wq, wk, wv, wo, wg, wu, wd, gains,
    output, input_home, heads_dealt, o_out, gate_dealt, up_dealt, d_out, gain_out,
    *scratch,
):
    send, recv, local = scratch[-3:]
    m = type("Memory", (), dict(zip([name for name, _, _ in SCRATCH], scratch)))
    w = Wires(send, recv)
    v, y, zh, zb, x, k = w.v, w.y, w.zh, w.zb, w.x, w.k
    rank = 2 * x + k
    w.greet()

    used = [0]

    def spare():
        used[0] += 1
        return local.at[used[0] - 1]

    def stay(source, target):
        copy = pltpu.make_async_copy(source, target, spare())
        copy.start()
        return copy

    def sequence_block(ref):
        return lambda zh, zb, x: ref.at[zh, zb, x]

    def deal_rows(packed, whole):
        return Deal(
            w,
            lambda x, k: packed.at[2 * x + k],
            lambda sx, sk: whole.at[y, sk, zh, zb, sx],
        )

    def group_rows(ref):
        return lambda v, y, zh: ref.at[y, :, zh, (v + zh) % 2]

    def own_rows(ref):
        return lambda v, y, zh: ref.at[y, k, zh, (v + zh) % 2, x]

    visit_rows = Visit(w, rows, sequence_block(m.rows_all), spare())
    visit_rows.start()
    pack_rows(head_columns, (wq, wk, wv), m.heads_pack)
    deal_heads = deal_rows(m.heads_pack, m.heads_all)
    deal_heads.start()
    spread_gains = Spread(w, "vy", own_rows(m.gains_all), gains)
    spread_gains.start()
    swap = w.copy(ids, m.ids_all.at[k], w.core(), w.slots(1))
    swap.start()
    spread_out = Spread(w, "vy", own_rows(m.out_all), wo)
    spread_out.start()
    pack_rows(hidden_columns, (wg,), m.gate_pack)
    pack_rows(hidden_columns, (wu,), m.up_pack)
    stays = [
        stay(m.heads_pack.at[rank], m.heads_all.at[y, k, zh, zb, x]),
        stay(m.gate_pack.at[rank], m.gate_all.at[y, k, zh, zb, x]),
        stay(m.up_pack.at[rank], m.up_all.at[y, k, zh, zb, x]),
        stay(wo, m.out_all.at[y, k, zh, zb, x]),
        stay(gains, m.gains_all.at[y, k, zh, zb, x]),
        stay(wd, m.down_all.at[y, zh, v]),
        stay(ids, m.ids_all.at[k]),
    ]
    deal_gate = deal_rows(m.gate_pack, m.gate_all)
    deal_up = deal_rows(m.up_pack, m.up_all)
    for copy in stays:
        copy.wait()
    deal_heads.arrive()
    spread_heads = Spread(w, "vy", group_rows(m.heads_all))
    spread_heads.start()
    spread_down = Spread(w, "vy", lambda v, y, zh: m.down_all.at[y, zh, v], wd)
    spread_down.start_rest()
    spread_gains.got_first()
    deal_gate.start()
    deal_up.start()
    visit_rows.arrive()
    share_rows = Share(w, lambda x, k: m.rows_all.at[:, k, x])
    share_rows.start()
    spread_gains.got_z()
    spread_heads.got_first()
    spread_out.got_first()
    spread_gains.got_last()
    deal_gate.arrive()
    spread_gate = Spread(w, "vy", group_rows(m.gate_all))
    spread_gate.start_rest()
    deal_up.arrive()
    spread_up = Spread(w, "yv", group_rows(m.up_all))
    spread_up.start_rest()
    spread_heads.got_z()
    spread_down.start_z()
    spread_gate.start_z()
    spread_up.start_z()
    spread_gains.arrive()
    share_gains = [Share(w, lambda x, k: m.gains_all.at[:, k, :, :, x])]
    for share in share_gains:
        share.start()
    share_rows.forward()
    swap.wait()
    m.ids_row[...] = m.ids_all[zh, v].astype(F32)
    for j in range(8):
        piece = slice(128 * j, 128 * j + 128)
        m.ids_col[piece, :] = jnp.broadcast_to(m.ids_row[:, piece], (128, 128)).T
    spread_out.got_z()
    spread_heads.got_last()
    for share in share_gains:
        share.forward()
    spread_down.got_first()
    share_rows.arrive()
    for share in share_gains:
        share.arrive()
    for j in range(8):
        four = [
            m.gains_all[j // 4, (j // 2) % 2, j % 2, i // 2, i % 2].astype(F32) for i in range(4)
        ]
        total = four[0] + four[1] + four[2] + four[3]
        for i in range(2):
            m.gain_rows[i, :, 128 * j : 128 * j + 128] = total[i : i + 1, :]

    def first_norm(b, _):
        block = m.rows_all[b // 2, b % 2].reshape(256, 1024).astype(F32)
        span = pl.ds(pl.multiple_of(256 * b, 256), 256)
        m.normed[span, :] = (block * inverse_size(block) * m.gain_rows[0]).astype(BF16)
        return 0

    lax.fori_loop(0, 4, first_norm, 0)
    spread_heads.arrive()
    heads = m.heads_all[...].reshape(1024, 768)
    for b in range(4):
        span = slice(256 * b, 256 * b + 256)
        made = dots(m.normed[span, :], heads, NN).astype(BF16)
        m.query[span, :], m.keys[span, :] = made[:, :256], made[:, 256:512]
        m.values[span, :] = made[:, 512:]
        m.keys_turned[:, span] = made[:, 256:512].T
        m.values_turned[:, span] = made[:, 512:].T
    spread_out.got_last()
    spread_gate.got_first()
    spread_up.got_first()

    def bias_of(b):
        start, count = 256 * b, 256 * b + 256
        column = m.ids_col[:count, :]
        same = jnp.concatenate([column, column], axis=1) == m.ids_row[:, start : start + 256]
        key = lax.broadcasted_iota(jnp.int32, (count, 256), 0)
        place = lax.broadcasted_iota(jnp.int32, (count, 256), 1) + start
        return jnp.where(jnp.logical_and(same, key <= place), 0.0, -1e30).astype(F32)

    def head_rows(h):
        return pl.ds(pl.multiple_of(h * HEAD, HEAD), HEAD)

    def rank_columns(x, k):
        return pl.ds(pl.multiple_of(256 * (2 * x + k), 256), 256)

    def mix(b):
        span, count = slice(256 * b, 256 * b + 256), 256 * b + 256
        bias = bias_of(b)

        def one(h, _):
            scores = dots(m.keys[:count, :], only_head(m.query[span, :], h), NT)
            scores = scores * (HEAD**-0.5 * LOG2E) + bias
            top = jnp.max(scores, axis=0, keepdims=True)
            lifted = jnp.exp2(scores - top)
            total = jnp.sum(lifted, axis=0, keepdims=True)
            probs = (lifted * (1.0 / total)).astype(BF16)
            mixed = dots(m.values_turned[head_rows(h), :count], probs, NN)
            m.mixed_turned[head_rows(h), span] = mixed.astype(BF16)
            m.logsum[h, :, span] = top + jnp.log2(total)
            return 0

        lax.fori_loop(0, 4, one, 0)
        m.mixed_all[b // 2, b % 2, :, rank_columns(x, k)] = m.mixed_turned[:, span].T

    def share_mixed(b):
        return Share(w, lambda x, k: m.mixed_all.at[b // 2, b % 2, :, rank_columns(x, k)])

    shares = [share_mixed(b) for b in range(4)]
    mix(0)
    shares[0].start()
    spread_down.got_z()
    mix(1)
    shares[1].start()
    visit_cots = Visit(w, cots, sequence_block(m.cots_all), spare())
    visit_cots.start()
    shares[0].forward()
    spread_out.arrive()
    share_out = [Share(w, lambda x, k: m.out_all.at[:, k, :, :, x])]
    for share in share_out:
        share.start()
    spread_gate.got_z()
    mix(2)
    shares[2].start()
    shares[1].forward()
    for share in share_out:
        share.forward()
    spread_up.got_z()
    spread_down.got_last()
    mix(3)
    shares[3].start()
    shares[2].forward()
    for share in share_out:
        share.arrive()

    for b in range(4):
        span = slice(256 * b, 256 * b + 256)
        if b == 2:
            shares[3].forward()
            spread_gate.got_last()
        shares[b].arrive()
        middle = m.rows_all[b // 2, b % 2].reshape(256, 1024).astype(F32)
        whole = m.out_all[...].reshape(1024, 1024)
        middle = middle + dots(m.mixed_all[b // 2, b % 2], whole, NN)
        m.normed_two[span, :] = (middle * inverse_size(middle) * m.gain_rows[1]).astype(BF16)

        @pl.when(k == b % 2)
        def _():
            m.middle_keep[b // 2] = middle

    visit_cots.arrive()
    share_cots = Share(w, lambda x, k: m.cots_all.at[:, k, x])
    share_cots.start()
    spread_up.got_last()
    share_cots.forward()
    for spread in (spread_gate, spread_up, spread_down):
        spread.arrive()
    share_cots.arrive()
    for share in shares:
        share.drain()
    total_out = Total(w, m.mixed_all, m.core_out, m.across_out)
    total_norm = Total(w, m.part_norm, m.core_norm, m.across_norm)

    def feed(i, part):
        span = pl.ds(pl.multiple_of(256 * (2 * i + part), 256), 256)
        upstream = m.cots_all[i, part].reshape(256, 1024)
        normed_two = m.normed_two[span, :]
        for n in range(4):
            columns = slice(256 * n, 256 * n + 256)
            gate_tile = m.gate_all[..., columns].reshape(1024, 256)
            up_tile = m.up_all[..., columns].reshape(1024, 256)
            down_tile = m.down_all[n // 2, n % 2].reshape(256, 1024)
            gate = dots(normed_two, gate_tile, NN)
            upward = dots(normed_two, up_tile, NN)
            grad_hidden = dots(upstream, down_tile, NT)
            sigma = 1.0 / (1.0 + jnp.exp(-gate))
            silu = gate * sigma
            m.hidden[span, columns] = (silu * upward).astype(BF16)
            m.grad_up[span, columns] = (grad_hidden * silu).astype(BF16)
            m.grad_gate[span, columns] = (
                grad_hidden * upward * (sigma + silu * (1.0 - sigma))
            ).astype(BF16)
        norm_part = dots(m.grad_gate[span, :], m.gate_all[...].reshape(1024, 1024), NT)
        norm_part = norm_part + dots(m.grad_up[span, :], m.up_all[...].reshape(1024, 1024), NT)
        return span, norm_part

    def out_of(span):
        return dots(m.hidden[span, :], m.down_all[...].reshape(1024, 1024), NN)

    def give(i, _):
        span, norm_part = feed(i, 1 - k)
        total_norm.give(i, norm_part)
        total_out.give(i, out_of(span))
        return 0

    def keep(i, _):
        span, norm_part = feed(i, k)
        total_norm.keep(i, norm_part)
        total_out.keep(i, out_of(span))
        return 0

    lax.fori_loop(0, 2, give, 0)
    lax.fori_loop(0, 2, keep, 0)
    for spread in (spread_gate, spread_up, spread_down):
        spread.drain()

    def lanes(plane, half):
        return pl.ds(pl.multiple_of(512 * plane + 256 * half, 256), 256)

    def down_part(plane):
        def one(half, _):
            made = dots(m.hidden[:, lanes(plane, half)], m.cots_all[...].reshape(1024, 1024), TN)
            m.down_all[plane, half] = made.astype(BF16).reshape(2, 128, 1024)
            return 0

        lax.fori_loop(0, 2, one, 0)

    def wide_part(whole, right, plane):
        def one(half, _):
            made = dots(m.normed_two[:, lanes(plane, half)], right[...], TN).astype(BF16)
            whole[plane, half] = made.reshape(2, 2, 2, 32, 1024)
            return 0

        lax.fori_loop(0, 2, one, 0)

    def fold_plane(whole, got_b, got_a, got_z):
        return Fold(
            w, "vy", lambda y: [whole.at[y]], lambda v, y, zh: whole.at[y, :, zh, (v + zh) % 2],
            [got_b], lambda v, zh: got_b.at[:, zh, (v + zh) % 2], got_a, got_z,
        )

    def fold_side(whole, got_b, got_a, got_z):
        return Fold(
            w, "yv", lambda v: [whole.at[:, :, 0, v], whole.at[:, :, 1, 1 - v]],
            lambda v, y, zh: whole.at[y, :, zh, (v + zh) % 2],
            [got_b.at[0], got_b.at[1]], lambda y, zh: got_b.at[zh, y], got_a, got_z,
        )

    def fold_block(whole, got_b, got_a, got_z):
        return Fold(
            w, "vy", lambda y: [whole.at[y]], lambda v, y, zh: whole.at[y, zh, v],
            [got_b], lambda v, zh: got_b.at[zh, v], got_a, got_z,
        )

    fold_down = fold_block(m.down_all, m.down_b, m.down_a, m.down_z)
    fold_gate = fold_plane(m.gate_all, m.gate_b, m.gate_a, m.gate_z)
    fold_up = fold_side(m.up_all, m.up_b, m.up_a, m.up_z)
    fold_heads = fold_plane(m.heads_part, m.heads_b, m.heads_a, m.heads_z)
    fold_gains = fold_block(m.gains_part, m.gains_b, m.gains_a, m.gains_z)
    down_part(1 - y)
    fold_down.start()
    wide_part(m.up_all, m.grad_up, 0)
    wide_part(m.up_all, m.grad_up, 1)
    fold_up.start()
    wide_part(m.gate_all, m.grad_gate, 1 - y)
    fold_gate.start()

    share_branch = Share(w, lambda x, k: m.branch.at[:, k, x])
    own_half = total_norm.rows(x)
    gain_sum = jnp.zeros((1, 1024), F32)
    for i in range(2):
        grad, term = norm_back(
            m.middle_keep[i, own_half], m.gain_rows[1], total_norm.take(i)
        )
        gain_sum = gain_sum + term
        m.done_out[i] = (m.middle_keep[i, own_half] + total_out.take(i)).astype(BF16)
        grad = grad + m.cots_all[i, k, x].astype(F32)
        m.middle_keep[i, own_half] = grad
        m.branch[i, k, x] = grad.astype(BF16)
    share_branch.start()
    return_out = Return(w, lambda i: m.done_out.at[i], output, spare())
    return_out.start()

    def gain_rows_part(row, total):
        for plane in range(2):
            for place in range(4):
                for half in range(2):
                    at = 512 * plane + 256 * half + 128 * (place // 2)
                    row_at = slice(2 * row + half, 2 * row + half + 1)
                    m.gains_part[plane, place // 2, place % 2, row_at, :] = total[:, at : at + 128]

    m.gains_part[...] = jnp.zeros_like(m.gains_part)
    gain_rows_part(1, gain_sum)
    down_part(y)
    share_branch.forward()
    wide_part(m.gate_all, m.grad_gate, y)
    share_branch.arrive()

    grad_mixed, grad_mixed_turned = m.grad_up.at[:, :256], m.hidden.at[:256]
    grad_heads = m.grad_gate.at[:, :768]
    out_own = m.out_all[x, k].reshape(256, 1024)
    for b in range(4):
        span = slice(256 * b, 256 * b + 256)
        made = dots(m.branch[b // 2, b % 2].reshape(256, 1024), out_own, NT).astype(BF16)
        grad_mixed[span, :] = made
        grad_mixed_turned[:, span] = made.T
    m.out_part[...] = (
        dots(m.mixed_turned[...], m.branch[...].reshape(1024, 1024), NN)
        .astype(BF16)
        .reshape(2, 2, 2, 32, 1024)
    )
    base = w.slots(6)
    owner = y == x
    out_across = w.copy(m.out_part, m.out_b, w.at(y=1 - y), base)
    pl.when(jnp.logical_not(owner))(lambda: out_across.start())
    m.grad_keys[...] = jnp.zeros_like(m.grad_keys)
    m.grad_values[...] = jnp.zeros_like(m.grad_values)

    def unmix(b):
        span, count = slice(256 * b, 256 * b + 256), 256 * b + 256
        bias = bias_of(b)

        def one(h, _):
            query, upstream = only_head(m.query[span, :], h), only_head(grad_mixed[span, :], h)
            scores = dots(m.keys[:count, :], query, NT)
            scores = scores * (HEAD**-0.5 * LOG2E) + bias
            probs = jnp.exp2(scores - m.logsum[h, :, span])
            grad_probs = dots(m.values[:count, :], upstream, NT)
            centre = jnp.sum(
                grad_mixed_turned[head_rows(h), span].astype(F32)
                * m.mixed_turned[head_rows(h), span].astype(F32),
                axis=0,
                keepdims=True,
            )
            grad_scores = (probs * (grad_probs - centre)).astype(BF16)
            turned = dots(m.keys_turned[head_rows(h), :count], grad_scores, NN)
            grad_mixed_turned[head_rows(h), span] = (turned * HEAD**-0.5).astype(BF16)
            m.grad_keys[:count, :] += dots(grad_scores, query, NN)
            m.grad_values[:count, :] += dots(probs.astype(BF16), upstream, NN)
            return 0

        lax.fori_loop(0, 4, one, 0)
        grad_heads[span, :256] = grad_mixed_turned[:, span].T

    unmix(0)
    unmix(1)
    fold_up.second()
    unmix(2)
    fold_down.second()
    unmix(3)
    grad_heads[:, 256:512] = (m.grad_keys[...] * HEAD**-0.5).astype(BF16)
    grad_heads[:, 512:] = m.grad_values[...].astype(BF16)

    for plane in range(2):
        for half in range(2):
            made = dots(m.normed[:, lanes(plane, half)], grad_heads[...], TN)
            m.heads_part[plane, half] = made.astype(BF16).reshape(2, 2, 2, 32, 768)
    fold_heads.start()
    total_norm.drain()
    total_first = Total(w, m.part_norm, m.core_norm, m.across_norm)

    def first_part(i, part):
        span = pl.ds(pl.multiple_of(256 * (2 * i + part), 256), 256)
        return dots(grad_heads[span, :], m.heads_all[...].reshape(1024, 768), NT)

    for i in range(2):
        total_first.give(i, first_part(i, 1 - k))
    for i in range(2):
        total_first.keep(i, first_part(i, k))
    fold_up.third()
    fold_down.third()
    gain_sum = jnp.zeros((1, 1024), F32)

    def done_in(i):
        return m.normed_two.at[pl.ds(128 * i, 128)]

    for i in range(2):
        grad, term = norm_back(
            m.rows_all[i, k, x].astype(F32), m.gain_rows[0], total_first.take(i)
        )
        gain_sum = gain_sum + term
        done_in(i)[...] = (m.middle_keep[i, own_half] + grad).astype(BF16)
    return_in = Return(w, done_in, input_home, spare())
    return_in.start()
    gain_rows_part(0, gain_sum)
    fold_gains.start()

    fold_gate.second()

    def out_side(z):
        side = 1 - zh if z else zh
        return w.copy(
            m.out_part.at[side, (1 - v + side) % 2], m.out_a.at[side], w.at(v=1 - v), base + 1 + z
        )

    def out_side_landed(z):
        ref = m.out_a.at[1 - zh if z else zh]
        return w.copy(ref, ref, w.at(v=1 - v), base + 1 + z)

    def out_two(side, v):
        at = (v + side) % 2
        return m.out_part[side, at].astype(F32) + m.out_b[side, at].astype(F32)

    far = (v + 1 - zh) % 2
    out_half = w.copy(m.out_part.at[1 - zh, far], m.out_z, w.at(zh=1 - zh), base + 3)
    out_last = w.copy(m.out_deal, m.out_home, w.across(), base + 4)

    @pl.when(owner)
    def _():
        out_across.wait_recv()
        for side in (1, 0):
            at = 1 - zh if side else zh
            m.out_part[at, (1 - v + at) % 2] = out_two(at, 1 - v).astype(BF16)
            out_side(side).start()

    fold_heads.second()
    fold_gains.second()
    fold_gate.third()

    @pl.when(owner)
    def _():
        out_side_landed(1).wait_recv()
        m.out_part[1 - zh, far] = (
            out_two(1 - zh, v) + m.out_a[1 - zh].astype(F32)
        ).astype(BF16)
        out_half.start()

    d_out[...] = fold_down.finish()

    def deal_grads(packed, dealt):
        return Deal(
            w, lambda x, k: packed.at[2 * k + x], lambda x, k: dealt.at[2 * x + k]
        )

    deal_up.drain()
    deal_gate.drain()
    deal_heads.drain()
    m.up_pack[...] = fold_up.finish().astype(BF16).reshape(4, 32, 1024)
    deal_up_grad = deal_grads(m.up_pack, up_dealt)
    deal_up_grad.start()
    fold_heads.third()
    fold_gains.third()
    m.gate_pack[...] = fold_gate.finish().astype(BF16).reshape(4, 32, 1024)
    deal_gate_grad = deal_grads(m.gate_pack, gate_dealt)
    deal_gate_grad.start()

    @pl.when(owner)
    def _():
        out_side_landed(0).wait_recv()
        out_half.wait_recv()
        out_total = out_two(zh, v) + m.out_a[zh].astype(F32) + m.out_z[...].astype(F32)
        first, second = out_total[0], out_total[1]
        m.out_deal[...] = jnp.where(x == 0, second, first).astype(BF16)
        out_last.start()
        o_out[...] = jnp.where(x == 0, first, second)

    return_in.arrive()
    m.gains_deal[...] = fold_gains.finish()
    m.gains_dealt[rank] = m.gains_deal[...]
    deal_gains = Deal(w, lambda x, k: m.gains_deal, lambda x, k: m.gains_dealt.at[2 * x + k])
    deal_gains.start()
    m.heads_pack[...] = fold_heads.finish().astype(BF16).reshape(4, 32, 768)
    deal_heads_grad = deal_grads(m.heads_pack, heads_dealt)
    deal_heads_grad.start()
    up_dealt[rank] = m.up_pack[2 * k + x]
    gate_dealt[rank] = m.gate_pack[2 * k + x]
    heads_dealt[rank] = m.heads_pack[2 * k + x]
    deal_up_grad.arrive()
    deal_gate_grad.arrive()
    deal_gains.arrive()
    gain_out[...] = m.gains_dealt[0] + m.gains_dealt[1] + m.gains_dealt[2] + m.gains_dealt[3]
    deal_heads_grad.arrive()

    @pl.when(jnp.logical_not(owner))
    def _():
        out_last.wait_recv()
        o_out[...] = m.out_home[...].astype(F32)

    return_out.arrive()
    for part in [
        visit_rows, visit_cots, spread_gains, spread_heads, spread_out, share_rows, share_cots,
        share_branch, total_out, total_first, fold_down, fold_gate, fold_up, fold_heads,
        fold_gains, return_out, return_in, deal_up_grad, deal_gate_grad, deal_heads_grad,
        deal_gains,
    ] + share_gains + share_out:
        part.drain()

    @pl.when(owner)
    def _():
        for side in range(2):
            out_side(side).wait_send()
        out_half.wait_send()
        out_last.wait_send()

    pl.when(jnp.logical_not(owner))(lambda: out_across.wait_send())


def finish_body(
    output, input_home, heads, out, gate, up, down,
    output_to, input_to, q_to, k_to, v_to, out_to, gate_to, up_to, down_to,
):
    for dealt, target in ((gate, gate_to), (up, up_to)):
        for r in range(4):
            for j, (start, width) in enumerate(hidden_columns(r)):
                piece = dealt[r, :, 128 * j : 128 * j + width]
                target[:, start : start + width] = piece.astype(F32)
    for r in range(4):
        for j, target in enumerate((q_to, k_to, v_to)):
            piece = heads[r, :, 256 * j : 256 * j + 256]
            target[:, 256 * r : 256 * r + 256] = piece.astype(F32)
    output_to[...] = output[...]
    input_to[...] = input_home[...].astype(F32)
    out_to[...] = out[...]
    down_to[...] = down[...]


def grouped(
    layer_input, doc_ids, attn_gain, query_weight, key_weight, value_weight, out_weight,
    mlp_gain, gate_weight, up_weight, down_weight, out_grad,
):
    dp, ctx = lax.axis_index("dp"), lax.axis_index("ctx")
    k = dp % 2
    piece = attn_gain.shape[0]
    lane = piece * (ctx % 4)
    gains = jnp.zeros((16, 128), BF16)
    gains = lax.dynamic_update_slice(gains, jnp.stack([attn_gain, mlp_gain]), (0, lane))
    d, f = layer_input.shape[2], gate_weight.shape[1]
    outs = (
        shaped(*layer_input.shape),
        shaped(*layer_input.shape),
        shaped(4, piece, 3 * d // 4),
        shaped(piece, d, dtype=F32),
        shaped(4, piece, f // 4),
        shaped(4, piece, f // 4),
        shaped(*down_weight.shape, dtype=F32),
        shaped(8, 128, dtype=F32),
    )
    finals = (
        shaped(*layer_input.shape),
        shaped(*layer_input.shape, dtype=F32),
        shaped(piece, d, dtype=F32),
        shaped(piece, d, dtype=F32),
        shaped(piece, d, dtype=F32),
        shaped(piece, d, dtype=F32),
        shaped(piece, f, dtype=F32),
        shaped(piece, f, dtype=F32),
        shaped(*down_weight.shape, dtype=F32),
    )
    rooms = [pltpu.VMEM(shape, dtype) for _, shape, dtype in SCRATCH]
    made = pl.pallas_call(
        layer_body,
        name="layer",
        out_shape=outs,
        in_specs=[ANY, ANY, ANY, VMEM, VMEM, VMEM, ANY, VMEM, VMEM, ANY, ANY],
        out_specs=(VMEM,) * len(outs),
        scratch_shapes=rooms
        + [
            pltpu.SemaphoreType.DMA((192,)),
            pltpu.SemaphoreType.DMA((192,)),
            pltpu.SemaphoreType.DMA((16,)),
        ],
        compiler_params=pltpu.CompilerParams(
            collective_id=0, has_side_effects=True, vmem_limit_bytes=61 << 20
        ),
    )(
        layer_input, out_grad, doc_ids.reshape(2, 1, -1), query_weight, key_weight, value_weight,
        out_weight, gate_weight, up_weight, down_weight, gains,
    )
    gain = made[-1]
    output, input_grad, q, k_, v, o, g, u, down = pl.pallas_call(
        finish_body,
        name="finish",
        out_shape=finals,
        in_specs=[VMEM] * 7,
        out_specs=(VMEM,) * len(finals),
        compiler_params=pltpu.CompilerParams(vmem_limit_bytes=58 << 20),
    )(*made[:-1])

    def gain_of(row):
        return lax.dynamic_slice(gain, (row + k, lane), (1, piece)).reshape(piece)

    return (output, input_grad, gain_of(0), q, k_, v, o, gain_of(2), g, u, down)


def plain_product(left, right):
    return jnp.dot(left, right, preferred_element_type=jnp.float32)


def plain_product_left(left, right):
    return lax.dot_general(
        left, right, (((0,), (0,)), ((), ())), preferred_element_type=jnp.float32
    )


def plain_product_right(left, right):
    return lax.dot_general(
        left, right, (((1,), (1,)), ((), ())), preferred_element_type=jnp.float32
    )


def normalize(rows, gain):
    inverse = lax.rsqrt(jnp.mean(rows * rows, axis=-1, keepdims=True) + EPS)
    return (rows * inverse * gain, inverse)


def plain_norm_back(rows, inverse, gain, upstream):
    normed = rows * inverse
    scaled = upstream * gain
    grad_rows = inverse * (scaled - normed * jnp.mean(scaled * normed, axis=-1, keepdims=True))
    return (grad_rows, jnp.sum(upstream * normed, axis=0))


def head_pair(array, start):
    piece = lax.dynamic_slice_in_dim(array, start, 2 * HEAD, 2)
    return piece.reshape(array.shape[0], array.shape[1], 2, HEAD)


def pair_scores(query, keys, allowed, start):
    scores = jnp.einsum(
        "sqhd,skhd->shqk",
        head_pair(query, start),
        head_pair(keys, start),
        preferred_element_type=jnp.float32,
    ) * HEAD ** (-0.5)
    return jnp.where(allowed[:, None], scores, -1e30)


def plain_attend(query, keys, values, allowed):
    groups, rows, width = query.shape

    def step(index, carry):
        mixed_all, logsum = carry
        start = index * 2 * HEAD
        scores = pair_scores(query, keys, allowed, start)
        top = jnp.max(scores, axis=-1, keepdims=True)
        lifted = jnp.exp(scores - top)
        total = jnp.sum(lifted, axis=-1, keepdims=True)
        probs = (lifted / total).astype(jnp.bfloat16)
        mixed = jnp.einsum(
            "shqk,skhd->sqhd", probs, head_pair(values, start), preferred_element_type=jnp.float32
        )
        mixed_all = lax.dynamic_update_slice_in_dim(
            mixed_all, mixed.reshape(groups, rows, 2 * HEAD).astype(jnp.bfloat16), start, 2
        )
        logsum = lax.dynamic_update_slice_in_dim(
            logsum, (top + jnp.log(total))[..., 0], index * 2, 1
        )
        return (mixed_all, logsum)

    start_state = (
        jnp.zeros((groups, rows, width), jnp.bfloat16),
        jnp.zeros((groups, width // HEAD, rows), jnp.float32),
    )
    return lax.fori_loop(0, width // (2 * HEAD), step, start_state)


def plain_attend_back(query, keys, values, allowed, logsum, grad_mixed):
    groups, rows, width = query.shape
    length = keys.shape[1]
    scale = HEAD ** (-0.5)

    def step(index, carry):
        grad_query, grad_keys, grad_values = carry
        start = index * 2 * HEAD
        scores = pair_scores(query, keys, allowed, start)
        kept = lax.dynamic_slice_in_dim(logsum, index * 2, 2, 1)
        probs = jnp.exp(scores - kept[..., None])
        upstream = head_pair(grad_mixed, start)
        grad_probs = jnp.einsum(
            "sqhd,skhd->shqk",
            upstream,
            head_pair(values, start),
            preferred_element_type=jnp.float32,
        )
        grad_scores = (
            probs * (grad_probs - jnp.sum(probs * grad_probs, axis=-1, keepdims=True))
        ).astype(jnp.bfloat16)
        part_query = (
            jnp.einsum(
                "shqk,skhd->sqhd",
                grad_scores,
                head_pair(keys, start),
                preferred_element_type=jnp.float32,
            )
            * scale
        )
        part_keys = (
            jnp.einsum(
                "shqk,sqhd->skhd",
                grad_scores,
                head_pair(query, start),
                preferred_element_type=jnp.float32,
            )
            * scale
        )
        part_values = jnp.einsum(
            "shqk,sqhd->skhd",
            probs.astype(jnp.bfloat16),
            upstream,
            preferred_element_type=jnp.float32,
        )
        grad_query = lax.dynamic_update_slice_in_dim(
            grad_query, part_query.reshape(groups, rows, 2 * HEAD), start, 2
        )
        grad_keys = lax.dynamic_update_slice_in_dim(
            grad_keys, part_keys.reshape(groups, length, 2 * HEAD), start, 2
        )
        grad_values = lax.dynamic_update_slice_in_dim(
            grad_values, part_values.reshape(groups, length, 2 * HEAD), start, 2
        )
        return (grad_query, grad_keys, grad_values)

    start_state = (
        jnp.zeros((groups, rows, width), jnp.float32),
        jnp.zeros((groups, length, width), jnp.float32),
        jnp.zeros((groups, length, width), jnp.float32),
    )
    return lax.fori_loop(0, width // (2 * HEAD), step, start_state)


def on_device(
    layer_input,
    doc_ids,
    attn_gain,
    query_weight,
    key_weight,
    value_weight,
    out_weight,
    mlp_gain,
    gate_weight,
    up_weight,
    down_weight,
    out_grad,
):
    groups, rows, width = layer_input.shape
    length = doc_ids.shape[1]
    gathered = (
        lax.all_gather(attn_gain, ("dp", "ctx"), axis=0, tiled=True),
        lax.all_gather(query_weight, ("dp", "ctx"), axis=0, tiled=True),
        lax.all_gather(key_weight, ("dp", "ctx"), axis=0, tiled=True),
        lax.all_gather(value_weight, ("dp", "ctx"), axis=0, tiled=True),
        lax.all_gather(out_weight, ("dp", "ctx"), axis=0, tiled=True),
        lax.all_gather(mlp_gain, ("dp", "ctx"), axis=0, tiled=True),
        lax.all_gather(gate_weight, ("dp", "ctx"), axis=0, tiled=True),
        lax.all_gather(up_weight, ("dp", "ctx"), axis=0, tiled=True),
        lax.all_gather(down_weight, ("dp", "ctx"), axis=0, tiled=True),
    )
    gain_one, w_query, w_key, w_value, w_out, gain_two, w_gate, w_up, w_down = gathered
    first = lax.axis_index("ctx") * rows
    places = jnp.arange(length)
    own_ids = lax.dynamic_slice_in_dim(doc_ids, first, rows, 1)
    own_places = first + jnp.arange(rows)
    allowed = (own_ids[:, :, None] == doc_ids[:, None, :]) & (
        places[None, None, :] <= own_places[None, :, None]
    )
    inputs = layer_input.reshape(groups * rows, width).astype(jnp.float32)
    gain_attn = gain_one.astype(jnp.float32)
    normed_full, inverse_one = normalize(inputs, gain_attn)
    normed = normed_full.astype(jnp.bfloat16)
    query = plain_product(normed, w_query).astype(jnp.bfloat16).reshape(groups, rows, width)
    keys_own = plain_product(normed, w_key).astype(jnp.bfloat16).reshape(groups, rows, width)
    values_own = plain_product(normed, w_value).astype(jnp.bfloat16).reshape(groups, rows, width)
    keys, values = (
        lax.all_gather(keys_own, "ctx", axis=1, tiled=True),
        lax.all_gather(values_own, "ctx", axis=1, tiled=True),
    )
    attended, logsum = plain_attend(query, keys, values, allowed)
    attended_rows = attended.reshape(groups * rows, width)
    middle = inputs + plain_product(attended_rows, w_out)
    gain_mlp = gain_two.astype(jnp.float32)
    normed_two_full, inverse_two = normalize(middle, gain_mlp)
    normed_two = normed_two_full.astype(jnp.bfloat16)
    gate = plain_product(normed_two, w_gate)
    upward = plain_product(normed_two, w_up)
    sigma = jax.nn.sigmoid(gate)
    hidden = (gate * sigma * upward).astype(jnp.bfloat16)
    layer_output = (middle + plain_product(hidden, w_down)).astype(jnp.bfloat16)
    gathered_back = (
        lax.all_gather(attn_gain, ("dp", "ctx"), axis=0, tiled=True),
        lax.all_gather(query_weight, ("dp", "ctx"), axis=0, tiled=True),
        lax.all_gather(key_weight, ("dp", "ctx"), axis=0, tiled=True),
        lax.all_gather(value_weight, ("dp", "ctx"), axis=0, tiled=True),
        lax.all_gather(out_weight, ("dp", "ctx"), axis=0, tiled=True),
        lax.all_gather(mlp_gain, ("dp", "ctx"), axis=0, tiled=True),
        lax.all_gather(gate_weight, ("dp", "ctx"), axis=0, tiled=True),
        lax.all_gather(up_weight, ("dp", "ctx"), axis=0, tiled=True),
        lax.all_gather(down_weight, ("dp", "ctx"), axis=0, tiled=True),
    )
    gain_one, w_query, w_key, w_value, w_out, gain_two, w_gate, w_up, w_down = gathered_back
    upstream = out_grad.reshape(groups * rows, width)
    down_grad = plain_product_left(hidden, upstream)
    grad_hidden = plain_product_right(upstream, w_down)
    grad_gate = (grad_hidden * upward * sigma * (1.0 + gate * (1.0 - sigma))).astype(jnp.bfloat16)
    grad_up = (grad_hidden * gate * sigma).astype(jnp.bfloat16)
    gate_grad = plain_product_left(normed_two, grad_gate)
    up_grad = plain_product_left(normed_two, grad_up)
    grad_normed_two = plain_product_right(grad_gate, w_gate) + plain_product_right(grad_up, w_up)
    grad_middle, mlp_gain_grad = plain_norm_back(
        middle, inverse_two, gain_two.astype(jnp.float32), grad_normed_two
    )
    grad_middle = grad_middle + upstream.astype(jnp.float32)
    grad_branch = grad_middle.astype(jnp.bfloat16)
    out_proj_grad = plain_product_left(attended_rows, grad_branch)
    grad_attended = (
        plain_product_right(grad_branch, w_out).astype(jnp.bfloat16).reshape(groups, rows, width)
    )
    grad_query, grad_keys_all, grad_values_all = plain_attend_back(
        query, keys, values, allowed, logsum, grad_attended
    )
    grad_keys, grad_values = (
        lax.psum_scatter(
            grad_keys_all.astype(jnp.bfloat16), "ctx", scatter_dimension=1, tiled=True
        ).astype(jnp.float32),
        lax.psum_scatter(
            grad_values_all.astype(jnp.bfloat16), "ctx", scatter_dimension=1, tiled=True
        ).astype(jnp.float32),
    )
    grad_query = grad_query.astype(jnp.bfloat16).reshape(groups * rows, width)
    grad_keys = grad_keys.astype(jnp.bfloat16).reshape(groups * rows, width)
    grad_values = grad_values.astype(jnp.bfloat16).reshape(groups * rows, width)
    query_grad = plain_product_left(normed, grad_query)
    key_grad = plain_product_left(normed, grad_keys)
    value_grad = plain_product_left(normed, grad_values)
    grad_normed = (
        plain_product_right(grad_query, w_query)
        + plain_product_right(grad_keys, w_key)
        + plain_product_right(grad_values, w_value)
    )
    grad_inputs, attn_gain_grad = plain_norm_back(
        inputs, inverse_one, gain_one.astype(jnp.float32), grad_normed
    )
    input_grad = (grad_middle + grad_inputs).reshape(groups, rows, width)
    shares = (
        lax.psum_scatter(attn_gain_grad, ("dp", "ctx"), scatter_dimension=0, tiled=True),
        lax.psum_scatter(query_grad, ("dp", "ctx"), scatter_dimension=0, tiled=True),
        lax.psum_scatter(key_grad, ("dp", "ctx"), scatter_dimension=0, tiled=True),
        lax.psum_scatter(value_grad, ("dp", "ctx"), scatter_dimension=0, tiled=True),
        lax.psum_scatter(out_proj_grad, ("dp", "ctx"), scatter_dimension=0, tiled=True),
        lax.psum_scatter(mlp_gain_grad, ("dp", "ctx"), scatter_dimension=0, tiled=True),
        lax.psum_scatter(gate_grad, ("dp", "ctx"), scatter_dimension=0, tiled=True),
        lax.psum_scatter(up_grad, ("dp", "ctx"), scatter_dimension=0, tiled=True),
        lax.psum_scatter(down_grad, ("dp", "ctx"), scatter_dimension=0, tiled=True),
    )
    return (
        layer_output.reshape(groups, rows, width),
        input_grad,
        shares[0],
        shares[1],
        shares[2],
        shares[3],
        shares[4],
        shares[5],
        shares[6],
        shares[7],
        shares[8],
    )


def solution(mesh):
    placed = (
        P("dp", "ctx", None),
        P("dp", None),
        P(("dp", "ctx")),
        P(("dp", "ctx"), None),
        P(("dp", "ctx"), None),
        P(("dp", "ctx"), None),
        P(("dp", "ctx"), None),
        P(("dp", "ctx")),
        P(("dp", "ctx"), None),
        P(("dp", "ctx"), None),
        P(("dp", "ctx"), None),
        P("dp", "ctx", None),
    )
    fits = mesh.shape["dp"] == 4 and mesh.shape["ctx"] == 8
    body = grouped if fits else on_device
    return jax.shard_map(
        body,
        mesh=mesh,
        in_specs=placed,
        out_specs=(
            P("dp", "ctx", None),
            P("dp", "ctx", None),
            P(("dp", "ctx")),
            P(("dp", "ctx"), None),
            P(("dp", "ctx"), None),
            P(("dp", "ctx"), None),
            P(("dp", "ctx"), None),
            P(("dp", "ctx")),
            P(("dp", "ctx"), None),
            P(("dp", "ctx"), None),
            P(("dp", "ctx"), None),
        ),
        check_vma=False,
    )
```

```python
import functools

import jax
import jax.numpy as jnp
from jax import lax
from jax.experimental import pallas as pl
from jax.experimental.pallas import tpu as pltpu
from jax.sharding import PartitionSpec as P

HEAD = 64


EPS = 1e-05
MESH = pl.DeviceIdType.MESH
F32 = jnp.float32
BF16 = jnp.bfloat16
LOG2E = 1.4426950408889634
ANY = pl.BlockSpec(memory_space=pl.ANY)
VMEM = pl.BlockSpec(memory_space=pltpu.VMEM)


class Wires:
    def __init__(self, send, recv):
        dp, ctx = lax.axis_index("dp"), lax.axis_index("ctx")
        self.x, self.y = ctx % 2, dp // 2
        self.zh, self.zb = ctx // 4, (ctx // 2) % 2
        self.v, self.k = (self.zb + self.zh) % 2, dp % 2
        self.send, self.recv = send, recv
        self.used = 0

    def slots(self, count):
        first = self.used
        self.used += count
        return first

    def at(self, v=None, y=None, zh=None, x=None, k=None):
        v = self.v if v is None else v
        y = self.y if y is None else y
        zh = self.zh if zh is None else zh
        x = self.x if x is None else x
        k = self.k if k is None else k
        return (2 * y + k, 4 * zh + 2 * ((v + zh) % 2) + x)

    def across(self):
        return self.at(x=1 - self.x)

    def core(self):
        return self.at(k=1 - self.k)

    def copy(self, source, target, device, slot, recv_slot=None):
        return pltpu.make_async_remote_copy(
            src_ref=source,
            dst_ref=target,
            send_sem=self.send.at[slot],
            recv_sem=self.recv.at[slot if recv_slot is None else recv_slot],
            device_id=device,
            device_id_type=MESH,
        )

    def greet(self):
        v, zh, zb, k = self.v, self.zh, self.zb, self.k
        barrier = pltpu.get_barrier_semaphore()

        def call(peer):
            pl.semaphore_signal(barrier, inc=1, device_id=peer, device_id_type=MESH)

        for peer in (
            self.across(), self.core(), self.at(x=1 - self.x, k=1 - k),
            self.at(v=1 - v), self.at(y=1 - self.y), self.at(zh=1 - zh),
        ):
            call(peer)
        count = 6
        for n in range(2):
            away = jnp.logical_not(every(v == n, zh == k, zb == k))
            pl.when(away)(lambda: call(self.at(v=n, zh=k, k=zb)))
            count = count + jnp.where(away, 1, 0)
            away = jnp.logical_not(every(zh == n, zb == k, zh == k))
            pl.when(away)(lambda: call(self.at(zh=n, v=(k + n) % 2, k=zh)))
            count = count + jnp.where(away, 1, 0)
        pl.semaphore_wait(barrier, count)


def every(*tests):
    all_of = tests[0]
    for test in tests[1:]:
        all_of = jnp.logical_and(all_of, test)
    return all_of


class Pairs:
    def __init__(self, wires, order):
        self.w, self.order = wires, order

    def place(self, z, a, b):
        w = self.w
        v, y = (a, b) if self.order == "vy" else (b, a)
        flip = lambda own, turn: 1 - own if turn else own
        return flip(w.v, v), flip(w.y, y), flip(w.zh, z)

    def partner(self, z, a, b):
        v, y, zh = self.place(z, a, b)
        return self.w.at(v=v, y=y, zh=zh)


class Spread(Pairs):
    SENDS = ((0, 0, 0), (0, 0, 0), (1, 0, 0), (0, 0, 0), (1, 0, 0), (0, 1, 0), (1, 1, 0))
    STEPS = ((1, 0, 0), (0, 1, 0), (0, 1, 0), (0, 0, 1), (0, 0, 1), (0, 0, 1), (0, 0, 1))

    def __init__(self, wires, order, block, own=None):
        super().__init__(wires, order)
        self.block, self.own = block, own
        self.first = wires.slots(7)

    def piece(self, n):
        ref = self.block(*self.place(*self.SENDS[n]))
        source = self.own if self.own is not None and not any(self.SENDS[n]) else ref
        return self.w.copy(source, ref, self.partner(*self.STEPS[n]), self.first + n)

    def landed(self, n):
        came = [i ^ j for i, j in zip(self.SENDS[n], self.STEPS[n])]
        ref = self.block(*self.place(*came))
        return self.w.copy(ref, ref, self.partner(*self.STEPS[n]), self.first + n)

    def start(self):
        self.start_z()
        self.start_rest()

    def start_z(self):
        self.piece(0).start()

    def start_rest(self):
        self.piece(1).start()
        self.piece(3).start()

    def got_first(self):
        self.landed(1).wait_recv()
        self.piece(5).start()

    def got_z(self):
        self.landed(0).wait_recv()
        self.piece(2).start()
        self.piece(4).start()

    def got_last(self):
        self.landed(2).wait_recv()
        self.piece(6).start()

    def arrive(self):
        for n in (3, 4, 5, 6):
            self.landed(n).wait_recv()

    def drain(self):
        for n in range(7):
            self.piece(n).wait_send()


class Share:
    def __init__(self, wires, block):
        self.w, self.block = wires, block
        self.first = wires.slots(3)

    def piece(self, i):
        w = self.w
        ref = self.block(w.x if i < 2 else 1 - w.x, w.k)
        return w.copy(ref, ref, w.across() if i == 0 else w.core(), self.first + i)

    def landed(self, i):
        w = self.w
        ref = self.block(*[(1 - w.x, w.k), (w.x, 1 - w.k), (1 - w.x, 1 - w.k)][i])
        return w.copy(ref, ref, w.core(), self.first + i)

    def start(self):
        self.piece(0).start()
        self.piece(1).start()

    def forward(self):
        self.landed(0).wait_recv()
        self.piece(2).start()

    def arrive(self):
        self.landed(1).wait_recv()
        self.landed(2).wait_recv()

    def drain(self):
        for i in range(3):
            self.piece(i).wait_send()


class Deal:
    def __init__(self, wires, outgoing, incoming):
        self.w, self.outgoing, self.incoming = wires, outgoing, incoming
        self.first = wires.slots(3)

    def mate(self, i):
        w = self.w
        return [(1 - w.x, w.k), (w.x, 1 - w.k), (1 - w.x, 1 - w.k)][i]

    def piece(self, i):
        w = self.w
        x, k = self.mate(i)
        return w.copy(
            self.outgoing(x, k), self.incoming(w.x, w.k), w.at(x=x, k=k), self.first + i
        )

    def landed(self, i):
        x, k = self.mate(i)
        ref = self.incoming(x, k)
        return self.w.copy(ref, ref, self.w.at(x=x, k=k), self.first + i)

    def start(self):
        for i in range(3):
            self.piece(i).start()

    def arrive(self):
        for i in range(3):
            self.landed(i).wait_recv()

    def drain(self):
        for i in range(3):
            self.piece(i).wait_send()


class Visit:
    def __init__(self, wires, home, full, local):
        self.w, self.home, self.full, self.local = wires, home, full, local
        self.first = wires.slots(2)
        w = wires
        self.own = [every(w.v == j, w.zh == w.k, w.zb == w.k) for j in range(2)]
        self.here = [every(w.zh == i, w.zb == w.k, w.zh == w.k) for i in range(2)]

    def piece(self, j):
        w = self.w
        return w.copy(
            self.home.at[j],
            self.full(w.zh, w.zb, w.x),
            w.at(v=j, zh=w.k, k=w.zb),
            self.first + j,
            self.first + w.zh,
        )

    def stay(self, j):
        w = self.w
        return pltpu.make_async_copy(self.home.at[j], self.full(w.zh, w.zb, w.x), self.local)

    def landed(self, i):
        w = self.w
        ref = self.full(i, w.k, w.x)
        return w.copy(ref, ref, w.core(), self.first + i)

    def start(self):
        for j in range(2):
            pl.when(self.own[j])(lambda: self.stay(j).start())
            pl.when(jnp.logical_not(self.own[j]))(lambda: self.piece(j).start())

    def arrive(self):
        for j in range(2):
            pl.when(self.own[j])(lambda: self.stay(j).wait())
        for i in range(2):
            pl.when(jnp.logical_not(self.here[i]))(lambda: self.landed(i).wait_recv())

    def drain(self):
        for j in range(2):
            pl.when(jnp.logical_not(self.own[j]))(lambda: self.piece(j).wait_send())


class Return:
    def __init__(self, wires, done, home, local):
        self.w, self.done, self.home, self.local = wires, done, home, local
        self.first = wires.slots(2)
        w = wires
        self.own = [every(w.zh == i, w.zb == w.k, w.k == w.zh) for i in range(2)]
        self.here = [every(w.v == j, w.zh == w.k, w.zb == w.k) for j in range(2)]

    def piece(self, i):
        w = self.w
        return w.copy(
            self.done(i),
            self.home.at[w.v],
            w.at(zh=i, v=(w.k + i) % 2, k=w.zh),
            self.first + i,
            self.first + w.v,
        )

    def stay(self, i):
        return pltpu.make_async_copy(self.done(i), self.home.at[self.w.v], self.local)

    def landed(self, j):
        ref = self.home.at[j]
        return self.w.copy(ref, ref, self.w.core(), self.first + j)

    def start(self, i):
        pl.when(self.own[i])(lambda: self.stay(i).start())
        pl.when(jnp.logical_not(self.own[i]))(lambda: self.piece(i).start())

    def arrive(self):
        for i in range(2):
            pl.when(self.own[i])(lambda: self.stay(i).wait())
        for j in range(2):
            pl.when(jnp.logical_not(self.here[j]))(lambda: self.landed(j).wait_recv())

    def drain(self):
        for i in range(2):
            pl.when(jnp.logical_not(self.own[i]))(lambda: self.piece(i).wait_send())


def shaped(*shape, dtype=BF16):
    return jax.ShapeDtypeStruct(shape, dtype)


def pack_rows(columns, shards, packed):
    for rank in range(4):
        at = 0
        for shard in shards:
            for start, width in columns(rank):
                packed[rank, :, at : at + width] = shard[:, start : start + width]
                at += width


def head_columns(rank):
    return [(256 * rank, 256)]


def hidden_columns(rank):
    x, k = rank // 2, rank % 2
    return [
        (128 * (16 * y + 8 * k + 4 * zh + 2 * (v ^ zh) + x), 128)
        for y in range(2)
        for zh in range(2)
        for v in range(2)
    ]


class Total:
    def __init__(self, wires, part, got_core, got_across):
        self.w, self.part, self.got_core, self.got_across = wires, part, got_core, got_across
        self.first = wires.slots(4)
        self.half = part.shape[2] // 2

    def core(self, i):
        w = self.w
        return w.copy(
            self.part.at[0, i], self.got_core.at[i], w.core(), self.first + i
        )

    def rows(self, v):
        return pl.ds(pl.multiple_of(self.half * v, self.half), self.half)

    def across(self, i):
        w = self.w
        return w.copy(
            self.part.at[1, i, self.rows(1 - w.x)],
            self.got_across.at[i],
            w.across(),
            self.first + 2 + i,
        )

    def give(self, i, value):
        self.part[0, i] = value.astype(BF16)
        self.core(i).start()

    def keep(self, i, value):
        self.core(i).wait_recv()
        self.part[1, i] = (value + self.got_core[i].astype(F32)).astype(BF16)

    def send(self, i):
        self.across(i).start()

    def take(self, i):
        self.across(i).wait_recv()
        own = self.part[1, i, self.rows(self.w.x)]
        return own.astype(F32) + self.got_across[i].astype(F32)

    def drain(self):
        for i in range(2):
            self.core(i).wait_send()
            self.across(i).wait_send()


class Parts:
    def __init__(self, copies):
        self.copies = copies

    def start(self):
        for copy in self.copies:
            copy.start()

    def wait_send(self):
        for copy in self.copies:
            copy.wait_send()

    def wait_recv(self):
        for copy in self.copies:
            copy.wait_recv()


class Fold(Pairs):
    def __init__(self, wires, order, whole, block, got_b, got_b_block, got_a, got_z):
        super().__init__(wires, order)
        self.whole, self.block = whole, block
        self.got_b, self.got_b_block, self.got_a, self.got_z = got_b, got_b_block, got_a, got_z
        self.first = wires.slots(5)

    def stage_b(self):
        w = self.w
        b = w.y if self.order == "vy" else w.v
        return Parts(
            [
                w.copy(source, target, self.partner(0, 0, 1), self.first + 4 * i)
                for i, (source, target) in enumerate(zip(self.whole(1 - b), self.got_b))
            ]
        )

    def stage_a(self, z):
        v, y, zh = self.place(z, 1, 0)
        return self.w.copy(
            self.block(v, y, zh), self.got_a.at[zh], self.partner(0, 1, 0), self.first + 1 + z,
            self.first + 1 + z,
        )

    def landed_a(self, z):
        v, y, zh = self.place(z, 0, 0)
        ref = self.got_a.at[zh]
        return self.w.copy(ref, ref, self.partner(0, 1, 0), self.first + 1 + z)

    def stage_z(self):
        ref = self.block(*self.place(1, 0, 0))
        return self.w.copy(ref, self.got_z, self.partner(1, 0, 0), self.first + 3)

    def two(self, z, a):
        v, y, zh = self.place(z, a, 0)
        own = self.block(v, y, zh)[...].astype(F32)
        return own + self.got_b_block(v if self.order == "vy" else y, zh)[...].astype(F32)

    def three(self, z):
        return self.two(z, 0) + self.got_a[self.place(z, 0, 0)[2]].astype(F32)

    def start(self):
        self.stage_b().start()

    def second(self):
        self.stage_b().wait_recv()
        for z in (1, 0):
            ref = self.block(*self.place(z, 1, 0))
            ref[...] = self.two(z, 1).astype(self.got_z.dtype)
            self.stage_a(z).start()

    def third(self):
        self.landed_a(1).wait_recv()
        ref = self.block(*self.place(1, 0, 0))
        ref[...] = self.three(1).astype(self.got_z.dtype)
        self.stage_z().start()

    def finish(self):
        self.landed_a(0).wait_recv()
        total = self.three(0)
        self.stage_z().wait_recv()
        return total + self.got_z[...].astype(F32)

    def drain(self):
        self.stage_b().wait_send()
        for z in range(2):
            self.stage_a(z).wait_send()
        self.stage_z().wait_send()


def dots(left, right, dims):
    return lax.dot_general(left, right, (dims, ((), ())), preferred_element_type=F32)


NN, NT, TN = ((1,), (0,)), ((1,), (1,)), ((0,), (0,))


def only_head(array, head):
    lane = lax.broadcasted_iota(jnp.int32, array.shape, 1)
    return jnp.where(lane // HEAD == head, array, jnp.zeros_like(array))


def inverse_size(rows):
    return lax.rsqrt(jnp.mean(rows * rows, axis=-1, keepdims=True) + EPS)


def norm_back(rows, gain, upstream):
    inverse = inverse_size(rows)
    normed = rows * inverse
    scaled = upstream * gain
    grad_rows = inverse * (scaled - normed * jnp.mean(scaled * normed, axis=-1, keepdims=True))
    return grad_rows, jnp.sum(upstream * normed, axis=0, keepdims=True)


SCRATCH = [
    ("rows_all", (2, 2, 2, 128, 1024), BF16),
    ("cots_all", (2, 2, 2, 128, 1024), BF16),
    ("ids_all", (2, 2, 1, 1024), jnp.int32),
    ("heads_all", (2, 2, 2, 2, 2, 32, 768), BF16),
    ("out_all", (2, 2, 2, 2, 2, 32, 1024), BF16),
    ("gate_all", (2, 2, 2, 2, 2, 32, 1024), BF16),
    ("up_all", (2, 2, 2, 2, 2, 32, 1024), BF16),
    ("down_all", (2, 2, 2, 128, 1024), BF16),
    ("gains_all", (2, 2, 2, 2, 2, 16, 128), BF16),
    ("heads_pack", (4, 32, 768), BF16),
    ("gate_pack", (4, 32, 1024), BF16),
    ("up_pack", (4, 32, 1024), BF16),
    ("normed", (1024, 1024), BF16),
    ("query", (1024, 256), BF16),
    ("keys", (1024, 256), BF16),
    ("values", (1024, 256), BF16),
    ("keys_turned", (256, 1024), BF16),
    ("values_turned", (256, 1024), BF16),
    ("mixed_turned", (256, 1024), BF16),
    ("mixed_all", (2, 2, 256, 1024), BF16),
    ("logsum", (4, 1, 1024), F32),
    ("gain_rows", (2, 1, 1024), F32),
    ("ids_row", (1, 1024), F32),
    ("ids_col", (1024, 128), F32),
    ("middle_keep", (2, 256, 1024), F32),
    ("normed_two", (1024, 1024), BF16),
    ("hidden", (1024, 1024), BF16),
    ("grad_gate", (1024, 1024), BF16),
    ("grad_up", (1024, 1024), BF16),
    ("part_norm", (2, 2, 256, 1024), BF16),
    ("core_out", (2, 256, 1024), BF16),
    ("core_norm", (2, 256, 1024), BF16),
    ("across_out", (2, 128, 1024), BF16),
    ("across_norm", (2, 128, 1024), BF16),
    ("branch", (2, 2, 2, 128, 1024), BF16),
    ("grad_keys", (1024, 256), F32),
    ("grad_values", (1024, 256), F32),
    ("heads_part", (2, 2, 2, 2, 2, 32, 768), BF16),
    ("out_part", (2, 2, 2, 32, 1024), BF16),
    ("gains_part", (2, 2, 2, 8, 128), F32),
    ("heads_b", (2, 2, 2, 2, 32, 768), BF16),
    ("heads_a", (2, 2, 2, 32, 768), BF16),
    ("heads_z", (2, 2, 32, 768), BF16),
    ("gate_b", (2, 2, 2, 2, 32, 1024), BF16),
    ("gate_a", (2, 2, 2, 32, 1024), BF16),
    ("gate_z", (2, 2, 32, 1024), BF16),
    ("up_b", (2, 2, 2, 2, 32, 1024), BF16),
    ("up_a", (2, 2, 2, 32, 1024), BF16),
    ("up_z", (2, 2, 32, 1024), BF16),
    ("down_b", (2, 2, 128, 1024), BF16),
    ("down_a", (2, 128, 1024), BF16),
    ("down_z", (128, 1024), BF16),
    ("out_b", (2, 2, 2, 32, 1024), BF16),
    ("out_a", (2, 2, 32, 1024), BF16),
    ("out_z", (2, 32, 1024), BF16),
    ("gains_b", (2, 2, 8, 128), F32),
    ("gains_a", (2, 8, 128), F32),
    ("gains_z", (8, 128), F32),
    ("gains_deal", (8, 128), F32),
    ("gains_dealt", (4, 8, 128), F32),
    ("out_deal", (32, 1024), BF16),
    ("out_home", (32, 1024), BF16),
    ("done_out", (2, 128, 1024), BF16),
]


def layer_body(
    rows, cots, ids, wq, wk, wv, wo, wg, wu, wd, gains,
    output, input_home, heads_dealt, o_out, gate_dealt, up_dealt, d_out, gain_out,
    *scratch,
):
    send, recv, local = scratch[-3:]
    m = type("Memory", (), dict(zip([name for name, _, _ in SCRATCH], scratch)))
    w = Wires(send, recv)
    v, y, zh, zb, x, k = w.v, w.y, w.zh, w.zb, w.x, w.k
    rank = 2 * x + k
    w.greet()

    used = [0]

    def spare():
        used[0] += 1
        return local.at[used[0] - 1]

    def stay(source, target):
        copy = pltpu.make_async_copy(source, target, spare())
        copy.start()
        return copy

    def sequence_block(ref):
        return lambda zh, zb, x: ref.at[zh, zb, x]

    def deal_rows(packed, whole):
        return Deal(
            w,
            lambda x, k: packed.at[2 * x + k],
            lambda sx, sk: whole.at[y, sk, zh, zb, sx],
        )

    def group_rows(ref):
        return lambda v, y, zh: ref.at[y, :, zh, (v + zh) % 2]

    def own_rows(ref):
        return lambda v, y, zh: ref.at[y, k, zh, (v + zh) % 2, x]

    visit_rows = Visit(w, rows, sequence_block(m.rows_all), spare())
    visit_rows.start()
    pack_rows(head_columns, (wq, wk, wv), m.heads_pack)
    deal_heads = deal_rows(m.heads_pack, m.heads_all)
    deal_heads.start()
    spread_gains = Spread(w, "vy", own_rows(m.gains_all), gains)
    spread_gains.start()
    swap = w.copy(ids, m.ids_all.at[k], w.core(), w.slots(1))
    swap.start()
    spread_out = Spread(w, "vy", own_rows(m.out_all), wo)
    spread_out.start()
    pack_rows(hidden_columns, (wg,), m.gate_pack)
    pack_rows(hidden_columns, (wu,), m.up_pack)
    stays = [
        stay(m.heads_pack.at[rank], m.heads_all.at[y, k, zh, zb, x]),
        stay(m.gate_pack.at[rank], m.gate_all.at[y, k, zh, zb, x]),
        stay(m.up_pack.at[rank], m.up_all.at[y, k, zh, zb, x]),
        stay(wo, m.out_all.at[y, k, zh, zb, x]),
        stay(gains, m.gains_all.at[y, k, zh, zb, x]),
        stay(wd, m.down_all.at[y, zh, v]),
        stay(ids, m.ids_all.at[k]),
    ]
    deal_gate = deal_rows(m.gate_pack, m.gate_all)
    deal_up = deal_rows(m.up_pack, m.up_all)
    for copy in stays:
        copy.wait()
    deal_heads.arrive()
    spread_heads = Spread(w, "vy", group_rows(m.heads_all))
    spread_heads.start()
    spread_down = Spread(w, "vy", lambda v, y, zh: m.down_all.at[y, zh, v], wd)
    spread_down.start_rest()
    spread_gains.got_first()
    deal_gate.start()
    deal_up.start()
    visit_rows.arrive()
    share_rows = Share(w, lambda x, k: m.rows_all.at[:, k, x])
    share_rows.start()
    spread_gains.got_z()
    spread_heads.got_first()
    spread_out.got_first()
    spread_gains.got_last()
    deal_gate.arrive()
    spread_gate = Spread(w, "vy", group_rows(m.gate_all))
    spread_gate.start_rest()
    deal_up.arrive()
    spread_up = Spread(w, "yv", group_rows(m.up_all))
    spread_up.start_rest()
    spread_heads.got_z()
    spread_down.start_z()
    spread_gate.start_z()
    spread_up.start_z()
    spread_gains.arrive()
    share_gains = [Share(w, lambda x, k: m.gains_all.at[:, k, :, :, x])]
    for share in share_gains:
        share.start()
    share_rows.forward()
    swap.wait()
    m.ids_row[...] = m.ids_all[zh, v].astype(F32)
    for j in range(8):
        piece = slice(128 * j, 128 * j + 128)
        m.ids_col[piece, :] = jnp.broadcast_to(m.ids_row[:, piece], (128, 128)).T
    spread_out.got_z()
    spread_heads.got_last()
    for share in share_gains:
        share.forward()
    spread_down.got_first()
    share_rows.arrive()
    for share in share_gains:
        share.arrive()
    for j in range(8):
        four = [
            m.gains_all[j // 4, (j // 2) % 2, j % 2, i // 2, i % 2].astype(F32) for i in range(4)
        ]
        total = four[0] + four[1] + four[2] + four[3]
        for i in range(2):
            m.gain_rows[i, :, 128 * j : 128 * j + 128] = total[i : i + 1, :]

    def first_norm(b, _):
        block = m.rows_all[b // 2, b % 2].reshape(256, 1024).astype(F32)
        span = pl.ds(pl.multiple_of(256 * b, 256), 256)
        m.normed[span, :] = (block * inverse_size(block) * m.gain_rows[0]).astype(BF16)
        return 0

    lax.fori_loop(0, 4, first_norm, 0)
    spread_heads.arrive()
    heads = m.heads_all[...].reshape(1024, 768)
    for b in range(4):
        span = slice(256 * b, 256 * b + 256)
        made = dots(m.normed[span, :], heads, NN).astype(BF16)
        m.query[span, :], m.keys[span, :] = made[:, :256], made[:, 256:512]
        m.values[span, :] = made[:, 512:]
        m.keys_turned[:, span] = made[:, 256:512].T
        m.values_turned[:, span] = made[:, 512:].T
    spread_out.got_last()
    spread_gate.got_first()
    spread_up.got_first()

    def bias_of(b):
        start, count = 256 * b, 256 * b + 256
        column = m.ids_col[:count, :]
        same = jnp.concatenate([column, column], axis=1) == m.ids_row[:, start : start + 256]
        key = lax.broadcasted_iota(jnp.int32, (count, 256), 0)
        place = lax.broadcasted_iota(jnp.int32, (count, 256), 1) + start
        return jnp.where(jnp.logical_and(same, key <= place), 0.0, -1e30).astype(F32)

    def head_rows(h):
        return pl.ds(pl.multiple_of(h * HEAD, HEAD), HEAD)

    def rank_columns(x, k):
        return pl.ds(pl.multiple_of(256 * (2 * x + k), 256), 256)

    def mix(b):
        span, count = slice(256 * b, 256 * b + 256), 256 * b + 256
        bias = bias_of(b)

        def one(h, _):
            scores = dots(m.keys[:count, :], only_head(m.query[span, :], h), NT)
            scores = scores * (HEAD**-0.5 * LOG2E) + bias
            top = jnp.max(scores, axis=0, keepdims=True)
            lifted = jnp.exp2(scores - top)
            total = jnp.sum(lifted, axis=0, keepdims=True)
            probs = (lifted * (1.0 / total)).astype(BF16)
            mixed = dots(m.values_turned[head_rows(h), :count], probs, NN)
            m.mixed_turned[head_rows(h), span] = mixed.astype(BF16)
            m.logsum[h, :, span] = top + jnp.log2(total)
            return 0

        lax.fori_loop(0, 4, one, 0)
        m.mixed_all[b // 2, b % 2, :, rank_columns(x, k)] = m.mixed_turned[:, span].T

    def share_mixed(b):
        return Share(w, lambda x, k: m.mixed_all.at[b // 2, b % 2, :, rank_columns(x, k)])

    shares = [share_mixed(b) for b in range(4)]
    mix(0)
    shares[0].start()
    spread_down.got_z()
    mix(1)
    shares[1].start()
    visit_cots = Visit(w, cots, sequence_block(m.cots_all), spare())
    visit_cots.start()
    shares[0].forward()
    spread_out.arrive()
    share_out = [Share(w, lambda x, k: m.out_all.at[:, k, :, :, x])]
    for share in share_out:
        share.start()
    spread_gate.got_z()
    mix(2)
    shares[2].start()
    shares[1].forward()
    for share in share_out:
        share.forward()
    spread_up.got_z()
    spread_down.got_last()
    mix(3)
    shares[3].start()
    shares[2].forward()
    for share in share_out:
        share.arrive()

    for b in range(4):
        span = slice(256 * b, 256 * b + 256)
        if b == 2:
            shares[3].forward()
            spread_gate.got_last()
        shares[b].arrive()
        middle = m.rows_all[b // 2, b % 2].reshape(256, 1024).astype(F32)
        whole = m.out_all[...].reshape(1024, 1024)
        middle = middle + dots(m.mixed_all[b // 2, b % 2], whole, NN)
        m.normed_two[span, :] = (middle * inverse_size(middle) * m.gain_rows[1]).astype(BF16)

        @pl.when(k == b % 2)
        def _():
            m.middle_keep[b // 2] = middle

    visit_cots.arrive()
    share_cots = Share(w, lambda x, k: m.cots_all.at[:, k, x])
    share_cots.start()
    spread_up.got_last()
    share_cots.forward()
    for spread in (spread_gate, spread_up, spread_down):
        spread.arrive()
    share_cots.arrive()
    for share in shares:
        share.drain()
    total_out = Total(w, m.mixed_all, m.core_out, m.across_out)
    total_norm = Total(w, m.part_norm, m.core_norm, m.across_norm)

    def feed(i, part):
        span = pl.ds(pl.multiple_of(256 * (2 * i + part), 256), 256)
        upstream = m.cots_all[i, part].reshape(256, 1024)
        normed_two = m.normed_two[span, :]
        for n in range(4):
            columns = slice(256 * n, 256 * n + 256)
            gate_tile = m.gate_all[..., columns].reshape(1024, 256)
            up_tile = m.up_all[..., columns].reshape(1024, 256)
            down_tile = m.down_all[n // 2, n % 2].reshape(256, 1024)
            gate = dots(normed_two, gate_tile, NN)
            upward = dots(normed_two, up_tile, NN)
            grad_hidden = dots(upstream, down_tile, NT)
            sigma = 1.0 / (1.0 + jnp.exp(-gate))
            silu = gate * sigma
            m.hidden[span, columns] = (silu * upward).astype(BF16)
            m.grad_up[span, columns] = (grad_hidden * silu).astype(BF16)
            m.grad_gate[span, columns] = (
                grad_hidden * upward * (sigma + silu * (1.0 - sigma))
            ).astype(BF16)
        norm_part = dots(m.grad_gate[span, :], m.gate_all[...].reshape(1024, 1024), NT)
        norm_part = norm_part + dots(m.grad_up[span, :], m.up_all[...].reshape(1024, 1024), NT)
        return span, norm_part

    def out_of(span):
        return dots(m.hidden[span, :], m.down_all[...].reshape(1024, 1024), NN)

    def give(i, _):
        span, norm_part = feed(i, 1 - k)
        total_norm.give(i, norm_part)
        total_out.give(i, out_of(span))
        return 0

    def keep(i, _):
        span, norm_part = feed(i, k)
        total_norm.keep(i, norm_part)
        total_norm.send(i)
        total_out.keep(i, out_of(span))
        return 0

    lax.fori_loop(0, 2, give, 0)
    lax.fori_loop(0, 2, keep, 0)
    for spread in (spread_gate, spread_up, spread_down):
        spread.drain()

    def lanes(plane, half):
        return pl.ds(pl.multiple_of(512 * plane + 256 * half, 256), 256)

    def down_part(plane):
        def one(half, _):
            made = dots(m.hidden[:, lanes(plane, half)], m.cots_all[...].reshape(1024, 1024), TN)
            m.down_all[plane, half] = made.astype(BF16).reshape(2, 128, 1024)
            return 0

        lax.fori_loop(0, 2, one, 0)

    def wide_part(whole, right, plane):
        def one(half, _):
            made = dots(m.normed_two[:, lanes(plane, half)], right[...], TN).astype(BF16)
            whole[plane, half] = made.reshape(2, 2, 2, 32, 1024)
            return 0

        lax.fori_loop(0, 2, one, 0)

    def fold_plane(whole, got_b, got_a, got_z):
        return Fold(
            w, "vy", lambda y: [whole.at[y]], lambda v, y, zh: whole.at[y, :, zh, (v + zh) % 2],
            [got_b], lambda v, zh: got_b.at[:, zh, (v + zh) % 2], got_a, got_z,
        )

    def fold_side(whole, got_b, got_a, got_z):
        return Fold(
            w, "yv", lambda v: [whole.at[:, :, 0, v], whole.at[:, :, 1, 1 - v]],
            lambda v, y, zh: whole.at[y, :, zh, (v + zh) % 2],
            [got_b.at[0], got_b.at[1]], lambda y, zh: got_b.at[zh, y], got_a, got_z,
        )

    def fold_block(whole, got_b, got_a, got_z):
        return Fold(
            w, "vy", lambda y: [whole.at[y]], lambda v, y, zh: whole.at[y, zh, v],
            [got_b], lambda v, zh: got_b.at[zh, v], got_a, got_z,
        )

    fold_down = fold_block(m.down_all, m.down_b, m.down_a, m.down_z)
    fold_gate = fold_plane(m.gate_all, m.gate_b, m.gate_a, m.gate_z)
    fold_up = fold_side(m.up_all, m.up_b, m.up_a, m.up_z)
    fold_heads = fold_plane(m.heads_part, m.heads_b, m.heads_a, m.heads_z)
    fold_gains = fold_block(m.gains_part, m.gains_b, m.gains_a, m.gains_z)
    shares_branch = [Share(w, lambda x, k, i=i: m.branch.at[i, k, x]) for i in range(2)]
    own_half, other_half = total_norm.rows(x), total_norm.rows(1 - x)

    def back_two(i):
        grad, term = norm_back(m.middle_keep[i, own_half], m.gain_rows[1], total_norm.take(i))
        grad = grad + m.cots_all[i, k, x].astype(F32)
        m.middle_keep[i, other_half] = grad
        m.branch[i, k, x] = grad.astype(BF16)
        shares_branch[i].start()
        return term

    gain_sum = back_two(0)
    down_part(1 - y)
    fold_down.start()
    wide_part(m.up_all, m.grad_up, 0)
    wide_part(m.up_all, m.grad_up, 1)
    fold_up.start()
    gain_sum = gain_sum + back_two(1)
    wide_part(m.gate_all, m.grad_gate, 1 - y)
    fold_gate.start()
    for i in range(2):
        total_out.send(i)

    def gain_rows_part(row, total):
        for plane in range(2):
            for place in range(4):
                for half in range(2):
                    at = 512 * plane + 256 * half + 128 * (place // 2)
                    row_at = slice(2 * row + half, 2 * row + half + 1)
                    m.gains_part[plane, place // 2, place % 2, row_at, :] = total[:, at : at + 128]

    m.gains_part[...] = jnp.zeros_like(m.gains_part)
    gain_rows_part(1, gain_sum)
    shares_branch[0].forward()
    down_part(y)
    shares_branch[1].forward()
    wide_part(m.gate_all, m.grad_gate, y)

    grad_mixed, grad_mixed_turned = m.grad_up.at[:, :256], m.hidden.at[:256]
    grad_heads = m.grad_gate.at[:, :768]
    out_own = m.out_all[x, k].reshape(256, 1024)
    for b in range(4):
        if b % 2 == 0:
            shares_branch[b // 2].arrive()
        if b == 2:
            fold_down.second()
        span = slice(256 * b, 256 * b + 256)
        made = dots(m.branch[b // 2, b % 2].reshape(256, 1024), out_own, NT).astype(BF16)
        grad_mixed[span, :] = made
        grad_mixed_turned[:, span] = made.T
    m.out_part[...] = (
        dots(m.mixed_turned[...], m.branch[...].reshape(1024, 1024), NN)
        .astype(BF16)
        .reshape(2, 2, 2, 32, 1024)
    )
    base = w.slots(6)
    owner = y == x
    out_across = w.copy(m.out_part, m.out_b, w.at(y=1 - y), base)
    pl.when(jnp.logical_not(owner))(lambda: out_across.start())
    m.grad_keys[...] = jnp.zeros_like(m.grad_keys)
    m.grad_values[...] = jnp.zeros_like(m.grad_values)

    def unmix(b):
        span, count = slice(256 * b, 256 * b + 256), 256 * b + 256
        bias = bias_of(b)

        def one(h, _):
            query, upstream = only_head(m.query[span, :], h), only_head(grad_mixed[span, :], h)
            scores = dots(m.keys[:count, :], query, NT)
            scores = scores * (HEAD**-0.5 * LOG2E) + bias
            probs = jnp.exp2(scores - m.logsum[h, :, span])
            grad_probs = dots(m.values[:count, :], upstream, NT)
            centre = jnp.sum(
                grad_mixed_turned[head_rows(h), span].astype(F32)
                * m.mixed_turned[head_rows(h), span].astype(F32),
                axis=0,
                keepdims=True,
            )
            grad_scores = (probs * (grad_probs - centre)).astype(BF16)
            turned = dots(m.keys_turned[head_rows(h), :count], grad_scores, NN)
            grad_mixed_turned[head_rows(h), span] = (turned * HEAD**-0.5).astype(BF16)
            m.grad_keys[:count, :] += dots(grad_scores, query, NN)
            m.grad_values[:count, :] += dots(probs.astype(BF16), upstream, NN)
            return 0

        lax.fori_loop(0, 4, one, 0)
        grad_heads[span, :256] = grad_mixed_turned[:, span].T

    for i in range(2):
        m.done_out[i] = (m.middle_keep[i, own_half] + total_out.take(i)).astype(BF16)
    return_out = Return(w, lambda i: m.done_out.at[i], output, spare())
    for i in range(2):
        return_out.start(i)
    fold_up.second()
    unmix(0)
    fold_gate.second()
    unmix(1)
    fold_down.third()
    unmix(2)
    fold_up.third()
    unmix(3)
    fold_gate.third()
    grad_heads[:, 256:512] = (m.grad_keys[...] * HEAD**-0.5).astype(BF16)
    grad_heads[:, 512:] = m.grad_values[...].astype(BF16)

    total_norm.drain()
    total_first = Total(w, m.part_norm, m.core_norm, m.across_norm)

    def first_part(i, part):
        span = pl.ds(pl.multiple_of(256 * (2 * i + part), 256), 256)
        return dots(grad_heads[span, :], m.heads_all[...].reshape(1024, 768), NT)

    for i in range(2):
        total_first.give(i, first_part(i, 1 - k))
    for plane in range(2):
        for half in range(2):
            made = dots(m.normed[:, lanes(plane, half)], grad_heads[...], TN)
            m.heads_part[plane, half] = made.astype(BF16).reshape(2, 2, 2, 32, 768)
    fold_heads.start()
    for i in range(2):
        total_first.keep(i, first_part(i, k))
        total_first.send(i)
    gain_sum = jnp.zeros((1, 1024), F32)

    def done_in(i):
        return m.normed_two.at[pl.ds(128 * i, 128)]

    return_in = Return(w, done_in, input_home, spare())
    for i in range(2):
        grad, term = norm_back(
            m.rows_all[i, k, x].astype(F32), m.gain_rows[0], total_first.take(i)
        )
        gain_sum = gain_sum + term
        done_in(i)[...] = (m.middle_keep[i, other_half] + grad).astype(BF16)
        return_in.start(i)
    gain_rows_part(0, gain_sum)
    fold_gains.start()


    def out_side(z):
        side = 1 - zh if z else zh
        return w.copy(
            m.out_part.at[side, (1 - v + side) % 2], m.out_a.at[side], w.at(v=1 - v), base + 1 + z
        )

    def out_side_landed(z):
        ref = m.out_a.at[1 - zh if z else zh]
        return w.copy(ref, ref, w.at(v=1 - v), base + 1 + z)

    def out_two(side, v):
        at = (v + side) % 2
        return m.out_part[side, at].astype(F32) + m.out_b[side, at].astype(F32)

    far = (v + 1 - zh) % 2
    out_half = w.copy(m.out_part.at[1 - zh, far], m.out_z, w.at(zh=1 - zh), base + 3)
    out_last = w.copy(m.out_deal, m.out_home, w.across(), base + 4)

    @pl.when(owner)
    def _():
        out_across.wait_recv()
        for side in (1, 0):
            at = 1 - zh if side else zh
            m.out_part[at, (1 - v + at) % 2] = out_two(at, 1 - v).astype(BF16)
            out_side(side).start()

    fold_heads.second()
    fold_gains.second()

    @pl.when(owner)
    def _():
        out_side_landed(1).wait_recv()
        m.out_part[1 - zh, far] = (
            out_two(1 - zh, v) + m.out_a[1 - zh].astype(F32)
        ).astype(BF16)
        out_half.start()

    d_out[...] = fold_down.finish()

    def deal_grads(packed, dealt):
        return Deal(
            w, lambda x, k: packed.at[2 * k + x], lambda x, k: dealt.at[2 * x + k]
        )

    deal_up.drain()
    deal_gate.drain()
    deal_heads.drain()
    m.up_pack[...] = fold_up.finish().astype(BF16).reshape(4, 32, 1024)
    deal_up_grad = deal_grads(m.up_pack, up_dealt)
    deal_up_grad.start()
    fold_heads.third()
    fold_gains.third()
    m.gate_pack[...] = fold_gate.finish().astype(BF16).reshape(4, 32, 1024)
    deal_gate_grad = deal_grads(m.gate_pack, gate_dealt)
    deal_gate_grad.start()

    @pl.when(owner)
    def _():
        out_side_landed(0).wait_recv()
        out_half.wait_recv()
        out_total = out_two(zh, v) + m.out_a[zh].astype(F32) + m.out_z[...].astype(F32)
        first, second = out_total[0], out_total[1]
        m.out_deal[...] = jnp.where(x == 0, second, first).astype(BF16)
        out_last.start()
        o_out[...] = jnp.where(x == 0, first, second)

    return_in.arrive()
    m.gains_deal[...] = fold_gains.finish()
    m.gains_dealt[rank] = m.gains_deal[...]
    deal_gains = Deal(w, lambda x, k: m.gains_deal, lambda x, k: m.gains_dealt.at[2 * x + k])
    deal_gains.start()
    m.heads_pack[...] = fold_heads.finish().astype(BF16).reshape(4, 32, 768)
    deal_heads_grad = deal_grads(m.heads_pack, heads_dealt)
    deal_heads_grad.start()
    up_dealt[rank] = m.up_pack[2 * k + x]
    gate_dealt[rank] = m.gate_pack[2 * k + x]
    heads_dealt[rank] = m.heads_pack[2 * k + x]
    deal_up_grad.arrive()
    deal_gate_grad.arrive()
    deal_gains.arrive()
    gain_out[...] = m.gains_dealt[0] + m.gains_dealt[1] + m.gains_dealt[2] + m.gains_dealt[3]
    deal_heads_grad.arrive()

    @pl.when(jnp.logical_not(owner))
    def _():
        out_last.wait_recv()
        o_out[...] = m.out_home[...].astype(F32)

    return_out.arrive()
    for part in [
        visit_rows, visit_cots, spread_gains, spread_heads, spread_out, share_rows, share_cots,
        total_out, total_first, fold_down, fold_gate, fold_up, fold_heads,
        fold_gains, return_out, return_in, deal_up_grad, deal_gate_grad, deal_heads_grad,
        deal_gains,
    ] + share_gains + share_out + shares_branch:
        part.drain()

    @pl.when(owner)
    def _():
        for side in range(2):
            out_side(side).wait_send()
        out_half.wait_send()
        out_last.wait_send()

    pl.when(jnp.logical_not(owner))(lambda: out_across.wait_send())


def finish_body(
    output, input_home, heads, out, gate, up, down,
    output_to, input_to, q_to, k_to, v_to, out_to, gate_to, up_to, down_to,
):
    for dealt, target in ((gate, gate_to), (up, up_to)):
        for r in range(4):
            for j, (start, width) in enumerate(hidden_columns(r)):
                piece = dealt[r, :, 128 * j : 128 * j + width]
                target[:, start : start + width] = piece.astype(F32)
    for r in range(4):
        for j, target in enumerate((q_to, k_to, v_to)):
            piece = heads[r, :, 256 * j : 256 * j + 256]
            target[:, 256 * r : 256 * r + 256] = piece.astype(F32)
    output_to[...] = output[...]
    input_to[...] = input_home[...].astype(F32)
    out_to[...] = out[...]
    down_to[...] = down[...]


def grouped(
    layer_input, doc_ids, attn_gain, query_weight, key_weight, value_weight, out_weight,
    mlp_gain, gate_weight, up_weight, down_weight, out_grad,
):
    dp, ctx = lax.axis_index("dp"), lax.axis_index("ctx")
    k = dp % 2
    piece = attn_gain.shape[0]
    lane = piece * (ctx % 4)
    gains = jnp.zeros((16, 128), BF16)
    gains = lax.dynamic_update_slice(gains, jnp.stack([attn_gain, mlp_gain]), (0, lane))
    d, f = layer_input.shape[2], gate_weight.shape[1]
    outs = (
        shaped(*layer_input.shape),
        shaped(*layer_input.shape),
        shaped(4, piece, 3 * d // 4),
        shaped(piece, d, dtype=F32),
        shaped(4, piece, f // 4),
        shaped(4, piece, f // 4),
        shaped(*down_weight.shape, dtype=F32),
        shaped(8, 128, dtype=F32),
    )
    finals = (
        shaped(*layer_input.shape),
        shaped(*layer_input.shape, dtype=F32),
        shaped(piece, d, dtype=F32),
        shaped(piece, d, dtype=F32),
        shaped(piece, d, dtype=F32),
        shaped(piece, d, dtype=F32),
        shaped(piece, f, dtype=F32),
        shaped(piece, f, dtype=F32),
        shaped(*down_weight.shape, dtype=F32),
    )
    rooms = [pltpu.VMEM(shape, dtype) for _, shape, dtype in SCRATCH]
    made = pl.pallas_call(
        layer_body,
        name="layer",
        out_shape=outs,
        in_specs=[ANY, ANY, ANY, VMEM, VMEM, VMEM, ANY, VMEM, VMEM, ANY, ANY],
        out_specs=(VMEM,) * len(outs),
        scratch_shapes=rooms
        + [
            pltpu.SemaphoreType.DMA((192,)),
            pltpu.SemaphoreType.DMA((192,)),
            pltpu.SemaphoreType.DMA((16,)),
        ],
        compiler_params=pltpu.CompilerParams(
            collective_id=0, has_side_effects=True, vmem_limit_bytes=61 << 20
        ),
    )(
        layer_input, out_grad, doc_ids.reshape(2, 1, -1), query_weight, key_weight, value_weight,
        out_weight, gate_weight, up_weight, down_weight, gains,
    )
    gain = made[-1]
    output, input_grad, q, k_, v, o, g, u, down = pl.pallas_call(
        finish_body,
        name="finish",
        out_shape=finals,
        in_specs=[VMEM] * 7,
        out_specs=(VMEM,) * len(finals),
        compiler_params=pltpu.CompilerParams(vmem_limit_bytes=58 << 20),
    )(*made[:-1])

    def gain_of(row):
        return lax.dynamic_slice(gain, (row + k, lane), (1, piece)).reshape(piece)

    return (output, input_grad, gain_of(0), q, k_, v, o, gain_of(2), g, u, down)


def plain_product(left, right):
    return jnp.dot(left, right, preferred_element_type=jnp.float32)


def plain_product_left(left, right):
    return lax.dot_general(
        left, right, (((0,), (0,)), ((), ())), preferred_element_type=jnp.float32
    )


def plain_product_right(left, right):
    return lax.dot_general(
        left, right, (((1,), (1,)), ((), ())), preferred_element_type=jnp.float32
    )


def normalize(rows, gain):
    inverse = lax.rsqrt(jnp.mean(rows * rows, axis=-1, keepdims=True) + EPS)
    return (rows * inverse * gain, inverse)


def plain_norm_back(rows, inverse, gain, upstream):
    normed = rows * inverse
    scaled = upstream * gain
    grad_rows = inverse * (scaled - normed * jnp.mean(scaled * normed, axis=-1, keepdims=True))
    return (grad_rows, jnp.sum(upstream * normed, axis=0))


def head_pair(array, start):
    piece = lax.dynamic_slice_in_dim(array, start, 2 * HEAD, 2)
    return piece.reshape(array.shape[0], array.shape[1], 2, HEAD)


def pair_scores(query, keys, allowed, start):
    scores = jnp.einsum(
        "sqhd,skhd->shqk",
        head_pair(query, start),
        head_pair(keys, start),
        preferred_element_type=jnp.float32,
    ) * HEAD ** (-0.5)
    return jnp.where(allowed[:, None], scores, -1e30)


def plain_attend(query, keys, values, allowed):
    groups, rows, width = query.shape

    def step(index, carry):
        mixed_all, logsum = carry
        start = index * 2 * HEAD
        scores = pair_scores(query, keys, allowed, start)
        top = jnp.max(scores, axis=-1, keepdims=True)
        lifted = jnp.exp(scores - top)
        total = jnp.sum(lifted, axis=-1, keepdims=True)
        probs = (lifted / total).astype(jnp.bfloat16)
        mixed = jnp.einsum(
            "shqk,skhd->sqhd", probs, head_pair(values, start), preferred_element_type=jnp.float32
        )
        mixed_all = lax.dynamic_update_slice_in_dim(
            mixed_all, mixed.reshape(groups, rows, 2 * HEAD).astype(jnp.bfloat16), start, 2
        )
        logsum = lax.dynamic_update_slice_in_dim(
            logsum, (top + jnp.log(total))[..., 0], index * 2, 1
        )
        return (mixed_all, logsum)

    start_state = (
        jnp.zeros((groups, rows, width), jnp.bfloat16),
        jnp.zeros((groups, width // HEAD, rows), jnp.float32),
    )
    return lax.fori_loop(0, width // (2 * HEAD), step, start_state)


def plain_attend_back(query, keys, values, allowed, logsum, grad_mixed):
    groups, rows, width = query.shape
    length = keys.shape[1]
    scale = HEAD ** (-0.5)

    def step(index, carry):
        grad_query, grad_keys, grad_values = carry
        start = index * 2 * HEAD
        scores = pair_scores(query, keys, allowed, start)
        kept = lax.dynamic_slice_in_dim(logsum, index * 2, 2, 1)
        probs = jnp.exp(scores - kept[..., None])
        upstream = head_pair(grad_mixed, start)
        grad_probs = jnp.einsum(
            "sqhd,skhd->shqk",
            upstream,
            head_pair(values, start),
            preferred_element_type=jnp.float32,
        )
        grad_scores = (
            probs * (grad_probs - jnp.sum(probs * grad_probs, axis=-1, keepdims=True))
        ).astype(jnp.bfloat16)
        part_query = (
            jnp.einsum(
                "shqk,skhd->sqhd",
                grad_scores,
                head_pair(keys, start),
                preferred_element_type=jnp.float32,
            )
            * scale
        )
        part_keys = (
            jnp.einsum(
                "shqk,sqhd->skhd",
                grad_scores,
                head_pair(query, start),
                preferred_element_type=jnp.float32,
            )
            * scale
        )
        part_values = jnp.einsum(
            "shqk,sqhd->skhd",
            probs.astype(jnp.bfloat16),
            upstream,
            preferred_element_type=jnp.float32,
        )
        grad_query = lax.dynamic_update_slice_in_dim(
            grad_query, part_query.reshape(groups, rows, 2 * HEAD), start, 2
        )
        grad_keys = lax.dynamic_update_slice_in_dim(
            grad_keys, part_keys.reshape(groups, length, 2 * HEAD), start, 2
        )
        grad_values = lax.dynamic_update_slice_in_dim(
            grad_values, part_values.reshape(groups, length, 2 * HEAD), start, 2
        )
        return (grad_query, grad_keys, grad_values)

    start_state = (
        jnp.zeros((groups, rows, width), jnp.float32),
        jnp.zeros((groups, length, width), jnp.float32),
        jnp.zeros((groups, length, width), jnp.float32),
    )
    return lax.fori_loop(0, width // (2 * HEAD), step, start_state)


def on_device(
    layer_input,
    doc_ids,
    attn_gain,
    query_weight,
    key_weight,
    value_weight,
    out_weight,
    mlp_gain,
    gate_weight,
    up_weight,
    down_weight,
    out_grad,
):
    groups, rows, width = layer_input.shape
    length = doc_ids.shape[1]
    gathered = (
        lax.all_gather(attn_gain, ("dp", "ctx"), axis=0, tiled=True),
        lax.all_gather(query_weight, ("dp", "ctx"), axis=0, tiled=True),
        lax.all_gather(key_weight, ("dp", "ctx"), axis=0, tiled=True),
        lax.all_gather(value_weight, ("dp", "ctx"), axis=0, tiled=True),
        lax.all_gather(out_weight, ("dp", "ctx"), axis=0, tiled=True),
        lax.all_gather(mlp_gain, ("dp", "ctx"), axis=0, tiled=True),
        lax.all_gather(gate_weight, ("dp", "ctx"), axis=0, tiled=True),
        lax.all_gather(up_weight, ("dp", "ctx"), axis=0, tiled=True),
        lax.all_gather(down_weight, ("dp", "ctx"), axis=0, tiled=True),
    )
    gain_one, w_query, w_key, w_value, w_out, gain_two, w_gate, w_up, w_down = gathered
    first = lax.axis_index("ctx") * rows
    places = jnp.arange(length)
    own_ids = lax.dynamic_slice_in_dim(doc_ids, first, rows, 1)
    own_places = first + jnp.arange(rows)
    allowed = (own_ids[:, :, None] == doc_ids[:, None, :]) & (
        places[None, None, :] <= own_places[None, :, None]
    )
    inputs = layer_input.reshape(groups * rows, width).astype(jnp.float32)
    gain_attn = gain_one.astype(jnp.float32)
    normed_full, inverse_one = normalize(inputs, gain_attn)
    normed = normed_full.astype(jnp.bfloat16)
    query = plain_product(normed, w_query).astype(jnp.bfloat16).reshape(groups, rows, width)
    keys_own = plain_product(normed, w_key).astype(jnp.bfloat16).reshape(groups, rows, width)
    values_own = plain_product(normed, w_value).astype(jnp.bfloat16).reshape(groups, rows, width)
    keys, values = (
        lax.all_gather(keys_own, "ctx", axis=1, tiled=True),
        lax.all_gather(values_own, "ctx", axis=1, tiled=True),
    )
    attended, logsum = plain_attend(query, keys, values, allowed)
    attended_rows = attended.reshape(groups * rows, width)
    middle = inputs + plain_product(attended_rows, w_out)
    gain_mlp = gain_two.astype(jnp.float32)
    normed_two_full, inverse_two = normalize(middle, gain_mlp)
    normed_two = normed_two_full.astype(jnp.bfloat16)
    gate = plain_product(normed_two, w_gate)
    upward = plain_product(normed_two, w_up)
    sigma = jax.nn.sigmoid(gate)
    hidden = (gate * sigma * upward).astype(jnp.bfloat16)
    layer_output = (middle + plain_product(hidden, w_down)).astype(jnp.bfloat16)
    gathered_back = (
        lax.all_gather(attn_gain, ("dp", "ctx"), axis=0, tiled=True),
        lax.all_gather(query_weight, ("dp", "ctx"), axis=0, tiled=True),
        lax.all_gather(key_weight, ("dp", "ctx"), axis=0, tiled=True),
        lax.all_gather(value_weight, ("dp", "ctx"), axis=0, tiled=True),
        lax.all_gather(out_weight, ("dp", "ctx"), axis=0, tiled=True),
        lax.all_gather(mlp_gain, ("dp", "ctx"), axis=0, tiled=True),
        lax.all_gather(gate_weight, ("dp", "ctx"), axis=0, tiled=True),
        lax.all_gather(up_weight, ("dp", "ctx"), axis=0, tiled=True),
        lax.all_gather(down_weight, ("dp", "ctx"), axis=0, tiled=True),
    )
    gain_one, w_query, w_key, w_value, w_out, gain_two, w_gate, w_up, w_down = gathered_back
    upstream = out_grad.reshape(groups * rows, width)
    down_grad = plain_product_left(hidden, upstream)
    grad_hidden = plain_product_right(upstream, w_down)
    grad_gate = (grad_hidden * upward * sigma * (1.0 + gate * (1.0 - sigma))).astype(jnp.bfloat16)
    grad_up = (grad_hidden * gate * sigma).astype(jnp.bfloat16)
    gate_grad = plain_product_left(normed_two, grad_gate)
    up_grad = plain_product_left(normed_two, grad_up)
    grad_normed_two = plain_product_right(grad_gate, w_gate) + plain_product_right(grad_up, w_up)
    grad_middle, mlp_gain_grad = plain_norm_back(
        middle, inverse_two, gain_two.astype(jnp.float32), grad_normed_two
    )
    grad_middle = grad_middle + upstream.astype(jnp.float32)
    grad_branch = grad_middle.astype(jnp.bfloat16)
    out_proj_grad = plain_product_left(attended_rows, grad_branch)
    grad_attended = (
        plain_product_right(grad_branch, w_out).astype(jnp.bfloat16).reshape(groups, rows, width)
    )
    grad_query, grad_keys_all, grad_values_all = plain_attend_back(
        query, keys, values, allowed, logsum, grad_attended
    )
    grad_keys, grad_values = (
        lax.psum_scatter(
            grad_keys_all.astype(jnp.bfloat16), "ctx", scatter_dimension=1, tiled=True
        ).astype(jnp.float32),
        lax.psum_scatter(
            grad_values_all.astype(jnp.bfloat16), "ctx", scatter_dimension=1, tiled=True
        ).astype(jnp.float32),
    )
    grad_query = grad_query.astype(jnp.bfloat16).reshape(groups * rows, width)
    grad_keys = grad_keys.astype(jnp.bfloat16).reshape(groups * rows, width)
    grad_values = grad_values.astype(jnp.bfloat16).reshape(groups * rows, width)
    query_grad = plain_product_left(normed, grad_query)
    key_grad = plain_product_left(normed, grad_keys)
    value_grad = plain_product_left(normed, grad_values)
    grad_normed = (
        plain_product_right(grad_query, w_query)
        + plain_product_right(grad_keys, w_key)
        + plain_product_right(grad_values, w_value)
    )
    grad_inputs, attn_gain_grad = plain_norm_back(
        inputs, inverse_one, gain_one.astype(jnp.float32), grad_normed
    )
    input_grad = (grad_middle + grad_inputs).reshape(groups, rows, width)
    shares = (
        lax.psum_scatter(attn_gain_grad, ("dp", "ctx"), scatter_dimension=0, tiled=True),
        lax.psum_scatter(query_grad, ("dp", "ctx"), scatter_dimension=0, tiled=True),
        lax.psum_scatter(key_grad, ("dp", "ctx"), scatter_dimension=0, tiled=True),
        lax.psum_scatter(value_grad, ("dp", "ctx"), scatter_dimension=0, tiled=True),
        lax.psum_scatter(out_proj_grad, ("dp", "ctx"), scatter_dimension=0, tiled=True),
        lax.psum_scatter(mlp_gain_grad, ("dp", "ctx"), scatter_dimension=0, tiled=True),
        lax.psum_scatter(gate_grad, ("dp", "ctx"), scatter_dimension=0, tiled=True),
        lax.psum_scatter(up_grad, ("dp", "ctx"), scatter_dimension=0, tiled=True),
        lax.psum_scatter(down_grad, ("dp", "ctx"), scatter_dimension=0, tiled=True),
    )
    return (
        layer_output.reshape(groups, rows, width),
        input_grad,
        shares[0],
        shares[1],
        shares[2],
        shares[3],
        shares[4],
        shares[5],
        shares[6],
        shares[7],
        shares[8],
    )


def solution(mesh):
    placed = (
        P("dp", "ctx", None),
        P("dp", None),
        P(("dp", "ctx")),
        P(("dp", "ctx"), None),
        P(("dp", "ctx"), None),
        P(("dp", "ctx"), None),
        P(("dp", "ctx"), None),
        P(("dp", "ctx")),
        P(("dp", "ctx"), None),
        P(("dp", "ctx"), None),
        P(("dp", "ctx"), None),
        P("dp", "ctx", None),
    )
    fits = mesh.shape["dp"] == 4 and mesh.shape["ctx"] == 8
    body = grouped if fits else on_device
    return jax.shard_map(
        body,
        mesh=mesh,
        in_specs=placed,
        out_specs=(
            P("dp", "ctx", None),
            P("dp", "ctx", None),
            P(("dp", "ctx")),
            P(("dp", "ctx"), None),
            P(("dp", "ctx"), None),
            P(("dp", "ctx"), None),
            P(("dp", "ctx"), None),
            P(("dp", "ctx")),
            P(("dp", "ctx"), None),
            P(("dp", "ctx"), None),
            P(("dp", "ctx"), None),
        ),
        check_vma=False,
    )
```

```python
import functools

import jax
import jax.numpy as jnp
from jax import lax
from jax.experimental import pallas as pl
from jax.experimental.pallas import tpu as pltpu
from jax.sharding import PartitionSpec as P

HEAD = 64


EPS = 1e-05
MESH = pl.DeviceIdType.MESH
F32 = jnp.float32
BF16 = jnp.bfloat16
LOG2E = 1.4426950408889634
ANY = pl.BlockSpec(memory_space=pl.ANY)
VMEM = pl.BlockSpec(memory_space=pltpu.VMEM)


class Wires:
    def __init__(self, send, recv):
        dp, ctx = lax.axis_index("dp"), lax.axis_index("ctx")
        self.x, self.y = ctx % 2, dp // 2
        self.zh, self.zb = ctx // 4, (ctx // 2) % 2
        self.v, self.k = (self.zb + self.zh) % 2, dp % 2
        self.send, self.recv = send, recv
        self.used = 0

    def slots(self, count):
        first = self.used
        self.used += count
        return first

    def at(self, v=None, y=None, zh=None, x=None, k=None):
        v = self.v if v is None else v
        y = self.y if y is None else y
        zh = self.zh if zh is None else zh
        x = self.x if x is None else x
        k = self.k if k is None else k
        return (2 * y + k, 4 * zh + 2 * ((v + zh) % 2) + x)

    def across(self):
        return self.at(x=1 - self.x)

    def core(self):
        return self.at(k=1 - self.k)

    def copy(self, source, target, device, slot, recv_slot=None):
        return pltpu.make_async_remote_copy(
            src_ref=source,
            dst_ref=target,
            send_sem=self.send.at[slot],
            recv_sem=self.recv.at[slot if recv_slot is None else recv_slot],
            device_id=device,
            device_id_type=MESH,
        )

    def greet(self):
        v, zh, zb, k = self.v, self.zh, self.zb, self.k
        barrier = pltpu.get_barrier_semaphore()

        def call(peer):
            pl.semaphore_signal(barrier, inc=1, device_id=peer, device_id_type=MESH)

        for peer in (
            self.across(), self.core(), self.at(x=1 - self.x, k=1 - k),
            self.at(v=1 - v), self.at(y=1 - self.y), self.at(zh=1 - zh),
        ):
            call(peer)
        count = 6
        for n in range(2):
            away = jnp.logical_not(every(v == n, zh == k, zb == k))
            pl.when(away)(lambda: call(self.at(v=n, zh=k, k=zb)))
            count = count + jnp.where(away, 1, 0)
            away = jnp.logical_not(every(zh == n, zb == k, zh == k))
            pl.when(away)(lambda: call(self.at(zh=n, v=(k + n) % 2, k=zh)))
            count = count + jnp.where(away, 1, 0)
        pl.semaphore_wait(barrier, count)


def every(*tests):
    all_of = tests[0]
    for test in tests[1:]:
        all_of = jnp.logical_and(all_of, test)
    return all_of


class Pairs:
    def __init__(self, wires, order):
        self.w, self.order = wires, order

    def place(self, z, a, b):
        w = self.w
        v, y = (a, b) if self.order == "vy" else (b, a)
        flip = lambda own, turn: 1 - own if turn else own
        return flip(w.v, v), flip(w.y, y), flip(w.zh, z)

    def partner(self, z, a, b):
        v, y, zh = self.place(z, a, b)
        return self.w.at(v=v, y=y, zh=zh)


class Spread(Pairs):
    SENDS = ((0, 0, 0), (0, 0, 0), (1, 0, 0), (0, 0, 0), (1, 0, 0), (0, 1, 0), (1, 1, 0))
    STEPS = ((1, 0, 0), (0, 1, 0), (0, 1, 0), (0, 0, 1), (0, 0, 1), (0, 0, 1), (0, 0, 1))

    def __init__(self, wires, order, block, own=None):
        super().__init__(wires, order)
        self.block, self.own = block, own
        self.first = wires.slots(7)

    def piece(self, n):
        ref = self.block(*self.place(*self.SENDS[n]))
        source = self.own if self.own is not None and not any(self.SENDS[n]) else ref
        return self.w.copy(source, ref, self.partner(*self.STEPS[n]), self.first + n)

    def landed(self, n):
        came = [i ^ j for i, j in zip(self.SENDS[n], self.STEPS[n])]
        ref = self.block(*self.place(*came))
        return self.w.copy(ref, ref, self.partner(*self.STEPS[n]), self.first + n)

    def start(self):
        self.start_z()
        self.start_rest()

    def start_z(self):
        self.piece(0).start()

    def start_rest(self):
        self.piece(1).start()
        self.piece(3).start()

    def got_first(self):
        self.landed(1).wait_recv()
        self.piece(5).start()

    def got_z(self):
        self.landed(0).wait_recv()
        self.piece(2).start()
        self.piece(4).start()

    def got_last(self):
        self.landed(2).wait_recv()
        self.piece(6).start()

    def arrive(self):
        for n in (3, 4, 5, 6):
            self.landed(n).wait_recv()

    def drain(self):
        for n in range(7):
            self.piece(n).wait_send()


class Share:
    def __init__(self, wires, block):
        self.w, self.block = wires, block
        self.first = wires.slots(3)

    def piece(self, i):
        w = self.w
        ref = self.block(w.x if i < 2 else 1 - w.x, w.k)
        return w.copy(ref, ref, w.across() if i == 0 else w.core(), self.first + i)

    def landed(self, i):
        w = self.w
        ref = self.block(*[(1 - w.x, w.k), (w.x, 1 - w.k), (1 - w.x, 1 - w.k)][i])
        return w.copy(ref, ref, w.core(), self.first + i)

    def start(self):
        self.piece(0).start()
        self.piece(1).start()

    def forward(self):
        self.landed(0).wait_recv()
        self.piece(2).start()

    def arrive(self):
        self.landed(1).wait_recv()
        self.landed(2).wait_recv()

    def drain(self):
        for i in range(3):
            self.piece(i).wait_send()


class Deal:
    def __init__(self, wires, outgoing, incoming):
        self.w, self.outgoing, self.incoming = wires, outgoing, incoming
        self.first = wires.slots(3)

    def mate(self, i):
        w = self.w
        return [(1 - w.x, w.k), (w.x, 1 - w.k), (1 - w.x, 1 - w.k)][i]

    def piece(self, i):
        w = self.w
        x, k = self.mate(i)
        return w.copy(
            self.outgoing(x, k), self.incoming(w.x, w.k), w.at(x=x, k=k), self.first + i
        )

    def landed(self, i):
        x, k = self.mate(i)
        ref = self.incoming(x, k)
        return self.w.copy(ref, ref, self.w.at(x=x, k=k), self.first + i)

    def start(self):
        for i in range(3):
            self.piece(i).start()

    def arrive(self):
        for i in range(3):
            self.landed(i).wait_recv()

    def drain(self):
        for i in range(3):
            self.piece(i).wait_send()


class Visit:
    def __init__(self, wires, home, full, local):
        self.w, self.home, self.full, self.local = wires, home, full, local
        self.first = wires.slots(2)
        w = wires
        self.own = [every(w.v == j, w.zh == w.k, w.zb == w.k) for j in range(2)]
        self.here = [every(w.zh == i, w.zb == w.k, w.zh == w.k) for i in range(2)]

    def piece(self, j):
        w = self.w
        return w.copy(
            self.home.at[j],
            self.full(w.zh, w.zb, w.x),
            w.at(v=j, zh=w.k, k=w.zb),
            self.first + j,
            self.first + w.zh,
        )

    def stay(self, j):
        w = self.w
        return pltpu.make_async_copy(self.home.at[j], self.full(w.zh, w.zb, w.x), self.local)

    def landed(self, i):
        w = self.w
        ref = self.full(i, w.k, w.x)
        return w.copy(ref, ref, w.core(), self.first + i)

    def start(self):
        for j in range(2):
            pl.when(self.own[j])(lambda: self.stay(j).start())
            pl.when(jnp.logical_not(self.own[j]))(lambda: self.piece(j).start())

    def arrive(self):
        for j in range(2):
            pl.when(self.own[j])(lambda: self.stay(j).wait())
        for i in range(2):
            pl.when(jnp.logical_not(self.here[i]))(lambda: self.landed(i).wait_recv())

    def drain(self):
        for j in range(2):
            pl.when(jnp.logical_not(self.own[j]))(lambda: self.piece(j).wait_send())


class Return:
    def __init__(self, wires, done, home, local):
        self.w, self.done, self.home, self.local = wires, done, home, local
        self.first = wires.slots(2)
        w = wires
        self.own = [every(w.zh == i, w.zb == w.k, w.k == w.zh) for i in range(2)]
        self.here = [every(w.v == j, w.zh == w.k, w.zb == w.k) for j in range(2)]

    def piece(self, i):
        w = self.w
        return w.copy(
            self.done(i),
            self.home.at[w.v],
            w.at(zh=i, v=(w.k + i) % 2, k=w.zh),
            self.first + i,
            self.first + w.v,
        )

    def stay(self, i):
        return pltpu.make_async_copy(self.done(i), self.home.at[self.w.v], self.local)

    def landed(self, j):
        ref = self.home.at[j]
        return self.w.copy(ref, ref, self.w.core(), self.first + j)

    def start(self, i):
        pl.when(self.own[i])(lambda: self.stay(i).start())
        pl.when(jnp.logical_not(self.own[i]))(lambda: self.piece(i).start())

    def arrive(self):
        for i in range(2):
            pl.when(self.own[i])(lambda: self.stay(i).wait())
        for j in range(2):
            pl.when(jnp.logical_not(self.here[j]))(lambda: self.landed(j).wait_recv())

    def drain(self):
        for i in range(2):
            pl.when(jnp.logical_not(self.own[i]))(lambda: self.piece(i).wait_send())


def shaped(*shape, dtype=BF16):
    return jax.ShapeDtypeStruct(shape, dtype)


def pack_rows(columns, shards, packed):
    for rank in range(4):
        at = 0
        for shard in shards:
            for start, width in columns(rank):
                packed[rank, :, at : at + width] = shard[:, start : start + width]
                at += width


def head_columns(rank):
    return [(256 * rank, 256)]


def hidden_columns(rank):
    x, k = rank // 2, rank % 2
    return [
        (128 * (16 * y + 8 * k + 4 * zh + 2 * (v ^ zh) + x), 128)
        for y in range(2)
        for zh in range(2)
        for v in range(2)
    ]


class Total:
    def __init__(self, wires, part, got_core, got_across):
        self.w, self.part, self.got_core, self.got_across = wires, part, got_core, got_across
        self.first = wires.slots(4)
        self.half = part.shape[2] // 2

    def core(self, i):
        w = self.w
        return w.copy(
            self.part.at[0, i], self.got_core.at[i], w.core(), self.first + i
        )

    def rows(self, v):
        return pl.ds(pl.multiple_of(self.half * v, self.half), self.half)

    def across(self, i):
        w = self.w
        return w.copy(
            self.part.at[1, i, self.rows(1 - w.x)],
            self.got_across.at[i],
            w.across(),
            self.first + 2 + i,
        )

    def give(self, i, value):
        self.part[0, i] = value.astype(BF16)
        self.core(i).start()

    def keep(self, i, value):
        self.core(i).wait_recv()
        self.part[1, i] = (value + self.got_core[i].astype(F32)).astype(BF16)

    def send(self, i):
        self.across(i).start()

    def take(self, i):
        self.across(i).wait_recv()
        own = self.part[1, i, self.rows(self.w.x)]
        return own.astype(F32) + self.got_across[i].astype(F32)

    def drain(self):
        for i in range(2):
            self.core(i).wait_send()
            self.across(i).wait_send()


class Parts:
    def __init__(self, copies):
        self.copies = copies

    def start(self):
        for copy in self.copies:
            copy.start()

    def wait_send(self):
        for copy in self.copies:
            copy.wait_send()

    def wait_recv(self):
        for copy in self.copies:
            copy.wait_recv()


class Fold(Pairs):
    def __init__(self, wires, order, whole, block, got_b, got_b_block, got_a, got_z):
        super().__init__(wires, order)
        self.whole, self.block = whole, block
        self.got_b, self.got_b_block, self.got_a, self.got_z = got_b, got_b_block, got_a, got_z
        self.first = wires.slots(5)

    def stage_b(self):
        w = self.w
        b = w.y if self.order == "vy" else w.v
        return Parts(
            [
                w.copy(source, target, self.partner(0, 0, 1), self.first + 4 * i)
                for i, (source, target) in enumerate(zip(self.whole(1 - b), self.got_b))
            ]
        )

    def stage_a(self, z):
        v, y, zh = self.place(z, 1, 0)
        return self.w.copy(
            self.block(v, y, zh), self.got_a.at[zh], self.partner(0, 1, 0), self.first + 1 + z,
            self.first + 1 + z,
        )

    def landed_a(self, z):
        v, y, zh = self.place(z, 0, 0)
        ref = self.got_a.at[zh]
        return self.w.copy(ref, ref, self.partner(0, 1, 0), self.first + 1 + z)

    def stage_z(self):
        ref = self.block(*self.place(1, 0, 0))
        return self.w.copy(ref, self.got_z, self.partner(1, 0, 0), self.first + 3)

    def two(self, z, a):
        v, y, zh = self.place(z, a, 0)
        own = self.block(v, y, zh)[...].astype(F32)
        return own + self.got_b_block(v if self.order == "vy" else y, zh)[...].astype(F32)

    def three(self, z):
        return self.two(z, 0) + self.got_a[self.place(z, 0, 0)[2]].astype(F32)

    def start(self):
        self.stage_b().start()

    def second(self):
        self.stage_b().wait_recv()
        for z in (1, 0):
            ref = self.block(*self.place(z, 1, 0))
            ref[...] = self.two(z, 1).astype(self.got_z.dtype)
            self.stage_a(z).start()

    def third(self):
        self.landed_a(1).wait_recv()
        ref = self.block(*self.place(1, 0, 0))
        ref[...] = self.three(1).astype(self.got_z.dtype)
        self.stage_z().start()

    def finish(self):
        self.landed_a(0).wait_recv()
        total = self.three(0)
        self.stage_z().wait_recv()
        return total + self.got_z[...].astype(F32)

    def drain(self):
        self.stage_b().wait_send()
        for z in range(2):
            self.stage_a(z).wait_send()
        self.stage_z().wait_send()


def dots(left, right, dims):
    return lax.dot_general(left, right, (dims, ((), ())), preferred_element_type=F32)


NN, NT, TN = ((1,), (0,)), ((1,), (1,)), ((0,), (0,))


def only_head(array, head):
    lane = lax.broadcasted_iota(jnp.int32, array.shape, 1)
    return jnp.where(lane // HEAD == head, array, jnp.zeros_like(array))


def inverse_size(rows):
    return lax.rsqrt(jnp.mean(rows * rows, axis=-1, keepdims=True) + EPS)


def norm_back(rows, gain, upstream):
    inverse = inverse_size(rows)
    normed = rows * inverse
    scaled = upstream * gain
    grad_rows = inverse * (scaled - normed * jnp.mean(scaled * normed, axis=-1, keepdims=True))
    return grad_rows, jnp.sum(upstream * normed, axis=0, keepdims=True)


SCRATCH = [
    ("rows_all", (2, 2, 2, 128, 1024), BF16),
    ("cots_all", (2, 2, 2, 128, 1024), BF16),
    ("ids_all", (2, 2, 1, 1024), jnp.int32),
    ("heads_all", (2, 2, 2, 2, 2, 32, 768), BF16),
    ("out_all", (2, 2, 2, 2, 2, 32, 1024), BF16),
    ("gate_all", (2, 2, 2, 2, 2, 32, 1024), BF16),
    ("up_all", (2, 2, 2, 2, 2, 32, 1024), BF16),
    ("down_all", (2, 2, 2, 128, 1024), BF16),
    ("gains_all", (2, 2, 2, 2, 2, 16, 128), BF16),
    ("heads_shards", (3, 32, 1024), BF16),
    ("wide_shards", (2, 32, 4096), BF16),
    ("heads_pack", (4, 32, 768), BF16),
    ("gate_pack", (4, 32, 1024), BF16),
    ("up_pack", (4, 32, 1024), BF16),
    ("normed", (1024, 1024), BF16),
    ("query", (1024, 256), BF16),
    ("keys", (1024, 256), BF16),
    ("values", (1024, 256), BF16),
    ("keys_turned", (256, 1024), BF16),
    ("values_turned", (256, 1024), BF16),
    ("mixed_turned", (256, 1024), BF16),
    ("mixed_all", (2, 2, 256, 1024), BF16),
    ("logsum", (4, 1, 1024), F32),
    ("gain_rows", (2, 1, 1024), F32),
    ("ids_row", (1, 1024), F32),
    ("ids_col", (1024, 128), F32),
    ("middle_keep", (2, 256, 1024), F32),
    ("normed_two", (1024, 1024), BF16),
    ("hidden", (1024, 1024), BF16),
    ("grad_gate", (1024, 1024), BF16),
    ("grad_up", (1024, 1024), BF16),
    ("part_norm", (2, 2, 256, 1024), BF16),
    ("core_out", (2, 256, 1024), BF16),
    ("core_norm", (2, 256, 1024), BF16),
    ("across_out", (2, 128, 1024), BF16),
    ("across_norm", (2, 128, 1024), BF16),
    ("branch", (2, 2, 2, 128, 1024), BF16),
    ("grad_keys", (1024, 256), F32),
    ("grad_values", (1024, 256), F32),
    ("heads_part", (2, 2, 2, 2, 2, 32, 768), BF16),
    ("out_part", (2, 2, 2, 32, 1024), BF16),
    ("gains_part", (2, 2, 2, 8, 128), F32),
    ("heads_b", (2, 2, 2, 2, 32, 768), BF16),
    ("heads_a", (2, 2, 2, 32, 768), BF16),
    ("heads_z", (2, 2, 32, 768), BF16),
    ("gate_b", (2, 2, 2, 2, 32, 1024), BF16),
    ("gate_a", (2, 2, 2, 32, 1024), BF16),
    ("gate_z", (2, 2, 32, 1024), BF16),
    ("up_b", (2, 2, 2, 2, 32, 1024), BF16),
    ("up_a", (2, 2, 2, 32, 1024), BF16),
    ("up_z", (2, 2, 32, 1024), BF16),
    ("down_b", (2, 2, 128, 1024), BF16),
    ("down_a", (2, 128, 1024), BF16),
    ("down_z", (128, 1024), BF16),
    ("out_b", (2, 2, 2, 32, 1024), BF16),
    ("out_a", (2, 2, 32, 1024), BF16),
    ("out_z", (2, 32, 1024), BF16),
    ("gains_b", (2, 2, 8, 128), F32),
    ("gains_a", (2, 8, 128), F32),
    ("gains_z", (8, 128), F32),
    ("gains_deal", (8, 128), F32),
    ("gains_dealt", (4, 8, 128), F32),
    ("out_deal", (32, 1024), BF16),
    ("out_home", (32, 1024), BF16),
    ("done_out", (2, 128, 1024), BF16),
]


def layer_body(
    rows, cots, ids, wq, wk, wv, wo, wg, wu, wd, gains,
    output, input_home, heads_dealt, o_out, gate_dealt, up_dealt, d_out, gain_out,
    *scratch,
):
    send, recv, local = scratch[-3:]
    m = type("Memory", (), dict(zip([name for name, _, _ in SCRATCH], scratch)))
    w = Wires(send, recv)
    v, y, zh, zb, x, k = w.v, w.y, w.zh, w.zb, w.x, w.k
    rank = 2 * x + k

    used = [0]

    def spare():
        used[0] += 1
        return local.at[used[0] - 1]

    def stay(source, target):
        copy = pltpu.make_async_copy(source, target, spare())
        copy.start()
        return copy

    shards = [stay(shard, m.heads_shards.at[i]) for i, shard in enumerate((wq, wk, wv))]
    shards += [stay(shard, m.wide_shards.at[i]) for i, shard in enumerate((wg, wu))]
    w.greet()

    def sequence_block(ref):
        return lambda zh, zb, x: ref.at[zh, zb, x]

    def deal_rows(packed, whole):
        return Deal(
            w,
            lambda x, k: packed.at[2 * x + k],
            lambda sx, sk: whole.at[y, sk, zh, zb, sx],
        )

    def group_rows(ref):
        return lambda v, y, zh: ref.at[y, :, zh, (v + zh) % 2]

    def own_rows(ref):
        return lambda v, y, zh: ref.at[y, k, zh, (v + zh) % 2, x]

    visit_rows = Visit(w, rows, sequence_block(m.rows_all), spare())
    visit_rows.start()
    for copy in shards:
        copy.wait()
    pack_rows(head_columns, [m.heads_shards.at[i] for i in range(3)], m.heads_pack)
    deal_heads = deal_rows(m.heads_pack, m.heads_all)
    deal_heads.start()
    spread_gains = Spread(w, "vy", own_rows(m.gains_all), gains)
    spread_gains.start()
    swap = w.copy(ids, m.ids_all.at[k], w.core(), w.slots(1))
    swap.start()
    spread_out = Spread(w, "vy", own_rows(m.out_all), wo)
    spread_out.start()
    pack_rows(hidden_columns, (m.wide_shards.at[0],), m.gate_pack)
    pack_rows(hidden_columns, (m.wide_shards.at[1],), m.up_pack)
    stays = [
        stay(m.heads_pack.at[rank], m.heads_all.at[y, k, zh, zb, x]),
        stay(m.gate_pack.at[rank], m.gate_all.at[y, k, zh, zb, x]),
        stay(m.up_pack.at[rank], m.up_all.at[y, k, zh, zb, x]),
        stay(wo, m.out_all.at[y, k, zh, zb, x]),
        stay(gains, m.gains_all.at[y, k, zh, zb, x]),
        stay(wd, m.down_all.at[y, zh, v]),
        stay(ids, m.ids_all.at[k]),
    ]
    deal_gate = deal_rows(m.gate_pack, m.gate_all)
    deal_up = deal_rows(m.up_pack, m.up_all)
    for copy in stays:
        copy.wait()
    deal_heads.arrive()
    spread_heads = Spread(w, "vy", group_rows(m.heads_all))
    spread_heads.start()
    spread_down = Spread(w, "vy", lambda v, y, zh: m.down_all.at[y, zh, v], wd)
    spread_down.start_rest()
    spread_gains.got_first()
    deal_gate.start()
    deal_up.start()
    visit_rows.arrive()
    share_rows = Share(w, lambda x, k: m.rows_all.at[:, k, x])
    share_rows.start()
    spread_gains.got_z()
    spread_heads.got_first()
    spread_out.got_first()
    spread_gains.got_last()
    deal_gate.arrive()
    spread_gate = Spread(w, "vy", group_rows(m.gate_all))
    spread_gate.start_rest()
    deal_up.arrive()
    spread_up = Spread(w, "yv", group_rows(m.up_all))
    spread_up.start_rest()
    spread_heads.got_z()
    spread_down.start_z()
    spread_gate.start_z()
    spread_up.start_z()
    spread_gains.arrive()
    share_gains = [Share(w, lambda x, k: m.gains_all.at[:, k, :, :, x])]
    for share in share_gains:
        share.start()
    share_rows.forward()
    swap.wait()
    m.ids_row[...] = m.ids_all[zh, v].astype(F32)
    for j in range(8):
        piece = slice(128 * j, 128 * j + 128)
        m.ids_col[piece, :] = jnp.broadcast_to(m.ids_row[:, piece], (128, 128)).T
    spread_out.got_z()
    spread_heads.got_last()
    for share in share_gains:
        share.forward()
    spread_down.got_first()
    share_rows.arrive()
    for share in share_gains:
        share.arrive()
    for j in range(8):
        four = [
            m.gains_all[j // 4, (j // 2) % 2, j % 2, i // 2, i % 2].astype(F32) for i in range(4)
        ]
        total = four[0] + four[1] + four[2] + four[3]
        for i in range(2):
            m.gain_rows[i, :, 128 * j : 128 * j + 128] = total[i : i + 1, :]

    def first_norm(b, _):
        block = m.rows_all[b // 2, b % 2].reshape(256, 1024).astype(F32)
        span = pl.ds(pl.multiple_of(256 * b, 256), 256)
        m.normed[span, :] = (block * inverse_size(block) * m.gain_rows[0]).astype(BF16)
        return 0

    lax.fori_loop(0, 4, first_norm, 0)
    spread_heads.arrive()
    heads = m.heads_all[...].reshape(1024, 768)
    for b in range(4):
        span = slice(256 * b, 256 * b + 256)
        made = dots(m.normed[span, :], heads, NN).astype(BF16)
        m.query[span, :], m.keys[span, :] = made[:, :256], made[:, 256:512]
        m.values[span, :] = made[:, 512:]
        m.keys_turned[:, span] = made[:, 256:512].T
        m.values_turned[:, span] = made[:, 512:].T
    spread_out.got_last()
    spread_gate.got_first()
    spread_up.got_first()

    def bias_of(b):
        start, count = 256 * b, 256 * b + 256
        column = m.ids_col[:count, :]
        same = jnp.concatenate([column, column], axis=1) == m.ids_row[:, start : start + 256]
        key = lax.broadcasted_iota(jnp.int32, (count, 256), 0)
        place = lax.broadcasted_iota(jnp.int32, (count, 256), 1) + start
        return jnp.where(jnp.logical_and(same, key <= place), 0.0, -1e30).astype(F32)

    def head_rows(h):
        return pl.ds(pl.multiple_of(h * HEAD, HEAD), HEAD)

    def rank_columns(x, k):
        return pl.ds(pl.multiple_of(256 * (2 * x + k), 256), 256)

    def mix(b):
        span, count = slice(256 * b, 256 * b + 256), 256 * b + 256
        bias = bias_of(b)

        def one(h, _):
            scores = dots(m.keys[:count, :], only_head(m.query[span, :], h), NT)
            scores = scores * (HEAD**-0.5 * LOG2E) + bias
            top = jnp.max(scores, axis=0, keepdims=True)
            lifted = jnp.exp2(scores - top)
            total = jnp.sum(lifted, axis=0, keepdims=True)
            probs = (lifted * (1.0 / total)).astype(BF16)
            mixed = dots(m.values_turned[head_rows(h), :count], probs, NN)
            m.mixed_turned[head_rows(h), span] = mixed.astype(BF16)
            m.logsum[h, :, span] = top + jnp.log2(total)
            return 0

        lax.fori_loop(0, 4, one, 0)
        m.mixed_all[b // 2, b % 2, :, rank_columns(x, k)] = m.mixed_turned[:, span].T

    def share_mixed(b):
        return Share(w, lambda x, k: m.mixed_all.at[b // 2, b % 2, :, rank_columns(x, k)])

    shares = [share_mixed(b) for b in range(4)]
    mix(0)
    shares[0].start()
    spread_down.got_z()
    mix(1)
    shares[1].start()
    visit_cots = Visit(w, cots, sequence_block(m.cots_all), spare())
    visit_cots.start()
    shares[0].forward()
    spread_out.arrive()
    share_out = [Share(w, lambda x, k: m.out_all.at[:, k, :, :, x])]
    for share in share_out:
        share.start()
    spread_gate.got_z()
    mix(2)
    shares[2].start()
    shares[1].forward()
    for share in share_out:
        share.forward()
    spread_up.got_z()
    spread_down.got_last()
    mix(3)
    shares[3].start()
    shares[2].forward()
    for share in share_out:
        share.arrive()

    for b in range(4):
        span = slice(256 * b, 256 * b + 256)
        if b == 2:
            shares[3].forward()
            spread_gate.got_last()
        shares[b].arrive()
        middle = m.rows_all[b // 2, b % 2].reshape(256, 1024).astype(F32)
        whole = m.out_all[...].reshape(1024, 1024)
        middle = middle + dots(m.mixed_all[b // 2, b % 2], whole, NN)
        m.normed_two[span, :] = (middle * inverse_size(middle) * m.gain_rows[1]).astype(BF16)

        @pl.when(k == b % 2)
        def _():
            m.middle_keep[b // 2] = middle

    visit_cots.arrive()
    share_cots = Share(w, lambda x, k: m.cots_all.at[:, k, x])
    share_cots.start()
    spread_up.got_last()
    share_cots.forward()
    for spread in (spread_gate, spread_up, spread_down):
        spread.arrive()
    share_cots.arrive()
    for share in shares:
        share.drain()
    total_out = Total(w, m.mixed_all, m.core_out, m.across_out)
    total_norm = Total(w, m.part_norm, m.core_norm, m.across_norm)

    def feed(i, part):
        span = pl.ds(pl.multiple_of(256 * (2 * i + part), 256), 256)
        upstream = m.cots_all[i, part].reshape(256, 1024)
        normed_two = m.normed_two[span, :]
        for n in range(4):
            columns = slice(256 * n, 256 * n + 256)
            gate_tile = m.gate_all[..., columns].reshape(1024, 256)
            up_tile = m.up_all[..., columns].reshape(1024, 256)
            down_tile = m.down_all[n // 2, n % 2].reshape(256, 1024)
            gate = dots(normed_two, gate_tile, NN)
            upward = dots(normed_two, up_tile, NN)
            grad_hidden = dots(upstream, down_tile, NT)
            sigma = 1.0 / (1.0 + jnp.exp(-gate))
            silu = gate * sigma
            m.hidden[span, columns] = (silu * upward).astype(BF16)
            m.grad_up[span, columns] = (grad_hidden * silu).astype(BF16)
            m.grad_gate[span, columns] = (
                grad_hidden * upward * (sigma + silu * (1.0 - sigma))
            ).astype(BF16)
        norm_part = dots(m.grad_gate[span, :], m.gate_all[...].reshape(1024, 1024), NT)
        norm_part = norm_part + dots(m.grad_up[span, :], m.up_all[...].reshape(1024, 1024), NT)
        return span, norm_part

    def out_of(span):
        return dots(m.hidden[span, :], m.down_all[...].reshape(1024, 1024), NN)

    def give(i, _):
        span, norm_part = feed(i, 1 - k)
        total_norm.give(i, norm_part)
        total_out.give(i, out_of(span))
        return 0

    def keep(i, _):
        span, norm_part = feed(i, k)
        total_norm.keep(i, norm_part)
        total_norm.send(i)
        total_out.keep(i, out_of(span))
        return 0

    lax.fori_loop(0, 2, give, 0)
    lax.fori_loop(0, 2, keep, 0)
    for spread in (spread_gate, spread_up, spread_down):
        spread.drain()

    def lanes(plane, half):
        return pl.ds(pl.multiple_of(512 * plane + 256 * half, 256), 256)

    def down_part(plane):
        def one(half, _):
            made = dots(m.hidden[:, lanes(plane, half)], m.cots_all[...].reshape(1024, 1024), TN)
            m.down_all[plane, half] = made.astype(BF16).reshape(2, 128, 1024)
            return 0

        lax.fori_loop(0, 2, one, 0)

    def wide_part(whole, right, plane):
        def one(half, _):
            made = dots(m.normed_two[:, lanes(plane, half)], right[...], TN).astype(BF16)
            whole[plane, half] = made.reshape(2, 2, 2, 32, 1024)
            return 0

        lax.fori_loop(0, 2, one, 0)

    def fold_plane(whole, got_b, got_a, got_z):
        return Fold(
            w, "vy", lambda y: [whole.at[y]], lambda v, y, zh: whole.at[y, :, zh, (v + zh) % 2],
            [got_b], lambda v, zh: got_b.at[:, zh, (v + zh) % 2], got_a, got_z,
        )

    def fold_side(whole, got_b, got_a, got_z):
        return Fold(
            w, "yv", lambda v: [whole.at[:, :, 0, v], whole.at[:, :, 1, 1 - v]],
            lambda v, y, zh: whole.at[y, :, zh, (v + zh) % 2],
            [got_b.at[0], got_b.at[1]], lambda y, zh: got_b.at[zh, y], got_a, got_z,
        )

    def fold_block(whole, got_b, got_a, got_z):
        return Fold(
            w, "vy", lambda y: [whole.at[y]], lambda v, y, zh: whole.at[y, zh, v],
            [got_b], lambda v, zh: got_b.at[zh, v], got_a, got_z,
        )

    fold_down = fold_block(m.down_all, m.down_b, m.down_a, m.down_z)
    fold_gate = fold_plane(m.gate_all, m.gate_b, m.gate_a, m.gate_z)
    fold_up = fold_side(m.up_all, m.up_b, m.up_a, m.up_z)
    fold_heads = fold_plane(m.heads_part, m.heads_b, m.heads_a, m.heads_z)
    fold_gains = fold_block(m.gains_part, m.gains_b, m.gains_a, m.gains_z)
    shares_branch = [Share(w, lambda x, k, i=i: m.branch.at[i, k, x]) for i in range(2)]
    own_half, other_half = total_norm.rows(x), total_norm.rows(1 - x)

    def back_two(i):
        grad, term = norm_back(m.middle_keep[i, own_half], m.gain_rows[1], total_norm.take(i))
        grad = grad + m.cots_all[i, k, x].astype(F32)
        m.middle_keep[i, other_half] = grad
        m.branch[i, k, x] = grad.astype(BF16)
        shares_branch[i].start()
        return term

    gain_sum = back_two(0)
    down_part(1 - y)
    fold_down.start()
    wide_part(m.up_all, m.grad_up, 0)
    wide_part(m.up_all, m.grad_up, 1)
    fold_up.start()
    gain_sum = gain_sum + back_two(1)
    wide_part(m.gate_all, m.grad_gate, 1 - y)
    fold_gate.start()
    for i in range(2):
        total_out.send(i)

    def gain_rows_part(row, total):
        for plane in range(2):
            for place in range(4):
                for half in range(2):
                    at = 512 * plane + 256 * half + 128 * (place // 2)
                    row_at = slice(2 * row + half, 2 * row + half + 1)
                    m.gains_part[plane, place // 2, place % 2, row_at, :] = total[:, at : at + 128]

    m.gains_part[...] = jnp.zeros_like(m.gains_part)
    gain_rows_part(1, gain_sum)
    shares_branch[0].forward()
    down_part(y)
    shares_branch[1].forward()
    wide_part(m.gate_all, m.grad_gate, y)

    grad_mixed, grad_mixed_turned = m.grad_up.at[:, :256], m.hidden.at[:256]
    grad_heads = m.grad_gate.at[:, :768]
    out_own = m.out_all[x, k].reshape(256, 1024)
    for b in range(4):
        if b % 2 == 0:
            shares_branch[b // 2].arrive()
        if b == 2:
            fold_down.second()
        span = slice(256 * b, 256 * b + 256)
        made = dots(m.branch[b // 2, b % 2].reshape(256, 1024), out_own, NT).astype(BF16)
        grad_mixed[span, :] = made
        grad_mixed_turned[:, span] = made.T
    m.out_part[...] = (
        dots(m.mixed_turned[...], m.branch[...].reshape(1024, 1024), NN)
        .astype(BF16)
        .reshape(2, 2, 2, 32, 1024)
    )
    base = w.slots(6)
    owner = y == x
    out_across = w.copy(m.out_part, m.out_b, w.at(y=1 - y), base)
    pl.when(jnp.logical_not(owner))(lambda: out_across.start())
    m.grad_keys[...] = jnp.zeros_like(m.grad_keys)
    m.grad_values[...] = jnp.zeros_like(m.grad_values)

    def unmix(b):
        span, count = slice(256 * b, 256 * b + 256), 256 * b + 256
        bias = bias_of(b)

        def one(h, _):
            query, upstream = only_head(m.query[span, :], h), only_head(grad_mixed[span, :], h)
            scores = dots(m.keys[:count, :], query, NT)
            scores = scores * (HEAD**-0.5 * LOG2E) + bias
            probs = jnp.exp2(scores - m.logsum[h, :, span])
            grad_probs = dots(m.values[:count, :], upstream, NT)
            centre = jnp.sum(
                grad_mixed_turned[head_rows(h), span].astype(F32)
                * m.mixed_turned[head_rows(h), span].astype(F32),
                axis=0,
                keepdims=True,
            )
            grad_scores = (probs * (grad_probs - centre)).astype(BF16)
            turned = dots(m.keys_turned[head_rows(h), :count], grad_scores, NN)
            grad_mixed_turned[head_rows(h), span] = (turned * HEAD**-0.5).astype(BF16)
            m.grad_keys[:count, :] += dots(grad_scores, query, NN)
            m.grad_values[:count, :] += dots(probs.astype(BF16), upstream, NN)
            return 0

        lax.fori_loop(0, 4, one, 0)
        grad_heads[span, :256] = grad_mixed_turned[:, span].T

    for i in range(2):
        m.done_out[i] = (m.middle_keep[i, own_half] + total_out.take(i)).astype(BF16)
    return_out = Return(w, lambda i: m.done_out.at[i], output, spare())
    for i in range(2):
        return_out.start(i)
    unmix(0)
    fold_up.second()
    unmix(1)
    fold_down.third()
    fold_gate.second()
    unmix(2)
    fold_up.third()
    unmix(3)
    fold_gate.third()
    grad_heads[:, 256:512] = (m.grad_keys[...] * HEAD**-0.5).astype(BF16)
    grad_heads[:, 512:] = m.grad_values[...].astype(BF16)

    total_norm.drain()
    total_first = Total(w, m.part_norm, m.core_norm, m.across_norm)

    def first_part(i, part):
        span = pl.ds(pl.multiple_of(256 * (2 * i + part), 256), 256)
        return dots(grad_heads[span, :], m.heads_all[...].reshape(1024, 768), NT)

    for i in range(2):
        total_first.give(i, first_part(i, 1 - k))
    for plane in range(2):
        for half in range(2):
            made = dots(m.normed[:, lanes(plane, half)], grad_heads[...], TN)
            m.heads_part[plane, half] = made.astype(BF16).reshape(2, 2, 2, 32, 768)
    fold_heads.start()
    for i in range(2):
        total_first.keep(i, first_part(i, k))
        total_first.send(i)
    gain_sum = jnp.zeros((1, 1024), F32)

    def done_in(i):
        return m.normed_two.at[pl.ds(128 * i, 128)]

    return_in = Return(w, done_in, input_home, spare())
    for i in range(2):
        grad, term = norm_back(
            m.rows_all[i, k, x].astype(F32), m.gain_rows[0], total_first.take(i)
        )
        gain_sum = gain_sum + term
        done_in(i)[...] = (m.middle_keep[i, other_half] + grad).astype(BF16)
        return_in.start(i)
    gain_rows_part(0, gain_sum)
    fold_gains.start()


    def out_side(z):
        side = 1 - zh if z else zh
        return w.copy(
            m.out_part.at[side, (1 - v + side) % 2], m.out_a.at[side], w.at(v=1 - v), base + 1 + z
        )

    def out_side_landed(z):
        ref = m.out_a.at[1 - zh if z else zh]
        return w.copy(ref, ref, w.at(v=1 - v), base + 1 + z)

    def out_two(side, v):
        at = (v + side) % 2
        return m.out_part[side, at].astype(F32) + m.out_b[side, at].astype(F32)

    far = (v + 1 - zh) % 2
    out_half = w.copy(m.out_part.at[1 - zh, far], m.out_z, w.at(zh=1 - zh), base + 3)
    out_last = w.copy(m.out_deal, m.out_home, w.across(), base + 4)

    @pl.when(owner)
    def _():
        out_across.wait_recv()
        for side in (1, 0):
            at = 1 - zh if side else zh
            m.out_part[at, (1 - v + at) % 2] = out_two(at, 1 - v).astype(BF16)
            out_side(side).start()

    fold_heads.second()
    fold_gains.second()

    @pl.when(owner)
    def _():
        out_side_landed(1).wait_recv()
        m.out_part[1 - zh, far] = (
            out_two(1 - zh, v) + m.out_a[1 - zh].astype(F32)
        ).astype(BF16)
        out_half.start()

    d_out[...] = fold_down.finish()

    def deal_grads(packed, dealt):
        return Deal(
            w, lambda x, k: packed.at[2 * k + x], lambda x, k: dealt.at[2 * x + k]
        )

    deal_up.drain()
    deal_gate.drain()
    deal_heads.drain()
    m.up_pack[...] = fold_up.finish().astype(BF16).reshape(4, 32, 1024)
    deal_up_grad = deal_grads(m.up_pack, up_dealt)
    deal_up_grad.start()
    fold_heads.third()
    fold_gains.third()
    m.gate_pack[...] = fold_gate.finish().astype(BF16).reshape(4, 32, 1024)
    deal_gate_grad = deal_grads(m.gate_pack, gate_dealt)
    deal_gate_grad.start()

    @pl.when(owner)
    def _():
        out_side_landed(0).wait_recv()
        out_half.wait_recv()
        out_total = out_two(zh, v) + m.out_a[zh].astype(F32) + m.out_z[...].astype(F32)
        first, second = out_total[0], out_total[1]
        m.out_deal[...] = jnp.where(x == 0, second, first).astype(BF16)
        out_last.start()
        o_out[...] = jnp.where(x == 0, first, second)

    return_in.arrive()
    m.gains_deal[...] = fold_gains.finish()
    m.gains_dealt[rank] = m.gains_deal[...]
    deal_gains = Deal(w, lambda x, k: m.gains_deal, lambda x, k: m.gains_dealt.at[2 * x + k])
    deal_gains.start()
    m.heads_pack[...] = fold_heads.finish().astype(BF16).reshape(4, 32, 768)
    deal_heads_grad = deal_grads(m.heads_pack, heads_dealt)
    deal_heads_grad.start()
    up_dealt[rank] = m.up_pack[2 * k + x]
    gate_dealt[rank] = m.gate_pack[2 * k + x]
    heads_dealt[rank] = m.heads_pack[2 * k + x]
    deal_up_grad.arrive()
    deal_gate_grad.arrive()
    deal_gains.arrive()
    gain_out[...] = m.gains_dealt[0] + m.gains_dealt[1] + m.gains_dealt[2] + m.gains_dealt[3]
    deal_heads_grad.arrive()

    @pl.when(jnp.logical_not(owner))
    def _():
        out_last.wait_recv()
        o_out[...] = m.out_home[...].astype(F32)

    return_out.arrive()
    for part in [
        visit_rows, visit_cots, spread_gains, spread_heads, spread_out, share_rows, share_cots,
        total_out, total_first, fold_down, fold_gate, fold_up, fold_heads,
        fold_gains, return_out, return_in, deal_up_grad, deal_gate_grad, deal_heads_grad,
        deal_gains,
    ] + share_gains + share_out + shares_branch:
        part.drain()

    @pl.when(owner)
    def _():
        for side in range(2):
            out_side(side).wait_send()
        out_half.wait_send()
        out_last.wait_send()

    pl.when(jnp.logical_not(owner))(lambda: out_across.wait_send())


def finish_body(
    output, input_home, heads, out, gate, up, down,
    output_to, input_to, q_to, k_to, v_to, out_to, gate_to, up_to, down_to,
):
    for dealt, target in ((gate, gate_to), (up, up_to)):
        for r in range(4):
            for j, (start, width) in enumerate(hidden_columns(r)):
                piece = dealt[r, :, 128 * j : 128 * j + width]
                target[:, start : start + width] = piece.astype(F32)
    for r in range(4):
        for j, target in enumerate((q_to, k_to, v_to)):
            piece = heads[r, :, 256 * j : 256 * j + 256]
            target[:, 256 * r : 256 * r + 256] = piece.astype(F32)
    output_to[...] = output[...]
    input_to[...] = input_home[...].astype(F32)
    out_to[...] = out[...]
    down_to[...] = down[...]


def grouped(
    layer_input, doc_ids, attn_gain, query_weight, key_weight, value_weight, out_weight,
    mlp_gain, gate_weight, up_weight, down_weight, out_grad,
):
    dp, ctx = lax.axis_index("dp"), lax.axis_index("ctx")
    k = dp % 2
    piece = attn_gain.shape[0]
    lane = piece * (ctx % 4)
    gains = jnp.zeros((16, 128), BF16)
    gains = lax.dynamic_update_slice(gains, jnp.stack([attn_gain, mlp_gain]), (0, lane))
    d, f = layer_input.shape[2], gate_weight.shape[1]
    outs = (
        shaped(*layer_input.shape),
        shaped(*layer_input.shape),
        shaped(4, piece, 3 * d // 4),
        shaped(piece, d, dtype=F32),
        shaped(4, piece, f // 4),
        shaped(4, piece, f // 4),
        shaped(*down_weight.shape, dtype=F32),
        shaped(8, 128, dtype=F32),
    )
    finals = (
        shaped(*layer_input.shape),
        shaped(*layer_input.shape, dtype=F32),
        shaped(piece, d, dtype=F32),
        shaped(piece, d, dtype=F32),
        shaped(piece, d, dtype=F32),
        shaped(piece, d, dtype=F32),
        shaped(piece, f, dtype=F32),
        shaped(piece, f, dtype=F32),
        shaped(*down_weight.shape, dtype=F32),
    )
    rooms = [pltpu.VMEM(shape, dtype) for _, shape, dtype in SCRATCH]
    made = pl.pallas_call(
        layer_body,
        name="layer",
        out_shape=outs,
        in_specs=[ANY] * 11,
        out_specs=(ANY, ANY) + (VMEM,) * (len(outs) - 2),
        scratch_shapes=rooms
        + [
            pltpu.SemaphoreType.DMA((192,)),
            pltpu.SemaphoreType.DMA((192,)),
            pltpu.SemaphoreType.DMA((24,)),
        ],
        compiler_params=pltpu.CompilerParams(
            collective_id=0, has_side_effects=True, vmem_limit_bytes=61 << 20
        ),
    )(
        layer_input, out_grad, doc_ids.reshape(2, 1, -1), query_weight, key_weight, value_weight,
        out_weight, gate_weight, up_weight, down_weight, gains,
    )
    gain = made[-1]
    output, input_grad, q, k_, v, o, g, u, down = pl.pallas_call(
        finish_body,
        name="finish",
        out_shape=finals,
        in_specs=[VMEM] * 7,
        out_specs=(VMEM,) * len(finals),
        compiler_params=pltpu.CompilerParams(vmem_limit_bytes=58 << 20),
    )(*made[:-1])

    def gain_of(row):
        return lax.dynamic_slice(gain, (row + k, lane), (1, piece)).reshape(piece)

    return (output, input_grad, gain_of(0), q, k_, v, o, gain_of(2), g, u, down)


def plain_product(left, right):
    return jnp.dot(left, right, preferred_element_type=jnp.float32)


def plain_product_left(left, right):
    return lax.dot_general(
        left, right, (((0,), (0,)), ((), ())), preferred_element_type=jnp.float32
    )


def plain_product_right(left, right):
    return lax.dot_general(
        left, right, (((1,), (1,)), ((), ())), preferred_element_type=jnp.float32
    )


def normalize(rows, gain):
    inverse = lax.rsqrt(jnp.mean(rows * rows, axis=-1, keepdims=True) + EPS)
    return (rows * inverse * gain, inverse)


def plain_norm_back(rows, inverse, gain, upstream):
    normed = rows * inverse
    scaled = upstream * gain
    grad_rows = inverse * (scaled - normed * jnp.mean(scaled * normed, axis=-1, keepdims=True))
    return (grad_rows, jnp.sum(upstream * normed, axis=0))


def head_pair(array, start):
    piece = lax.dynamic_slice_in_dim(array, start, 2 * HEAD, 2)
    return piece.reshape(array.shape[0], array.shape[1], 2, HEAD)


def pair_scores(query, keys, allowed, start):
    scores = jnp.einsum(
        "sqhd,skhd->shqk",
        head_pair(query, start),
        head_pair(keys, start),
        preferred_element_type=jnp.float32,
    ) * HEAD ** (-0.5)
    return jnp.where(allowed[:, None], scores, -1e30)


def plain_attend(query, keys, values, allowed):
    groups, rows, width = query.shape

    def step(index, carry):
        mixed_all, logsum = carry
        start = index * 2 * HEAD
        scores = pair_scores(query, keys, allowed, start)
        top = jnp.max(scores, axis=-1, keepdims=True)
        lifted = jnp.exp(scores - top)
        total = jnp.sum(lifted, axis=-1, keepdims=True)
        probs = (lifted / total).astype(jnp.bfloat16)
        mixed = jnp.einsum(
            "shqk,skhd->sqhd", probs, head_pair(values, start), preferred_element_type=jnp.float32
        )
        mixed_all = lax.dynamic_update_slice_in_dim(
            mixed_all, mixed.reshape(groups, rows, 2 * HEAD).astype(jnp.bfloat16), start, 2
        )
        logsum = lax.dynamic_update_slice_in_dim(
            logsum, (top + jnp.log(total))[..., 0], index * 2, 1
        )
        return (mixed_all, logsum)

    start_state = (
        jnp.zeros((groups, rows, width), jnp.bfloat16),
        jnp.zeros((groups, width // HEAD, rows), jnp.float32),
    )
    return lax.fori_loop(0, width // (2 * HEAD), step, start_state)


def plain_attend_back(query, keys, values, allowed, logsum, grad_mixed):
    groups, rows, width = query.shape
    length = keys.shape[1]
    scale = HEAD ** (-0.5)

    def step(index, carry):
        grad_query, grad_keys, grad_values = carry
        start = index * 2 * HEAD
        scores = pair_scores(query, keys, allowed, start)
        kept = lax.dynamic_slice_in_dim(logsum, index * 2, 2, 1)
        probs = jnp.exp(scores - kept[..., None])
        upstream = head_pair(grad_mixed, start)
        grad_probs = jnp.einsum(
            "sqhd,skhd->shqk",
            upstream,
            head_pair(values, start),
            preferred_element_type=jnp.float32,
        )
        grad_scores = (
            probs * (grad_probs - jnp.sum(probs * grad_probs, axis=-1, keepdims=True))
        ).astype(jnp.bfloat16)
        part_query = (
            jnp.einsum(
                "shqk,skhd->sqhd",
                grad_scores,
                head_pair(keys, start),
                preferred_element_type=jnp.float32,
            )
            * scale
        )
        part_keys = (
            jnp.einsum(
                "shqk,sqhd->skhd",
                grad_scores,
                head_pair(query, start),
                preferred_element_type=jnp.float32,
            )
            * scale
        )
        part_values = jnp.einsum(
            "shqk,sqhd->skhd",
            probs.astype(jnp.bfloat16),
            upstream,
            preferred_element_type=jnp.float32,
        )
        grad_query = lax.dynamic_update_slice_in_dim(
            grad_query, part_query.reshape(groups, rows, 2 * HEAD), start, 2
        )
        grad_keys = lax.dynamic_update_slice_in_dim(
            grad_keys, part_keys.reshape(groups, length, 2 * HEAD), start, 2
        )
        grad_values = lax.dynamic_update_slice_in_dim(
            grad_values, part_values.reshape(groups, length, 2 * HEAD), start, 2
        )
        return (grad_query, grad_keys, grad_values)

    start_state = (
        jnp.zeros((groups, rows, width), jnp.float32),
        jnp.zeros((groups, length, width), jnp.float32),
        jnp.zeros((groups, length, width), jnp.float32),
    )
    return lax.fori_loop(0, width // (2 * HEAD), step, start_state)


def on_device(
    layer_input,
    doc_ids,
    attn_gain,
    query_weight,
    key_weight,
    value_weight,
    out_weight,
    mlp_gain,
    gate_weight,
    up_weight,
    down_weight,
    out_grad,
):
    groups, rows, width = layer_input.shape
    length = doc_ids.shape[1]
    gathered = (
        lax.all_gather(attn_gain, ("dp", "ctx"), axis=0, tiled=True),
        lax.all_gather(query_weight, ("dp", "ctx"), axis=0, tiled=True),
        lax.all_gather(key_weight, ("dp", "ctx"), axis=0, tiled=True),
        lax.all_gather(value_weight, ("dp", "ctx"), axis=0, tiled=True),
        lax.all_gather(out_weight, ("dp", "ctx"), axis=0, tiled=True),
        lax.all_gather(mlp_gain, ("dp", "ctx"), axis=0, tiled=True),
        lax.all_gather(gate_weight, ("dp", "ctx"), axis=0, tiled=True),
        lax.all_gather(up_weight, ("dp", "ctx"), axis=0, tiled=True),
        lax.all_gather(down_weight, ("dp", "ctx"), axis=0, tiled=True),
    )
    gain_one, w_query, w_key, w_value, w_out, gain_two, w_gate, w_up, w_down = gathered
    first = lax.axis_index("ctx") * rows
    places = jnp.arange(length)
    own_ids = lax.dynamic_slice_in_dim(doc_ids, first, rows, 1)
    own_places = first + jnp.arange(rows)
    allowed = (own_ids[:, :, None] == doc_ids[:, None, :]) & (
        places[None, None, :] <= own_places[None, :, None]
    )
    inputs = layer_input.reshape(groups * rows, width).astype(jnp.float32)
    gain_attn = gain_one.astype(jnp.float32)
    normed_full, inverse_one = normalize(inputs, gain_attn)
    normed = normed_full.astype(jnp.bfloat16)
    query = plain_product(normed, w_query).astype(jnp.bfloat16).reshape(groups, rows, width)
    keys_own = plain_product(normed, w_key).astype(jnp.bfloat16).reshape(groups, rows, width)
    values_own = plain_product(normed, w_value).astype(jnp.bfloat16).reshape(groups, rows, width)
    keys, values = (
        lax.all_gather(keys_own, "ctx", axis=1, tiled=True),
        lax.all_gather(values_own, "ctx", axis=1, tiled=True),
    )
    attended, logsum = plain_attend(query, keys, values, allowed)
    attended_rows = attended.reshape(groups * rows, width)
    middle = inputs + plain_product(attended_rows, w_out)
    gain_mlp = gain_two.astype(jnp.float32)
    normed_two_full, inverse_two = normalize(middle, gain_mlp)
    normed_two = normed_two_full.astype(jnp.bfloat16)
    gate = plain_product(normed_two, w_gate)
    upward = plain_product(normed_two, w_up)
    sigma = jax.nn.sigmoid(gate)
    hidden = (gate * sigma * upward).astype(jnp.bfloat16)
    layer_output = (middle + plain_product(hidden, w_down)).astype(jnp.bfloat16)
    gathered_back = (
        lax.all_gather(attn_gain, ("dp", "ctx"), axis=0, tiled=True),
        lax.all_gather(query_weight, ("dp", "ctx"), axis=0, tiled=True),
        lax.all_gather(key_weight, ("dp", "ctx"), axis=0, tiled=True),
        lax.all_gather(value_weight, ("dp", "ctx"), axis=0, tiled=True),
        lax.all_gather(out_weight, ("dp", "ctx"), axis=0, tiled=True),
        lax.all_gather(mlp_gain, ("dp", "ctx"), axis=0, tiled=True),
        lax.all_gather(gate_weight, ("dp", "ctx"), axis=0, tiled=True),
        lax.all_gather(up_weight, ("dp", "ctx"), axis=0, tiled=True),
        lax.all_gather(down_weight, ("dp", "ctx"), axis=0, tiled=True),
    )
    gain_one, w_query, w_key, w_value, w_out, gain_two, w_gate, w_up, w_down = gathered_back
    upstream = out_grad.reshape(groups * rows, width)
    down_grad = plain_product_left(hidden, upstream)
    grad_hidden = plain_product_right(upstream, w_down)
    grad_gate = (grad_hidden * upward * sigma * (1.0 + gate * (1.0 - sigma))).astype(jnp.bfloat16)
    grad_up = (grad_hidden * gate * sigma).astype(jnp.bfloat16)
    gate_grad = plain_product_left(normed_two, grad_gate)
    up_grad = plain_product_left(normed_two, grad_up)
    grad_normed_two = plain_product_right(grad_gate, w_gate) + plain_product_right(grad_up, w_up)
    grad_middle, mlp_gain_grad = plain_norm_back(
        middle, inverse_two, gain_two.astype(jnp.float32), grad_normed_two
    )
    grad_middle = grad_middle + upstream.astype(jnp.float32)
    grad_branch = grad_middle.astype(jnp.bfloat16)
    out_proj_grad = plain_product_left(attended_rows, grad_branch)
    grad_attended = (
        plain_product_right(grad_branch, w_out).astype(jnp.bfloat16).reshape(groups, rows, width)
    )
    grad_query, grad_keys_all, grad_values_all = plain_attend_back(
        query, keys, values, allowed, logsum, grad_attended
    )
    grad_keys, grad_values = (
        lax.psum_scatter(
            grad_keys_all.astype(jnp.bfloat16), "ctx", scatter_dimension=1, tiled=True
        ).astype(jnp.float32),
        lax.psum_scatter(
            grad_values_all.astype(jnp.bfloat16), "ctx", scatter_dimension=1, tiled=True
        ).astype(jnp.float32),
    )
    grad_query = grad_query.astype(jnp.bfloat16).reshape(groups * rows, width)
    grad_keys = grad_keys.astype(jnp.bfloat16).reshape(groups * rows, width)
    grad_values = grad_values.astype(jnp.bfloat16).reshape(groups * rows, width)
    query_grad = plain_product_left(normed, grad_query)
    key_grad = plain_product_left(normed, grad_keys)
    value_grad = plain_product_left(normed, grad_values)
    grad_normed = (
        plain_product_right(grad_query, w_query)
        + plain_product_right(grad_keys, w_key)
        + plain_product_right(grad_values, w_value)
    )
    grad_inputs, attn_gain_grad = plain_norm_back(
        inputs, inverse_one, gain_one.astype(jnp.float32), grad_normed
    )
    input_grad = (grad_middle + grad_inputs).reshape(groups, rows, width)
    shares = (
        lax.psum_scatter(attn_gain_grad, ("dp", "ctx"), scatter_dimension=0, tiled=True),
        lax.psum_scatter(query_grad, ("dp", "ctx"), scatter_dimension=0, tiled=True),
        lax.psum_scatter(key_grad, ("dp", "ctx"), scatter_dimension=0, tiled=True),
        lax.psum_scatter(value_grad, ("dp", "ctx"), scatter_dimension=0, tiled=True),
        lax.psum_scatter(out_proj_grad, ("dp", "ctx"), scatter_dimension=0, tiled=True),
        lax.psum_scatter(mlp_gain_grad, ("dp", "ctx"), scatter_dimension=0, tiled=True),
        lax.psum_scatter(gate_grad, ("dp", "ctx"), scatter_dimension=0, tiled=True),
        lax.psum_scatter(up_grad, ("dp", "ctx"), scatter_dimension=0, tiled=True),
        lax.psum_scatter(down_grad, ("dp", "ctx"), scatter_dimension=0, tiled=True),
    )
    return (
        layer_output.reshape(groups, rows, width),
        input_grad,
        shares[0],
        shares[1],
        shares[2],
        shares[3],
        shares[4],
        shares[5],
        shares[6],
        shares[7],
        shares[8],
    )


def solution(mesh):
    placed = (
        P("dp", "ctx", None),
        P("dp", None),
        P(("dp", "ctx")),
        P(("dp", "ctx"), None),
        P(("dp", "ctx"), None),
        P(("dp", "ctx"), None),
        P(("dp", "ctx"), None),
        P(("dp", "ctx")),
        P(("dp", "ctx"), None),
        P(("dp", "ctx"), None),
        P(("dp", "ctx"), None),
        P("dp", "ctx", None),
    )
    fits = mesh.shape["dp"] == 4 and mesh.shape["ctx"] == 8
    body = grouped if fits else on_device
    return jax.shard_map(
        body,
        mesh=mesh,
        in_specs=placed,
        out_specs=(
            P("dp", "ctx", None),
            P("dp", "ctx", None),
            P(("dp", "ctx")),
            P(("dp", "ctx"), None),
            P(("dp", "ctx"), None),
            P(("dp", "ctx"), None),
            P(("dp", "ctx"), None),
            P(("dp", "ctx")),
            P(("dp", "ctx"), None),
            P(("dp", "ctx"), None),
            P(("dp", "ctx"), None),
        ),
        check_vma=False,
    )
```

```python
import functools

import jax
import jax.numpy as jnp
from jax import lax
from jax.experimental import pallas as pl
from jax.experimental.pallas import tpu as pltpu
from jax.sharding import PartitionSpec as P

HEAD = 64


EPS = 1e-05
MESH = pl.DeviceIdType.MESH
F32 = jnp.float32
BF16 = jnp.bfloat16
LOG2E = 1.4426950408889634
ANY = pl.BlockSpec(memory_space=pl.ANY)
VMEM = pl.BlockSpec(memory_space=pltpu.VMEM)


class Wires:
    def __init__(self, send, recv):
        dp, ctx = lax.axis_index("dp"), lax.axis_index("ctx")
        self.x, self.y = ctx % 2, dp // 2
        self.zh, self.zb = ctx // 4, (ctx // 2) % 2
        self.v, self.k = (self.zb + self.zh) % 2, dp % 2
        self.send, self.recv = send, recv
        self.used = 0

    def slots(self, count):
        first = self.used
        self.used += count
        return first

    def at(self, v=None, y=None, zh=None, x=None, k=None):
        v = self.v if v is None else v
        y = self.y if y is None else y
        zh = self.zh if zh is None else zh
        x = self.x if x is None else x
        k = self.k if k is None else k
        return (2 * y + k, 4 * zh + 2 * ((v + zh) % 2) + x)

    def across(self):
        return self.at(x=1 - self.x)

    def core(self):
        return self.at(k=1 - self.k)

    def copy(self, source, target, device, slot, recv_slot=None):
        return pltpu.make_async_remote_copy(
            src_ref=source,
            dst_ref=target,
            send_sem=self.send.at[slot],
            recv_sem=self.recv.at[slot if recv_slot is None else recv_slot],
            device_id=device,
            device_id_type=MESH,
        )

    def greet(self):
        v, zh, zb, k = self.v, self.zh, self.zb, self.k
        barrier = pltpu.get_barrier_semaphore()

        def call(peer):
            pl.semaphore_signal(barrier, inc=1, device_id=peer, device_id_type=MESH)

        for peer in (
            self.across(), self.core(), self.at(x=1 - self.x, k=1 - k),
            self.at(v=1 - v), self.at(y=1 - self.y), self.at(zh=1 - zh),
        ):
            call(peer)
        count = 6
        for n in range(2):
            away = jnp.logical_not(every(v == n, zh == k, zb == k))
            pl.when(away)(lambda: call(self.at(v=n, zh=k, k=zb)))
            count = count + jnp.where(away, 1, 0)
            away = jnp.logical_not(every(zh == n, zb == k, zh == k))
            pl.when(away)(lambda: call(self.at(zh=n, v=(k + n) % 2, k=zh)))
            count = count + jnp.where(away, 1, 0)
        pl.semaphore_wait(barrier, count)


def every(*tests):
    all_of = tests[0]
    for test in tests[1:]:
        all_of = jnp.logical_and(all_of, test)
    return all_of


class Pairs:
    def __init__(self, wires, order):
        self.w, self.order = wires, order

    def place(self, z, a, b):
        w = self.w
        v, y = (a, b) if self.order == "vy" else (b, a)
        flip = lambda own, turn: 1 - own if turn else own
        return flip(w.v, v), flip(w.y, y), flip(w.zh, z)

    def partner(self, z, a, b):
        v, y, zh = self.place(z, a, b)
        return self.w.at(v=v, y=y, zh=zh)


class Spread(Pairs):
    SENDS = ((0, 0, 0), (0, 0, 0), (1, 0, 0), (0, 0, 0), (1, 0, 0), (0, 1, 0), (1, 1, 0))
    STEPS = ((1, 0, 0), (0, 1, 0), (0, 1, 0), (0, 0, 1), (0, 0, 1), (0, 0, 1), (0, 0, 1))

    def __init__(self, wires, order, block, own=None):
        super().__init__(wires, order)
        self.block, self.own = block, own
        self.first = wires.slots(7)

    def piece(self, n):
        ref = self.block(*self.place(*self.SENDS[n]))
        source = self.own if self.own is not None and not any(self.SENDS[n]) else ref
        return self.w.copy(source, ref, self.partner(*self.STEPS[n]), self.first + n)

    def landed(self, n):
        came = [i ^ j for i, j in zip(self.SENDS[n], self.STEPS[n])]
        ref = self.block(*self.place(*came))
        return self.w.copy(ref, ref, self.partner(*self.STEPS[n]), self.first + n)

    def start(self):
        self.start_z()
        self.start_rest()

    def start_z(self):
        self.piece(0).start()

    def start_rest(self):
        self.piece(1).start()
        self.piece(3).start()

    def got_first(self):
        self.landed(1).wait_recv()
        self.piece(5).start()

    def got_z(self):
        self.landed(0).wait_recv()
        self.piece(2).start()
        self.piece(4).start()

    def got_last(self):
        self.landed(2).wait_recv()
        self.piece(6).start()

    def arrive(self):
        for n in (3, 4, 5, 6):
            self.landed(n).wait_recv()

    def drain(self):
        for n in range(7):
            self.piece(n).wait_send()


class Share:
    def __init__(self, wires, block):
        self.w, self.block = wires, block
        self.first = wires.slots(3)

    def piece(self, i):
        w = self.w
        ref = self.block(w.x if i < 2 else 1 - w.x, w.k)
        return w.copy(ref, ref, w.across() if i == 0 else w.core(), self.first + i)

    def landed(self, i):
        w = self.w
        ref = self.block(*[(1 - w.x, w.k), (w.x, 1 - w.k), (1 - w.x, 1 - w.k)][i])
        return w.copy(ref, ref, w.core(), self.first + i)

    def start(self):
        self.piece(0).start()
        self.piece(1).start()

    def forward(self):
        self.landed(0).wait_recv()
        self.piece(2).start()

    def arrive(self):
        self.landed(1).wait_recv()
        self.landed(2).wait_recv()

    def drain(self):
        for i in range(3):
            self.piece(i).wait_send()


class Deal:
    def __init__(self, wires, outgoing, incoming):
        self.w, self.outgoing, self.incoming = wires, outgoing, incoming
        self.first = wires.slots(3)

    def mate(self, i):
        w = self.w
        return [(1 - w.x, w.k), (w.x, 1 - w.k), (1 - w.x, 1 - w.k)][i]

    def piece(self, i):
        w = self.w
        x, k = self.mate(i)
        return w.copy(
            self.outgoing(x, k), self.incoming(w.x, w.k), w.at(x=x, k=k), self.first + i
        )

    def landed(self, i):
        x, k = self.mate(i)
        ref = self.incoming(x, k)
        return self.w.copy(ref, ref, self.w.at(x=x, k=k), self.first + i)

    def start(self):
        for i in range(3):
            self.piece(i).start()

    def arrive(self):
        for i in range(3):
            self.landed(i).wait_recv()

    def drain(self):
        for i in range(3):
            self.piece(i).wait_send()


class Visit:
    def __init__(self, wires, home, full, local):
        self.w, self.home, self.full, self.local = wires, home, full, local
        self.first = wires.slots(2)
        w = wires
        self.own = [every(w.v == j, w.zh == w.k, w.zb == w.k) for j in range(2)]
        self.here = [every(w.zh == i, w.zb == w.k, w.zh == w.k) for i in range(2)]

    def piece(self, j):
        w = self.w
        return w.copy(
            self.home.at[j],
            self.full(w.zh, w.zb, w.x),
            w.at(v=j, zh=w.k, k=w.zb),
            self.first + j,
            self.first + w.zh,
        )

    def stay(self, j):
        w = self.w
        return pltpu.make_async_copy(self.home.at[j], self.full(w.zh, w.zb, w.x), self.local)

    def landed(self, i):
        w = self.w
        ref = self.full(i, w.k, w.x)
        return w.copy(ref, ref, w.core(), self.first + i)

    def start(self):
        for j in range(2):
            pl.when(self.own[j])(lambda: self.stay(j).start())
            pl.when(jnp.logical_not(self.own[j]))(lambda: self.piece(j).start())

    def arrive(self):
        for j in range(2):
            pl.when(self.own[j])(lambda: self.stay(j).wait())
        for i in range(2):
            pl.when(jnp.logical_not(self.here[i]))(lambda: self.landed(i).wait_recv())

    def drain(self):
        for j in range(2):
            pl.when(jnp.logical_not(self.own[j]))(lambda: self.piece(j).wait_send())


class Return:
    def __init__(self, wires, done, home, local):
        self.w, self.done, self.home, self.local = wires, done, home, local
        self.first = wires.slots(2)
        w = wires
        self.own = [every(w.zh == i, w.zb == w.k, w.k == w.zh) for i in range(2)]
        self.here = [every(w.v == j, w.zh == w.k, w.zb == w.k) for j in range(2)]

    def piece(self, i):
        w = self.w
        return w.copy(
            self.done(i),
            self.home.at[w.v],
            w.at(zh=i, v=(w.k + i) % 2, k=w.zh),
            self.first + i,
            self.first + w.v,
        )

    def stay(self, i):
        return pltpu.make_async_copy(self.done(i), self.home.at[self.w.v], self.local)

    def landed(self, j):
        ref = self.home.at[j]
        return self.w.copy(ref, ref, self.w.core(), self.first + j)

    def start(self, i):
        pl.when(self.own[i])(lambda: self.stay(i).start())
        pl.when(jnp.logical_not(self.own[i]))(lambda: self.piece(i).start())

    def arrive(self):
        for i in range(2):
            pl.when(self.own[i])(lambda: self.stay(i).wait())
        for j in range(2):
            pl.when(jnp.logical_not(self.here[j]))(lambda: self.landed(j).wait_recv())

    def drain(self):
        for i in range(2):
            pl.when(jnp.logical_not(self.own[i]))(lambda: self.piece(i).wait_send())


def shaped(*shape, dtype=BF16):
    return jax.ShapeDtypeStruct(shape, dtype)


def pack_rows(columns, shards, packed):
    for rank in range(4):
        at = 0
        for shard in shards:
            for start, width in columns(rank):
                packed[rank, :, at : at + width] = shard[:, start : start + width]
                at += width


def head_columns(rank):
    return [(256 * rank, 256)]


def hidden_columns(rank):
    x, k = rank // 2, rank % 2
    return [
        (128 * (16 * y + 8 * k + 4 * zh + 2 * (v ^ zh) + x), 128)
        for y in range(2)
        for zh in range(2)
        for v in range(2)
    ]


class Total:
    def __init__(self, wires, part, got_core, got_across):
        self.w, self.part, self.got_core, self.got_across = wires, part, got_core, got_across
        self.first = wires.slots(4)
        self.half = part.shape[2] // 2

    def core(self, i):
        w = self.w
        return w.copy(
            self.part.at[0, i], self.got_core.at[i], w.core(), self.first + i
        )

    def rows(self, v):
        return pl.ds(pl.multiple_of(self.half * v, self.half), self.half)

    def across(self, i):
        w = self.w
        return w.copy(
            self.part.at[1, i, self.rows(1 - w.x)],
            self.got_across.at[i],
            w.across(),
            self.first + 2 + i,
        )

    def give(self, i, value):
        self.part[0, i] = value.astype(BF16)
        self.core(i).start()

    def keep(self, i, value):
        self.core(i).wait_recv()
        self.part[1, i] = (value + self.got_core[i].astype(F32)).astype(BF16)

    def send(self, i):
        self.across(i).start()

    def take(self, i):
        self.across(i).wait_recv()
        own = self.part[1, i, self.rows(self.w.x)]
        return own.astype(F32) + self.got_across[i].astype(F32)

    def drain(self):
        for i in range(2):
            self.core(i).wait_send()
            self.across(i).wait_send()


class Parts:
    def __init__(self, copies):
        self.copies = copies

    def start(self):
        for copy in self.copies:
            copy.start()

    def wait_send(self):
        for copy in self.copies:
            copy.wait_send()

    def wait_recv(self):
        for copy in self.copies:
            copy.wait_recv()


class Fold(Pairs):
    def __init__(self, wires, order, whole, block, got_b, got_b_block, got_a, got_z):
        super().__init__(wires, order)
        self.whole, self.block = whole, block
        self.got_b, self.got_b_block, self.got_a, self.got_z = got_b, got_b_block, got_a, got_z
        self.first = wires.slots(5)

    def stage_b(self):
        w = self.w
        b = w.y if self.order == "vy" else w.v
        return Parts(
            [
                w.copy(source, target, self.partner(0, 0, 1), self.first + 4 * i)
                for i, (source, target) in enumerate(zip(self.whole(1 - b), self.got_b))
            ]
        )

    def stage_a(self, z):
        v, y, zh = self.place(z, 1, 0)
        return self.w.copy(
            self.block(v, y, zh), self.got_a.at[zh], self.partner(0, 1, 0), self.first + 1 + z,
            self.first + 1 + z,
        )

    def landed_a(self, z):
        v, y, zh = self.place(z, 0, 0)
        ref = self.got_a.at[zh]
        return self.w.copy(ref, ref, self.partner(0, 1, 0), self.first + 1 + z)

    def stage_z(self):
        ref = self.block(*self.place(1, 0, 0))
        return self.w.copy(ref, self.got_z, self.partner(1, 0, 0), self.first + 3)

    def two(self, z, a):
        v, y, zh = self.place(z, a, 0)
        own = self.block(v, y, zh)[...].astype(F32)
        return own + self.got_b_block(v if self.order == "vy" else y, zh)[...].astype(F32)

    def three(self, z):
        return self.two(z, 0) + self.got_a[self.place(z, 0, 0)[2]].astype(F32)

    def start(self):
        self.stage_b().start()

    def second(self):
        self.stage_b().wait_recv()
        for z in (1, 0):
            ref = self.block(*self.place(z, 1, 0))
            ref[...] = self.two(z, 1).astype(self.got_z.dtype)
            self.stage_a(z).start()

    def third(self):
        self.landed_a(1).wait_recv()
        ref = self.block(*self.place(1, 0, 0))
        ref[...] = self.three(1).astype(self.got_z.dtype)
        self.stage_z().start()

    def finish(self):
        self.landed_a(0).wait_recv()
        total = self.three(0)
        self.stage_z().wait_recv()
        return total + self.got_z[...].astype(F32)

    def drain(self):
        self.stage_b().wait_send()
        for z in range(2):
            self.stage_a(z).wait_send()
        self.stage_z().wait_send()


def dots(left, right, dims):
    return lax.dot_general(left, right, (dims, ((), ())), preferred_element_type=F32)


NN, NT, TN = ((1,), (0,)), ((1,), (1,)), ((0,), (0,))


def only_head(array, head):
    lane = lax.broadcasted_iota(jnp.int32, array.shape, 1)
    return jnp.where(lane // HEAD == head, array, jnp.zeros_like(array))


def inverse_size(rows):
    return lax.rsqrt(jnp.mean(rows * rows, axis=-1, keepdims=True) + EPS)


def norm_back(rows, gain, upstream):
    inverse = inverse_size(rows)
    normed = rows * inverse
    scaled = upstream * gain
    grad_rows = inverse * (scaled - normed * jnp.mean(scaled * normed, axis=-1, keepdims=True))
    return grad_rows, jnp.sum(upstream * normed, axis=0, keepdims=True)


SCRATCH = [
    ("rows_all", (2, 2, 2, 128, 1024), BF16),
    ("cots_all", (2, 2, 2, 128, 1024), BF16),
    ("ids_all", (2, 2, 1, 1024), jnp.int32),
    ("heads_all", (2, 2, 2, 2, 2, 32, 768), BF16),
    ("out_all", (2, 2, 2, 2, 2, 32, 1024), BF16),
    ("gate_all", (2, 2, 2, 2, 2, 32, 1024), BF16),
    ("up_all", (2, 2, 2, 2, 2, 32, 1024), BF16),
    ("down_all", (2, 2, 2, 128, 1024), BF16),
    ("gains_all", (2, 2, 2, 2, 2, 16, 128), BF16),
    ("heads_shards", (3, 32, 1024), BF16),
    ("wide_shards", (2, 32, 4096), BF16),
    ("heads_pack", (4, 32, 768), BF16),
    ("gate_pack", (4, 32, 1024), BF16),
    ("up_pack", (4, 32, 1024), BF16),
    ("normed", (1024, 1024), BF16),
    ("query", (1024, 256), BF16),
    ("keys", (1024, 256), BF16),
    ("values", (1024, 256), BF16),
    ("keys_turned", (256, 1024), BF16),
    ("values_turned", (256, 1024), BF16),
    ("mixed_turned", (256, 1024), BF16),
    ("mixed_all", (2, 2, 256, 1024), BF16),
    ("logsum", (4, 1, 1024), F32),
    ("gain_rows", (2, 1, 1024), F32),
    ("ids_row", (1, 1024), F32),
    ("ids_col", (1024, 128), F32),
    ("middle_keep", (2, 256, 1024), F32),
    ("normed_two", (1024, 1024), BF16),
    ("hidden", (1024, 1024), BF16),
    ("grad_gate", (1024, 1024), BF16),
    ("grad_up", (1024, 1024), BF16),
    ("part_norm", (2, 2, 256, 1024), BF16),
    ("core_out", (2, 256, 1024), BF16),
    ("core_norm", (2, 256, 1024), BF16),
    ("across_out", (2, 128, 1024), BF16),
    ("across_norm", (2, 128, 1024), BF16),
    ("branch", (2, 2, 2, 128, 1024), BF16),
    ("grad_keys", (1024, 256), F32),
    ("grad_values", (1024, 256), F32),
    ("heads_part", (2, 2, 2, 2, 2, 32, 768), BF16),
    ("out_part", (2, 2, 2, 32, 1024), BF16),
    ("gains_part", (2, 2, 2, 8, 128), F32),
    ("heads_b", (2, 2, 2, 2, 32, 768), BF16),
    ("heads_a", (2, 2, 2, 32, 768), BF16),
    ("heads_z", (2, 2, 32, 768), BF16),
    ("gate_b", (2, 2, 2, 2, 32, 1024), BF16),
    ("gate_a", (2, 2, 2, 32, 1024), BF16),
    ("gate_z", (2, 2, 32, 1024), BF16),
    ("up_b", (2, 2, 2, 2, 32, 1024), BF16),
    ("up_a", (2, 2, 2, 32, 1024), BF16),
    ("up_z", (2, 2, 32, 1024), BF16),
    ("down_b", (2, 2, 128, 1024), BF16),
    ("down_a", (2, 128, 1024), BF16),
    ("down_z", (128, 1024), BF16),
    ("out_b", (2, 2, 2, 32, 1024), BF16),
    ("out_a", (2, 2, 32, 1024), BF16),
    ("out_z", (2, 32, 1024), BF16),
    ("gains_b", (2, 2, 8, 128), F32),
    ("gains_a", (2, 8, 128), F32),
    ("gains_z", (8, 128), F32),
    ("gains_deal", (8, 128), F32),
    ("gains_dealt", (4, 8, 128), F32),
    ("out_deal", (32, 1024), BF16),
    ("out_home", (32, 1024), BF16),
    ("done_out", (2, 128, 1024), BF16),
]


def layer_body(
    rows, cots, ids, wq, wk, wv, wo, wg, wu, wd, gains,
    output, input_home, heads_dealt, o_out, gate_dealt, up_dealt, d_out, gain_out,
    *scratch,
):
    send, recv, local = scratch[-3:]
    m = type("Memory", (), dict(zip([name for name, _, _ in SCRATCH], scratch)))
    w = Wires(send, recv)
    v, y, zh, zb, x, k = w.v, w.y, w.zh, w.zb, w.x, w.k
    rank = 2 * x + k

    used = [0]

    def spare():
        used[0] += 1
        return local.at[used[0] - 1]

    def stay(source, target):
        copy = pltpu.make_async_copy(source, target, spare())
        copy.start()
        return copy

    shards = [stay(shard, m.heads_shards.at[i]) for i, shard in enumerate((wq, wk, wv))]
    shards += [stay(shard, m.wide_shards.at[i]) for i, shard in enumerate((wg, wu))]
    w.greet()

    def sequence_block(ref):
        return lambda zh, zb, x: ref.at[zh, zb, x]

    def deal_rows(packed, whole):
        return Deal(
            w,
            lambda x, k: packed.at[2 * x + k],
            lambda sx, sk: whole.at[y, sk, zh, zb, sx],
        )

    def group_rows(ref):
        return lambda v, y, zh: ref.at[y, :, zh, (v + zh) % 2]

    def own_rows(ref):
        return lambda v, y, zh: ref.at[y, k, zh, (v + zh) % 2, x]

    visit_rows = Visit(w, rows, sequence_block(m.rows_all), spare())
    visit_rows.start()
    for copy in shards:
        copy.wait()
    pack_rows(head_columns, [m.heads_shards.at[i] for i in range(3)], m.heads_pack)
    deal_heads = deal_rows(m.heads_pack, m.heads_all)
    deal_heads.start()
    spread_gains = Spread(w, "vy", own_rows(m.gains_all), gains)
    spread_gains.start()
    swap = w.copy(ids, m.ids_all.at[k], w.core(), w.slots(1))
    swap.start()
    spread_out = Spread(w, "vy", own_rows(m.out_all), wo)
    spread_out.start()
    pack_rows(hidden_columns, (m.wide_shards.at[0],), m.gate_pack)
    pack_rows(hidden_columns, (m.wide_shards.at[1],), m.up_pack)
    stays = [
        stay(m.heads_pack.at[rank], m.heads_all.at[y, k, zh, zb, x]),
        stay(m.gate_pack.at[rank], m.gate_all.at[y, k, zh, zb, x]),
        stay(m.up_pack.at[rank], m.up_all.at[y, k, zh, zb, x]),
        stay(wo, m.out_all.at[y, k, zh, zb, x]),
        stay(gains, m.gains_all.at[y, k, zh, zb, x]),
        stay(wd, m.down_all.at[y, zh, v]),
        stay(ids, m.ids_all.at[k]),
    ]
    deal_gate = deal_rows(m.gate_pack, m.gate_all)
    deal_up = deal_rows(m.up_pack, m.up_all)
    for copy in stays:
        copy.wait()
    deal_heads.arrive()
    spread_heads = Spread(w, "vy", group_rows(m.heads_all))
    spread_heads.start()
    spread_down = Spread(w, "vy", lambda v, y, zh: m.down_all.at[y, zh, v], wd)
    spread_down.start_rest()
    spread_gains.got_first()
    deal_gate.start()
    deal_up.start()
    visit_rows.arrive()
    share_rows = Share(w, lambda x, k: m.rows_all.at[:, k, x])
    share_rows.start()
    spread_gains.got_z()
    spread_heads.got_first()
    spread_out.got_first()
    spread_gains.got_last()
    deal_gate.arrive()
    spread_gate = Spread(w, "vy", group_rows(m.gate_all))
    spread_gate.start_rest()
    deal_up.arrive()
    spread_up = Spread(w, "yv", group_rows(m.up_all))
    spread_up.start_rest()
    spread_heads.got_z()
    spread_down.start_z()
    spread_gate.start_z()
    spread_up.start_z()
    spread_gains.arrive()
    share_gains = [Share(w, lambda x, k: m.gains_all.at[:, k, :, :, x])]
    for share in share_gains:
        share.start()
    share_rows.forward()
    swap.wait()
    m.ids_row[...] = m.ids_all[zh, v].astype(F32)
    for j in range(8):
        piece = slice(128 * j, 128 * j + 128)
        m.ids_col[piece, :] = jnp.broadcast_to(m.ids_row[:, piece], (128, 128)).T
    spread_out.got_z()
    spread_heads.got_last()
    for share in share_gains:
        share.forward()
    spread_down.got_first()
    share_rows.arrive()
    for share in share_gains:
        share.arrive()
    for j in range(8):
        four = [
            m.gains_all[j // 4, (j // 2) % 2, j % 2, i // 2, i % 2].astype(F32) for i in range(4)
        ]
        total = four[0] + four[1] + four[2] + four[3]
        for i in range(2):
            m.gain_rows[i, :, 128 * j : 128 * j + 128] = total[i : i + 1, :]

    def first_norm(b, _):
        block = m.rows_all[b // 2, b % 2].reshape(256, 1024).astype(F32)
        span = pl.ds(pl.multiple_of(256 * b, 256), 256)
        m.normed[span, :] = (block * inverse_size(block) * m.gain_rows[0]).astype(BF16)
        return 0

    lax.fori_loop(0, 4, first_norm, 0)
    spread_heads.arrive()
    heads = m.heads_all[...].reshape(1024, 768)
    for b in range(4):
        span = slice(256 * b, 256 * b + 256)
        made = dots(m.normed[span, :], heads, NN).astype(BF16)
        m.query[span, :], m.keys[span, :] = made[:, :256], made[:, 256:512]
        m.values[span, :] = made[:, 512:]
        m.keys_turned[:, span] = made[:, 256:512].T
        m.values_turned[:, span] = made[:, 512:].T
    spread_out.got_last()
    spread_gate.got_first()
    spread_up.got_first()

    def bias_of(b):
        start, count = 256 * b, 256 * b + 256
        column = m.ids_col[:count, :]
        same = jnp.concatenate([column, column], axis=1) == m.ids_row[:, start : start + 256]
        key = lax.broadcasted_iota(jnp.int32, (count, 256), 0)
        place = lax.broadcasted_iota(jnp.int32, (count, 256), 1) + start
        return jnp.where(jnp.logical_and(same, key <= place), 0.0, -1e30).astype(F32)

    def head_rows(h):
        return pl.ds(pl.multiple_of(h * HEAD, HEAD), HEAD)

    def rank_columns(x, k):
        return pl.ds(pl.multiple_of(256 * (2 * x + k), 256), 256)

    def mix(b):
        span, count = slice(256 * b, 256 * b + 256), 256 * b + 256
        bias = bias_of(b)

        def one(h, _):
            scores = dots(m.keys[:count, :], only_head(m.query[span, :], h), NT)
            scores = scores * (HEAD**-0.5 * LOG2E) + bias
            top = jnp.max(scores, axis=0, keepdims=True)
            lifted = jnp.exp2(scores - top)
            total = jnp.sum(lifted, axis=0, keepdims=True)
            probs = (lifted * (1.0 / total)).astype(BF16)
            mixed = dots(m.values_turned[head_rows(h), :count], probs, NN)
            m.mixed_turned[head_rows(h), span] = mixed.astype(BF16)
            m.logsum[h, :, span] = top + jnp.log2(total)
            return 0

        lax.fori_loop(0, 4, one, 0)
        m.mixed_all[b // 2, b % 2, :, rank_columns(x, k)] = m.mixed_turned[:, span].T

    def share_mixed(b):
        return Share(w, lambda x, k: m.mixed_all.at[b // 2, b % 2, :, rank_columns(x, k)])

    shares = [share_mixed(b) for b in range(4)]
    mix(0)
    shares[0].start()
    spread_down.got_z()
    mix(1)
    shares[1].start()
    visit_cots = Visit(w, cots, sequence_block(m.cots_all), spare())
    visit_cots.start()
    shares[0].forward()
    spread_out.arrive()
    share_out = [Share(w, lambda x, k: m.out_all.at[:, k, :, :, x])]
    for share in share_out:
        share.start()
    spread_gate.got_z()
    mix(2)
    shares[2].start()
    shares[1].forward()
    for share in share_out:
        share.forward()
    spread_up.got_z()
    spread_down.got_last()
    mix(3)
    shares[3].start()
    shares[2].forward()
    for share in share_out:
        share.arrive()

    for b in range(4):
        span = slice(256 * b, 256 * b + 256)
        if b == 2:
            shares[3].forward()
            spread_gate.got_last()
        shares[b].arrive()
        middle = m.rows_all[b // 2, b % 2].reshape(256, 1024).astype(F32)
        whole = m.out_all[...].reshape(1024, 1024)
        middle = middle + dots(m.mixed_all[b // 2, b % 2], whole, NN)
        m.normed_two[span, :] = (middle * inverse_size(middle) * m.gain_rows[1]).astype(BF16)

        @pl.when(k == b % 2)
        def _():
            m.middle_keep[b // 2] = middle

    visit_cots.arrive()
    share_cots = Share(w, lambda x, k: m.cots_all.at[:, k, x])
    share_cots.start()
    spread_up.got_last()
    share_cots.forward()
    for spread in (spread_gate, spread_up, spread_down):
        spread.arrive()
    share_cots.arrive()
    for share in shares:
        share.drain()
    total_out = Total(w, m.mixed_all, m.core_out, m.across_out)
    total_norm = Total(w, m.part_norm, m.core_norm, m.across_norm)

    def feed(i, part):
        span = pl.ds(pl.multiple_of(256 * (2 * i + part), 256), 256)
        upstream = m.cots_all[i, part].reshape(256, 1024)
        normed_two = m.normed_two[span, :]
        for n in range(4):
            columns = slice(256 * n, 256 * n + 256)
            gate_tile = m.gate_all[..., columns].reshape(1024, 256)
            up_tile = m.up_all[..., columns].reshape(1024, 256)
            down_tile = m.down_all[n // 2, n % 2].reshape(256, 1024)
            gate = dots(normed_two, gate_tile, NN)
            upward = dots(normed_two, up_tile, NN)
            grad_hidden = dots(upstream, down_tile, NT)
            sigma = 1.0 / (1.0 + jnp.exp(-gate))
            silu = gate * sigma
            m.hidden[span, columns] = (silu * upward).astype(BF16)
            m.grad_up[span, columns] = (grad_hidden * silu).astype(BF16)
            m.grad_gate[span, columns] = (
                grad_hidden * upward * (sigma + silu * (1.0 - sigma))
            ).astype(BF16)
        norm_part = dots(m.grad_gate[span, :], m.gate_all[...].reshape(1024, 1024), NT)
        norm_part = norm_part + dots(m.grad_up[span, :], m.up_all[...].reshape(1024, 1024), NT)
        return span, norm_part

    def out_of(span):
        return dots(m.hidden[span, :], m.down_all[...].reshape(1024, 1024), NN)

    def give(i, _):
        span, norm_part = feed(i, 1 - k)
        total_norm.give(i, norm_part)
        total_out.give(i, out_of(span))
        return 0

    def keep(i, _):
        span, norm_part = feed(i, k)
        total_norm.keep(i, norm_part)
        total_norm.send(i)
        total_out.keep(i, out_of(span))
        return 0

    lax.fori_loop(0, 2, give, 0)
    lax.fori_loop(0, 2, keep, 0)
    for spread in (spread_gate, spread_up, spread_down):
        spread.drain()

    def lanes(plane, half):
        return pl.ds(pl.multiple_of(512 * plane + 256 * half, 256), 256)

    def down_part(plane):
        def one(half, _):
            made = dots(m.hidden[:, lanes(plane, half)], m.cots_all[...].reshape(1024, 1024), TN)
            m.down_all[plane, half] = made.astype(BF16).reshape(2, 128, 1024)
            return 0

        lax.fori_loop(0, 2, one, 0)

    def wide_part(whole, right, plane):
        def one(half, _):
            made = dots(m.normed_two[:, lanes(plane, half)], right[...], TN).astype(BF16)
            whole[plane, half] = made.reshape(2, 2, 2, 32, 1024)
            return 0

        lax.fori_loop(0, 2, one, 0)

    def fold_plane(whole, got_b, got_a, got_z):
        return Fold(
            w, "vy", lambda y: [whole.at[y]], lambda v, y, zh: whole.at[y, :, zh, (v + zh) % 2],
            [got_b], lambda v, zh: got_b.at[:, zh, (v + zh) % 2], got_a, got_z,
        )

    def fold_side(whole, got_b, got_a, got_z):
        return Fold(
            w, "yv", lambda v: [whole.at[:, :, 0, v], whole.at[:, :, 1, 1 - v]],
            lambda v, y, zh: whole.at[y, :, zh, (v + zh) % 2],
            [got_b.at[0], got_b.at[1]], lambda y, zh: got_b.at[zh, y], got_a, got_z,
        )

    def fold_block(whole, got_b, got_a, got_z):
        return Fold(
            w, "vy", lambda y: [whole.at[y]], lambda v, y, zh: whole.at[y, zh, v],
            [got_b], lambda v, zh: got_b.at[zh, v], got_a, got_z,
        )

    fold_down = fold_block(m.down_all, m.down_b, m.down_a, m.down_z)
    fold_gate = fold_plane(m.gate_all, m.gate_b, m.gate_a, m.gate_z)
    fold_up = fold_side(m.up_all, m.up_b, m.up_a, m.up_z)
    fold_heads = fold_plane(m.heads_part, m.heads_b, m.heads_a, m.heads_z)
    fold_gains = fold_block(m.gains_part, m.gains_b, m.gains_a, m.gains_z)
    shares_branch = [Share(w, lambda x, k, i=i: m.branch.at[i, k, x]) for i in range(2)]
    own_half, other_half = total_norm.rows(x), total_norm.rows(1 - x)

    def back_two(i):
        grad, term = norm_back(m.middle_keep[i, own_half], m.gain_rows[1], total_norm.take(i))
        grad = grad + m.cots_all[i, k, x].astype(F32)
        m.middle_keep[i, other_half] = grad
        m.branch[i, k, x] = grad.astype(BF16)
        shares_branch[i].start()
        return term

    gain_sum = back_two(0)
    down_part(1 - y)
    fold_down.start()
    wide_part(m.up_all, m.grad_up, 0)
    wide_part(m.up_all, m.grad_up, 1)
    fold_up.start()
    gain_sum = gain_sum + back_two(1)
    wide_part(m.gate_all, m.grad_gate, 1 - y)
    fold_gate.start()
    for i in range(2):
        total_out.send(i)

    def gain_rows_part(row, total):
        for plane in range(2):
            for place in range(4):
                for half in range(2):
                    at = 512 * plane + 256 * half + 128 * (place // 2)
                    row_at = slice(2 * row + half, 2 * row + half + 1)
                    m.gains_part[plane, place // 2, place % 2, row_at, :] = total[:, at : at + 128]

    m.gains_part[...] = jnp.zeros_like(m.gains_part)
    gain_rows_part(1, gain_sum)
    shares_branch[0].forward()
    down_part(y)
    shares_branch[1].forward()
    wide_part(m.gate_all, m.grad_gate, y)

    grad_mixed, grad_mixed_turned = m.grad_up.at[:, :256], m.hidden.at[:256]
    grad_heads = m.grad_gate.at[:, :768]
    out_own = m.out_all[x, k].reshape(256, 1024)
    for b in range(4):
        if b % 2 == 0:
            shares_branch[b // 2].arrive()
        if b == 2:
            fold_down.second()
        span = slice(256 * b, 256 * b + 256)
        made = dots(m.branch[b // 2, b % 2].reshape(256, 1024), out_own, NT).astype(BF16)
        grad_mixed[span, :] = made
        grad_mixed_turned[:, span] = made.T
    m.out_part[...] = (
        dots(m.mixed_turned[...], m.branch[...].reshape(1024, 1024), NN)
        .astype(BF16)
        .reshape(2, 2, 2, 32, 1024)
    )
    base = w.slots(6)
    owner = y == x
    out_across = w.copy(m.out_part, m.out_b, w.at(y=1 - y), base)
    pl.when(jnp.logical_not(owner))(lambda: out_across.start())
    m.grad_keys[...] = jnp.zeros_like(m.grad_keys)
    m.grad_values[...] = jnp.zeros_like(m.grad_values)

    def unmix(b):
        span, count = slice(256 * b, 256 * b + 256), 256 * b + 256
        bias = bias_of(b)

        def one(h, _):
            query, upstream = only_head(m.query[span, :], h), only_head(grad_mixed[span, :], h)
            scores = dots(m.keys[:count, :], query, NT)
            scores = scores * (HEAD**-0.5 * LOG2E) + bias
            probs = jnp.exp2(scores - m.logsum[h, :, span])
            grad_probs = dots(m.values[:count, :], upstream, NT)
            centre = jnp.sum(
                grad_mixed_turned[head_rows(h), span].astype(F32)
                * m.mixed_turned[head_rows(h), span].astype(F32),
                axis=0,
                keepdims=True,
            )
            grad_scores = (probs * (grad_probs - centre)).astype(BF16)
            turned = dots(m.keys_turned[head_rows(h), :count], grad_scores, NN)
            grad_mixed_turned[head_rows(h), span] = (turned * HEAD**-0.5).astype(BF16)
            m.grad_keys[:count, :] += dots(grad_scores, query, NN)
            m.grad_values[:count, :] += dots(probs.astype(BF16), upstream, NN)
            return 0

        lax.fori_loop(0, 4, one, 0)
        grad_heads[span, :256] = grad_mixed_turned[:, span].T

    for i in range(2):
        m.done_out[i] = (m.middle_keep[i, own_half] + total_out.take(i)).astype(BF16)
    return_out = Return(w, lambda i: m.done_out.at[i], output, spare())
    for i in range(2):
        return_out.start(i)
    unmix(0)
    fold_up.second()
    unmix(1)
    fold_down.third()
    fold_gate.second()
    unmix(2)
    fold_up.third()
    unmix(3)
    fold_gate.third()
    grad_heads[:, 256:512] = (m.grad_keys[...] * HEAD**-0.5).astype(BF16)
    grad_heads[:, 512:] = m.grad_values[...].astype(BF16)

    total_norm.drain()
    total_first = Total(w, m.part_norm, m.core_norm, m.across_norm)

    def first_part(i, part):
        span = pl.ds(pl.multiple_of(256 * (2 * i + part), 256), 256)
        return dots(grad_heads[span, :], m.heads_all[...].reshape(1024, 768), NT)

    for i in range(2):
        total_first.give(i, first_part(i, 1 - k))
    for i in range(2):
        total_first.keep(i, first_part(i, k))
        total_first.send(i)
    for plane in range(2):
        for half in range(2):
            made = dots(m.normed[:, lanes(plane, half)], grad_heads[...], TN)
            m.heads_part[plane, half] = made.astype(BF16).reshape(2, 2, 2, 32, 768)
    fold_heads.start()
    gain_sum = jnp.zeros((1, 1024), F32)

    def done_in(i):
        return m.normed_two.at[pl.ds(128 * i, 128)]

    return_in = Return(w, done_in, input_home, spare())
    for i in range(2):
        grad, term = norm_back(
            m.rows_all[i, k, x].astype(F32), m.gain_rows[0], total_first.take(i)
        )
        gain_sum = gain_sum + term
        done_in(i)[...] = (m.middle_keep[i, other_half] + grad).astype(BF16)
        return_in.start(i)
    gain_rows_part(0, gain_sum)
    fold_gains.start()


    def out_side(z):
        side = 1 - zh if z else zh
        return w.copy(
            m.out_part.at[side, (1 - v + side) % 2], m.out_a.at[side], w.at(v=1 - v), base + 1 + z
        )

    def out_side_landed(z):
        ref = m.out_a.at[1 - zh if z else zh]
        return w.copy(ref, ref, w.at(v=1 - v), base + 1 + z)

    def out_two(side, v):
        at = (v + side) % 2
        return m.out_part[side, at].astype(F32) + m.out_b[side, at].astype(F32)

    far = (v + 1 - zh) % 2
    out_half = w.copy(m.out_part.at[1 - zh, far], m.out_z, w.at(zh=1 - zh), base + 3)
    out_last = w.copy(m.out_deal, m.out_home, w.across(), base + 4)

    @pl.when(owner)
    def _():
        out_across.wait_recv()
        for side in (1, 0):
            at = 1 - zh if side else zh
            m.out_part[at, (1 - v + at) % 2] = out_two(at, 1 - v).astype(BF16)
            out_side(side).start()

    fold_heads.second()
    fold_gains.second()

    @pl.when(owner)
    def _():
        out_side_landed(1).wait_recv()
        m.out_part[1 - zh, far] = (
            out_two(1 - zh, v) + m.out_a[1 - zh].astype(F32)
        ).astype(BF16)
        out_half.start()

    d_out[...] = fold_down.finish()

    def deal_grads(packed, dealt):
        return Deal(
            w, lambda x, k: packed.at[2 * k + x], lambda x, k: dealt.at[2 * x + k]
        )

    deal_up.drain()
    deal_gate.drain()
    deal_heads.drain()
    m.up_pack[...] = fold_up.finish().astype(BF16).reshape(4, 32, 1024)
    deal_up_grad = deal_grads(m.up_pack, up_dealt)
    deal_up_grad.start()
    fold_heads.third()
    fold_gains.third()
    m.gate_pack[...] = fold_gate.finish().astype(BF16).reshape(4, 32, 1024)
    deal_gate_grad = deal_grads(m.gate_pack, gate_dealt)
    deal_gate_grad.start()

    @pl.when(owner)
    def _():
        out_side_landed(0).wait_recv()
        out_half.wait_recv()
        out_total = out_two(zh, v) + m.out_a[zh].astype(F32) + m.out_z[...].astype(F32)
        first, second = out_total[0], out_total[1]
        m.out_deal[...] = jnp.where(x == 0, second, first).astype(BF16)
        out_last.start()
        o_out[...] = jnp.where(x == 0, first, second)

    return_in.arrive()
    m.gains_deal[...] = fold_gains.finish()
    m.gains_dealt[rank] = m.gains_deal[...]
    deal_gains = Deal(w, lambda x, k: m.gains_deal, lambda x, k: m.gains_dealt.at[2 * x + k])
    deal_gains.start()
    m.heads_pack[...] = fold_heads.finish().astype(BF16).reshape(4, 32, 768)
    deal_heads_grad = deal_grads(m.heads_pack, heads_dealt)
    deal_heads_grad.start()
    up_dealt[rank] = m.up_pack[2 * k + x]
    gate_dealt[rank] = m.gate_pack[2 * k + x]
    heads_dealt[rank] = m.heads_pack[2 * k + x]
    deal_up_grad.arrive()
    deal_gate_grad.arrive()
    deal_gains.arrive()
    gain_out[...] = m.gains_dealt[0] + m.gains_dealt[1] + m.gains_dealt[2] + m.gains_dealt[3]
    deal_heads_grad.arrive()

    @pl.when(jnp.logical_not(owner))
    def _():
        out_last.wait_recv()
        o_out[...] = m.out_home[...].astype(F32)

    return_out.arrive()
    for part in [
        visit_rows, visit_cots, spread_gains, spread_heads, spread_out, share_rows, share_cots,
        total_out, total_first, fold_down, fold_gate, fold_up, fold_heads,
        fold_gains, return_out, return_in, deal_up_grad, deal_gate_grad, deal_heads_grad,
        deal_gains,
    ] + share_gains + share_out + shares_branch:
        part.drain()

    @pl.when(owner)
    def _():
        for side in range(2):
            out_side(side).wait_send()
        out_half.wait_send()
        out_last.wait_send()

    pl.when(jnp.logical_not(owner))(lambda: out_across.wait_send())


def finish_body(
    output, input_home, heads, out, gate, up, down,
    output_to, input_to, q_to, k_to, v_to, out_to, gate_to, up_to, down_to,
):
    for dealt, target in ((gate, gate_to), (up, up_to)):
        for r in range(4):
            for j, (start, width) in enumerate(hidden_columns(r)):
                piece = dealt[r, :, 128 * j : 128 * j + width]
                target[:, start : start + width] = piece.astype(F32)
    for r in range(4):
        for j, target in enumerate((q_to, k_to, v_to)):
            piece = heads[r, :, 256 * j : 256 * j + 256]
            target[:, 256 * r : 256 * r + 256] = piece.astype(F32)
    output_to[...] = output[...]
    input_to[...] = input_home[...].astype(F32)
    out_to[...] = out[...]
    down_to[...] = down[...]


def grouped(
    layer_input, doc_ids, attn_gain, query_weight, key_weight, value_weight, out_weight,
    mlp_gain, gate_weight, up_weight, down_weight, out_grad,
):
    dp, ctx = lax.axis_index("dp"), lax.axis_index("ctx")
    k = dp % 2
    piece = attn_gain.shape[0]
    lane = piece * (ctx % 4)
    gains = jnp.zeros((16, 128), BF16)
    gains = lax.dynamic_update_slice(gains, jnp.stack([attn_gain, mlp_gain]), (0, lane))
    d, f = layer_input.shape[2], gate_weight.shape[1]
    outs = (
        shaped(*layer_input.shape),
        shaped(*layer_input.shape),
        shaped(4, piece, 3 * d // 4),
        shaped(piece, d, dtype=F32),
        shaped(4, piece, f // 4),
        shaped(4, piece, f // 4),
        shaped(*down_weight.shape, dtype=F32),
        shaped(8, 128, dtype=F32),
    )
    finals = (
        shaped(*layer_input.shape),
        shaped(*layer_input.shape, dtype=F32),
        shaped(piece, d, dtype=F32),
        shaped(piece, d, dtype=F32),
        shaped(piece, d, dtype=F32),
        shaped(piece, d, dtype=F32),
        shaped(piece, f, dtype=F32),
        shaped(piece, f, dtype=F32),
        shaped(*down_weight.shape, dtype=F32),
    )
    rooms = [pltpu.VMEM(shape, dtype) for _, shape, dtype in SCRATCH]
    made = pl.pallas_call(
        layer_body,
        name="layer",
        out_shape=outs,
        in_specs=[ANY] * 11,
        out_specs=(ANY, ANY) + (VMEM,) * (len(outs) - 2),
        scratch_shapes=rooms
        + [
            pltpu.SemaphoreType.DMA((192,)),
            pltpu.SemaphoreType.DMA((192,)),
            pltpu.SemaphoreType.DMA((24,)),
        ],
        compiler_params=pltpu.CompilerParams(
            collective_id=0, has_side_effects=True, vmem_limit_bytes=61 << 20
        ),
    )(
        layer_input, out_grad, doc_ids.reshape(2, 1, -1), query_weight, key_weight, value_weight,
        out_weight, gate_weight, up_weight, down_weight, gains,
    )
    gain = made[-1]
    output, input_grad, q, k_, v, o, g, u, down = pl.pallas_call(
        finish_body,
        name="finish",
        out_shape=finals,
        in_specs=[VMEM] * 7,
        out_specs=(VMEM,) * len(finals),
        compiler_params=pltpu.CompilerParams(vmem_limit_bytes=58 << 20),
    )(*made[:-1])

    def gain_of(row):
        return lax.dynamic_slice(gain, (row + k, lane), (1, piece)).reshape(piece)

    return (output, input_grad, gain_of(0), q, k_, v, o, gain_of(2), g, u, down)


def plain_product(left, right):
    return jnp.dot(left, right, preferred_element_type=jnp.float32)


def plain_product_left(left, right):
    return lax.dot_general(
        left, right, (((0,), (0,)), ((), ())), preferred_element_type=jnp.float32
    )


def plain_product_right(left, right):
    return lax.dot_general(
        left, right, (((1,), (1,)), ((), ())), preferred_element_type=jnp.float32
    )


def normalize(rows, gain):
    inverse = lax.rsqrt(jnp.mean(rows * rows, axis=-1, keepdims=True) + EPS)
    return (rows * inverse * gain, inverse)


def plain_norm_back(rows, inverse, gain, upstream):
    normed = rows * inverse
    scaled = upstream * gain
    grad_rows = inverse * (scaled - normed * jnp.mean(scaled * normed, axis=-1, keepdims=True))
    return (grad_rows, jnp.sum(upstream * normed, axis=0))


def head_pair(array, start):
    piece = lax.dynamic_slice_in_dim(array, start, 2 * HEAD, 2)
    return piece.reshape(array.shape[0], array.shape[1], 2, HEAD)


def pair_scores(query, keys, allowed, start):
    scores = jnp.einsum(
        "sqhd,skhd->shqk",
        head_pair(query, start),
        head_pair(keys, start),
        preferred_element_type=jnp.float32,
    ) * HEAD ** (-0.5)
    return jnp.where(allowed[:, None], scores, -1e30)


def plain_attend(query, keys, values, allowed):
    groups, rows, width = query.shape

    def step(index, carry):
        mixed_all, logsum = carry
        start = index * 2 * HEAD
        scores = pair_scores(query, keys, allowed, start)
        top = jnp.max(scores, axis=-1, keepdims=True)
        lifted = jnp.exp(scores - top)
        total = jnp.sum(lifted, axis=-1, keepdims=True)
        probs = (lifted / total).astype(jnp.bfloat16)
        mixed = jnp.einsum(
            "shqk,skhd->sqhd", probs, head_pair(values, start), preferred_element_type=jnp.float32
        )
        mixed_all = lax.dynamic_update_slice_in_dim(
            mixed_all, mixed.reshape(groups, rows, 2 * HEAD).astype(jnp.bfloat16), start, 2
        )
        logsum = lax.dynamic_update_slice_in_dim(
            logsum, (top + jnp.log(total))[..., 0], index * 2, 1
        )
        return (mixed_all, logsum)

    start_state = (
        jnp.zeros((groups, rows, width), jnp.bfloat16),
        jnp.zeros((groups, width // HEAD, rows), jnp.float32),
    )
    return lax.fori_loop(0, width // (2 * HEAD), step, start_state)


def plain_attend_back(query, keys, values, allowed, logsum, grad_mixed):
    groups, rows, width = query.shape
    length = keys.shape[1]
    scale = HEAD ** (-0.5)

    def step(index, carry):
        grad_query, grad_keys, grad_values = carry
        start = index * 2 * HEAD
        scores = pair_scores(query, keys, allowed, start)
        kept = lax.dynamic_slice_in_dim(logsum, index * 2, 2, 1)
        probs = jnp.exp(scores - kept[..., None])
        upstream = head_pair(grad_mixed, start)
        grad_probs = jnp.einsum(
            "sqhd,skhd->shqk",
            upstream,
            head_pair(values, start),
            preferred_element_type=jnp.float32,
        )
        grad_scores = (
            probs * (grad_probs - jnp.sum(probs * grad_probs, axis=-1, keepdims=True))
        ).astype(jnp.bfloat16)
        part_query = (
            jnp.einsum(
                "shqk,skhd->sqhd",
                grad_scores,
                head_pair(keys, start),
                preferred_element_type=jnp.float32,
            )
            * scale
        )
        part_keys = (
            jnp.einsum(
                "shqk,sqhd->skhd",
                grad_scores,
                head_pair(query, start),
                preferred_element_type=jnp.float32,
            )
            * scale
        )
        part_values = jnp.einsum(
            "shqk,sqhd->skhd",
            probs.astype(jnp.bfloat16),
            upstream,
            preferred_element_type=jnp.float32,
        )
        grad_query = lax.dynamic_update_slice_in_dim(
            grad_query, part_query.reshape(groups, rows, 2 * HEAD), start, 2
        )
        grad_keys = lax.dynamic_update_slice_in_dim(
            grad_keys, part_keys.reshape(groups, length, 2 * HEAD), start, 2
        )
        grad_values = lax.dynamic_update_slice_in_dim(
            grad_values, part_values.reshape(groups, length, 2 * HEAD), start, 2
        )
        return (grad_query, grad_keys, grad_values)

    start_state = (
        jnp.zeros((groups, rows, width), jnp.float32),
        jnp.zeros((groups, length, width), jnp.float32),
        jnp.zeros((groups, length, width), jnp.float32),
    )
    return lax.fori_loop(0, width // (2 * HEAD), step, start_state)


def on_device(
    layer_input,
    doc_ids,
    attn_gain,
    query_weight,
    key_weight,
    value_weight,
    out_weight,
    mlp_gain,
    gate_weight,
    up_weight,
    down_weight,
    out_grad,
):
    groups, rows, width = layer_input.shape
    length = doc_ids.shape[1]
    gathered = (
        lax.all_gather(attn_gain, ("dp", "ctx"), axis=0, tiled=True),
        lax.all_gather(query_weight, ("dp", "ctx"), axis=0, tiled=True),
        lax.all_gather(key_weight, ("dp", "ctx"), axis=0, tiled=True),
        lax.all_gather(value_weight, ("dp", "ctx"), axis=0, tiled=True),
        lax.all_gather(out_weight, ("dp", "ctx"), axis=0, tiled=True),
        lax.all_gather(mlp_gain, ("dp", "ctx"), axis=0, tiled=True),
        lax.all_gather(gate_weight, ("dp", "ctx"), axis=0, tiled=True),
        lax.all_gather(up_weight, ("dp", "ctx"), axis=0, tiled=True),
        lax.all_gather(down_weight, ("dp", "ctx"), axis=0, tiled=True),
    )
    gain_one, w_query, w_key, w_value, w_out, gain_two, w_gate, w_up, w_down = gathered
    first = lax.axis_index("ctx") * rows
    places = jnp.arange(length)
    own_ids = lax.dynamic_slice_in_dim(doc_ids, first, rows, 1)
    own_places = first + jnp.arange(rows)
    allowed = (own_ids[:, :, None] == doc_ids[:, None, :]) & (
        places[None, None, :] <= own_places[None, :, None]
    )
    inputs = layer_input.reshape(groups * rows, width).astype(jnp.float32)
    gain_attn = gain_one.astype(jnp.float32)
    normed_full, inverse_one = normalize(inputs, gain_attn)
    normed = normed_full.astype(jnp.bfloat16)
    query = plain_product(normed, w_query).astype(jnp.bfloat16).reshape(groups, rows, width)
    keys_own = plain_product(normed, w_key).astype(jnp.bfloat16).reshape(groups, rows, width)
    values_own = plain_product(normed, w_value).astype(jnp.bfloat16).reshape(groups, rows, width)
    keys, values = (
        lax.all_gather(keys_own, "ctx", axis=1, tiled=True),
        lax.all_gather(values_own, "ctx", axis=1, tiled=True),
    )
    attended, logsum = plain_attend(query, keys, values, allowed)
    attended_rows = attended.reshape(groups * rows, width)
    middle = inputs + plain_product(attended_rows, w_out)
    gain_mlp = gain_two.astype(jnp.float32)
    normed_two_full, inverse_two = normalize(middle, gain_mlp)
    normed_two = normed_two_full.astype(jnp.bfloat16)
    gate = plain_product(normed_two, w_gate)
    upward = plain_product(normed_two, w_up)
    sigma = jax.nn.sigmoid(gate)
    hidden = (gate * sigma * upward).astype(jnp.bfloat16)
    layer_output = (middle + plain_product(hidden, w_down)).astype(jnp.bfloat16)
    gathered_back = (
        lax.all_gather(attn_gain, ("dp", "ctx"), axis=0, tiled=True),
        lax.all_gather(query_weight, ("dp", "ctx"), axis=0, tiled=True),
        lax.all_gather(key_weight, ("dp", "ctx"), axis=0, tiled=True),
        lax.all_gather(value_weight, ("dp", "ctx"), axis=0, tiled=True),
        lax.all_gather(out_weight, ("dp", "ctx"), axis=0, tiled=True),
        lax.all_gather(mlp_gain, ("dp", "ctx"), axis=0, tiled=True),
        lax.all_gather(gate_weight, ("dp", "ctx"), axis=0, tiled=True),
        lax.all_gather(up_weight, ("dp", "ctx"), axis=0, tiled=True),
        lax.all_gather(down_weight, ("dp", "ctx"), axis=0, tiled=True),
    )
    gain_one, w_query, w_key, w_value, w_out, gain_two, w_gate, w_up, w_down = gathered_back
    upstream = out_grad.reshape(groups * rows, width)
    down_grad = plain_product_left(hidden, upstream)
    grad_hidden = plain_product_right(upstream, w_down)
    grad_gate = (grad_hidden * upward * sigma * (1.0 + gate * (1.0 - sigma))).astype(jnp.bfloat16)
    grad_up = (grad_hidden * gate * sigma).astype(jnp.bfloat16)
    gate_grad = plain_product_left(normed_two, grad_gate)
    up_grad = plain_product_left(normed_two, grad_up)
    grad_normed_two = plain_product_right(grad_gate, w_gate) + plain_product_right(grad_up, w_up)
    grad_middle, mlp_gain_grad = plain_norm_back(
        middle, inverse_two, gain_two.astype(jnp.float32), grad_normed_two
    )
    grad_middle = grad_middle + upstream.astype(jnp.float32)
    grad_branch = grad_middle.astype(jnp.bfloat16)
    out_proj_grad = plain_product_left(attended_rows, grad_branch)
    grad_attended = (
        plain_product_right(grad_branch, w_out).astype(jnp.bfloat16).reshape(groups, rows, width)
    )
    grad_query, grad_keys_all, grad_values_all = plain_attend_back(
        query, keys, values, allowed, logsum, grad_attended
    )
    grad_keys, grad_values = (
        lax.psum_scatter(
            grad_keys_all.astype(jnp.bfloat16), "ctx", scatter_dimension=1, tiled=True
        ).astype(jnp.float32),
        lax.psum_scatter(
            grad_values_all.astype(jnp.bfloat16), "ctx", scatter_dimension=1, tiled=True
        ).astype(jnp.float32),
    )
    grad_query = grad_query.astype(jnp.bfloat16).reshape(groups * rows, width)
    grad_keys = grad_keys.astype(jnp.bfloat16).reshape(groups * rows, width)
    grad_values = grad_values.astype(jnp.bfloat16).reshape(groups * rows, width)
    query_grad = plain_product_left(normed, grad_query)
    key_grad = plain_product_left(normed, grad_keys)
    value_grad = plain_product_left(normed, grad_values)
    grad_normed = (
        plain_product_right(grad_query, w_query)
        + plain_product_right(grad_keys, w_key)
        + plain_product_right(grad_values, w_value)
    )
    grad_inputs, attn_gain_grad = plain_norm_back(
        inputs, inverse_one, gain_one.astype(jnp.float32), grad_normed
    )
    input_grad = (grad_middle + grad_inputs).reshape(groups, rows, width)
    shares = (
        lax.psum_scatter(attn_gain_grad, ("dp", "ctx"), scatter_dimension=0, tiled=True),
        lax.psum_scatter(query_grad, ("dp", "ctx"), scatter_dimension=0, tiled=True),
        lax.psum_scatter(key_grad, ("dp", "ctx"), scatter_dimension=0, tiled=True),
        lax.psum_scatter(value_grad, ("dp", "ctx"), scatter_dimension=0, tiled=True),
        lax.psum_scatter(out_proj_grad, ("dp", "ctx"), scatter_dimension=0, tiled=True),
        lax.psum_scatter(mlp_gain_grad, ("dp", "ctx"), scatter_dimension=0, tiled=True),
        lax.psum_scatter(gate_grad, ("dp", "ctx"), scatter_dimension=0, tiled=True),
        lax.psum_scatter(up_grad, ("dp", "ctx"), scatter_dimension=0, tiled=True),
        lax.psum_scatter(down_grad, ("dp", "ctx"), scatter_dimension=0, tiled=True),
    )
    return (
        layer_output.reshape(groups, rows, width),
        input_grad,
        shares[0],
        shares[1],
        shares[2],
        shares[3],
        shares[4],
        shares[5],
        shares[6],
        shares[7],
        shares[8],
    )


def solution(mesh):
    placed = (
        P("dp", "ctx", None),
        P("dp", None),
        P(("dp", "ctx")),
        P(("dp", "ctx"), None),
        P(("dp", "ctx"), None),
        P(("dp", "ctx"), None),
        P(("dp", "ctx"), None),
        P(("dp", "ctx")),
        P(("dp", "ctx"), None),
        P(("dp", "ctx"), None),
        P(("dp", "ctx"), None),
        P("dp", "ctx", None),
    )
    fits = mesh.shape["dp"] == 4 and mesh.shape["ctx"] == 8
    body = grouped if fits else on_device
    return jax.shard_map(
        body,
        mesh=mesh,
        in_specs=placed,
        out_specs=(
            P("dp", "ctx", None),
            P("dp", "ctx", None),
            P(("dp", "ctx")),
            P(("dp", "ctx"), None),
            P(("dp", "ctx"), None),
            P(("dp", "ctx"), None),
            P(("dp", "ctx"), None),
            P(("dp", "ctx")),
            P(("dp", "ctx"), None),
            P(("dp", "ctx"), None),
            P(("dp", "ctx"), None),
        ),
        check_vma=False,
    )
```
